32 devices in a mesh: dp: 8 (over y, x, core), stream: 4 (over z).
Axes of the slice: x: 2, y: 2, z: 4, core: 2. Of those that a mesh axis runs over, the one named last changes fastest.
Arguments:
- history: bfloat16 [8, 4096, 2048], P(None, 'dp'), may hold values from -6 to 6
- mixing: float32 [4096, 4, 8], P('dp', 'stream'), may hold values from -2 to 2
- shard_offset: int32 [8], P('dp'), may hold values from 0 to 3584, as said below
- norm_gain: bfloat16 [4, 2048], P('stream'), may hold values from 0.099609375 to 1.8984375
- norm_bias: bfloat16 [4, 2048], P('stream'), may hold values from -1.75 to 1.75
- w_heads: bfloat16 [3, 2048, 2048], P(None, 'dp', 'stream'), may hold values from -0.125 to 0.125
- w_merge: bfloat16 [2048, 2048], P('stream', 'dp'), may hold values from -3 to 3
- w_up: bfloat16 [2048, 8192], P('dp', 'stream'), may hold values from -0.125 to 0.125
- w_down: bfloat16 [8192, 2048], P('stream', 'dp'), may hold values from -0.0625 to 0.0625
- mixer_first: bfloat16 [2048, 36], P('stream'), may hold values from -0.125 to 0.125
- mixer_second: bfloat16 [36, 4, 9], P(None, 'stream'), may hold values from -1 to 1
- out_cotangent: bfloat16 [4096, 2048], P('dp', 'stream'), may hold values from -6 to 6
- next_cotangent: float32 [4096, 4, 9], P('dp', 'stream'), may hold values from -6 to 6
Outputs:
- block_out: bfloat16 [4096, 2048], P('dp', 'stream')
- next_mixing: float32 [4096, 4, 9], P('dp', 'stream')
- grad_history: float32 [8, 4096, 2048], P('stream', 'dp')
- grad_mixing: float32 [4096, 4, 8], P('dp', 'stream')
- grad_gain: float32 [4, 2048], P('stream')
- grad_bias: float32 [4, 2048], P('stream')
- grad_heads: float32 [3, 2048, 2048], P(None, 'dp', 'stream')
- grad_merge: float32 [2048, 2048], P('stream', 'dp')
- grad_up: float32 [2048, 8192], P('dp', 'stream')
- grad_down: float32 [8192, 2048], P('stream', 'dp')
- grad_first: float32 [2048, 36], P('stream')
- grad_second: float32 [36, 4, 9], P(None, 'stream')
The draws below stay inside these ranges and needn't reach their ends.
Inputs may be any that keep to these rules, and one draw needn't show every extreme that they name: `shard_offset`: sequences of 2048 and 4096 tokens are packed end to end, each new one starting at the first token of a shard; the first may have begun before the first token and the last may be cut off at the end. Entry i is the position, within its sequence, of the first token of shard i.
All inputs are finite; a program needn't handle non-finite values.
Results may differ from the reference program's by a relative error of at most 0.012.
Values may be sent and summed in bfloat16 or wider, within the bound.
No kernel may reach another device: no remote copies, remote signals or barrier semaphores. Data moves between devices by JAX's collectives and lax.ppermute only.
A program may use at most 256 MiB of HBM per device.

```python
import math
from functools import partial
import jax
import jax.numpy as jnp
from jax import lax

D = 2048
HEADS = 16
HD = 128
ROT = 32
FF = 8192
STREAMS = 4
HIST = 8
SEQ = 2048
TOK_DP = 512
NEXT = 9
MIXH = 36
SHARDS = 8
TOKENS = 4096


def draw_shard_offset(key, part):
    units = SEQ // TOK_DP
    count = SHARDS // units + 2
    coins = jax.random.randint(jax.random.fold_in(key, 21), (count,), 1, 3)
    lengths = jnp.where(jnp.arange(count, dtype=jnp.int32) == 0, 2, coins) * units
    ends = jnp.cumsum(lengths).astype(jnp.int32)
    entry = jax.random.randint(jax.random.fold_in(key, 22), (), 0, 2 * units)
    place = jnp.arange(SHARDS, dtype=jnp.int32) + entry
    starts = jnp.max(jnp.where(ends[None, :] <= place[:, None], ends[None, :], 0), axis=1)
    return ((place - starts) * TOK_DP).astype(jnp.int32)


def levels(rng, shape, cuts, low, largest):
    loudness, own = 1.0, jax.random.fold_in(rng, 6)
    for dim, parts in cuts:
        steps = jnp.exp(jax.random.uniform(jax.random.fold_in(own, dim), (parts,), jnp.float32, low / len(cuts), largest / len(cuts)))
        loudness = loudness * jnp.repeat(steps, shape[dim] // parts).reshape([-1 if axis == dim else 1 for axis in range(len(shape))])
    return loudness


def gaussian(stream_key, dims, spread, bound, cuts=(), kind=jnp.bfloat16):
    values = spread * jax.random.normal(stream_key, dims, jnp.float32)
    if cuts:
        values = values * levels(stream_key, dims, cuts, -0.22, 0.18)
    return jnp.clip(values, -bound, bound).astype(kind)


def setup_inputs(seed: int = 0) -> dict:
    key_list = jax.random.split(jax.random.key(seed), 14)
    return {
        "history": gaussian(key_list[0], (HIST, TOKENS, D), 1.0, 6.0, ((1, 8),)),
        "mixing": gaussian(key_list[1], (TOKENS, STREAMS, HIST), 0.35, 2.0, ((0, 8), (1, 4)), jnp.float32),
        "shard_offset": draw_shard_offset(jax.random.fold_in(key_list[13], 71), 0),
        "norm_gain": jnp.clip(1.0 + 0.18 * jax.random.normal(key_list[3], (STREAMS, D), jnp.float32), 0.099609375, 1.8984375).astype(jnp.bfloat16),
        "norm_bias": gaussian(key_list[4], (STREAMS, D), 0.3, 1.75, ((0, 4),)),
        "w_heads": gaussian(key_list[5], (3, D, D), D ** -0.5, 0.125, ((1, 8), (2, 4))),
        "w_merge": gaussian(key_list[6], (D, D), (max(1, 4 * D // SEQ)) ** -0.5, 3.0, ((0, 4), (1, 8))),
        "w_up": gaussian(key_list[7], (D, FF), D ** -0.5, 0.125, ((0, 8), (1, 4))),
        "w_down": gaussian(key_list[8], (FF, D), FF ** -0.5, 0.0625, ((0, 4), (1, 8))),
        "mixer_first": gaussian(key_list[9], (D, MIXH), D ** -0.5, 0.125, ((0, 4),)),
        "mixer_second": gaussian(key_list[10], (MIXH, STREAMS, NEXT), MIXH ** -0.5, 1.0, ((1, 4),)),
        "out_cotangent": gaussian(key_list[11], (TOKENS, D), 1.0, 6.0, ((0, 8), (1, 4))),
        "next_cotangent": gaussian(key_list[12], (TOKENS, STREAMS, NEXT), 1.0, 6.0, ((0, 8), (1, 4)), jnp.float32),
    }


@jax.custom_vjp
def low(v):
    return lax.optimization_barrier(v.astype(jnp.bfloat16)).astype(jnp.float32)

@jax.custom_vjp
def low_back(v):
    return v

def low_keep(v):
    return (low(v), None)

def low_pass(kept, grad):
    return (grad,)

def back_keep(v):
    return (v, None)

def back_low(kept, grad):
    return (low(grad),)
low.defvjp(low_keep, low_pass)
low_back.defvjp(back_keep, back_low)

def matmul_high(left, right):
    return jnp.dot(left, right, precision=lax.Precision.HIGHEST, preferred_element_type=jnp.float32)

def rotate(vectors, positions, sign):
    half = ROT // 2
    counter = jnp.arange(half, dtype=jnp.float32)
    freqs = jnp.exp(counter * (-2.0 * math.log(10000.0) / ROT))
    angles = positions.astype(jnp.float32)[:, None] * freqs[None, :]
    cosine = jnp.cos(angles)[:, None, :]
    sine = sign * jnp.sin(angles)[:, None, :]
    first = vectors[..., :half]
    second = vectors[..., half:ROT]
    return jnp.concatenate([first * cosine - second * sine, second * cosine + first * sine, vectors[..., ROT:]], axis=-1)

def layer_norm(vectors, gain, bias):
    center = vectors - lax.optimization_barrier(jnp.mean(vectors, axis=-1, keepdims=True))
    variance = lax.optimization_barrier(jnp.mean(center * center, axis=-1, keepdims=True))
    return center * lax.rsqrt(variance + 1e-05) * gain + bias

def head_attention(query, key, value, allowed):
    logits = low_back(matmul_high(query, key.T) * (1.0 / math.sqrt(HD)))
    logits = jnp.where(allowed, logits, -1e+30)
    shifted = jnp.exp(logits - lax.optimization_barrier(jnp.max(logits, axis=-1, keepdims=True)))
    weights = shifted / lax.optimization_barrier(jnp.sum(shifted, axis=-1, keepdims=True))
    return matmul_high(low(weights), value)

def sequence_block(pieces):
    queries, keys, values, query_starts, key_starts = pieces
    rows = query_starts.shape[0]
    query_count = jnp.arange(rows, dtype=jnp.int32) + rows
    key_count = jnp.arange(key_starts.shape[0], dtype=jnp.int32)
    allowed = (query_starts[:, None] == key_starts[None, :]) & (key_count[None, :] <= query_count[:, None])

    def one_head(items):
        return head_attention(items[0], items[1], items[2], allowed)
    outputs = lax.map(jax.checkpoint(one_head), (jnp.transpose(queries, (1, 0, 2)), jnp.transpose(keys, (1, 0, 2)), jnp.transpose(values, (1, 0, 2))))
    return jnp.transpose(outputs, (1, 0, 2))

def forward(history, mixing, norm_gain, norm_bias, w_heads, w_merge, w_up, w_down, mixer_first, mixer_second, positions):
    tokens = history.shape[1]
    streams = jnp.einsum('tsj,jtd->std', mixing, history, precision=lax.Precision.HIGHEST)
    normed = low(layer_norm(streams, norm_gain[:, None, :], norm_bias[:, None, :]))

    def split_heads(matrix):
        return matrix.reshape(tokens, HEADS, HD)
    queries = low(rotate(split_heads(low_back(matmul_high(normed[0], w_heads[0]))), positions, 1.0))
    keys = low(rotate(split_heads(low_back(matmul_high(normed[1], w_heads[1]))), positions, 1.0))
    values = low(split_heads(low_back(matmul_high(normed[2], w_heads[2]))))
    starts = jnp.arange(tokens, dtype=jnp.int32) - positions
    block_len = 2 * SEQ
    count = tokens // block_len

    def blocked(matrix):
        return matrix.reshape(count, block_len, HEADS, HD)

    def paired(matrix):
        cur = blocked(matrix)
        prev = jnp.concatenate([jnp.zeros_like(cur[:1]), cur[:-1]], axis=0)
        return jnp.concatenate([prev, cur], axis=1)
    start_blocks = starts.reshape(count, block_len)
    prev_starts = jnp.concatenate([jnp.full((1, block_len), -2 ** 30, jnp.int32), start_blocks[:-1]], axis=0)
    key_starts = jnp.concatenate([prev_starts, start_blocks], axis=1).astype(jnp.int32)
    attended = lax.map(jax.checkpoint(sequence_block), (blocked(queries), paired(keys), paired(values), start_blocks, key_starts))
    attended = low(low_back(attended.reshape(tokens, D)))
    up = low_back(matmul_high(normed[3], w_up))
    hidden = low(jax.nn.gelu(up, approximate=False))
    block_out = low(low_back(streams[3] + matmul_high(attended, w_merge) + matmul_high(hidden, w_down)))
    scale_rows = lax.rsqrt(lax.optimization_barrier(jnp.mean(block_out * block_out, axis=-1, keepdims=True)) + 1e-06)
    mixer = jax.nn.gelu(scale_rows * low_back(matmul_high(block_out, mixer_first)), approximate=False)
    next_mixing = matmul_high(mixer, mixer_second.reshape(MIXH, STREAMS * NEXT)).reshape(tokens, STREAMS, NEXT)
    return (block_out, next_mixing)

def reference(history, mixing, shard_offset, norm_gain, norm_bias, w_heads, w_merge, w_up, w_down, mixer_first, mixer_second, out_cotangent, next_cotangent):
    positions = (shard_offset[:, None] + jnp.arange(TOK_DP, dtype=jnp.int32)[None, :]).reshape(-1).astype(jnp.int32)
    floats = tuple((item.astype(jnp.float32) for item in (history, mixing, norm_gain, norm_bias, w_heads, w_merge, w_up, w_down, mixer_first, mixer_second)))
    outputs, pullback = jax.vjp(partial(forward, positions=positions), *floats)
    grads = pullback((out_cotangent.astype(jnp.float32), next_cotangent.astype(jnp.float32)))
    return (outputs[0].astype(jnp.bfloat16), outputs[1], grads[0], grads[1], grads[2], grads[3], grads[4], grads[5], grads[6], grads[7], grads[8], grads[9])
```

```python
import math

import jax
import jax.numpy as jnp
from jax import lax
from jax.experimental import pallas as pl
from jax.experimental.pallas import tpu as pltpu
from jax.sharding import PartitionSpec as P

HD = 128
ROT = 32
SEQ = 2048


def passed_along(shard, axis, by):
    peers = lax.axis_size(axis)
    pairs = [(i, i + by) for i in range(peers) if 0 <= i + by < peers]
    return lax.ppermute(shard, axis, pairs)


def rotate(vectors, positions, sign):
    half = ROT // 2
    counter = jnp.arange(half, dtype=jnp.float32)
    freqs = jnp.exp(counter * (-2.0 * math.log(10000.0) / ROT))
    angles = positions.astype(jnp.float32)[:, None] * freqs[None, :]
    cosine = jnp.cos(angles)[:, None, :]
    sine = sign * jnp.sin(angles)[:, None, :]
    first = vectors[..., :half]
    second = vectors[..., half:ROT]
    return jnp.concatenate(
        [first * cosine - second * sine, second * cosine + first * sine, vectors[..., ROT:]],
        axis=-1,
    )


def exact_gelu(vectors):
    return jax.nn.gelu(vectors, approximate=False)


def block_logits(queries, keys_block, diagonal):
    logits = jnp.einsum("qhd,khd->hqk", queries, keys_block, preferred_element_type=jnp.float32) * (
        1.0 / math.sqrt(queries.shape[-1])
    )
    if diagonal:
        counter = jnp.arange(queries.shape[0], dtype=jnp.int32)
        allowed = counter[None, :] <= counter[:, None]
        logits = jnp.where(allowed[None], logits, -1e30)
    return logits


def keep_same(state):
    return state


BF = jnp.bfloat16
F32 = jnp.float32
OUTWARD = [(0, 1), (3, 2)]
MIDDLE = [(1, 2), (2, 1)]
INWARD = [(1, 0), (2, 3)]


def dot(left, right):
    return jnp.dot(left, right, preferred_element_type=F32)


def dot_rows(left, right):
    return lax.dot_general(left, right, (((0,), (0,)), ((), ())), preferred_element_type=F32)


def dot_cols(left, right):
    return lax.dot_general(left, right, (((1,), (1,)), ((), ())), preferred_element_type=F32)


def partner(shard, bit):
    peers = lax.axis_size("dp")
    return lax.ppermute(shard, "dp", [(i, i ^ bit) for i in range(peers)])


def line_hop(shard, pairs):
    return lax.ppermute(shard, "stream", pairs)


def after(value, *others):
    return lax.optimization_barrier((value, *others))[0]


def gather_weights(shards):
    peers = lax.axis_size("dp")
    if peers != 8:
        return [lax.all_gather(shard, "dp", axis=0) for shard in shards]
    index = lax.axis_index("dp")
    full = []
    ahead = None
    for shard in shards:
        if ahead is not None:
            shard = after(shard, *ahead)
        by_x = partner(shard, 2)
        by_y = partner(shard, 4)
        ahead = (by_x, by_y)
        cut = max(range(shard.ndim - 1), key=lambda dim: shard.shape[dim])
        half = shard.shape[cut] // 2
        low = lax.slice_in_dim(by_y, 0, half, axis=cut)
        high = lax.slice_in_dim(by_x, half, 2 * half, axis=cut)
        pieces = [
            (shard, 0, 0),
            (by_x, 2, 0),
            (by_y, 4, 0),
            (partner(low, 2), 6, 0),
            (partner(high, 4), 6, half),
        ]
        pieces += [(partner(piece, 1), code ^ 1, start) for piece, code, start in pieces]
        whole = jnp.zeros((peers, *shard.shape), shard.dtype)
        for piece, code, start in pieces:
            place = [jnp.int32(0)] * (shard.ndim + 1)
            place[0] = index ^ code
            place[cut + 1] = jnp.int32(start)
            whole = lax.dynamic_update_slice(whole, piece[None], place)
        full.append(whole)
    return full


def rope_tables(positions, sign):
    half = ROT // 2
    lane = jnp.arange(HD, dtype=jnp.int32)
    counter = (lane % half).astype(F32)
    freqs = jnp.exp(counter * (-2.0 * math.log(10000.0) / ROT))
    angles = positions.astype(F32)[:, None] * freqs[None, :]
    cosine = jnp.where(lane < ROT, jnp.cos(angles), 1.0)
    sine = sign * jnp.sin(angles)
    up = jnp.where(lane < half, -sine, 0.0)
    down = jnp.where((lane >= half) & (lane < ROT), sine, 0.0)
    return jnp.stack([cosine, up, down])


def turned(block, tables):
    half = ROT // 2
    return (
        block * tables[0]
        + pltpu.roll(block, HD - half, 1) * tables[1]
        + pltpu.roll(block, half, 1) * tables[2]
    )


def make_streams(history, mix_rows, gains, biases):
    entries, tokens, width = history.shape
    streams = gains.shape[0]
    rows, sub, lanes = min(64, tokens), 16, 512

    def kernel(hist, mix, gain, bias, normed, unit, inv, last, scratch):
        def step(r, carry):
            here = pl.ds(pl.multiple_of(r * sub, sub), sub)
            weights = mix[here, :]
            columns = [
                [weights[:, s * entries + j : s * entries + j + 1] for j in range(entries)]
                for s in range(streams)
            ]
            for lane in range(0, width, lanes):
                span = slice(lane, lane + lanes)
                sums = [None] * streams
                for j in range(entries):
                    part = hist[j, here, span].astype(F32)
                    for s in range(streams):
                        term = columns[s][j] * part
                        sums[s] = term if j == 0 else sums[s] + term
                for s in range(streams):
                    scratch[s, :, span] = sums[s]
            stds = []
            for s in range(streams):
                values = scratch[s]
                center = values - jnp.sum(values, axis=-1, keepdims=True) * (1.0 / width)
                var = jnp.sum(center * center, axis=-1, keepdims=True) * (1.0 / width)
                std = lax.rsqrt(var + 1e-05)
                stds.append(std)
                scaled = center * std
                unit[s, here, :] = scaled.astype(BF)
                normed[s, here, :] = (scaled * gain[s : s + 1] + bias[s : s + 1]).astype(BF)
            last[here, :] = scratch[streams - 1]
            inv[here, :] = jnp.concatenate(stds, axis=-1)
            return carry

        lax.fori_loop(0, rows // sub, step, 0)

    wide = jax.ShapeDtypeStruct((streams, tokens, width), BF)
    return pl.pallas_call(
        kernel,
        grid=(tokens // rows,),
        in_specs=[
            pl.BlockSpec((entries, rows, width), lambda i: (0, i, 0)),
            pl.BlockSpec((rows, streams * entries), lambda i: (i, 0)),
            pl.BlockSpec((streams, width), lambda i: (0, 0)),
            pl.BlockSpec((streams, width), lambda i: (0, 0)),
        ],
        out_specs=[
            pl.BlockSpec((streams, rows, width), lambda i: (0, i, 0)),
            pl.BlockSpec((streams, rows, width), lambda i: (0, i, 0)),
            pl.BlockSpec((rows, streams), lambda i: (i, 0)),
            pl.BlockSpec((rows, width), lambda i: (i, 0)),
        ],
        out_shape=[
            wide,
            wide,
            jax.ShapeDtypeStruct((tokens, streams), F32),
            jax.ShapeDtypeStruct((tokens, width), F32),
        ],
        scratch_shapes=[pltpu.VMEM((streams, sub, width), F32)],
        name="make_streams",
    )(history, mix_rows, gains, biases)


def project(normed, w_heads, tables):
    _, tokens, width = normed.shape
    columns = w_heads.shape[3]
    heads, half = columns // HD, tokens // 2

    def kernel(x, w, table, out):
        flat = dot(x[0], w[...].reshape(width, columns))
        turn = pl.program_id(0) < 2

        def put(head, block):
            out[2 * head, 0] = block[:half].astype(BF)
            out[2 * head + 1, 0] = block[half:].astype(BF)

        @pl.when(turn)
        def _():
            for head in range(heads):
                put(head, turned(flat[:, head * HD : (head + 1) * HD], table[...]))

        @pl.when(jnp.logical_not(turn))
        def _():
            for head in range(heads):
                put(head, flat[:, head * HD : (head + 1) * HD])

    return pl.pallas_call(
        kernel,
        grid=(3,),
        in_specs=[
            pl.BlockSpec((1, tokens, width), lambda c: (c, 0, 0)),
            pl.BlockSpec((w_heads.shape[0], 1, w_heads.shape[2], columns), lambda c: (0, c, 0, 0)),
            pl.BlockSpec((3, tokens, HD), lambda c: (0, 0, 0)),
        ],
        out_specs=pl.BlockSpec((2 * heads, 1, half, HD), lambda c: (0, c, 0, 0)),
        out_shape=jax.ShapeDtypeStruct((2 * heads, 3, half, HD), BF),
        name="project",
    )(normed, w_heads, tables)


def attend(own, other, first_key, side):
    shards, _, half, _ = own.shape
    factor = 1.0 / math.sqrt(HD)

    def kernel(first, part, mine, theirs, out, exact, norm):
        s = pl.program_id(0)
        query = mine[s, 0]

        def fold(state, keys, values, mask):
            top, total, acc = state
            logits = dot_cols(query, keys) * factor
            if mask is not None:
                logits = jnp.where(mask, logits, -1e30)
            new_top = jnp.maximum(top, jnp.max(logits, axis=-1, keepdims=True))
            probs = jnp.exp(logits - new_top)
            keep = jnp.exp(top - new_top)
            return (
                new_top,
                total * keep + jnp.sum(probs, axis=-1, keepdims=True),
                acc * keep + dot(probs.astype(BF), values),
            )

        row = lax.broadcasted_iota(jnp.int32, (half, half), 0)
        col = lax.broadcasted_iota(jnp.int32, (half, half), 1)
        state = (
            jnp.full((half, 1), -1e30, F32),
            jnp.zeros((half, 1), F32),
            jnp.zeros((half, HD), F32),
        )
        state = fold(state, mine[s, 1], mine[s, 2], col <= row)
        state = lax.fori_loop(
            0, part[0], lambda i, st: fold(st, theirs[s, 0], theirs[s, 1], None), state
        )

        def shard_step(b, st):
            st = fold(st, mine[b, 1], mine[b, 2], None)
            return fold(st, theirs[b, 0], theirs[b, 1], None)

        top, total, acc = lax.fori_loop(first[s], s, shard_step, state)
        result = acc / total
        out[0] = result.astype(BF)
        exact[0] = result
        norm[0] = top + jnp.log(total)

    return pl.pallas_call(
        kernel,
        grid_spec=pltpu.PrefetchScalarGridSpec(
            num_scalar_prefetch=2,
            grid=(shards,),
            in_specs=[
                pl.BlockSpec((shards, 3, half, HD), lambda s, *_: (0, 0, 0, 0)),
                pl.BlockSpec((shards, 2, half, HD), lambda s, *_: (0, 0, 0, 0)),
            ],
            out_specs=[
                pl.BlockSpec((1, half, HD), lambda s, *_: (s, 0, 0)),
                pl.BlockSpec((1, half, HD), lambda s, *_: (s, 0, 0)),
                pl.BlockSpec((1, half, 1), lambda s, *_: (s, 0, 0)),
            ],
        ),
        out_shape=[
            jax.ShapeDtypeStruct((shards, half, HD), BF),
            jax.ShapeDtypeStruct((shards, half, HD), F32),
            jax.ShapeDtypeStruct((shards, half, 1), F32),
        ],
        name="attend",
    )(first_key, side, own, other)


def attend_back(own, other, grads, exact, norm, first_key, side):
    shards, _, half, _ = own.shape
    factor = 1.0 / math.sqrt(HD)

    def kernel(first, part, mine, theirs, grad_ref, exact_ref, norm_ref, kept, given, sums):
        s = pl.program_id(0)
        query = mine[s, 0]
        grad = grad_ref[s]
        delta = jnp.sum(grad.astype(F32) * exact_ref[0], axis=-1, keepdims=True)
        level = norm_ref[0]
        lowered = grad

        @pl.when(s == 0)
        def _():
            sums[...] = jnp.zeros_like(sums)

        def fold(query_grad, keys, values, mask, slot, b):
            logits = dot_cols(query, keys) * factor
            probs = jnp.exp(logits - level)
            if mask is not None:
                probs = jnp.where(mask, probs, 0.0)
            score = (probs * (dot_cols(grad, values) - delta)).astype(BF)
            sums[slot, b] += dot_rows(score, query)
            sums[slot + 1, b] += dot_rows(probs.astype(BF), lowered)
            return query_grad + dot(score, keys)

        row = lax.broadcasted_iota(jnp.int32, (half, half), 0)
        col = lax.broadcasted_iota(jnp.int32, (half, half), 1)
        total = fold(jnp.zeros((half, HD), F32), mine[s, 1], mine[s, 2], col <= row, 0, s)
        total = lax.fori_loop(
            0, part[0], lambda i, q: fold(q, theirs[s, 0], theirs[s, 1], None, 2, s), total
        )

        def shard_step(b, q):
            q = fold(q, mine[b, 1], mine[b, 2], None, 0, b)
            return fold(q, theirs[b, 0], theirs[b, 1], None, 2, b)

        total = lax.fori_loop(first[s], s, shard_step, total)
        kept[s, 0] = (total * factor).astype(BF)

        @pl.when(s == shards - 1)
        def _():
            for b in range(shards):
                kept[b, 1] = (sums[0, b] * factor).astype(BF)
                kept[b, 2] = sums[1, b].astype(BF)
                given[b, 0] = (sums[2, b] * factor).astype(BF)
                given[b, 1] = sums[3, b].astype(BF)

    whole = lambda n: pl.BlockSpec((shards, n, half, HD), lambda s, *_: (0, 0, 0, 0))
    return pl.pallas_call(
        kernel,
        grid_spec=pltpu.PrefetchScalarGridSpec(
            num_scalar_prefetch=2,
            grid=(shards,),
            in_specs=[
                whole(3),
                whole(2),
                pl.BlockSpec((shards, half, HD), lambda s, *_: (0, 0, 0)),
                pl.BlockSpec((1, half, HD), lambda s, *_: (s, 0, 0)),
                pl.BlockSpec((1, half, 1), lambda s, *_: (s, 0, 0)),
            ],
            out_specs=[whole(3), whole(2)],
            scratch_shapes=[pltpu.VMEM((4, shards, half, HD), F32)],
        ),
        out_shape=[
            jax.ShapeDtypeStruct((shards, 3, half, HD), BF),
            jax.ShapeDtypeStruct((shards, 2, half, HD), BF),
        ],
        name="attend_back",
    )(first_key, side, own, other, grads, exact, norm)


def norm_back(grad, unit, inv, gain, extra):
    width = grad.shape[1]
    scaled = grad * gain
    mean = jnp.sum(scaled, axis=-1, keepdims=True) * (1.0 / width)
    slope = jnp.sum(scaled * unit, axis=-1, keepdims=True) * (1.0 / width)
    result = inv * (scaled - mean - unit * slope)
    return result if extra is None else result + extra


def heads_back(parts, w_heads, normed, unit, inv, gains, tables):
    _, tokens, width = normed.shape
    columns = w_heads.shape[3]
    heads, half = columns // HD, tokens // 2
    block = min(128, tokens)

    def kernel(part, w, x, u, istd, gain, table, stream, weight, stats, grad, wide):
        c = pl.program_id(0)
        turn = c < 2

        def take(head):
            return jnp.concatenate([part[2 * head, 0], part[2 * head + 1, 0]], axis=0).astype(F32)

        @pl.when(turn)
        def _():
            for head in range(heads):
                grad[:, head * HD : (head + 1) * HD] = turned(take(head), table[...]).astype(BF)

        @pl.when(jnp.logical_not(turn))
        def _():
            for head in range(heads):
                grad[:, head * HD : (head + 1) * HD] = take(head).astype(BF)

        wide[...] = dot_cols(grad[...], w[...].reshape(width, columns))
        weight[0] = dot_rows(x[0], grad[...]).astype(BF)
        stats[...] = jnp.zeros_like(stats)
        column = lax.broadcasted_iota(jnp.int32, (block, istd.shape[1]), 1)

        def step(r, carry):
            here = pl.ds(pl.multiple_of(r * block, block), block)
            values = wide[here, :]
            units = u[0, here, :].astype(F32)
            std = jnp.sum(jnp.where(column == c, istd[here, :], 0.0), axis=-1, keepdims=True)
            stream[0, here, :] = norm_back(values, units, std, gain[0], None).astype(BF)
            stats[0, 0:1] += jnp.sum(values * units, axis=0, keepdims=True)
            stats[0, 1:2] += jnp.sum(values, axis=0, keepdims=True)
            return carry

        lax.fori_loop(0, tokens // block, step, 0)

    return pl.pallas_call(
        kernel,
        grid=(3,),
        in_specs=[
            pl.BlockSpec((2 * heads, 1, half, HD), lambda c: (0, c, 0, 0)),
            pl.BlockSpec((w_heads.shape[0], 1, w_heads.shape[2], columns), lambda c: (0, c, 0, 0)),
            pl.BlockSpec((1, tokens, width), lambda c: (c, 0, 0)),
            pl.BlockSpec((1, tokens, width), lambda c: (c, 0, 0)),
            pl.BlockSpec((tokens, inv.shape[1]), lambda c: (0, 0)),
            pl.BlockSpec((1, 1, width), lambda c: (c, 0, 0)),
            pl.BlockSpec((3, tokens, HD), lambda c: (0, 0, 0)),
        ],
        out_specs=[
            pl.BlockSpec((1, tokens, width), lambda c: (c, 0, 0)),
            pl.BlockSpec((1, width, columns), lambda c: (c, 0, 0)),
            pl.BlockSpec((1, 2, width), lambda c: (c, 0, 0)),
        ],
        out_shape=[
            jax.ShapeDtypeStruct((3, tokens, width), BF),
            jax.ShapeDtypeStruct((3, width, columns), BF),
            jax.ShapeDtypeStruct((3, 2, width), F32),
        ],
        scratch_shapes=[pltpu.VMEM((tokens, columns), BF), pltpu.VMEM((tokens, width), F32)],
        name="heads_back",
    )(parts, w_heads, normed, unit, inv, gains[:, None, :], tables)


def last_back(grad, unit, inv, gain, extra, flag):
    tokens, width = grad.shape
    block = min(128, tokens)

    def kernel(g, u, istd, gain_ref, e, flag_ref, stream, stats):
        @pl.when(pl.program_id(0) == 0)
        def _():
            stats[...] = jnp.zeros_like(stats)

        values = g[...]
        units = u[...].astype(F32)
        std = istd[...][:, -1:]
        added = e[...].astype(F32) * flag_ref[0]
        stream[...] = norm_back(values, units, std, gain_ref[...], added).astype(BF)
        stats[0:1] += jnp.sum(values * units, axis=0, keepdims=True)
        stats[1:2] += jnp.sum(values, axis=0, keepdims=True)

    row = lambda n: pl.BlockSpec((block, n), lambda i: (i, 0))
    return pl.pallas_call(
        kernel,
        grid=(tokens // block,),
        in_specs=[
            row(width),
            row(width),
            row(inv.shape[1]),
            pl.BlockSpec((1, width), lambda i: (0, 0)),
            row(width),
            pl.BlockSpec(memory_space=pltpu.SMEM),
        ],
        out_specs=[row(width), pl.BlockSpec((2, width), lambda i: (0, 0))],
        out_shape=[
            jax.ShapeDtypeStruct((tokens, width), BF),
            jax.ShapeDtypeStruct((2, width), F32),
        ],
        name="last_back",
    )(grad, unit, inv, gain, extra, flag)


def mixing_back(heads_part, last_part, history):
    entries, tokens, width = history.shape
    streams = heads_part.shape[0] + 1
    rows, sub, lanes = min(64, tokens), 16, 256

    def kernel(first, last, hist, out):
        def step(r, carry):
            here = pl.ds(pl.multiple_of(r * sub, sub), sub)
            for s in range(streams):
                sums = [None] * entries
                for lane in range(0, width, lanes):
                    span = slice(lane, lane + lanes)
                    part = first[s, here, span] if s < streams - 1 else last[here, span]
                    part = part.astype(F32)
                    for j in range(entries):
                        term = part * hist[j, here, span].astype(F32)
                        sums[j] = term if lane == 0 else sums[j] + term
                columns = [jnp.sum(item, axis=-1, keepdims=True) for item in sums]
                out[s, here, :] = jnp.concatenate(columns, axis=-1)
            return carry

        lax.fori_loop(0, rows // sub, step, 0)

    return pl.pallas_call(
        kernel,
        grid=(tokens // rows,),
        in_specs=[
            pl.BlockSpec((streams - 1, rows, width), lambda i: (0, i, 0)),
            pl.BlockSpec((rows, width), lambda i: (i, 0)),
            pl.BlockSpec((entries, rows, width), lambda i: (0, i, 0)),
        ],
        out_specs=pl.BlockSpec((streams, rows, entries), lambda i: (0, i, 0)),
        out_shape=jax.ShapeDtypeStruct((streams, tokens, entries), F32),
        name="mixing_back",
    )(heads_part, last_part, history)


def far_attend(queries, keys, values, shard_offset):
    tokens, heads_here, head_size = queries.shape
    data_index = lax.axis_index("dp")
    pairs = [jnp.stack([keys, values])]
    reach = 2 * SEQ // tokens
    for back in range(1, reach):
        pairs.append(passed_along(pairs[0], "dp", back))
    usable = [(shard_offset[0] >= back * tokens) & (data_index >= back) for back in range(reach)]
    first_logits = block_logits(queries, keys, True)
    top = jnp.max(first_logits, axis=-1)
    total = jnp.sum(jnp.exp(first_logits - top[..., None]), axis=-1)
    for back in range(1, reach):

        def widen(state, block=pairs[back][0]):
            logits = block_logits(queries, block, False)
            new_top = jnp.maximum(state[0], jnp.max(logits, axis=-1))
            summed = state[1] * jnp.exp(state[0] - new_top) + jnp.sum(
                jnp.exp(logits - new_top[..., None]), axis=-1
            )
            return (new_top, summed)

        top, total = lax.cond(usable[back], widen, keep_same, (top, total))
    log_total = top + jnp.log(total)
    attended = jnp.zeros((tokens, heads_here, head_size), F32)
    for back in range(reach):

        def accumulate(current, block=pairs[back], diagonal=back == 0):
            probs = jnp.exp(block_logits(queries, block[0], diagonal) - log_total[..., None])
            return current + jnp.einsum(
                "hqk,khd->qhd", probs.astype(BF), block[1], preferred_element_type=F32
            )

        attended = lax.cond(usable[back], accumulate, keep_same, attended)
    return attended, (pairs, usable, log_total)


def far_attend_back(queries, attended_grad, kept):
    tokens, heads_here, head_size = queries.shape
    factor = 1.0 / math.sqrt(head_size)
    pairs, usable, log_total = kept
    reach = len(pairs)

    def weights_of(block, diagonal):
        return jnp.exp(block_logits(queries, block, diagonal) - log_total[..., None])

    def prob_grads(block):
        return jnp.einsum("qhd,khd->hqk", attended_grad, block[1], preferred_element_type=F32)

    delta = jnp.zeros((heads_here, tokens), F32)
    for back in range(reach):

        def gather_delta(current, block=pairs[back], diagonal=back == 0):
            return current + jnp.sum(weights_of(block[0], diagonal) * prob_grads(block), axis=-1)

        delta = lax.cond(usable[back], gather_delta, keep_same, delta)

    def skip_block(current):
        return (current, jnp.zeros((2, tokens, heads_here, head_size), F32))

    query_grad = jnp.zeros((tokens, heads_here, head_size), F32)
    key_value_grad = jnp.zeros((2, tokens, heads_here, head_size), F32)
    for back in range(reach):

        def spread(current, block=pairs[back], diagonal=back == 0):
            probs = weights_of(block[0], diagonal)
            score_grad = (probs * (prob_grads(block) - delta[..., None])).astype(BF)
            query_part = (
                current
                + jnp.einsum("hqk,khd->qhd", score_grad, block[0], preferred_element_type=F32)
                * factor
            )
            key_part = (
                jnp.einsum("hqk,qhd->khd", score_grad, queries, preferred_element_type=F32)
                * factor
            )
            value_part = jnp.einsum(
                "hqk,qhd->khd", probs.astype(BF), attended_grad, preferred_element_type=F32
            )
            return (query_part, jnp.stack([key_part, value_part]))

        query_grad, pair_grad = lax.cond(usable[back], spread, skip_block, query_grad)
        if back == 0:
            key_value_grad = pair_grad
        else:
            key_value_grad = key_value_grad + passed_along(pair_grad, "dp", -back)
    return jnp.concatenate([query_grad[None], key_value_grad])


def merge_branches(attended, hidden, w_merge, w_down, stream, flag):
    tokens, inner = attended.shape
    shards, units, cols = w_down.shape
    if cols % 128:
        merged = jnp.einsum("te,ned->tnd", attended, w_merge, preferred_element_type=F32)
        merged = merged + jnp.einsum("tf,nfd->tnd", hidden, w_down, preferred_element_type=F32)
        return merged.reshape(tokens, -1) + flag * stream

    def kernel(a, h, wm, wd, st, flag_ref, out):
        out[...] = dot(a[...], wm[0]) + dot(h[...], wd[0]) + flag_ref[0] * st[...]

    return pl.pallas_call(
        kernel,
        grid=(shards,),
        in_specs=[
            pl.BlockSpec((tokens, inner), lambda n: (0, 0)),
            pl.BlockSpec((tokens, units), lambda n: (0, 0)),
            pl.BlockSpec((1, inner, cols), lambda n: (n, 0, 0)),
            pl.BlockSpec((1, units, cols), lambda n: (n, 0, 0)),
            pl.BlockSpec((tokens, cols), lambda n: (0, n)),
            pl.BlockSpec(memory_space=pltpu.SMEM),
        ],
        out_specs=pl.BlockSpec((tokens, cols), lambda n: (0, n)),
        out_shape=jax.ShapeDtypeStruct((tokens, shards * cols), F32),
        name="merge_branches",
    )(attended, hidden, w_merge, w_down, stream, flag)


def back_through(grad, stacked, slope):
    tokens = grad.shape[0]
    shards, units, cols = stacked.shape
    if cols % 128:
        split = grad.reshape(tokens, shards, cols)
        total = jnp.einsum("tnd,nfd->tf", split, stacked, preferred_element_type=F32)
        return (total if slope is None else total * slope.astype(F32)).astype(BF)

    def kernel(*refs):
        g, w = refs[:2]
        out, acc = refs[-2:]
        n = pl.program_id(0)
        part = dot_cols(g[...], w[0])

        @pl.when(n == 0)
        def _():
            acc[...] = part

        @pl.when(n > 0)
        def _():
            acc[...] += part

        @pl.when(n == shards - 1)
        def _():
            total = acc[...]
            if slope is not None:
                total = total * refs[2][...].astype(F32)
            out[...] = total.astype(BF)

    specs = [
        pl.BlockSpec((tokens, cols), lambda n: (0, n)),
        pl.BlockSpec((1, units, cols), lambda n: (n, 0, 0)),
    ]
    args = [grad, stacked]
    if slope is not None:
        specs.append(pl.BlockSpec((tokens, units), lambda n: (0, 0)))
        args.append(slope)
    return pl.pallas_call(
        kernel,
        grid=(shards,),
        in_specs=specs,
        out_specs=pl.BlockSpec((tokens, units), lambda n: (0, 0)),
        out_shape=jax.ShapeDtypeStruct((tokens, units), BF),
        scratch_shapes=[pltpu.VMEM((tokens, units), F32)],
        name="back_through",
    )(*args)


def body(
    history,
    mixing,
    shard_offset,
    norm_gain,
    norm_bias,
    w_heads,
    w_merge,
    w_up,
    w_down,
    mixer_first,
    mixer_second,
    out_cotangent,
    next_cotangent,
):
    member = lax.axis_index("stream")
    members = lax.axis_size("stream")
    shards = lax.axis_size("dp")
    index = lax.axis_index("dp")
    entries, tokens, width = history.shape
    heads_here = w_heads.shape[2] // HD
    half = tokens // 2
    highest = lax.Precision.HIGHEST
    flag = (member == members - 1).astype(F32)
    flags = flag.reshape(1)
    near = shards == 8 and heads_here * 2 == shards and tokens * shards == 2 * SEQ

    mix_all = lax.all_gather(mixing[:, 0, :], "stream", axis=0)
    norms = lax.all_gather(jnp.concatenate([norm_gain, norm_bias]), "stream", axis=0)
    gains, biases = norms[:, 0].astype(F32), norms[:, 1].astype(F32)
    mix_rows = jnp.transpose(mix_all, (1, 0, 2)).reshape(tokens, members * entries)
    spread = jnp.broadcast_to(shard_offset[:, None], (8, 128))
    offsets = lax.all_gather(spread, "dp", axis=0)[:, 0, 0]
    first_full = lax.all_gather(mixer_first, "stream", axis=0, tiled=True)
    second_full = lax.all_gather(mixer_second[:, 0, :], "stream", axis=0).astype(F32)
    next_full = lax.all_gather(next_cotangent[:, 0, :], "stream", axis=0)
    cotangent = lax.all_gather(out_cotangent, "stream", axis=1, tiled=True)
    full_heads, full_up, full_merge, full_down = gather_weights([w_heads, w_up, w_merge, w_down])
    flat_up = full_up.reshape(width, -1)

    normed, unit, inv, stream = make_streams(history, mix_rows, gains, biases)
    positions = shard_offset[0] + jnp.arange(tokens, dtype=jnp.int32)
    projected = project(normed, full_heads, rope_tables(positions, 1.0))
    if near:
        side = (index % 2).astype(jnp.int32).reshape(1)
        place = jnp.arange(shards, dtype=jnp.int32)
        first_key = jnp.maximum(place - offsets // tokens, 0).astype(jnp.int32)
        own = lax.all_to_all(projected, "dp", 0, 0, tiled=True)
        other = partner(own[:, 1:], 1)
        result, exact, level = attend(own, other, first_key, side)
        back = lax.all_to_all(result, "dp", 0, 0, tiled=True)
        attended = jnp.transpose(back.reshape(heads_here, tokens, HD), (1, 0, 2)).reshape(tokens, -1)
    else:
        split = projected.reshape(heads_here, 2, 3, half, HD)
        split = jnp.transpose(split, (2, 1, 3, 0, 4)).reshape(3, tokens, heads_here, HD)
        result, kept = far_attend(split[0], split[1], split[2], shard_offset)
        attended = result.reshape(tokens, -1).astype(BF)

    up = dot(normed[members - 1], flat_up)
    hidden, gelu_back = jax.vjp(exact_gelu, up)
    hidden = hidden.astype(BF)
    slope = gelu_back(jnp.ones_like(up))[0].astype(BF)
    share = merge_branches(attended, hidden, full_merge, full_down, stream, flags)

    inner = (member == 1) | (member == 2)
    pieces = []
    count = 4
    for i in range(count):
        part = lax.slice_in_dim(share, i * tokens // count, (i + 1) * tokens // count)
        one = line_hop(part.astype(BF), OUTWARD)
        nearer = part + one.astype(F32)
        two = line_hop(nearer.astype(BF), MIDDLE)
        total = (nearer + two.astype(F32)).astype(BF)
        pieces.append(jnp.where(inner, total, line_hop(total, INWARD)))
    block_full = jnp.concatenate(pieces)

    mine = member * (width // members)
    block_out = lax.dynamic_slice_in_dim(block_full, mine, width // members, axis=1)
    out_float = block_full.astype(F32)
    scale = lax.rsqrt(jnp.sum(out_float * out_float, axis=-1) / width + 1e-06)
    proj = dot(block_full, first_full)
    mixer, mixer_back = jax.vjp(exact_gelu, scale[:, None] * proj)
    second_here = mixer_second[:, 0, :].astype(F32)
    next_here = jnp.dot(mixer, second_here, precision=highest, preferred_element_type=F32)
    mixer_grad = jnp.einsum(
        "stn,scn->tc", next_full, second_full, precision=highest, preferred_element_type=F32
    )
    pre_grad = mixer_back(mixer_grad)[0]
    proj_grad = (scale[:, None] * pre_grad).astype(BF)
    scale_grad = jnp.sum(pre_grad * proj, axis=-1)
    second_local = jnp.dot(
        mixer.T, next_cotangent[:, 0, :], precision=highest, preferred_element_type=F32
    )
    first_local = dot_rows(block_out, proj_grad)
    grad_out = (
        cotangent.astype(F32)
        + dot_cols(proj_grad, first_full)
        - (scale * scale * scale * scale_grad)[:, None] * out_float / width
    ).astype(BF)

    attended_grad = back_through(grad_out, full_merge, None)
    if near:
        sent = attended_grad.reshape(tokens, heads_here, HD)
        sent = jnp.transpose(sent, (1, 0, 2)).reshape(shards, half, HD)
        grads = lax.all_to_all(sent, "dp", 0, 0, tiled=True)
        kept_grads, given = attend_back(own, other, grads, exact, level, first_key, side)
        taken = partner(given, 1)
        summed = kept_grads[:, 1:].astype(F32) + taken.astype(F32)
        packed = jnp.concatenate([kept_grads[:, :1], summed.astype(BF)], axis=1)
        parts = lax.all_to_all(packed, "dp", 0, 0, tiled=True)
    else:
        grads = far_attend_back(split[0], attended_grad.reshape(tokens, heads_here, HD), kept)
        parts = grads.reshape(3, 2, half, heads_here, HD)
        parts = jnp.transpose(parts, (3, 1, 0, 2, 4)).reshape(2 * heads_here, 3, half, HD)

    up_grad = back_through(grad_out, full_down, slope)
    down_grad = dot_rows(hidden, grad_out).astype(BF)
    merge_grad = dot_rows(attended, grad_out).astype(BF)
    last_normed = dot_cols(up_grad, flat_up)
    last_share, last_stats = last_back(
        last_normed, unit[members - 1], inv, gains[members - 1 :], grad_out, flags
    )
    up_back = dot_rows(normed[members - 1], up_grad).astype(BF)
    heads_share, heads_grad, heads_stats = heads_back(
        parts, full_heads, normed, unit, inv, gains, rope_tables(positions, -1.0)
    )

    grad_down = lax.psum_scatter(down_grad, "dp", scatter_dimension=1, tiled=True).astype(F32)
    grad_merge = lax.psum_scatter(merge_grad, "dp", scatter_dimension=1, tiled=True).astype(F32)
    grad_up = lax.psum_scatter(up_back, "dp", scatter_dimension=0, tiled=True).astype(F32)
    grad_heads = lax.psum_scatter(heads_grad, "dp", scatter_dimension=1, tiled=True).astype(F32)

    shares = [last_share] + [heads_share[c] for c in range(members - 1)]
    order = [members - 1] + list(range(members - 1))
    ones, twos = [], []
    for item in shares:
        one = line_hop(item, OUTWARD)
        ones.append(one)
        twos.append(line_hop((item.astype(F32) + one.astype(F32)).astype(BF), MIDDLE))
    each = entries // members
    target = jnp.where(member == 1, 0, members - 1)

    def weights_for(owner):
        block = lax.dynamic_slice_in_dim(mix_all, owner * each, each, axis=2)
        return [[block[s, :, e : e + 1] for s in order] for e in range(each)]

    def weighted(weights, values):
        sums = []
        for e in range(each):
            total = weights[e][0] * values[0]
            for weight, value in zip(weights[e][1:], values[1:]):
                total = total + weight * value
            sums.append(total)
        return jnp.stack(sums)

    there, here = weights_for(target), weights_for(member)
    history_parts = []
    for i in range(count):
        low, high = i * tokens // count, (i + 1) * tokens // count
        cut = lambda array: lax.slice_in_dim(array, low, high).astype(F32)
        rows = lambda weights: [[w[low:high] for w in line] for line in weights]
        inward = [cut(item) + cut(two) for item, two in zip(shares, twos)]
        three = line_hop(weighted(rows(there), inward).astype(BF), INWARD)
        sums = [value + cut(one) for value, one in zip(inward, ones)]
        history_parts.append(weighted(rows(here), sums) + three.astype(F32))
    grad_history = jnp.concatenate(history_parts, axis=1)

    mix_parts = mixing_back(heads_share, last_share, history)
    mix_parts = lax.all_to_all(mix_parts, "stream", 0, 0, tiled=True)
    grad_mixing = jnp.sum(mix_parts, axis=0)[:, None, :]

    stats = jnp.concatenate([heads_stats, last_stats[None]])
    stats = jnp.sum(lax.all_to_all(stats, "stream", 0, 0, tiled=True), axis=0)
    stats = jnp.sum(lax.all_gather(stats, "dp", axis=0), axis=0)
    grad_first = jnp.sum(lax.all_gather(first_local, "dp", axis=0), axis=0)
    grad_second = jnp.sum(lax.all_gather(second_local, "dp", axis=0), axis=0)
    return (
        block_out,
        next_here[:, None, :],
        grad_history,
        grad_mixing,
        stats[:1],
        stats[1:],
        grad_heads,
        grad_merge,
        grad_up,
        grad_down,
        grad_first,
        grad_second[:, None, :],
    )


def solution(mesh):
    in_specs = (
        P(None, "dp", None),
        P("dp", "stream", None),
        P("dp"),
        P("stream", None),
        P("stream", None),
        P(None, "dp", "stream"),
        P("stream", "dp"),
        P("dp", "stream"),
        P("stream", "dp"),
        P("stream", None),
        P(None, "stream", None),
        P("dp", "stream"),
        P("dp", "stream", None),
    )
    out_specs = (
        P("dp", "stream"),
        P("dp", "stream", None),
        P("stream", "dp", None),
        P("dp", "stream", None),
        P("stream", None),
        P("stream", None),
        P(None, "dp", "stream"),
        P("stream", "dp"),
        P("dp", "stream"),
        P("stream", "dp"),
        P("stream", None),
        P(None, "stream", None),
    )
    return jax.shard_map(body, mesh=mesh, in_specs=in_specs, out_specs=out_specs, check_vma=False)
```

```python
import math

import jax
import jax.numpy as jnp
from jax import lax
from jax.experimental import pallas as pl
from jax.experimental.pallas import tpu as pltpu
from jax.sharding import PartitionSpec as P

HD = 128
ROT = 32
SEQ = 2048


def passed_along(shard, axis, by):
    peers = lax.axis_size(axis)
    pairs = [(i, i + by) for i in range(peers) if 0 <= i + by < peers]
    return lax.ppermute(shard, axis, pairs)


def rotate(vectors, positions, sign):
    half = ROT // 2
    counter = jnp.arange(half, dtype=jnp.float32)
    freqs = jnp.exp(counter * (-2.0 * math.log(10000.0) / ROT))
    angles = positions.astype(jnp.float32)[:, None] * freqs[None, :]
    cosine = jnp.cos(angles)[:, None, :]
    sine = sign * jnp.sin(angles)[:, None, :]
    first = vectors[..., :half]
    second = vectors[..., half:ROT]
    return jnp.concatenate(
        [first * cosine - second * sine, second * cosine + first * sine, vectors[..., ROT:]],
        axis=-1,
    )


def exact_gelu(vectors):
    return jax.nn.gelu(vectors, approximate=False)


def block_logits(queries, keys_block, diagonal):
    logits = jnp.einsum("qhd,khd->hqk", queries, keys_block, preferred_element_type=jnp.float32) * (
        1.0 / math.sqrt(queries.shape[-1])
    )
    if diagonal:
        counter = jnp.arange(queries.shape[0], dtype=jnp.int32)
        allowed = counter[None, :] <= counter[:, None]
        logits = jnp.where(allowed[None], logits, -1e30)
    return logits


def keep_same(state):
    return state


BF = jnp.bfloat16
F32 = jnp.float32
OUTWARD = [(0, 1), (3, 2)]
MIDDLE = [(1, 2), (2, 1)]
INWARD = [(1, 0), (2, 3)]


def dot(left, right):
    return jnp.dot(left, right, preferred_element_type=F32)


def dot_rows(left, right):
    return lax.dot_general(left, right, (((0,), (0,)), ((), ())), preferred_element_type=F32)


def dot_cols(left, right):
    return lax.dot_general(left, right, (((1,), (1,)), ((), ())), preferred_element_type=F32)


def partner(shard, bit):
    peers = lax.axis_size("dp")
    return lax.ppermute(shard, "dp", [(i, i ^ bit) for i in range(peers)])


def line_hop(shard, pairs):
    return lax.ppermute(shard, "stream", pairs)


def after(value, *others):
    return lax.optimization_barrier((value, *others))[0]


class Gathered:
    def __init__(self, shard, direct=False):
        self.shard = shard
        self.peers = lax.axis_size("dp")
        if self.peers != 8:
            self.by_x = self.by_y = shard
            return
        self.cut = max(range(shard.ndim - 1), key=lambda dim: shard.shape[dim])
        self.by_x = partner(shard, 2)
        self.by_y = partner(shard, 4)
        self.across = partner(shard, 6) if direct else None

    def whole(self, *earlier):
        shard = self.shard
        if self.peers != 8:
            return lax.all_gather(shard, "dp", axis=0)
        index = lax.axis_index("dp")
        cut = self.cut
        half = shard.shape[cut] // 2
        pieces = [(shard, 0, 0), (self.by_x, 2, 0), (self.by_y, 4, 0)]
        if self.across is None:
            low = lax.slice_in_dim(self.by_y, 0, half, axis=cut)
            high = lax.slice_in_dim(self.by_x, half, 2 * half, axis=cut)
            if earlier:
                low, high = after(low, *earlier), after(high, *earlier)
            pieces += [(partner(low, 2), 6, 0), (partner(high, 4), 6, half)]
        else:
            pieces.append((self.across, 6, 0))
        pieces += [(partner(piece, 1), code ^ 1, start) for piece, code, start in pieces]
        whole = jnp.zeros((self.peers, *shard.shape), shard.dtype)
        for piece, code, start in pieces:
            place = [jnp.int32(0)] * (shard.ndim + 1)
            place[0] = index ^ code
            place[cut + 1] = jnp.int32(start)
            whole = lax.dynamic_update_slice(whole, piece[None], place)
        return whole


def along_line(count, first, second, third):
    ones, twos, threes = [], [], []
    for step in range(count + 2):
        if step < count:
            gates = []
            if step >= 2:
                gates.append(ones[step - 2])
            if step >= 3:
                gates.append(twos[step - 3])
            if step >= 4:
                gates.append(threes[step - 4])
            ones.append(line_hop(first(step, gates), OUTWARD))
        if 0 <= step - 1 < count:
            twos.append(line_hop(second(step - 1, ones[step - 1]), MIDDLE))
        if 0 <= step - 2 < count:
            threes.append(line_hop(third(step - 2, ones[step - 2], twos[step - 2]), INWARD))
    return ones, twos, threes


def gated(value, gates):
    return after(value, *gates) if gates else value


def rope_tables(positions, sign):
    half = ROT // 2
    lane = jnp.arange(HD, dtype=jnp.int32)
    counter = (lane % half).astype(F32)
    freqs = jnp.exp(counter * (-2.0 * math.log(10000.0) / ROT))
    angles = positions.astype(F32)[:, None] * freqs[None, :]
    cosine = jnp.where(lane < ROT, jnp.cos(angles), 1.0)
    sine = sign * jnp.sin(angles)
    up = jnp.where(lane < half, -sine, 0.0)
    down = jnp.where((lane >= half) & (lane < ROT), sine, 0.0)
    return jnp.stack([cosine, up, down])


def turned(block, tables):
    half = ROT // 2
    return (
        block * tables[0]
        + pltpu.roll(block, HD - half, 1) * tables[1]
        + pltpu.roll(block, half, 1) * tables[2]
    )


def make_streams(history, mix_rows, gains, biases):
    entries, tokens, width = history.shape
    streams = gains.shape[0]
    rows, sub, lanes = min(64, tokens), 16, 512

    def kernel(hist, mix, gain, bias, normed, unit, inv, last, scratch):
        def step(r, carry):
            here = pl.ds(pl.multiple_of(r * sub, sub), sub)
            weights = mix[here, :]
            columns = [
                [weights[:, s * entries + j : s * entries + j + 1] for j in range(entries)]
                for s in range(streams)
            ]
            for lane in range(0, width, lanes):
                span = slice(lane, lane + lanes)
                sums = [None] * streams
                for j in range(entries):
                    part = hist[j, here, span].astype(F32)
                    for s in range(streams):
                        term = columns[s][j] * part
                        sums[s] = term if j == 0 else sums[s] + term
                for s in range(streams):
                    scratch[s, :, span] = sums[s]
            stds = []
            for s in range(streams):
                values = scratch[s]
                center = values - jnp.sum(values, axis=-1, keepdims=True) * (1.0 / width)
                var = jnp.sum(center * center, axis=-1, keepdims=True) * (1.0 / width)
                std = lax.rsqrt(var + 1e-05)
                stds.append(std)
                scaled = center * std
                unit[s, here, :] = scaled.astype(BF)
                normed[s, here, :] = (scaled * gain[s : s + 1] + bias[s : s + 1]).astype(BF)
            last[here, :] = scratch[streams - 1]
            inv[here, :] = jnp.concatenate(stds, axis=-1)
            return carry

        lax.fori_loop(0, rows // sub, step, 0)

    wide = jax.ShapeDtypeStruct((streams, tokens, width), BF)
    return pl.pallas_call(
        kernel,
        grid=(tokens // rows,),
        in_specs=[
            pl.BlockSpec((entries, rows, width), lambda i: (0, i, 0)),
            pl.BlockSpec((rows, streams * entries), lambda i: (i, 0)),
            pl.BlockSpec((streams, width), lambda i: (0, 0)),
            pl.BlockSpec((streams, width), lambda i: (0, 0)),
        ],
        out_specs=[
            pl.BlockSpec((streams, rows, width), lambda i: (0, i, 0)),
            pl.BlockSpec((streams, rows, width), lambda i: (0, i, 0)),
            pl.BlockSpec((rows, streams), lambda i: (i, 0)),
            pl.BlockSpec((rows, width), lambda i: (i, 0)),
        ],
        out_shape=[
            wide,
            wide,
            jax.ShapeDtypeStruct((tokens, streams), F32),
            jax.ShapeDtypeStruct((tokens, width), F32),
        ],
        scratch_shapes=[pltpu.VMEM((streams, sub, width), F32)],
        name="make_streams",
    )(history, mix_rows, gains, biases)


def project(normed, w_heads, tables):
    _, tokens, width = normed.shape
    columns = w_heads.shape[3]
    heads, half = columns // HD, tokens // 2

    def kernel(x, w, table, out):
        flat = dot(x[0], w[...].reshape(width, columns))
        turn = pl.program_id(0) < 2

        def put(head, block):
            out[2 * head, 0] = block[:half].astype(BF)
            out[2 * head + 1, 0] = block[half:].astype(BF)

        @pl.when(turn)
        def _():
            for head in range(heads):
                put(head, turned(flat[:, head * HD : (head + 1) * HD], table[...]))

        @pl.when(jnp.logical_not(turn))
        def _():
            for head in range(heads):
                put(head, flat[:, head * HD : (head + 1) * HD])

    return pl.pallas_call(
        kernel,
        grid=(3,),
        in_specs=[
            pl.BlockSpec((1, tokens, width), lambda c: (c, 0, 0)),
            pl.BlockSpec((w_heads.shape[0], 1, w_heads.shape[2], columns), lambda c: (0, c, 0, 0)),
            pl.BlockSpec((3, tokens, HD), lambda c: (0, 0, 0)),
        ],
        out_specs=pl.BlockSpec((2 * heads, 1, half, HD), lambda c: (0, c, 0, 0)),
        out_shape=jax.ShapeDtypeStruct((2 * heads, 3, half, HD), BF),
        name="project",
    )(normed, w_heads, tables)


def attend(own, other, first_key, side):
    shards, _, half, _ = own.shape
    factor = 1.0 / math.sqrt(HD)

    def kernel(first, part, mine, theirs, out, exact, norm):
        s = pl.program_id(0)
        query = mine[s, 0]

        def fold(state, keys, values, mask):
            top, total, acc = state
            logits = dot_cols(query, keys) * factor
            if mask is not None:
                logits = jnp.where(mask, logits, -1e30)
            new_top = jnp.maximum(top, jnp.max(logits, axis=-1, keepdims=True))
            probs = jnp.exp(logits - new_top)
            keep = jnp.exp(top - new_top)
            return (
                new_top,
                total * keep + jnp.sum(probs, axis=-1, keepdims=True),
                acc * keep + dot(probs.astype(BF), values),
            )

        row = lax.broadcasted_iota(jnp.int32, (half, half), 0)
        col = lax.broadcasted_iota(jnp.int32, (half, half), 1)
        state = (
            jnp.full((half, 1), -1e30, F32),
            jnp.zeros((half, 1), F32),
            jnp.zeros((half, HD), F32),
        )
        state = fold(state, mine[s, 1], mine[s, 2], col <= row)
        state = lax.fori_loop(
            0, part[0], lambda i, st: fold(st, theirs[s, 0], theirs[s, 1], None), state
        )

        def shard_step(b, st):
            st = fold(st, mine[b, 1], mine[b, 2], None)
            return fold(st, theirs[b, 0], theirs[b, 1], None)

        top, total, acc = lax.fori_loop(first[s], s, shard_step, state)
        result = acc / total
        out[0] = result.astype(BF)
        exact[0] = result
        norm[0] = top + jnp.log(total)

    return pl.pallas_call(
        kernel,
        grid_spec=pltpu.PrefetchScalarGridSpec(
            num_scalar_prefetch=2,
            grid=(shards,),
            in_specs=[
                pl.BlockSpec((shards, 3, half, HD), lambda s, *_: (0, 0, 0, 0)),
                pl.BlockSpec((shards, 2, half, HD), lambda s, *_: (0, 0, 0, 0)),
            ],
            out_specs=[
                pl.BlockSpec((1, half, HD), lambda s, *_: (s, 0, 0)),
                pl.BlockSpec((1, half, HD), lambda s, *_: (s, 0, 0)),
                pl.BlockSpec((1, half, 1), lambda s, *_: (s, 0, 0)),
            ],
        ),
        out_shape=[
            jax.ShapeDtypeStruct((shards, half, HD), BF),
            jax.ShapeDtypeStruct((shards, half, HD), F32),
            jax.ShapeDtypeStruct((shards, half, 1), F32),
        ],
        name="attend",
    )(first_key, side, own, other)


def attend_back(own, other, grads, exact, norm, first_key, side):
    shards, _, half, _ = own.shape
    factor = 1.0 / math.sqrt(HD)

    def kernel(first, part, mine, theirs, grad_ref, exact_ref, norm_ref, kept, given, sums):
        s = pl.program_id(0)
        query = mine[s, 0]
        grad = grad_ref[s]
        delta = jnp.sum(grad.astype(F32) * exact_ref[0], axis=-1, keepdims=True)
        level = norm_ref[0]
        lowered = grad

        @pl.when(s == 0)
        def _():
            sums[...] = jnp.zeros_like(sums)

        def fold(query_grad, keys, values, mask, slot, b):
            logits = dot_cols(query, keys) * factor
            probs = jnp.exp(logits - level)
            if mask is not None:
                probs = jnp.where(mask, probs, 0.0)
            score = (probs * (dot_cols(grad, values) - delta)).astype(BF)
            sums[slot, b] += dot_rows(score, query)
            sums[slot + 1, b] += dot_rows(probs.astype(BF), lowered)
            return query_grad + dot(score, keys)

        row = lax.broadcasted_iota(jnp.int32, (half, half), 0)
        col = lax.broadcasted_iota(jnp.int32, (half, half), 1)
        total = fold(jnp.zeros((half, HD), F32), mine[s, 1], mine[s, 2], col <= row, 0, s)
        total = lax.fori_loop(
            0, part[0], lambda i, q: fold(q, theirs[s, 0], theirs[s, 1], None, 2, s), total
        )

        def shard_step(b, q):
            q = fold(q, mine[b, 1], mine[b, 2], None, 0, b)
            return fold(q, theirs[b, 0], theirs[b, 1], None, 2, b)

        total = lax.fori_loop(first[s], s, shard_step, total)
        kept[s, 0] = (total * factor).astype(BF)

        @pl.when(s == shards - 1)
        def _():
            for b in range(shards):
                kept[b, 1] = (sums[0, b] * factor).astype(BF)
                kept[b, 2] = sums[1, b].astype(BF)
                given[b, 0] = (sums[2, b] * factor).astype(BF)
                given[b, 1] = sums[3, b].astype(BF)

    whole = lambda n: pl.BlockSpec((shards, n, half, HD), lambda s, *_: (0, 0, 0, 0))
    return pl.pallas_call(
        kernel,
        grid_spec=pltpu.PrefetchScalarGridSpec(
            num_scalar_prefetch=2,
            grid=(shards,),
            in_specs=[
                whole(3),
                whole(2),
                pl.BlockSpec((shards, half, HD), lambda s, *_: (0, 0, 0)),
                pl.BlockSpec((1, half, HD), lambda s, *_: (s, 0, 0)),
                pl.BlockSpec((1, half, 1), lambda s, *_: (s, 0, 0)),
            ],
            out_specs=[whole(3), whole(2)],
            scratch_shapes=[pltpu.VMEM((4, shards, half, HD), F32)],
        ),
        out_shape=[
            jax.ShapeDtypeStruct((shards, 3, half, HD), BF),
            jax.ShapeDtypeStruct((shards, 2, half, HD), BF),
        ],
        name="attend_back",
    )(first_key, side, own, other, grads, exact, norm)


def norm_back(grad, unit, inv, gain, extra):
    width = grad.shape[1]
    scaled = grad * gain
    mean = jnp.sum(scaled, axis=-1, keepdims=True) * (1.0 / width)
    slope = jnp.sum(scaled * unit, axis=-1, keepdims=True) * (1.0 / width)
    result = inv * (scaled - mean - unit * slope)
    return result if extra is None else result + extra


def heads_back(parts, w_heads, normed, unit, inv, gains, tables, count):
    _, tokens, width = normed.shape
    columns = w_heads.shape[3]
    heads, half = columns // HD, tokens // 2
    block = tokens // count

    def kernel(part, w, x, u, istd, gain, table, *refs):
        pieces, (stream, weight, stats, grad, wide) = refs[:count], refs[count:]
        c = pl.program_id(0)
        turn = c < 2

        def take(head):
            return jnp.concatenate([part[2 * head, 0], part[2 * head + 1, 0]], axis=0).astype(F32)

        @pl.when(turn)
        def _():
            for head in range(heads):
                grad[:, head * HD : (head + 1) * HD] = turned(take(head), table[...]).astype(BF)

        @pl.when(jnp.logical_not(turn))
        def _():
            for head in range(heads):
                grad[:, head * HD : (head + 1) * HD] = take(head).astype(BF)

        wide[...] = dot_cols(grad[...], w[...].reshape(width, columns))
        weight[0] = dot_rows(x[0], grad[...]).astype(BF)
        stats[...] = jnp.zeros_like(stats)
        column = lax.broadcasted_iota(jnp.int32, (block, istd.shape[1]), 1)

        for r in range(count):
            here = slice(r * block, (r + 1) * block)
            values = wide[here, :]
            units = u[0, here, :].astype(F32)
            std = jnp.sum(jnp.where(column == c, istd[here, :], 0.0), axis=-1, keepdims=True)
            result = norm_back(values, units, std, gain[0], None).astype(BF)
            stream[0, here, :] = result
            pieces[r][0] = result
            stats[0, 0:1] += jnp.sum(values * units, axis=0, keepdims=True)
            stats[0, 1:2] += jnp.sum(values, axis=0, keepdims=True)

    return pl.pallas_call(
        kernel,
        grid=(3,),
        in_specs=[
            pl.BlockSpec((2 * heads, 1, half, HD), lambda c: (0, c, 0, 0)),
            pl.BlockSpec((w_heads.shape[0], 1, w_heads.shape[2], columns), lambda c: (0, c, 0, 0)),
            pl.BlockSpec((1, tokens, width), lambda c: (c, 0, 0)),
            pl.BlockSpec((1, tokens, width), lambda c: (c, 0, 0)),
            pl.BlockSpec((tokens, inv.shape[1]), lambda c: (0, 0)),
            pl.BlockSpec((1, 1, width), lambda c: (c, 0, 0)),
            pl.BlockSpec((3, tokens, HD), lambda c: (0, 0, 0)),
        ],
        out_specs=[pl.BlockSpec((1, block, width), lambda c: (c, 0, 0))] * count
        + [
            pl.BlockSpec((1, tokens, width), lambda c: (c, 0, 0)),
            pl.BlockSpec((1, width, columns), lambda c: (c, 0, 0)),
            pl.BlockSpec((1, 2, width), lambda c: (c, 0, 0)),
        ],
        out_shape=[jax.ShapeDtypeStruct((3, block, width), BF)] * count
        + [
            jax.ShapeDtypeStruct((3, tokens, width), BF),
            jax.ShapeDtypeStruct((3, width, columns), BF),
            jax.ShapeDtypeStruct((3, 2, width), F32),
        ],
        scratch_shapes=[pltpu.VMEM((tokens, columns), BF), pltpu.VMEM((tokens, width), F32)],
        name="heads_back",
    )(parts, w_heads, normed, unit, inv, gains[:, None, :], tables)


def last_back(grad, unit, inv, gain, extra, flag):
    tokens, width = grad.shape
    block = min(128, tokens)

    def kernel(g, u, istd, gain_ref, e, flag_ref, stream, stats):
        @pl.when(pl.program_id(0) == 0)
        def _():
            stats[...] = jnp.zeros_like(stats)

        values = g[...]
        units = u[...].astype(F32)
        std = istd[...][:, -1:]
        added = e[...].astype(F32) * flag_ref[0]
        stream[...] = norm_back(values, units, std, gain_ref[...], added).astype(BF)
        stats[0:1] += jnp.sum(values * units, axis=0, keepdims=True)
        stats[1:2] += jnp.sum(values, axis=0, keepdims=True)

    row = lambda n: pl.BlockSpec((block, n), lambda i: (i, 0))
    return pl.pallas_call(
        kernel,
        grid=(tokens // block,),
        in_specs=[
            row(width),
            row(width),
            row(inv.shape[1]),
            pl.BlockSpec((1, width), lambda i: (0, 0)),
            row(width),
            pl.BlockSpec(memory_space=pltpu.SMEM),
        ],
        out_specs=[row(width), pl.BlockSpec((2, width), lambda i: (0, 0))],
        out_shape=[
            jax.ShapeDtypeStruct((tokens, width), BF),
            jax.ShapeDtypeStruct((2, width), F32),
        ],
        name="last_back",
    )(grad, unit, inv, gain, extra, flag)


def mixing_back(heads_part, last_part, history):
    entries, tokens, width = history.shape
    streams = heads_part.shape[0] + 1
    rows, sub, lanes = min(64, tokens), 16, 256

    def kernel(first, last, hist, out):
        def step(r, carry):
            here = pl.ds(pl.multiple_of(r * sub, sub), sub)
            for s in range(streams):
                sums = [None] * entries
                for lane in range(0, width, lanes):
                    span = slice(lane, lane + lanes)
                    part = first[s, here, span] if s < streams - 1 else last[here, span]
                    part = part.astype(F32)
                    for j in range(entries):
                        term = part * hist[j, here, span].astype(F32)
                        sums[j] = term if lane == 0 else sums[j] + term
                columns = [jnp.sum(item, axis=-1, keepdims=True) for item in sums]
                out[s, here, :] = jnp.concatenate(columns, axis=-1)
            return carry

        lax.fori_loop(0, rows // sub, step, 0)

    return pl.pallas_call(
        kernel,
        grid=(tokens // rows,),
        in_specs=[
            pl.BlockSpec((streams - 1, rows, width), lambda i: (0, i, 0)),
            pl.BlockSpec((rows, width), lambda i: (i, 0)),
            pl.BlockSpec((entries, rows, width), lambda i: (0, i, 0)),
        ],
        out_specs=pl.BlockSpec((streams, rows, entries), lambda i: (0, i, 0)),
        out_shape=jax.ShapeDtypeStruct((streams, tokens, entries), F32),
        name="mixing_back",
    )(heads_part, last_part, history)


def far_attend(queries, keys, values, shard_offset):
    tokens, heads_here, head_size = queries.shape
    data_index = lax.axis_index("dp")
    pairs = [jnp.stack([keys, values])]
    reach = 2 * SEQ // tokens
    for back in range(1, reach):
        pairs.append(passed_along(pairs[0], "dp", back))
    usable = [(shard_offset[0] >= back * tokens) & (data_index >= back) for back in range(reach)]
    first_logits = block_logits(queries, keys, True)
    top = jnp.max(first_logits, axis=-1)
    total = jnp.sum(jnp.exp(first_logits - top[..., None]), axis=-1)
    for back in range(1, reach):

        def widen(state, block=pairs[back][0]):
            logits = block_logits(queries, block, False)
            new_top = jnp.maximum(state[0], jnp.max(logits, axis=-1))
            summed = state[1] * jnp.exp(state[0] - new_top) + jnp.sum(
                jnp.exp(logits - new_top[..., None]), axis=-1
            )
            return (new_top, summed)

        top, total = lax.cond(usable[back], widen, keep_same, (top, total))
    log_total = top + jnp.log(total)
    attended = jnp.zeros((tokens, heads_here, head_size), F32)
    for back in range(reach):

        def accumulate(current, block=pairs[back], diagonal=back == 0):
            probs = jnp.exp(block_logits(queries, block[0], diagonal) - log_total[..., None])
            return current + jnp.einsum(
                "hqk,khd->qhd", probs.astype(BF), block[1], preferred_element_type=F32
            )

        attended = lax.cond(usable[back], accumulate, keep_same, attended)
    return attended, (pairs, usable, log_total)


def far_attend_back(queries, attended_grad, kept):
    tokens, heads_here, head_size = queries.shape
    factor = 1.0 / math.sqrt(head_size)
    pairs, usable, log_total = kept
    reach = len(pairs)

    def weights_of(block, diagonal):
        return jnp.exp(block_logits(queries, block, diagonal) - log_total[..., None])

    def prob_grads(block):
        return jnp.einsum("qhd,khd->hqk", attended_grad, block[1], preferred_element_type=F32)

    delta = jnp.zeros((heads_here, tokens), F32)
    for back in range(reach):

        def gather_delta(current, block=pairs[back], diagonal=back == 0):
            return current + jnp.sum(weights_of(block[0], diagonal) * prob_grads(block), axis=-1)

        delta = lax.cond(usable[back], gather_delta, keep_same, delta)

    def skip_block(current):
        return (current, jnp.zeros((2, tokens, heads_here, head_size), F32))

    query_grad = jnp.zeros((tokens, heads_here, head_size), F32)
    key_value_grad = jnp.zeros((2, tokens, heads_here, head_size), F32)
    for back in range(reach):

        def spread(current, block=pairs[back], diagonal=back == 0):
            probs = weights_of(block[0], diagonal)
            score_grad = (probs * (prob_grads(block) - delta[..., None])).astype(BF)
            query_part = (
                current
                + jnp.einsum("hqk,khd->qhd", score_grad, block[0], preferred_element_type=F32)
                * factor
            )
            key_part = (
                jnp.einsum("hqk,qhd->khd", score_grad, queries, preferred_element_type=F32)
                * factor
            )
            value_part = jnp.einsum(
                "hqk,qhd->khd", probs.astype(BF), attended_grad, preferred_element_type=F32
            )
            return (query_part, jnp.stack([key_part, value_part]))

        query_grad, pair_grad = lax.cond(usable[back], spread, skip_block, query_grad)
        if back == 0:
            key_value_grad = pair_grad
        else:
            key_value_grad = key_value_grad + passed_along(pair_grad, "dp", -back)
    return jnp.concatenate([query_grad[None], key_value_grad])


def mix_block(i, coefficients, shares, last_share, extras, last_extras, arrived, whole):
    streams, block, width = shares.shape
    each = coefficients.shape[1] // (streams + 1)
    groups = 1 + len(extras)
    final = arrived is not None
    lanes = 512

    def kernel(*refs):
        weights = refs[0][...]
        heads, lasts = refs[1 : 1 + groups], refs[1 + groups : 1 + 2 * groups]
        out = refs[-1]
        columns = [weights[:, n : n + 1] for n in range(weights.shape[1])]
        for lane in range(0, width, lanes):
            span = slice(lane, lane + lanes)
            values = []
            for s in range(streams + 1):
                picks = [r[s, :, span] if s < streams else l[:, span] for r, l in zip(heads, lasts)]
                total = picks[0].astype(F32)
                for pick in picks[1:]:
                    total = total + pick.astype(F32)
                values.append(total)
            for e in range(each):
                total = columns[e * (streams + 1)] * values[0]
                for s in range(1, streams + 1):
                    total = total + columns[e * (streams + 1) + s] * values[s]
                if final:
                    total = total + refs[1 + 2 * groups][e, :, span].astype(F32)
                out[e, :, span] = total.astype(out.dtype)

    piece = pl.BlockSpec((streams, block, width), lambda n: (0, 0, 0))
    row = pl.BlockSpec((block, width), lambda n: (i, 0))
    small = pl.BlockSpec((each, block, width), lambda n: (0, 0, 0))
    specs = [pl.BlockSpec((block, coefficients.shape[1]), lambda n: (i, 0))]
    specs += [piece] * groups + [row] * groups
    args = [coefficients, shares, *extras, last_share, *last_extras]
    alias = {}
    if final:
        specs.append(small)
        args.append(arrived)
        if whole is not None:
            specs.append(pl.BlockSpec(memory_space=pl.ANY))
            args.append(whole)
            alias = {len(args) - 1: 0}
        out_spec = pl.BlockSpec((each, block, width), lambda n: (0, i, 0))
        out_shape = jax.ShapeDtypeStruct((each, coefficients.shape[0], width), F32)
    else:
        out_spec, out_shape = small, jax.ShapeDtypeStruct((each, block, width), BF)
    return pl.pallas_call(
        kernel,
        grid=(1,),
        in_specs=specs,
        out_specs=out_spec,
        out_shape=out_shape,
        input_output_aliases=alias,
        name="mix_final" if final else "mix_inward",
    )(*args)


def hidden_units(x, w_up):
    tokens, width = x.shape
    units = w_up.shape[1]
    block = min(512, units)

    def kernel(x_ref, w, out, slope):
        up = dot(x_ref[...], w[...])
        inside = 0.5 * (1.0 + lax.erf(up * math.sqrt(0.5)))
        out[...] = (up * inside).astype(BF)
        bell = jnp.exp(-0.5 * up * up) * (1.0 / math.sqrt(2.0 * math.pi))
        slope[...] = (inside + up * bell).astype(BF)

    column = pl.BlockSpec((tokens, block), lambda i: (0, i))
    return pl.pallas_call(
        kernel,
        grid=(units // block,),
        in_specs=[
            pl.BlockSpec((tokens, width), lambda i: (0, 0)),
            pl.BlockSpec((width, block), lambda i: (0, i)),
        ],
        out_specs=[column, column],
        out_shape=[jax.ShapeDtypeStruct((tokens, units), BF)] * 2,
        name="hidden_units",
    )(x, w_up)


def merge_branches(attended, hidden, w_merge, w_down, stream, flag):
    tokens, inner = attended.shape
    shards, units, cols = w_down.shape
    if cols % 128:
        merged = jnp.einsum("te,ned->tnd", attended, w_merge, preferred_element_type=F32)
        merged = merged + jnp.einsum("tf,nfd->tnd", hidden, w_down, preferred_element_type=F32)
        return merged.reshape(tokens, -1) + flag * stream

    def kernel(a, h, wm, wd, st, flag_ref, out):
        out[...] = dot(a[...], wm[0]) + dot(h[...], wd[0]) + flag_ref[0] * st[...]

    return pl.pallas_call(
        kernel,
        grid=(shards,),
        in_specs=[
            pl.BlockSpec((tokens, inner), lambda n: (0, 0)),
            pl.BlockSpec((tokens, units), lambda n: (0, 0)),
            pl.BlockSpec((1, inner, cols), lambda n: (n, 0, 0)),
            pl.BlockSpec((1, units, cols), lambda n: (n, 0, 0)),
            pl.BlockSpec((tokens, cols), lambda n: (0, n)),
            pl.BlockSpec(memory_space=pltpu.SMEM),
        ],
        out_specs=pl.BlockSpec((tokens, cols), lambda n: (0, n)),
        out_shape=jax.ShapeDtypeStruct((tokens, shards * cols), F32),
        name="merge_branches",
    )(attended, hidden, w_merge, w_down, stream, flag)


def back_through(grad, stacked, slope):
    tokens = grad.shape[0]
    shards, units, cols = stacked.shape
    if cols % 128:
        split = grad.reshape(tokens, shards, cols)
        total = jnp.einsum("tnd,nfd->tf", split, stacked, preferred_element_type=F32)
        return (total if slope is None else total * slope.astype(F32)).astype(BF)

    def kernel(*refs):
        g, w = refs[:2]
        out, acc = refs[-2:]
        n = pl.program_id(0)
        part = dot_cols(g[...], w[0])

        @pl.when(n == 0)
        def _():
            acc[...] = part

        @pl.when(n > 0)
        def _():
            acc[...] += part

        @pl.when(n == shards - 1)
        def _():
            total = acc[...]
            if slope is not None:
                total = total * refs[2][...].astype(F32)
            out[...] = total.astype(BF)

    specs = [
        pl.BlockSpec((tokens, cols), lambda n: (0, n)),
        pl.BlockSpec((1, units, cols), lambda n: (n, 0, 0)),
    ]
    args = [grad, stacked]
    if slope is not None:
        specs.append(pl.BlockSpec((tokens, units), lambda n: (0, 0)))
        args.append(slope)
    return pl.pallas_call(
        kernel,
        grid=(shards,),
        in_specs=specs,
        out_specs=pl.BlockSpec((tokens, units), lambda n: (0, 0)),
        out_shape=jax.ShapeDtypeStruct((tokens, units), BF),
        scratch_shapes=[pltpu.VMEM((tokens, units), F32)],
        name="back_through",
    )(*args)


def body(
    history,
    mixing,
    shard_offset,
    norm_gain,
    norm_bias,
    w_heads,
    w_merge,
    w_up,
    w_down,
    mixer_first,
    mixer_second,
    out_cotangent,
    next_cotangent,
):
    member = lax.axis_index("stream")
    members = lax.axis_size("stream")
    shards = lax.axis_size("dp")
    index = lax.axis_index("dp")
    entries, tokens, width = history.shape
    heads_here = w_heads.shape[2] // HD
    half = tokens // 2
    highest = lax.Precision.HIGHEST
    flag = (member == members - 1).astype(F32)
    flags = flag.reshape(1)
    near = shards == 8 and heads_here * 2 == shards and tokens * shards == 2 * SEQ

    got_heads = Gathered(w_heads, direct=near)
    got_up = Gathered(after(w_up, got_heads.shard))
    got_merge = Gathered(w_merge)
    cotangent = lax.all_gather(out_cotangent, "stream", axis=1, tiled=True)
    lanes = jnp.concatenate([norm_gain, norm_bias]).astype(F32).reshape(tokens, -1)
    packed = lax.all_gather(jnp.concatenate([mixing[:, 0, :], lanes], axis=1), "stream", axis=0)
    mix_all = packed[:, :, :entries]
    norms = packed[:, :, entries:].reshape(members, 2, width)
    gains, biases = norms[:, 0], norms[:, 1]
    mix_rows = jnp.transpose(mix_all, (1, 0, 2)).reshape(tokens, members * entries)

    normed, unit, inv, stream = make_streams(history, mix_rows, gains, biases)
    full_heads = got_heads.whole()
    positions = shard_offset[0] + jnp.arange(tokens, dtype=jnp.int32)
    projected = project(normed, full_heads, rope_tables(positions, 1.0))

    first_rows = mixer_first.astype(F32).reshape(tokens, -1)
    second_flat = mixer_second[:, 0, :].astype(F32).reshape(-1)
    hidden_count = mixer_second.shape[0]
    lines = -(-second_flat.shape[0] // tokens)
    second_rows = jnp.pad(second_flat, (0, lines * tokens - second_flat.shape[0]))
    rest = jnp.concatenate(
        [next_cotangent[:, 0, :], first_rows, second_rows.reshape(tokens, lines)], axis=1
    )
    rest = lax.all_gather(after(rest, projected), "stream", axis=0)
    outputs = next_cotangent.shape[2]
    cut = outputs + first_rows.shape[1]
    next_full = rest[:, :, :outputs]
    first_full = rest[:, :, outputs:cut].astype(BF).reshape(width, -1)
    second_full = rest[:, :, cut:].reshape(members, -1)[:, : second_flat.shape[0]]
    second_full = second_full.reshape(members, hidden_count, outputs)

    if near:
        spread = after(jnp.broadcast_to(shard_offset[:, None], (8, 128)), projected)
        offsets = lax.all_gather(spread, "dp", axis=0)[:, 0, 0]
        side = (index % 2).astype(jnp.int32).reshape(1)
        place = jnp.arange(shards, dtype=jnp.int32)
        first_key = jnp.maximum(place - offsets // tokens, 0).astype(jnp.int32)
        own = lax.all_to_all(projected, "dp", 0, 0, tiled=True)
        own = after(own, next_full, first_full, second_full, cotangent)
        got_down = Gathered(after(w_down, own))
        other = partner(own[:, 1:], 1)
        full_up = got_up.whole()
        full_merge = got_merge.whole()
        result, exact, level = attend(own, other, first_key, side)
        back = lax.all_to_all(result, "dp", 0, 0, tiled=True)
        attended = jnp.transpose(back.reshape(heads_here, tokens, HD), (1, 0, 2)).reshape(tokens, -1)
    else:
        got_down = Gathered(w_down)
        full_up = got_up.whole()
        full_merge = got_merge.whole()
        split = projected.reshape(heads_here, 2, 3, half, HD)
        split = jnp.transpose(split, (2, 1, 3, 0, 4)).reshape(3, tokens, heads_here, HD)
        result, kept = far_attend(split[0], split[1], split[2], shard_offset)
        attended = result.reshape(tokens, -1).astype(BF)
    full_down = got_down.whole()
    flat_up = full_up.reshape(width, -1)
    hidden, slope = hidden_units(normed[members - 1], flat_up)
    attended = after(attended, hidden)
    share = merge_branches(attended, hidden, full_merge, full_down, stream, flags)

    inner = (member == 1) | (member == 2)
    count = 4
    rows = [lax.slice_in_dim(share, i * tokens // count, (i + 1) * tokens // count) for i in range(count)]
    totals = {}

    def middle(i, one):
        return (rows[i] + one.astype(F32)).astype(BF)

    def ends(i, one, two):
        totals[i] = (rows[i] + one.astype(F32) + two.astype(F32)).astype(BF)
        return totals[i]

    _, _, arrived = along_line(count, lambda i, gates: gated(rows[i].astype(BF), gates), middle, ends)
    block_full = jnp.concatenate([jnp.where(inner, totals[i], arrived[i]) for i in range(count)])

    mine = member * (width // members)
    block_out = lax.dynamic_slice_in_dim(block_full, mine, width // members, axis=1)
    out_float = block_full.astype(F32)
    scale = lax.rsqrt(jnp.sum(out_float * out_float, axis=-1) / width + 1e-06)
    proj = dot(block_full, first_full)
    mixer, mixer_back = jax.vjp(exact_gelu, scale[:, None] * proj)
    second_here = mixer_second[:, 0, :].astype(F32)
    next_here = jnp.dot(mixer, second_here, precision=highest, preferred_element_type=F32)
    mixer_grad = jnp.einsum(
        "stn,scn->tc", next_full, second_full, precision=highest, preferred_element_type=F32
    )
    pre_grad = mixer_back(mixer_grad)[0]
    proj_grad = (scale[:, None] * pre_grad).astype(BF)
    scale_grad = jnp.sum(pre_grad * proj, axis=-1)
    second_local = jnp.dot(
        mixer.T, next_cotangent[:, 0, :], precision=highest, preferred_element_type=F32
    )
    first_local = dot_rows(block_out, proj_grad)
    grad_out = (
        cotangent.astype(F32)
        + dot_cols(proj_grad, first_full)
        - (scale * scale * scale * scale_grad)[:, None] * out_float / width
    ).astype(BF)

    attended_grad = back_through(grad_out, full_merge, None)
    up_grad = back_through(grad_out, full_down, slope)
    merge_grad = dot_rows(attended, grad_out).astype(BF)
    if near:
        sent = attended_grad.reshape(tokens, heads_here, HD)
        sent = jnp.transpose(sent, (1, 0, 2)).reshape(shards, half, HD)
        grads = lax.all_to_all(sent, "dp", 0, 0, tiled=True)
        grads = after(grads, up_grad)
        kept_grads, given = attend_back(own, other, grads, exact, level, first_key, side)
        taken = partner(given, 1)
        summed = kept_grads[:, 1:].astype(F32) + taken.astype(F32)
        pair = jnp.concatenate([kept_grads[:, :1], summed.astype(BF)], axis=1)
        parts = lax.all_to_all(pair, "dp", 0, 0, tiled=True)
        up_grad = after(up_grad, pair)
    else:
        grads = far_attend_back(split[0], attended_grad.reshape(tokens, heads_here, HD), kept)
        parts = grads.reshape(3, 2, half, heads_here, HD)
        parts = jnp.transpose(parts, (3, 1, 0, 2, 4)).reshape(2 * heads_here, 3, half, HD)

    last_normed = dot_cols(up_grad, flat_up)
    last_share, last_stats = last_back(
        last_normed, unit[members - 1], inv, gains[members - 1 :], grad_out, flags
    )
    last_one = line_hop(last_share, OUTWARD)
    down_grad = dot_rows(after(hidden, last_share), grad_out).astype(BF)
    parts = after(parts, last_share, down_grad)
    blocks = 8
    *pieces, heads_share, heads_grad, heads_stats = heads_back(
        parts, full_heads, normed, unit, inv, gains, rope_tables(positions, -1.0), blocks
    )
    last_two = line_hop((last_share.astype(F32) + last_one.astype(F32)).astype(BF), MIDDLE)
    up_back = dot_rows(normed[members - 1], after(up_grad, heads_share)).astype(BF)

    grad_merge = lax.psum_scatter(merge_grad, "dp", scatter_dimension=1, tiled=True).astype(F32)
    grad_down = lax.psum_scatter(down_grad, "dp", scatter_dimension=1, tiled=True).astype(F32)
    grad_heads = lax.psum_scatter(heads_grad, "dp", scatter_dimension=1, tiled=True).astype(F32)
    grad_up = lax.psum_scatter(up_back, "dp", scatter_dimension=0, tiled=True).astype(F32)

    each = entries // members

    def weights_for(owner):
        block = lax.dynamic_slice_in_dim(mix_all, owner * each, each, axis=2)
        return jnp.transpose(block, (1, 2, 0)).reshape(tokens, each * members)

    there = weights_for(jnp.where(member == 1, 0, members - 1))
    here = weights_for(member)
    extra = {}

    def first_hop(i, gates):
        if i == 1:
            mix_parts = mixing_back(heads_share, last_share, history)
            stats = jnp.concatenate([heads_stats, last_stats[None]])
            both = jnp.concatenate([mix_parts, stats.reshape(members, tokens, -1)], axis=2)
            extra["both"] = jnp.sum(lax.all_to_all(both, "stream", 0, 0, tiled=True), axis=0)
        if i == 4:
            sums = extra["both"][:, entries:]
            second_sums = jnp.pad(second_local.reshape(-1), (0, lines * tokens - second_flat.shape[0]))
            local = jnp.concatenate(
                [sums, first_local.reshape(tokens, -1), second_sums.reshape(tokens, lines)], axis=1
            )
            extra["all"] = jnp.sum(lax.all_gather(local, "dp", axis=0), axis=0)
            gates = gates + [extra["both"]]
        if i == 7:
            gates = gates + [extra["all"]]
        return gated(pieces[i], gates)

    def second_hop(i, one):
        return (pieces[i].astype(F32) + one.astype(F32)).astype(BF)

    def third_hop(i, one, two):
        return mix_block(i, there, pieces[i], last_share, [two], [last_two], None, None)

    ones, twos, threes = along_line(blocks, first_hop, second_hop, third_hop)
    grad_history = None
    for i in range(blocks):
        grad_history = mix_block(
            i, here, pieces[i], last_share, [ones[i], twos[i]], [last_one, last_two], threes[i], grad_history
        )

    grad_mixing = extra["both"][:, :entries][:, None, :]
    sums = extra["all"]
    spans = 2 * width // tokens
    stats = sums[:, :spans].reshape(2, width)
    grad_first = sums[:, spans:-lines].reshape(mixer_first.shape)
    grad_second = sums[:, -lines:].reshape(-1)[: second_flat.shape[0]].reshape(hidden_count, outputs)
    return (
        block_out,
        next_here[:, None, :],
        grad_history,
        grad_mixing,
        stats[:1],
        stats[1:],
        grad_heads,
        grad_merge,
        grad_up,
        grad_down,
        grad_first,
        grad_second[:, None, :],
    )


def solution(mesh):
    in_specs = (
        P(None, "dp", None),
        P("dp", "stream", None),
        P("dp"),
        P("stream", None),
        P("stream", None),
        P(None, "dp", "stream"),
        P("stream", "dp"),
        P("dp", "stream"),
        P("stream", "dp"),
        P("stream", None),
        P(None, "stream", None),
        P("dp", "stream"),
        P("dp", "stream", None),
    )
    out_specs = (
        P("dp", "stream"),
        P("dp", "stream", None),
        P("stream", "dp", None),
        P("dp", "stream", None),
        P("stream", None),
        P("stream", None),
        P(None, "dp", "stream"),
        P("stream", "dp"),
        P("dp", "stream"),
        P("stream", "dp"),
        P("stream", None),
        P(None, "stream", None),
    )
    return jax.shard_map(body, mesh=mesh, in_specs=in_specs, out_specs=out_specs, check_vma=False)
```

```python
import math

import jax
import jax.numpy as jnp
from jax import lax
from jax.experimental import pallas as pl
from jax.experimental.pallas import tpu as pltpu
from jax.sharding import PartitionSpec as P

HD = 128
ROT = 32
SEQ = 2048


def passed_along(shard, axis, by):
    peers = lax.axis_size(axis)
    pairs = [(i, i + by) for i in range(peers) if 0 <= i + by < peers]
    return lax.ppermute(shard, axis, pairs)


def rotate(vectors, positions, sign):
    half = ROT // 2
    counter = jnp.arange(half, dtype=jnp.float32)
    freqs = jnp.exp(counter * (-2.0 * math.log(10000.0) / ROT))
    angles = positions.astype(jnp.float32)[:, None] * freqs[None, :]
    cosine = jnp.cos(angles)[:, None, :]
    sine = sign * jnp.sin(angles)[:, None, :]
    first = vectors[..., :half]
    second = vectors[..., half:ROT]
    return jnp.concatenate(
        [first * cosine - second * sine, second * cosine + first * sine, vectors[..., ROT:]],
        axis=-1,
    )


def exact_gelu(vectors):
    return jax.nn.gelu(vectors, approximate=False)


def block_logits(queries, keys_block, diagonal):
    logits = jnp.einsum("qhd,khd->hqk", queries, keys_block, preferred_element_type=jnp.float32) * (
        1.0 / math.sqrt(queries.shape[-1])
    )
    if diagonal:
        counter = jnp.arange(queries.shape[0], dtype=jnp.int32)
        allowed = counter[None, :] <= counter[:, None]
        logits = jnp.where(allowed[None], logits, -1e30)
    return logits


def keep_same(state):
    return state


BF = jnp.bfloat16
F32 = jnp.float32
OUTWARD = [(0, 1), (3, 2)]
MIDDLE = [(1, 2), (2, 1)]
INWARD = [(1, 0), (2, 3)]


def dot(left, right):
    return jnp.dot(left, right, preferred_element_type=F32)


def dot_rows(left, right):
    return lax.dot_general(left, right, (((0,), (0,)), ((), ())), preferred_element_type=F32)


def dot_cols(left, right):
    return lax.dot_general(left, right, (((1,), (1,)), ((), ())), preferred_element_type=F32)


def partner(shard, bit):
    peers = lax.axis_size("dp")
    return lax.ppermute(shard, "dp", [(i, i ^ bit) for i in range(peers)])


def line_hop(shard, pairs):
    return lax.ppermute(shard, "stream", pairs)


def cost(microseconds):
    return pl.CostEstimate(
        flops=int(microseconds * 0.9e9), bytes_accessed=int(microseconds * 3e6), transcendentals=0
    )


def after(value, *others):
    return lax.optimization_barrier((value, *others))[0]


class Gathered:
    def __init__(self, shard, direct=False):
        self.shard = shard
        self.peers = lax.axis_size("dp")
        if self.peers != 8:
            self.by_x = self.by_y = shard
            return
        self.cut = max(range(shard.ndim - 1), key=lambda dim: shard.shape[dim])
        self.by_x = partner(shard, 2)
        self.by_y = partner(shard, 4)
        self.across = partner(shard, 6) if direct else None

    def whole(self, *earlier):
        shard = self.shard
        if self.peers != 8:
            return lax.all_gather(shard, "dp", axis=0)
        index = lax.axis_index("dp")
        cut = self.cut
        half = shard.shape[cut] // 2
        shard, by_x, by_y = [gated(item, earlier) for item in (shard, self.by_x, self.by_y)]
        pieces = [(shard, 0, 0), (by_x, 2, 0), (by_y, 4, 0)]
        if self.across is None:
            low = lax.slice_in_dim(by_y, 0, half, axis=cut)
            high = lax.slice_in_dim(by_x, half, 2 * half, axis=cut)
            pieces += [(partner(low, 2), 6, 0), (partner(high, 4), 6, half)]
        else:
            pieces.append((self.across, 6, 0))
        pieces += [(partner(piece, 1), code ^ 1, start) for piece, code, start in pieces]
        return put_together(pieces, shard, self.peers, cut, index)


def put_together(pieces, shard, peers, cut, index):
    codes = [(code, start) for _, code, start in pieces]
    arrays = [piece for piece, _, _ in pieces]

    def kernel(place, *refs):
        out, sems = refs[-2:]
        copies = []
        for n, (code, start) in enumerate(codes):
            size = refs[n].shape[cut]
            span = tuple(
                pl.ds(start, size) if dim == cut else slice(None) for dim in range(shard.ndim)
            )
            target = out.at[(place[0] ^ code, *span)]
            copies.append(pltpu.make_async_copy(refs[n], target, sems.at[n]))
        for copy in copies:
            copy.start()
        for copy in copies:
            copy.wait()

    anywhere = pl.BlockSpec(memory_space=pl.ANY)
    size = peers * shard.size * shard.dtype.itemsize
    return pl.pallas_call(
        kernel,
        in_specs=[pl.BlockSpec(memory_space=pltpu.SMEM)] + [anywhere] * len(arrays),
        out_specs=anywhere,
        out_shape=jax.ShapeDtypeStruct((peers, *shard.shape), shard.dtype),
        scratch_shapes=[pltpu.SemaphoreType.DMA((len(arrays),))],
        cost_estimate=cost(2 * size / 3e6),
        name="put_together",
    )(index.astype(jnp.int32).reshape(1), *arrays)


def along_line(count, first, second, third, finish=None):
    ones, twos, threes, ends = [], [], [], []
    for step in range(count + 2):
        if step < count:
            gates = []
            if step >= 2:
                gates.append(ones[step - 2])
            if step >= 3:
                gates.append(twos[step - 3])
            if step >= 4:
                gates.append(threes[step - 4] if finish is None else ends[step - 4])
            ones.append(line_hop(first(step, gates), OUTWARD))
        if 0 <= step - 1 < count:
            twos.append(line_hop(second(step - 1, ones[step - 1]), MIDDLE))
        if 0 <= step - 2 < count:
            back = step - 2
            threes.append(line_hop(third(back, ones[back], twos[back]), INWARD))
            if finish is not None:
                ends.append(finish(back, ones[back], twos[back], threes[back]))
    return ones, twos, threes


def gated(value, gates):
    return after(value, *gates) if gates else value


def rope_tables(positions, sign):
    half = ROT // 2
    lane = jnp.arange(HD, dtype=jnp.int32)
    counter = (lane % half).astype(F32)
    freqs = jnp.exp(counter * (-2.0 * math.log(10000.0) / ROT))
    angles = positions.astype(F32)[:, None] * freqs[None, :]
    cosine = jnp.where(lane < ROT, jnp.cos(angles), 1.0)
    sine = sign * jnp.sin(angles)
    up = jnp.where(lane < half, -sine, 0.0)
    down = jnp.where((lane >= half) & (lane < ROT), sine, 0.0)
    return jnp.stack([cosine, up, down])


def turned(block, tables):
    half = ROT // 2
    return (
        block * tables[0]
        + pltpu.roll(block, HD - half, 1) * tables[1]
        + pltpu.roll(block, half, 1) * tables[2]
    )


def make_streams(history, mix_rows, gains, biases):
    entries, tokens, width = history.shape
    streams = gains.shape[0]
    rows, sub, lanes = min(64, tokens), 16, 512

    def kernel(hist, mix, gain, bias, normed, unit, inv, last, scratch):
        def step(r, carry):
            here = pl.ds(pl.multiple_of(r * sub, sub), sub)
            weights = mix[here, :]
            columns = [
                [weights[:, s * entries + j : s * entries + j + 1] for j in range(entries)]
                for s in range(streams)
            ]
            for lane in range(0, width, lanes):
                span = slice(lane, lane + lanes)
                sums = [None] * streams
                for j in range(entries):
                    part = hist[j, here, span].astype(F32)
                    for s in range(streams):
                        term = columns[s][j] * part
                        sums[s] = term if j == 0 else sums[s] + term
                for s in range(streams):
                    scratch[s, :, span] = sums[s]
            stds = []
            for s in range(streams):
                values = scratch[s]
                center = values - jnp.sum(values, axis=-1, keepdims=True) * (1.0 / width)
                var = jnp.sum(center * center, axis=-1, keepdims=True) * (1.0 / width)
                std = lax.rsqrt(var + 1e-05)
                stds.append(std)
                scaled = center * std
                unit[s, here, :] = scaled.astype(BF)
                normed[s, here, :] = (scaled * gain[s : s + 1] + bias[s : s + 1]).astype(BF)
            last[here, :] = scratch[streams - 1]
            inv[here, :] = jnp.concatenate(stds, axis=-1)
            return carry

        lax.fori_loop(0, rows // sub, step, 0)

    wide = jax.ShapeDtypeStruct((streams, tokens, width), BF)
    return pl.pallas_call(
        kernel,
        grid=(tokens // rows,),
        in_specs=[
            pl.BlockSpec((entries, rows, width), lambda i: (0, i, 0)),
            pl.BlockSpec((rows, streams * entries), lambda i: (i, 0)),
            pl.BlockSpec((streams, width), lambda i: (0, 0)),
            pl.BlockSpec((streams, width), lambda i: (0, 0)),
        ],
        out_specs=[
            pl.BlockSpec((streams, rows, width), lambda i: (0, i, 0)),
            pl.BlockSpec((streams, rows, width), lambda i: (0, i, 0)),
            pl.BlockSpec((rows, streams), lambda i: (i, 0)),
            pl.BlockSpec((rows, width), lambda i: (i, 0)),
        ],
        out_shape=[
            wide,
            wide,
            jax.ShapeDtypeStruct((tokens, streams), F32),
            jax.ShapeDtypeStruct((tokens, width), F32),
        ],
        scratch_shapes=[pltpu.VMEM((streams, sub, width), F32)],
        cost_estimate=cost(22),
        name="make_streams",
    )(history, mix_rows, gains, biases)


def project(normed, w_heads, tables):
    _, tokens, width = normed.shape
    columns = w_heads.shape[3]
    heads, half = columns // HD, tokens // 2

    def kernel(x, w, table, out):
        flat = dot(x[0], w[...].reshape(width, columns))
        turn = pl.program_id(0) < 2

        def put(head, block):
            out[2 * head, 0] = block[:half].astype(BF)
            out[2 * head + 1, 0] = block[half:].astype(BF)

        @pl.when(turn)
        def _():
            for head in range(heads):
                put(head, turned(flat[:, head * HD : (head + 1) * HD], table[...]))

        @pl.when(jnp.logical_not(turn))
        def _():
            for head in range(heads):
                put(head, flat[:, head * HD : (head + 1) * HD])

    return pl.pallas_call(
        kernel,
        grid=(3,),
        in_specs=[
            pl.BlockSpec((1, tokens, width), lambda c: (c, 0, 0)),
            pl.BlockSpec((w_heads.shape[0], 1, w_heads.shape[2], columns), lambda c: (0, c, 0, 0)),
            pl.BlockSpec((3, tokens, HD), lambda c: (0, 0, 0)),
        ],
        out_specs=pl.BlockSpec((2 * heads, 1, half, HD), lambda c: (0, c, 0, 0)),
        out_shape=jax.ShapeDtypeStruct((2 * heads, 3, half, HD), BF),
        cost_estimate=cost(9),
        name="project",
    )(normed, w_heads, tables)


def attend(own, other, first_key, side):
    shards, _, half, _ = own.shape
    factor = 1.0 / math.sqrt(HD)

    def kernel(first, part, mine, theirs, out, exact, norm):
        s = pl.program_id(0)
        query = mine[s, 0]

        def fold(state, keys, values, mask):
            top, total, acc = state
            logits = dot_cols(query, keys) * factor
            if mask is not None:
                logits = jnp.where(mask, logits, -1e30)
            new_top = jnp.maximum(top, jnp.max(logits, axis=-1, keepdims=True))
            probs = jnp.exp(logits - new_top)
            keep = jnp.exp(top - new_top)
            return (
                new_top,
                total * keep + jnp.sum(probs, axis=-1, keepdims=True),
                acc * keep + dot(probs.astype(BF), values),
            )

        row = lax.broadcasted_iota(jnp.int32, (half, half), 0)
        col = lax.broadcasted_iota(jnp.int32, (half, half), 1)
        state = (
            jnp.full((half, 1), -1e30, F32),
            jnp.zeros((half, 1), F32),
            jnp.zeros((half, HD), F32),
        )
        state = fold(state, mine[s, 1], mine[s, 2], col <= row)
        state = lax.fori_loop(
            0, part[0], lambda i, st: fold(st, theirs[s, 0], theirs[s, 1], None), state
        )

        def shard_step(b, st):
            st = fold(st, mine[b, 1], mine[b, 2], None)
            return fold(st, theirs[b, 0], theirs[b, 1], None)

        top, total, acc = lax.fori_loop(first[s], s, shard_step, state)
        result = acc / total
        out[0] = result.astype(BF)
        exact[0] = result
        norm[0] = top + jnp.log(total)

    return pl.pallas_call(
        kernel,
        grid_spec=pltpu.PrefetchScalarGridSpec(
            num_scalar_prefetch=2,
            grid=(shards,),
            in_specs=[
                pl.BlockSpec((shards, 3, half, HD), lambda s, *_: (0, 0, 0, 0)),
                pl.BlockSpec((shards, 2, half, HD), lambda s, *_: (0, 0, 0, 0)),
            ],
            out_specs=[
                pl.BlockSpec((1, half, HD), lambda s, *_: (s, 0, 0)),
                pl.BlockSpec((1, half, HD), lambda s, *_: (s, 0, 0)),
                pl.BlockSpec((1, half, 1), lambda s, *_: (s, 0, 0)),
            ],
        ),
        out_shape=[
            jax.ShapeDtypeStruct((shards, half, HD), BF),
            jax.ShapeDtypeStruct((shards, half, HD), F32),
            jax.ShapeDtypeStruct((shards, half, 1), F32),
        ],
        cost_estimate=cost(16),
        name="attend",
    )(first_key, side, own, other)


def attend_back(own, other, grads, exact, norm, first_key, side):
    shards, _, half, _ = own.shape
    factor = 1.0 / math.sqrt(HD)

    def kernel(first, part, mine, theirs, grad_ref, exact_ref, norm_ref, kept, given, sums):
        s = pl.program_id(0)
        query = mine[s, 0]
        grad = grad_ref[s]
        delta = jnp.sum(grad.astype(F32) * exact_ref[0], axis=-1, keepdims=True)
        level = norm_ref[0]
        lowered = grad

        @pl.when(s == 0)
        def _():
            sums[...] = jnp.zeros_like(sums)

        def fold(query_grad, keys, values, mask, slot, b):
            logits = dot_cols(query, keys) * factor
            probs = jnp.exp(logits - level)
            if mask is not None:
                probs = jnp.where(mask, probs, 0.0)
            score = (probs * (dot_cols(grad, values) - delta)).astype(BF)
            sums[slot, b] += dot_rows(score, query)
            sums[slot + 1, b] += dot_rows(probs.astype(BF), lowered)
            return query_grad + dot(score, keys)

        row = lax.broadcasted_iota(jnp.int32, (half, half), 0)
        col = lax.broadcasted_iota(jnp.int32, (half, half), 1)
        total = fold(jnp.zeros((half, HD), F32), mine[s, 1], mine[s, 2], col <= row, 0, s)
        total = lax.fori_loop(
            0, part[0], lambda i, q: fold(q, theirs[s, 0], theirs[s, 1], None, 2, s), total
        )

        def shard_step(b, q):
            q = fold(q, mine[b, 1], mine[b, 2], None, 0, b)
            return fold(q, theirs[b, 0], theirs[b, 1], None, 2, b)

        total = lax.fori_loop(first[s], s, shard_step, total)
        kept[s, 0] = (total * factor).astype(BF)

        @pl.when(s == shards - 1)
        def _():
            for b in range(shards):
                kept[b, 1] = (sums[0, b] * factor).astype(BF)
                kept[b, 2] = sums[1, b].astype(BF)
                given[b, 0] = (sums[2, b] * factor).astype(BF)
                given[b, 1] = sums[3, b].astype(BF)

    whole = lambda n: pl.BlockSpec((shards, n, half, HD), lambda s, *_: (0, 0, 0, 0))
    return pl.pallas_call(
        kernel,
        grid_spec=pltpu.PrefetchScalarGridSpec(
            num_scalar_prefetch=2,
            grid=(shards,),
            in_specs=[
                whole(3),
                whole(2),
                pl.BlockSpec((shards, half, HD), lambda s, *_: (0, 0, 0)),
                pl.BlockSpec((1, half, HD), lambda s, *_: (s, 0, 0)),
                pl.BlockSpec((1, half, 1), lambda s, *_: (s, 0, 0)),
            ],
            out_specs=[whole(3), whole(2)],
            scratch_shapes=[pltpu.VMEM((4, shards, half, HD), F32)],
        ),
        out_shape=[
            jax.ShapeDtypeStruct((shards, 3, half, HD), BF),
            jax.ShapeDtypeStruct((shards, 2, half, HD), BF),
        ],
        cost_estimate=cost(22),
        name="attend_back",
    )(first_key, side, own, other, grads, exact, norm)


def norm_back(grad, unit, inv, gain, extra):
    width = grad.shape[1]
    scaled = grad * gain
    mean = jnp.sum(scaled, axis=-1, keepdims=True) * (1.0 / width)
    slope = jnp.sum(scaled * unit, axis=-1, keepdims=True) * (1.0 / width)
    result = inv * (scaled - mean - unit * slope)
    return result if extra is None else result + extra


def heads_back(parts, w_heads, normed, unit, inv, gains, tables, count):
    _, tokens, width = normed.shape
    columns = w_heads.shape[3]
    heads, half = columns // HD, tokens // 2
    block = tokens // count

    def kernel(part, w, x, u, istd, gain, table, *refs):
        pieces, (stream, weight, stats, grad, wide) = refs[:count], refs[count:]
        c = pl.program_id(0)
        turn = c < 2

        def take(head):
            return jnp.concatenate([part[2 * head, 0], part[2 * head + 1, 0]], axis=0).astype(F32)

        @pl.when(turn)
        def _():
            for head in range(heads):
                grad[:, head * HD : (head + 1) * HD] = turned(take(head), table[...]).astype(BF)

        @pl.when(jnp.logical_not(turn))
        def _():
            for head in range(heads):
                grad[:, head * HD : (head + 1) * HD] = take(head).astype(BF)

        wide[...] = dot_cols(grad[...], w[...].reshape(width, columns))
        weight[0] = dot_rows(x[0], grad[...]).astype(BF)
        stats[...] = jnp.zeros_like(stats)
        column = lax.broadcasted_iota(jnp.int32, (block, istd.shape[1]), 1)

        for r in range(count):
            here = slice(r * block, (r + 1) * block)
            values = wide[here, :]
            units = u[0, here, :].astype(F32)
            std = jnp.sum(jnp.where(column == c, istd[here, :], 0.0), axis=-1, keepdims=True)
            result = norm_back(values, units, std, gain[0], None).astype(BF)
            stream[0, here, :] = result
            pieces[r][0] = result
            stats[0, 0:1] += jnp.sum(values * units, axis=0, keepdims=True)
            stats[0, 1:2] += jnp.sum(values, axis=0, keepdims=True)

    return pl.pallas_call(
        kernel,
        grid=(3,),
        in_specs=[
            pl.BlockSpec((2 * heads, 1, half, HD), lambda c: (0, c, 0, 0)),
            pl.BlockSpec((w_heads.shape[0], 1, w_heads.shape[2], columns), lambda c: (0, c, 0, 0)),
            pl.BlockSpec((1, tokens, width), lambda c: (c, 0, 0)),
            pl.BlockSpec((1, tokens, width), lambda c: (c, 0, 0)),
            pl.BlockSpec((tokens, inv.shape[1]), lambda c: (0, 0)),
            pl.BlockSpec((1, 1, width), lambda c: (c, 0, 0)),
            pl.BlockSpec((3, tokens, HD), lambda c: (0, 0, 0)),
        ],
        out_specs=[pl.BlockSpec((1, block, width), lambda c: (c, 0, 0))] * count
        + [
            pl.BlockSpec((1, tokens, width), lambda c: (c, 0, 0)),
            pl.BlockSpec((1, width, columns), lambda c: (c, 0, 0)),
            pl.BlockSpec((1, 2, width), lambda c: (c, 0, 0)),
        ],
        out_shape=[jax.ShapeDtypeStruct((3, block, width), BF)] * count
        + [
            jax.ShapeDtypeStruct((3, tokens, width), BF),
            jax.ShapeDtypeStruct((3, width, columns), BF),
            jax.ShapeDtypeStruct((3, 2, width), F32),
        ],
        scratch_shapes=[pltpu.VMEM((tokens, columns), BF), pltpu.VMEM((tokens, width), F32)],
        cost_estimate=cost(18),
        name="heads_back",
    )(parts, w_heads, normed, unit, inv, gains[:, None, :], tables)


def last_back(grad, unit, inv, gain, extra, flag):
    tokens, width = grad.shape
    block = min(128, tokens)

    def kernel(g, u, istd, gain_ref, e, flag_ref, stream, stats):
        @pl.when(pl.program_id(0) == 0)
        def _():
            stats[...] = jnp.zeros_like(stats)

        values = g[...]
        units = u[...].astype(F32)
        std = istd[...][:, -1:]
        added = e[...].astype(F32) * flag_ref[0]
        stream[...] = norm_back(values, units, std, gain_ref[...], added).astype(BF)
        stats[0:1] += jnp.sum(values * units, axis=0, keepdims=True)
        stats[1:2] += jnp.sum(values, axis=0, keepdims=True)

    row = lambda n: pl.BlockSpec((block, n), lambda i: (i, 0))
    return pl.pallas_call(
        kernel,
        grid=(tokens // block,),
        in_specs=[
            row(width),
            row(width),
            row(inv.shape[1]),
            pl.BlockSpec((1, width), lambda i: (0, 0)),
            row(width),
            pl.BlockSpec(memory_space=pltpu.SMEM),
        ],
        out_specs=[row(width), pl.BlockSpec((2, width), lambda i: (0, 0))],
        out_shape=[
            jax.ShapeDtypeStruct((tokens, width), BF),
            jax.ShapeDtypeStruct((2, width), F32),
        ],
        cost_estimate=cost(7),
        name="last_back",
    )(grad, unit, inv, gain, extra, flag)


def mixing_back(heads_part, last_part, history):
    entries, tokens, width = history.shape
    streams = heads_part.shape[0] + 1
    rows, sub, lanes = min(64, tokens), 16, 256

    def kernel(first, last, hist, out):
        def step(r, carry):
            here = pl.ds(pl.multiple_of(r * sub, sub), sub)
            for s in range(streams):
                sums = [None] * entries
                for lane in range(0, width, lanes):
                    span = slice(lane, lane + lanes)
                    part = first[s, here, span] if s < streams - 1 else last[here, span]
                    part = part.astype(F32)
                    for j in range(entries):
                        term = part * hist[j, here, span].astype(F32)
                        sums[j] = term if lane == 0 else sums[j] + term
                columns = [jnp.sum(item, axis=-1, keepdims=True) for item in sums]
                out[s, here, :] = jnp.concatenate(columns, axis=-1)
            return carry

        lax.fori_loop(0, rows // sub, step, 0)

    return pl.pallas_call(
        kernel,
        grid=(tokens // rows,),
        in_specs=[
            pl.BlockSpec((streams - 1, rows, width), lambda i: (0, i, 0)),
            pl.BlockSpec((rows, width), lambda i: (i, 0)),
            pl.BlockSpec((entries, rows, width), lambda i: (0, i, 0)),
        ],
        out_specs=pl.BlockSpec((streams, rows, entries), lambda i: (0, i, 0)),
        out_shape=jax.ShapeDtypeStruct((streams, tokens, entries), F32),
        cost_estimate=cost(18),
        name="mixing_back",
    )(heads_part, last_part, history)


def far_attend(queries, keys, values, shard_offset):
    tokens, heads_here, head_size = queries.shape
    data_index = lax.axis_index("dp")
    pairs = [jnp.stack([keys, values])]
    reach = 2 * SEQ // tokens
    for back in range(1, reach):
        pairs.append(passed_along(pairs[0], "dp", back))
    usable = [(shard_offset[0] >= back * tokens) & (data_index >= back) for back in range(reach)]
    first_logits = block_logits(queries, keys, True)
    top = jnp.max(first_logits, axis=-1)
    total = jnp.sum(jnp.exp(first_logits - top[..., None]), axis=-1)
    for back in range(1, reach):

        def widen(state, block=pairs[back][0]):
            logits = block_logits(queries, block, False)
            new_top = jnp.maximum(state[0], jnp.max(logits, axis=-1))
            summed = state[1] * jnp.exp(state[0] - new_top) + jnp.sum(
                jnp.exp(logits - new_top[..., None]), axis=-1
            )
            return (new_top, summed)

        top, total = lax.cond(usable[back], widen, keep_same, (top, total))
    log_total = top + jnp.log(total)
    attended = jnp.zeros((tokens, heads_here, head_size), F32)
    for back in range(reach):

        def accumulate(current, block=pairs[back], diagonal=back == 0):
            probs = jnp.exp(block_logits(queries, block[0], diagonal) - log_total[..., None])
            return current + jnp.einsum(
                "hqk,khd->qhd", probs.astype(BF), block[1], preferred_element_type=F32
            )

        attended = lax.cond(usable[back], accumulate, keep_same, attended)
    return attended, (pairs, usable, log_total)


def far_attend_back(queries, attended_grad, kept):
    tokens, heads_here, head_size = queries.shape
    factor = 1.0 / math.sqrt(head_size)
    pairs, usable, log_total = kept
    reach = len(pairs)

    def weights_of(block, diagonal):
        return jnp.exp(block_logits(queries, block, diagonal) - log_total[..., None])

    def prob_grads(block):
        return jnp.einsum("qhd,khd->hqk", attended_grad, block[1], preferred_element_type=F32)

    delta = jnp.zeros((heads_here, tokens), F32)
    for back in range(reach):

        def gather_delta(current, block=pairs[back], diagonal=back == 0):
            return current + jnp.sum(weights_of(block[0], diagonal) * prob_grads(block), axis=-1)

        delta = lax.cond(usable[back], gather_delta, keep_same, delta)

    def skip_block(current):
        return (current, jnp.zeros((2, tokens, heads_here, head_size), F32))

    query_grad = jnp.zeros((tokens, heads_here, head_size), F32)
    key_value_grad = jnp.zeros((2, tokens, heads_here, head_size), F32)
    for back in range(reach):

        def spread(current, block=pairs[back], diagonal=back == 0):
            probs = weights_of(block[0], diagonal)
            score_grad = (probs * (prob_grads(block) - delta[..., None])).astype(BF)
            query_part = (
                current
                + jnp.einsum("hqk,khd->qhd", score_grad, block[0], preferred_element_type=F32)
                * factor
            )
            key_part = (
                jnp.einsum("hqk,qhd->khd", score_grad, queries, preferred_element_type=F32)
                * factor
            )
            value_part = jnp.einsum(
                "hqk,qhd->khd", probs.astype(BF), attended_grad, preferred_element_type=F32
            )
            return (query_part, jnp.stack([key_part, value_part]))

        query_grad, pair_grad = lax.cond(usable[back], spread, skip_block, query_grad)
        if back == 0:
            key_value_grad = pair_grad
        else:
            key_value_grad = key_value_grad + passed_along(pair_grad, "dp", -back)
    return jnp.concatenate([query_grad[None], key_value_grad])


def mix_block(i, coefficients, shares, last_share, extras, last_extras, arrived, whole):
    streams, block, width = shares.shape
    each = coefficients.shape[1] // (streams + 1)
    groups = 1 + len(extras)
    final = arrived is not None
    lanes = 512

    def kernel(*refs):
        weights = refs[0][...]
        heads, lasts = refs[1 : 1 + groups], refs[1 + groups : 1 + 2 * groups]
        out = refs[-2] if final else refs[-1]
        if final:
            refs[-1][...] = jnp.zeros_like(refs[-1])
        columns = [weights[:, n : n + 1] for n in range(weights.shape[1])]
        for lane in range(0, width, lanes):
            span = slice(lane, lane + lanes)
            values = []
            for s in range(streams + 1):
                picks = [r[s, :, span] if s < streams else l[:, span] for r, l in zip(heads, lasts)]
                total = picks[0].astype(F32)
                for pick in picks[1:]:
                    total = total + pick.astype(F32)
                values.append(total)
            for e in range(each):
                total = columns[e * (streams + 1)] * values[0]
                for s in range(1, streams + 1):
                    total = total + columns[e * (streams + 1) + s] * values[s]
                if final:
                    total = total + refs[1 + 2 * groups][e, :, span].astype(F32)
                out[e, :, span] = total.astype(out.dtype)

    piece = pl.BlockSpec((streams, block, width), lambda n: (0, 0, 0))
    row = pl.BlockSpec((block, width), lambda n: (i, 0))
    small = pl.BlockSpec((each, block, width), lambda n: (0, 0, 0))
    specs = [pl.BlockSpec((block, coefficients.shape[1]), lambda n: (i, 0))]
    specs += [piece] * groups + [row] * groups
    args = [coefficients, shares, *extras, last_share, *last_extras]
    alias = {}
    if final:
        specs.append(small)
        args.append(arrived)
        if whole is not None:
            specs.append(pl.BlockSpec(memory_space=pl.ANY))
            args.append(whole)
            alias = {len(args) - 1: 0}
        out_spec = [
            pl.BlockSpec((each, block, width), lambda n: (0, i, 0)),
            pl.BlockSpec((8, 128), lambda n: (0, 0)),
        ]
        out_shape = [
            jax.ShapeDtypeStruct((each, coefficients.shape[0], width), F32),
            jax.ShapeDtypeStruct((8, 128), F32),
        ]
    else:
        out_spec, out_shape = small, jax.ShapeDtypeStruct((each, block, width), BF)
    return pl.pallas_call(
        kernel,
        grid=(1,),
        in_specs=specs,
        out_specs=out_spec,
        out_shape=out_shape,
        input_output_aliases=alias,
        cost_estimate=cost(4 if final else 3),
        name="mix_final" if final else "mix_inward",
    )(*args)


def hidden_units(x, w_up):
    tokens, width = x.shape
    units = w_up.shape[1]
    block = min(512, units)

    def kernel(x_ref, w, out, slope):
        up = dot(x_ref[...], w[...])
        inside = 0.5 * (1.0 + lax.erf(up * math.sqrt(0.5)))
        out[...] = (up * inside).astype(BF)
        bell = jnp.exp(-0.5 * up * up) * (1.0 / math.sqrt(2.0 * math.pi))
        slope[...] = (inside + up * bell).astype(BF)

    column = pl.BlockSpec((tokens, block), lambda i: (0, i))
    return pl.pallas_call(
        kernel,
        grid=(units // block,),
        in_specs=[
            pl.BlockSpec((tokens, width), lambda i: (0, 0)),
            pl.BlockSpec((width, block), lambda i: (0, i)),
        ],
        out_specs=[column, column],
        out_shape=[jax.ShapeDtypeStruct((tokens, units), BF)] * 2,
        cost_estimate=cost(9),
        name="hidden_units",
    )(x, w_up)


def merge_branches(attended, hidden, w_merge, w_down, stream, flag):
    tokens, inner = attended.shape
    shards, units, cols = w_down.shape
    if cols % 128:
        merged = jnp.einsum("te,ned->tnd", attended, w_merge, preferred_element_type=F32)
        merged = merged + jnp.einsum("tf,nfd->tnd", hidden, w_down, preferred_element_type=F32)
        return merged.reshape(tokens, -1) + flag * stream

    def kernel(a, h, wm, wd, st, flag_ref, out):
        out[...] = dot(a[...], wm[0]) + dot(h[...], wd[0]) + flag_ref[0] * st[...]

    return pl.pallas_call(
        kernel,
        grid=(shards,),
        in_specs=[
            pl.BlockSpec((tokens, inner), lambda n: (0, 0)),
            pl.BlockSpec((tokens, units), lambda n: (0, 0)),
            pl.BlockSpec((1, inner, cols), lambda n: (n, 0, 0)),
            pl.BlockSpec((1, units, cols), lambda n: (n, 0, 0)),
            pl.BlockSpec((tokens, cols), lambda n: (0, n)),
            pl.BlockSpec(memory_space=pltpu.SMEM),
        ],
        out_specs=pl.BlockSpec((tokens, cols), lambda n: (0, n)),
        out_shape=jax.ShapeDtypeStruct((tokens, shards * cols), F32),
        cost_estimate=cost(13),
        name="merge_branches",
    )(attended, hidden, w_merge, w_down, stream, flag)


def back_through(grad, stacked, slope):
    tokens = grad.shape[0]
    shards, units, cols = stacked.shape
    if cols % 128:
        split = grad.reshape(tokens, shards, cols)
        total = jnp.einsum("tnd,nfd->tf", split, stacked, preferred_element_type=F32)
        return (total if slope is None else total * slope.astype(F32)).astype(BF)

    def kernel(*refs):
        g, w = refs[:2]
        out, acc = refs[-2:]
        n = pl.program_id(0)
        part = dot_cols(g[...], w[0])

        @pl.when(n == 0)
        def _():
            acc[...] = part

        @pl.when(n > 0)
        def _():
            acc[...] += part

        @pl.when(n == shards - 1)
        def _():
            total = acc[...]
            if slope is not None:
                total = total * refs[2][...].astype(F32)
            out[...] = total.astype(BF)

    specs = [
        pl.BlockSpec((tokens, cols), lambda n: (0, n)),
        pl.BlockSpec((1, units, cols), lambda n: (n, 0, 0)),
    ]
    args = [grad, stacked]
    if slope is not None:
        specs.append(pl.BlockSpec((tokens, units), lambda n: (0, 0)))
        args.append(slope)
    return pl.pallas_call(
        kernel,
        grid=(shards,),
        in_specs=specs,
        out_specs=pl.BlockSpec((tokens, units), lambda n: (0, 0)),
        out_shape=jax.ShapeDtypeStruct((tokens, units), BF),
        scratch_shapes=[pltpu.VMEM((tokens, units), F32)],
        cost_estimate=cost(13 if slope is not None else 7),
        name="back_through",
    )(*args)


def body(
    history,
    mixing,
    shard_offset,
    norm_gain,
    norm_bias,
    w_heads,
    w_merge,
    w_up,
    w_down,
    mixer_first,
    mixer_second,
    out_cotangent,
    next_cotangent,
):
    member = lax.axis_index("stream")
    members = lax.axis_size("stream")
    shards = lax.axis_size("dp")
    index = lax.axis_index("dp")
    entries, tokens, width = history.shape
    heads_here = w_heads.shape[2] // HD
    half = tokens // 2
    highest = lax.Precision.HIGHEST
    flag = (member == members - 1).astype(F32)
    flags = flag.reshape(1)
    near = shards == 8 and heads_here * 2 == shards and tokens * shards == 2 * SEQ

    got_heads = Gathered(w_heads, direct=near)
    cotangent = lax.all_gather(out_cotangent, "stream", axis=1, tiled=True)
    lanes = jnp.concatenate([norm_gain, norm_bias]).astype(F32).reshape(tokens, -1)
    packed = lax.all_gather(jnp.concatenate([mixing[:, 0, :], lanes], axis=1), "stream", axis=0)
    if near:
        early = (got_heads.by_x, got_heads.by_y, got_heads.across)
        history = after(history, *early)
        w_up, w_merge = after(w_up, *early[:2]), after(w_merge, *early[:2])
    got_up = Gathered(w_up)
    got_merge = Gathered(w_merge)
    mix_all = packed[:, :, :entries]
    norms = packed[:, :, entries:].reshape(members, 2, width)
    gains, biases = norms[:, 0], norms[:, 1]
    mix_rows = jnp.transpose(mix_all, (1, 0, 2)).reshape(tokens, members * entries)

    normed, unit, inv, stream = make_streams(history, mix_rows, gains, biases)
    full_heads = got_heads.whole()
    positions = shard_offset[0] + jnp.arange(tokens, dtype=jnp.int32)
    projected = project(after(normed, got_up.by_x, got_up.by_y), full_heads, rope_tables(positions, 1.0))

    first_rows = mixer_first.astype(F32).reshape(tokens, -1)
    second_flat = mixer_second[:, 0, :].astype(F32).reshape(-1)
    hidden_count = mixer_second.shape[0]
    lines = -(-second_flat.shape[0] // tokens)
    second_rows = jnp.pad(second_flat, (0, lines * tokens - second_flat.shape[0]))
    rest = jnp.concatenate(
        [next_cotangent[:, 0, :], first_rows, second_rows.reshape(tokens, lines)], axis=1
    )
    rest = lax.all_gather(after(rest, projected), "stream", axis=0)
    outputs = next_cotangent.shape[2]
    cut = outputs + first_rows.shape[1]
    next_full = rest[:, :, :outputs]
    first_full = rest[:, :, outputs:cut].astype(BF).reshape(width, -1)
    second_full = rest[:, :, cut:].reshape(members, -1)[:, : second_flat.shape[0]]
    second_full = second_full.reshape(members, hidden_count, outputs)

    if near:
        spread = after(jnp.broadcast_to(shard_offset[:, None], (8, 128)), projected)
        offsets = lax.all_gather(spread, "dp", axis=0)[:, 0, 0]
        side = (index % 2).astype(jnp.int32).reshape(1)
        place = jnp.arange(shards, dtype=jnp.int32)
        first_key = jnp.maximum(place - offsets // tokens, 0).astype(jnp.int32)
        own = lax.all_to_all(projected, "dp", 0, 0, tiled=True)
        own = after(own, next_full, first_full, second_full, cotangent)
        got_down = Gathered(after(w_down, own))
        other = partner(own[:, 1:], 1)
        full_up = got_up.whole(projected)
        full_merge = got_merge.whole(projected)
        result, exact, level = attend(own, other, first_key, side)
        back = lax.all_to_all(result, "dp", 0, 0, tiled=True)
        attended = jnp.transpose(back.reshape(heads_here, tokens, HD), (1, 0, 2)).reshape(tokens, -1)
    else:
        got_down = Gathered(w_down)
        full_up = got_up.whole()
        full_merge = got_merge.whole()
        split = projected.reshape(heads_here, 2, 3, half, HD)
        split = jnp.transpose(split, (2, 1, 3, 0, 4)).reshape(3, tokens, heads_here, HD)
        result, kept = far_attend(split[0], split[1], split[2], shard_offset)
        attended = result.reshape(tokens, -1).astype(BF)
    full_down = got_down.whole()
    flat_up = full_up.reshape(width, -1)
    hidden, slope = hidden_units(normed[members - 1], flat_up)
    attended = after(attended, hidden)
    share = merge_branches(attended, hidden, full_merge, full_down, stream, flags)

    inner = (member == 1) | (member == 2)
    count = 8
    rows = [lax.slice_in_dim(share, i * tokens // count, (i + 1) * tokens // count) for i in range(count)]
    totals = {}

    def middle(i, one):
        return (rows[i] + one.astype(F32)).astype(BF)

    def ends(i, one, two):
        totals[i] = (rows[i] + one.astype(F32) + two.astype(F32)).astype(BF)
        return totals[i]

    _, _, arrived = along_line(count, lambda i, gates: gated(rows[i].astype(BF), gates), middle, ends)
    block_full = jnp.concatenate([jnp.where(inner, totals[i], arrived[i]) for i in range(count)])

    mine = member * (width // members)
    block_out = lax.dynamic_slice_in_dim(block_full, mine, width // members, axis=1)
    out_float = block_full.astype(F32)
    scale = lax.rsqrt(jnp.sum(out_float * out_float, axis=-1) / width + 1e-06)
    proj = dot(block_full, first_full)
    mixer, mixer_back = jax.vjp(exact_gelu, scale[:, None] * proj)
    second_here = mixer_second[:, 0, :].astype(F32)
    next_here = jnp.dot(mixer, second_here, precision=highest, preferred_element_type=F32)
    mixer_grad = jnp.einsum(
        "stn,scn->tc", next_full, second_full, precision=highest, preferred_element_type=F32
    )
    pre_grad = mixer_back(mixer_grad)[0]
    proj_grad = (scale[:, None] * pre_grad).astype(BF)
    scale_grad = jnp.sum(pre_grad * proj, axis=-1)
    second_local = jnp.dot(
        mixer.T, next_cotangent[:, 0, :], precision=highest, preferred_element_type=F32
    )
    first_local = dot_rows(block_out, proj_grad)
    grad_out = (
        cotangent.astype(F32)
        + dot_cols(proj_grad, first_full)
        - (scale * scale * scale * scale_grad)[:, None] * out_float / width
    ).astype(BF)

    attended_grad = back_through(grad_out, full_merge, None)
    up_grad = back_through(grad_out, full_down, slope)
    merge_grad = dot_rows(attended, grad_out).astype(BF)
    last_normed = dot_cols(up_grad, flat_up)
    last_share, last_stats = last_back(
        last_normed, unit[members - 1], inv, gains[members - 1 :], grad_out, flags
    )
    last_one = line_hop(last_share, OUTWARD)
    last_two = line_hop((last_share.astype(F32) + last_one.astype(F32)).astype(BF), MIDDLE)
    if near:
        sent = attended_grad.reshape(tokens, heads_here, HD)
        sent = jnp.transpose(sent, (1, 0, 2)).reshape(shards, half, HD)
        grads = lax.all_to_all(sent, "dp", 0, 0, tiled=True)
        grads = after(grads, last_share)
        kept_grads, given = attend_back(own, other, grads, exact, level, first_key, side)
        taken = partner(given, 1)
        summed = kept_grads[:, 1:].astype(F32) + taken.astype(F32)
        pair = jnp.concatenate([kept_grads[:, :1], summed.astype(BF)], axis=1)
        parts = lax.all_to_all(pair, "dp", 0, 0, tiled=True)
        hidden = after(hidden, pair)
    else:
        grads = far_attend_back(split[0], attended_grad.reshape(tokens, heads_here, HD), kept)
        parts = grads.reshape(3, 2, half, heads_here, HD)
        parts = jnp.transpose(parts, (3, 1, 0, 2, 4)).reshape(2 * heads_here, 3, half, HD)

    down_grad = dot_rows(hidden, grad_out).astype(BF)
    parts = after(parts, last_one, down_grad)
    blocks = 8
    *pieces, heads_share, heads_grad, heads_stats = heads_back(
        parts, full_heads, normed, unit, inv, gains, rope_tables(positions, -1.0), blocks
    )
    up_back = dot_rows(normed[members - 1], after(up_grad, heads_share)).astype(BF)

    grad_merge = lax.psum_scatter(merge_grad, "dp", scatter_dimension=1, tiled=True).astype(F32)
    grad_down = lax.psum_scatter(down_grad, "dp", scatter_dimension=1, tiled=True).astype(F32)
    grad_heads = lax.psum_scatter(heads_grad, "dp", scatter_dimension=1, tiled=True).astype(F32)
    grad_up = lax.psum_scatter(up_back, "dp", scatter_dimension=0, tiled=True).astype(F32)

    each = entries // members

    def weights_for(owner):
        block = lax.dynamic_slice_in_dim(mix_all, owner * each, each, axis=2)
        return jnp.transpose(block, (1, 2, 0)).reshape(tokens, each * members)

    there = weights_for(jnp.where(member == 1, 0, members - 1))
    here = weights_for(member)
    extra = {}

    def first_hop(i, gates):
        if i == 1:
            mix_parts = mixing_back(heads_share, last_share, history)
            stats = jnp.concatenate([heads_stats, last_stats[None]])
            both = jnp.concatenate([mix_parts, stats.reshape(members, tokens, -1)], axis=2)
            extra["both"] = jnp.sum(lax.all_to_all(both, "stream", 0, 0, tiled=True), axis=0)
        if i == 4:
            sums = extra["both"][:, entries:]
            second_sums = jnp.pad(second_local.reshape(-1), (0, lines * tokens - second_flat.shape[0]))
            local = jnp.concatenate(
                [sums, first_local.reshape(tokens, -1), second_sums.reshape(tokens, lines)], axis=1
            )
            extra["all"] = jnp.sum(lax.all_gather(local, "dp", axis=0), axis=0)
            gates = gates + [extra["both"]]
        if i == 2:
            gates = gates + [last_two]
        if i == 7:
            gates = gates + [extra["all"]]
        return gated(pieces[i], gates)

    def second_hop(i, one):
        return (pieces[i].astype(F32) + one.astype(F32)).astype(BF)

    def third_hop(i, one, two):
        return mix_block(i, there, pieces[i], last_share, [two], [last_two], None, None)

    def finish(i, one, two, three):
        extra["history"], token = mix_block(
            i,
            here,
            pieces[i],
            last_share,
            [one, two],
            [last_one, last_two],
            three,
            extra.get("history"),
        )
        return token

    along_line(blocks, first_hop, second_hop, third_hop, finish)
    grad_history = extra["history"]

    grad_mixing = extra["both"][:, :entries][:, None, :]
    sums = extra["all"]
    spans = 2 * width // tokens
    stats = sums[:, :spans].reshape(2, width)
    grad_first = sums[:, spans:-lines].reshape(mixer_first.shape)
    grad_second = sums[:, -lines:].reshape(-1)[: second_flat.shape[0]].reshape(hidden_count, outputs)
    return (
        block_out,
        next_here[:, None, :],
        grad_history,
        grad_mixing,
        stats[:1],
        stats[1:],
        grad_heads,
        grad_merge,
        grad_up,
        grad_down,
        grad_first,
        grad_second[:, None, :],
    )


def solution(mesh):
    in_specs = (
        P(None, "dp", None),
        P("dp", "stream", None),
        P("dp"),
        P("stream", None),
        P("stream", None),
        P(None, "dp", "stream"),
        P("stream", "dp"),
        P("dp", "stream"),
        P("stream", "dp"),
        P("stream", None),
        P(None, "stream", None),
        P("dp", "stream"),
        P("dp", "stream", None),
    )
    out_specs = (
        P("dp", "stream"),
        P("dp", "stream", None),
        P("stream", "dp", None),
        P("dp", "stream", None),
        P("stream", None),
        P("stream", None),
        P(None, "dp", "stream"),
        P("stream", "dp"),
        P("dp", "stream"),
        P("stream", "dp"),
        P("stream", None),
        P(None, "stream", None),
    )
    return jax.shard_map(body, mesh=mesh, in_specs=in_specs, out_specs=out_specs, check_vma=False)
```

```python
import math

import jax
import jax.numpy as jnp
from jax import lax
from jax.experimental import pallas as pl
from jax.experimental.pallas import tpu as pltpu
from jax.sharding import PartitionSpec as P

HD = 128
ROT = 32
SEQ = 2048


def passed_along(shard, axis, by):
    peers = lax.axis_size(axis)
    pairs = [(i, i + by) for i in range(peers) if 0 <= i + by < peers]
    return lax.ppermute(shard, axis, pairs)


def rotate(vectors, positions, sign):
    half = ROT // 2
    counter = jnp.arange(half, dtype=jnp.float32)
    freqs = jnp.exp(counter * (-2.0 * math.log(10000.0) / ROT))
    angles = positions.astype(jnp.float32)[:, None] * freqs[None, :]
    cosine = jnp.cos(angles)[:, None, :]
    sine = sign * jnp.sin(angles)[:, None, :]
    first = vectors[..., :half]
    second = vectors[..., half:ROT]
    return jnp.concatenate(
        [first * cosine - second * sine, second * cosine + first * sine, vectors[..., ROT:]],
        axis=-1,
    )


def exact_gelu(vectors):
    return jax.nn.gelu(vectors, approximate=False)


def block_logits(queries, keys_block, diagonal):
    logits = jnp.einsum("qhd,khd->hqk", queries, keys_block, preferred_element_type=jnp.float32) * (
        1.0 / math.sqrt(queries.shape[-1])
    )
    if diagonal:
        counter = jnp.arange(queries.shape[0], dtype=jnp.int32)
        allowed = counter[None, :] <= counter[:, None]
        logits = jnp.where(allowed[None], logits, -1e30)
    return logits


def keep_same(state):
    return state


BF = jnp.bfloat16
F32 = jnp.float32
OUTWARD = [(0, 1), (3, 2)]
MIDDLE = [(1, 2), (2, 1)]
INWARD = [(1, 0), (2, 3)]


def dot(left, right):
    return jnp.dot(left, right, preferred_element_type=F32)


def dot_rows(left, right):
    return lax.dot_general(left, right, (((0,), (0,)), ((), ())), preferred_element_type=F32)


def dot_cols(left, right):
    return lax.dot_general(left, right, (((1,), (1,)), ((), ())), preferred_element_type=F32)


def partner(shard, bit):
    peers = lax.axis_size("dp")
    return lax.ppermute(shard, "dp", [(i, i ^ bit) for i in range(peers)])


def line_hop(shard, pairs):
    return lax.ppermute(shard, "stream", pairs)


def cost(microseconds):
    return pl.CostEstimate(
        flops=int(microseconds * 0.9e9), bytes_accessed=int(microseconds * 3e6), transcendentals=0
    )


def after(value, *others):
    return lax.optimization_barrier((value, *others))[0]


class Gathered:
    def __init__(self, shard, direct=False):
        self.shard = shard
        self.peers = lax.axis_size("dp")
        if self.peers != 8:
            self.by_x = self.by_y = shard
            return
        self.cut = max(range(shard.ndim - 1), key=lambda dim: shard.shape[dim])
        self.by_x = partner(shard, 2)
        self.by_y = partner(shard, 4)
        self.across = partner(shard, 6) if direct else None

    def whole(self, *earlier):
        shard = self.shard
        if self.peers != 8:
            return lax.all_gather(shard, "dp", axis=0)
        index = lax.axis_index("dp")
        cut = self.cut
        half = shard.shape[cut] // 2
        shard, by_x, by_y = [gated(item, earlier) for item in (shard, self.by_x, self.by_y)]
        pieces = [(shard, 0, 0), (by_x, 2, 0), (by_y, 4, 0)]
        if self.across is None:
            low = lax.slice_in_dim(by_y, 0, half, axis=cut)
            high = lax.slice_in_dim(by_x, half, 2 * half, axis=cut)
            pieces += [(partner(low, 2), 6, 0), (partner(high, 4), 6, half)]
        else:
            pieces.append((self.across, 6, 0))
        pieces += [(partner(piece, 1), code ^ 1, start) for piece, code, start in pieces]
        return put_together(pieces, shard, self.peers, cut, index)


def put_together(pieces, shard, peers, cut, index):
    codes = [(code, start) for _, code, start in pieces]
    arrays = [piece for piece, _, _ in pieces]

    def kernel(place, *refs):
        out, held, sems, sent = refs[-4:]
        owners = {}
        for n, (code, start) in enumerate(codes):
            size = refs[n].shape[cut]
            span = tuple(
                pl.ds(start, size) if dim == cut else slice(None) for dim in range(shard.ndim)
            )
            copy = pltpu.make_async_copy(refs[n], held.at[(code, *span)], sems.at[n])
            copy.start()
            owners.setdefault(code, []).append(copy)
        leaving = []
        for code, copies in owners.items():
            for copy in copies:
                copy.wait()
            copy = pltpu.make_async_copy(held.at[code], out.at[place[0] ^ code], sent.at[code])
            copy.start()
            leaving.append(copy)
        for copy in leaving:
            copy.wait()

    anywhere = pl.BlockSpec(memory_space=pl.ANY)
    size = peers * shard.size * shard.dtype.itemsize
    return pl.pallas_call(
        kernel,
        in_specs=[pl.BlockSpec(memory_space=pltpu.SMEM)] + [anywhere] * len(arrays),
        out_specs=anywhere,
        out_shape=jax.ShapeDtypeStruct((peers, *shard.shape), shard.dtype),
        scratch_shapes=[
            pltpu.VMEM((peers, *shard.shape), shard.dtype),
            pltpu.SemaphoreType.DMA((len(arrays),)),
            pltpu.SemaphoreType.DMA((peers,)),
        ],
        cost_estimate=cost(2 * size / 3e6),
        name="put_together",
    )(index.astype(jnp.int32).reshape(1), *arrays)


def along_line(count, first, second, third, finish=None):
    ones, twos, threes, ends = [], [], [], []
    for step in range(count + 2):
        if step < count:
            gates = []
            if step >= 2:
                gates.append(ones[step - 2])
            if step >= 3:
                gates.append(twos[step - 3])
            if step >= 4:
                gates.append(threes[step - 4] if finish is None else ends[step - 4])
            ones.append(line_hop(first(step, gates), OUTWARD))
        if 0 <= step - 1 < count:
            twos.append(line_hop(second(step - 1, ones[step - 1]), MIDDLE))
        if 0 <= step - 2 < count:
            back = step - 2
            threes.append(line_hop(third(back, ones[back], twos[back]), INWARD))
            if finish is not None:
                ends.append(finish(back, ones[back], twos[back], threes[back]))
    return ones, twos, threes


def gated(value, gates):
    return after(value, *gates) if gates else value


def rope_tables(positions, sign):
    half = ROT // 2
    lane = jnp.arange(HD, dtype=jnp.int32)
    counter = (lane % half).astype(F32)
    freqs = jnp.exp(counter * (-2.0 * math.log(10000.0) / ROT))
    angles = positions.astype(F32)[:, None] * freqs[None, :]
    cosine = jnp.where(lane < ROT, jnp.cos(angles), 1.0)
    sine = sign * jnp.sin(angles)
    up = jnp.where(lane < half, -sine, 0.0)
    down = jnp.where((lane >= half) & (lane < ROT), sine, 0.0)
    return jnp.stack([cosine, up, down])


def turned(block, tables):
    half = ROT // 2
    return (
        block * tables[0]
        + pltpu.roll(block, HD - half, 1) * tables[1]
        + pltpu.roll(block, half, 1) * tables[2]
    )


def make_streams(history, mix_rows, gains, biases):
    entries, tokens, width = history.shape
    streams = gains.shape[0]
    rows, sub, lanes = min(64, tokens), 16, 512

    def kernel(hist, mix, gain, bias, normed, unit, inv, last, scratch):
        def step(r, carry):
            here = pl.ds(pl.multiple_of(r * sub, sub), sub)
            weights = mix[here, :]
            columns = [
                [weights[:, s * entries + j : s * entries + j + 1] for j in range(entries)]
                for s in range(streams)
            ]
            for lane in range(0, width, lanes):
                span = slice(lane, lane + lanes)
                sums = [None] * streams
                for j in range(entries):
                    part = hist[j, here, span].astype(F32)
                    for s in range(streams):
                        term = columns[s][j] * part
                        sums[s] = term if j == 0 else sums[s] + term
                for s in range(streams):
                    scratch[s, :, span] = sums[s]
            stds = []
            for s in range(streams):
                values = scratch[s]
                center = values - jnp.sum(values, axis=-1, keepdims=True) * (1.0 / width)
                var = jnp.sum(center * center, axis=-1, keepdims=True) * (1.0 / width)
                std = lax.rsqrt(var + 1e-05)
                stds.append(std)
                scaled = center * std
                unit[s, here, :] = scaled.astype(BF)
                normed[s, here, :] = (scaled * gain[s : s + 1] + bias[s : s + 1]).astype(BF)
            last[here, :] = scratch[streams - 1]
            inv[here, :] = jnp.concatenate(stds, axis=-1)
            return carry

        lax.fori_loop(0, rows // sub, step, 0)

    wide = jax.ShapeDtypeStruct((streams, tokens, width), BF)
    return pl.pallas_call(
        kernel,
        grid=(tokens // rows,),
        in_specs=[
            pl.BlockSpec((entries, rows, width), lambda i: (0, i, 0)),
            pl.BlockSpec((rows, streams * entries), lambda i: (i, 0)),
            pl.BlockSpec((streams, width), lambda i: (0, 0)),
            pl.BlockSpec((streams, width), lambda i: (0, 0)),
        ],
        out_specs=[
            pl.BlockSpec((streams, rows, width), lambda i: (0, i, 0)),
            pl.BlockSpec((streams, rows, width), lambda i: (0, i, 0)),
            pl.BlockSpec((rows, streams), lambda i: (i, 0)),
            pl.BlockSpec((rows, width), lambda i: (i, 0)),
        ],
        out_shape=[
            wide,
            wide,
            jax.ShapeDtypeStruct((tokens, streams), F32),
            jax.ShapeDtypeStruct((tokens, width), F32),
        ],
        scratch_shapes=[pltpu.VMEM((streams, sub, width), F32)],
        cost_estimate=cost(22),
        name="make_streams",
    )(history, mix_rows, gains, biases)


def project(normed, w_heads, tables):
    _, tokens, width = normed.shape
    columns = w_heads.shape[3]
    heads, half = columns // HD, tokens // 2

    def kernel(x, w, table, out):
        flat = dot(x[0], w[...].reshape(width, columns))
        turn = pl.program_id(0) < 2

        def put(head, block):
            out[2 * head, 0] = block[:half].astype(BF)
            out[2 * head + 1, 0] = block[half:].astype(BF)

        @pl.when(turn)
        def _():
            for head in range(heads):
                put(head, turned(flat[:, head * HD : (head + 1) * HD], table[...]))

        @pl.when(jnp.logical_not(turn))
        def _():
            for head in range(heads):
                put(head, flat[:, head * HD : (head + 1) * HD])

    return pl.pallas_call(
        kernel,
        grid=(3,),
        in_specs=[
            pl.BlockSpec((1, tokens, width), lambda c: (c, 0, 0)),
            pl.BlockSpec((w_heads.shape[0], 1, w_heads.shape[2], columns), lambda c: (0, c, 0, 0)),
            pl.BlockSpec((3, tokens, HD), lambda c: (0, 0, 0)),
        ],
        out_specs=pl.BlockSpec((2 * heads, 1, half, HD), lambda c: (0, c, 0, 0)),
        out_shape=jax.ShapeDtypeStruct((2 * heads, 3, half, HD), BF),
        cost_estimate=cost(9),
        name="project",
    )(normed, w_heads, tables)


def attend(own, other, first_key, side):
    shards, _, half, _ = own.shape
    factor = 1.0 / math.sqrt(HD)

    def kernel(first, part, mine, theirs, out, exact, norm):
        s = pl.program_id(0)
        query = mine[s, 0]

        def fold(state, keys, values, mask):
            top, total, acc = state
            logits = dot_cols(query, keys) * factor
            if mask is not None:
                logits = jnp.where(mask, logits, -1e30)
            new_top = jnp.maximum(top, jnp.max(logits, axis=-1, keepdims=True))
            probs = jnp.exp(logits - new_top)
            keep = jnp.exp(top - new_top)
            return (
                new_top,
                total * keep + jnp.sum(probs, axis=-1, keepdims=True),
                acc * keep + dot(probs.astype(BF), values),
            )

        row = lax.broadcasted_iota(jnp.int32, (half, half), 0)
        col = lax.broadcasted_iota(jnp.int32, (half, half), 1)
        state = (
            jnp.full((half, 1), -1e30, F32),
            jnp.zeros((half, 1), F32),
            jnp.zeros((half, HD), F32),
        )
        state = fold(state, mine[s, 1], mine[s, 2], col <= row)
        state = lax.fori_loop(
            0, part[0], lambda i, st: fold(st, theirs[s, 0], theirs[s, 1], None), state
        )

        def shard_step(b, st):
            st = fold(st, mine[b, 1], mine[b, 2], None)
            return fold(st, theirs[b, 0], theirs[b, 1], None)

        top, total, acc = lax.fori_loop(first[s], s, shard_step, state)
        result = acc / total
        out[0] = result.astype(BF)
        exact[0] = result
        norm[0] = top + jnp.log(total)

    return pl.pallas_call(
        kernel,
        grid_spec=pltpu.PrefetchScalarGridSpec(
            num_scalar_prefetch=2,
            grid=(shards,),
            in_specs=[
                pl.BlockSpec((shards, 3, half, HD), lambda s, *_: (0, 0, 0, 0)),
                pl.BlockSpec((shards, 2, half, HD), lambda s, *_: (0, 0, 0, 0)),
            ],
            out_specs=[
                pl.BlockSpec((1, half, HD), lambda s, *_: (s, 0, 0)),
                pl.BlockSpec((1, half, HD), lambda s, *_: (s, 0, 0)),
                pl.BlockSpec((1, half, 1), lambda s, *_: (s, 0, 0)),
            ],
        ),
        out_shape=[
            jax.ShapeDtypeStruct((shards, half, HD), BF),
            jax.ShapeDtypeStruct((shards, half, HD), F32),
            jax.ShapeDtypeStruct((shards, half, 1), F32),
        ],
        cost_estimate=cost(16),
        name="attend",
    )(first_key, side, own, other)


def attend_back(own, other, grads, exact, norm, first_key, side):
    shards, _, half, _ = own.shape
    factor = 1.0 / math.sqrt(HD)

    def kernel(first, part, mine, theirs, grad_ref, exact_ref, norm_ref, kept, given, sums):
        s = pl.program_id(0)
        query = mine[s, 0]
        grad = grad_ref[s]
        delta = jnp.sum(grad.astype(F32) * exact_ref[0], axis=-1, keepdims=True)
        level = norm_ref[0]
        lowered = grad

        @pl.when(s == 0)
        def _():
            sums[...] = jnp.zeros_like(sums)

        def fold(query_grad, keys, values, mask, slot, b):
            logits = dot_cols(query, keys) * factor
            probs = jnp.exp(logits - level)
            if mask is not None:
                probs = jnp.where(mask, probs, 0.0)
            score = (probs * (dot_cols(grad, values) - delta)).astype(BF)
            sums[slot, b] += dot_rows(score, query)
            sums[slot + 1, b] += dot_rows(probs.astype(BF), lowered)
            return query_grad + dot(score, keys)

        row = lax.broadcasted_iota(jnp.int32, (half, half), 0)
        col = lax.broadcasted_iota(jnp.int32, (half, half), 1)
        total = fold(jnp.zeros((half, HD), F32), mine[s, 1], mine[s, 2], col <= row, 0, s)
        total = lax.fori_loop(
            0, part[0], lambda i, q: fold(q, theirs[s, 0], theirs[s, 1], None, 2, s), total
        )

        def shard_step(b, q):
            q = fold(q, mine[b, 1], mine[b, 2], None, 0, b)
            return fold(q, theirs[b, 0], theirs[b, 1], None, 2, b)

        total = lax.fori_loop(first[s], s, shard_step, total)
        kept[s, 0] = (total * factor).astype(BF)

        @pl.when(s == shards - 1)
        def _():
            for b in range(shards):
                kept[b, 1] = (sums[0, b] * factor).astype(BF)
                kept[b, 2] = sums[1, b].astype(BF)
                given[b, 0] = (sums[2, b] * factor).astype(BF)
                given[b, 1] = sums[3, b].astype(BF)

    whole = lambda n: pl.BlockSpec((shards, n, half, HD), lambda s, *_: (0, 0, 0, 0))
    return pl.pallas_call(
        kernel,
        grid_spec=pltpu.PrefetchScalarGridSpec(
            num_scalar_prefetch=2,
            grid=(shards,),
            in_specs=[
                whole(3),
                whole(2),
                pl.BlockSpec((shards, half, HD), lambda s, *_: (0, 0, 0)),
                pl.BlockSpec((1, half, HD), lambda s, *_: (s, 0, 0)),
                pl.BlockSpec((1, half, 1), lambda s, *_: (s, 0, 0)),
            ],
            out_specs=[whole(3), whole(2)],
            scratch_shapes=[pltpu.VMEM((4, shards, half, HD), F32)],
        ),
        out_shape=[
            jax.ShapeDtypeStruct((shards, 3, half, HD), BF),
            jax.ShapeDtypeStruct((shards, 2, half, HD), BF),
        ],
        cost_estimate=cost(22),
        name="attend_back",
    )(first_key, side, own, other, grads, exact, norm)


def norm_back(grad, unit, inv, gain, extra):
    width = grad.shape[1]
    scaled = grad * gain
    mean = jnp.sum(scaled, axis=-1, keepdims=True) * (1.0 / width)
    slope = jnp.sum(scaled * unit, axis=-1, keepdims=True) * (1.0 / width)
    result = inv * (scaled - mean - unit * slope)
    return result if extra is None else result + extra


def heads_back(parts, w_heads, normed, unit, inv, gains, tables, count):
    _, tokens, width = normed.shape
    columns = w_heads.shape[3]
    heads, half = columns // HD, tokens // 2
    block = tokens // count

    def kernel(part, w, x, u, istd, gain, table, *refs):
        pieces, (stream, weight, stats, grad, wide) = refs[:count], refs[count:]
        c = pl.program_id(0)
        turn = c < 2

        def take(head):
            return jnp.concatenate([part[2 * head, 0], part[2 * head + 1, 0]], axis=0).astype(F32)

        @pl.when(turn)
        def _():
            for head in range(heads):
                grad[:, head * HD : (head + 1) * HD] = turned(take(head), table[...]).astype(BF)

        @pl.when(jnp.logical_not(turn))
        def _():
            for head in range(heads):
                grad[:, head * HD : (head + 1) * HD] = take(head).astype(BF)

        wide[...] = dot_cols(grad[...], w[...].reshape(width, columns))
        weight[0] = dot_rows(x[0], grad[...]).astype(BF)
        stats[...] = jnp.zeros_like(stats)
        column = lax.broadcasted_iota(jnp.int32, (block, istd.shape[1]), 1)

        for r in range(count):
            here = slice(r * block, (r + 1) * block)
            values = wide[here, :]
            units = u[0, here, :].astype(F32)
            std = jnp.sum(jnp.where(column == c, istd[here, :], 0.0), axis=-1, keepdims=True)
            result = norm_back(values, units, std, gain[0], None).astype(BF)
            stream[0, here, :] = result
            pieces[r][0] = result
            stats[0, 0:1] += jnp.sum(values * units, axis=0, keepdims=True)
            stats[0, 1:2] += jnp.sum(values, axis=0, keepdims=True)

    return pl.pallas_call(
        kernel,
        grid=(3,),
        in_specs=[
            pl.BlockSpec((2 * heads, 1, half, HD), lambda c: (0, c, 0, 0)),
            pl.BlockSpec((w_heads.shape[0], 1, w_heads.shape[2], columns), lambda c: (0, c, 0, 0)),
            pl.BlockSpec((1, tokens, width), lambda c: (c, 0, 0)),
            pl.BlockSpec((1, tokens, width), lambda c: (c, 0, 0)),
            pl.BlockSpec((tokens, inv.shape[1]), lambda c: (0, 0)),
            pl.BlockSpec((1, 1, width), lambda c: (c, 0, 0)),
            pl.BlockSpec((3, tokens, HD), lambda c: (0, 0, 0)),
        ],
        out_specs=[pl.BlockSpec((1, block, width), lambda c: (c, 0, 0))] * count
        + [
            pl.BlockSpec((1, tokens, width), lambda c: (c, 0, 0)),
            pl.BlockSpec((1, width, columns), lambda c: (c, 0, 0)),
            pl.BlockSpec((1, 2, width), lambda c: (c, 0, 0)),
        ],
        out_shape=[jax.ShapeDtypeStruct((3, block, width), BF)] * count
        + [
            jax.ShapeDtypeStruct((3, tokens, width), BF),
            jax.ShapeDtypeStruct((3, width, columns), BF),
            jax.ShapeDtypeStruct((3, 2, width), F32),
        ],
        scratch_shapes=[pltpu.VMEM((tokens, columns), BF), pltpu.VMEM((tokens, width), F32)],
        cost_estimate=cost(18),
        name="heads_back",
    )(parts, w_heads, normed, unit, inv, gains[:, None, :], tables)


def last_back(grad, unit, inv, gain, extra, flag):
    tokens, width = grad.shape
    block = min(128, tokens)

    def kernel(g, u, istd, gain_ref, e, flag_ref, stream, stats):
        @pl.when(pl.program_id(0) == 0)
        def _():
            stats[...] = jnp.zeros_like(stats)

        values = g[...]
        units = u[...].astype(F32)
        std = istd[...][:, -1:]
        added = e[...].astype(F32) * flag_ref[0]
        stream[...] = norm_back(values, units, std, gain_ref[...], added).astype(BF)
        stats[0:1] += jnp.sum(values * units, axis=0, keepdims=True)
        stats[1:2] += jnp.sum(values, axis=0, keepdims=True)

    row = lambda n: pl.BlockSpec((block, n), lambda i: (i, 0))
    return pl.pallas_call(
        kernel,
        grid=(tokens // block,),
        in_specs=[
            row(width),
            row(width),
            row(inv.shape[1]),
            pl.BlockSpec((1, width), lambda i: (0, 0)),
            row(width),
            pl.BlockSpec(memory_space=pltpu.SMEM),
        ],
        out_specs=[row(width), pl.BlockSpec((2, width), lambda i: (0, 0))],
        out_shape=[
            jax.ShapeDtypeStruct((tokens, width), BF),
            jax.ShapeDtypeStruct((2, width), F32),
        ],
        cost_estimate=cost(7),
        name="last_back",
    )(grad, unit, inv, gain, extra, flag)


def mixing_back(heads_part, last_part, history):
    entries, tokens, width = history.shape
    streams = heads_part.shape[0] + 1
    rows, sub, lanes = min(64, tokens), 16, 256

    def kernel(first, last, hist, out):
        def step(r, carry):
            here = pl.ds(pl.multiple_of(r * sub, sub), sub)
            for s in range(streams):
                sums = [None] * entries
                for lane in range(0, width, lanes):
                    span = slice(lane, lane + lanes)
                    part = first[s, here, span] if s < streams - 1 else last[here, span]
                    part = part.astype(F32)
                    for j in range(entries):
                        term = part * hist[j, here, span].astype(F32)
                        sums[j] = term if lane == 0 else sums[j] + term
                columns = [jnp.sum(item, axis=-1, keepdims=True) for item in sums]
                out[s, here, :] = jnp.concatenate(columns, axis=-1)
            return carry

        lax.fori_loop(0, rows // sub, step, 0)

    return pl.pallas_call(
        kernel,
        grid=(tokens // rows,),
        in_specs=[
            pl.BlockSpec((streams - 1, rows, width), lambda i: (0, i, 0)),
            pl.BlockSpec((rows, width), lambda i: (i, 0)),
            pl.BlockSpec((entries, rows, width), lambda i: (0, i, 0)),
        ],
        out_specs=pl.BlockSpec((streams, rows, entries), lambda i: (0, i, 0)),
        out_shape=jax.ShapeDtypeStruct((streams, tokens, entries), F32),
        cost_estimate=cost(18),
        name="mixing_back",
    )(heads_part, last_part, history)


def far_attend(queries, keys, values, shard_offset):
    tokens, heads_here, head_size = queries.shape
    data_index = lax.axis_index("dp")
    pairs = [jnp.stack([keys, values])]
    reach = 2 * SEQ // tokens
    for back in range(1, reach):
        pairs.append(passed_along(pairs[0], "dp", back))
    usable = [(shard_offset[0] >= back * tokens) & (data_index >= back) for back in range(reach)]
    first_logits = block_logits(queries, keys, True)
    top = jnp.max(first_logits, axis=-1)
    total = jnp.sum(jnp.exp(first_logits - top[..., None]), axis=-1)
    for back in range(1, reach):

        def widen(state, block=pairs[back][0]):
            logits = block_logits(queries, block, False)
            new_top = jnp.maximum(state[0], jnp.max(logits, axis=-1))
            summed = state[1] * jnp.exp(state[0] - new_top) + jnp.sum(
                jnp.exp(logits - new_top[..., None]), axis=-1
            )
            return (new_top, summed)

        top, total = lax.cond(usable[back], widen, keep_same, (top, total))
    log_total = top + jnp.log(total)
    attended = jnp.zeros((tokens, heads_here, head_size), F32)
    for back in range(reach):

        def accumulate(current, block=pairs[back], diagonal=back == 0):
            probs = jnp.exp(block_logits(queries, block[0], diagonal) - log_total[..., None])
            return current + jnp.einsum(
                "hqk,khd->qhd", probs.astype(BF), block[1], preferred_element_type=F32
            )

        attended = lax.cond(usable[back], accumulate, keep_same, attended)
    return attended, (pairs, usable, log_total)


def far_attend_back(queries, attended_grad, kept):
    tokens, heads_here, head_size = queries.shape
    factor = 1.0 / math.sqrt(head_size)
    pairs, usable, log_total = kept
    reach = len(pairs)

    def weights_of(block, diagonal):
        return jnp.exp(block_logits(queries, block, diagonal) - log_total[..., None])

    def prob_grads(block):
        return jnp.einsum("qhd,khd->hqk", attended_grad, block[1], preferred_element_type=F32)

    delta = jnp.zeros((heads_here, tokens), F32)
    for back in range(reach):

        def gather_delta(current, block=pairs[back], diagonal=back == 0):
            return current + jnp.sum(weights_of(block[0], diagonal) * prob_grads(block), axis=-1)

        delta = lax.cond(usable[back], gather_delta, keep_same, delta)

    def skip_block(current):
        return (current, jnp.zeros((2, tokens, heads_here, head_size), F32))

    query_grad = jnp.zeros((tokens, heads_here, head_size), F32)
    key_value_grad = jnp.zeros((2, tokens, heads_here, head_size), F32)
    for back in range(reach):

        def spread(current, block=pairs[back], diagonal=back == 0):
            probs = weights_of(block[0], diagonal)
            score_grad = (probs * (prob_grads(block) - delta[..., None])).astype(BF)
            query_part = (
                current
                + jnp.einsum("hqk,khd->qhd", score_grad, block[0], preferred_element_type=F32)
                * factor
            )
            key_part = (
                jnp.einsum("hqk,qhd->khd", score_grad, queries, preferred_element_type=F32)
                * factor
            )
            value_part = jnp.einsum(
                "hqk,qhd->khd", probs.astype(BF), attended_grad, preferred_element_type=F32
            )
            return (query_part, jnp.stack([key_part, value_part]))

        query_grad, pair_grad = lax.cond(usable[back], spread, skip_block, query_grad)
        if back == 0:
            key_value_grad = pair_grad
        else:
            key_value_grad = key_value_grad + passed_along(pair_grad, "dp", -back)
    return jnp.concatenate([query_grad[None], key_value_grad])


def mix_block(i, coefficients, shares, last_share, extras, last_extras, arrived, whole):
    streams, block, width = shares.shape
    each = coefficients.shape[1] // (streams + 1)
    groups = 1 + len(extras)
    final = arrived is not None
    lanes = 512

    def kernel(*refs):
        weights = refs[0][...]
        heads, lasts = refs[1 : 1 + groups], refs[1 + groups : 1 + 2 * groups]
        out = refs[-2] if final else refs[-1]
        if final:
            refs[-1][...] = jnp.zeros_like(refs[-1])
        columns = [weights[:, n : n + 1] for n in range(weights.shape[1])]
        for lane in range(0, width, lanes):
            span = slice(lane, lane + lanes)
            values = []
            for s in range(streams + 1):
                picks = [r[s, :, span] if s < streams else l[:, span] for r, l in zip(heads, lasts)]
                total = picks[0].astype(F32)
                for pick in picks[1:]:
                    total = total + pick.astype(F32)
                values.append(total)
            for e in range(each):
                total = columns[e * (streams + 1)] * values[0]
                for s in range(1, streams + 1):
                    total = total + columns[e * (streams + 1) + s] * values[s]
                if final:
                    total = total + refs[1 + 2 * groups][e, :, span].astype(F32)
                out[e, :, span] = total.astype(out.dtype)

    piece = pl.BlockSpec((streams, block, width), lambda n: (0, 0, 0))
    row = pl.BlockSpec((block, width), lambda n: (i, 0))
    small = pl.BlockSpec((each, block, width), lambda n: (0, 0, 0))
    specs = [pl.BlockSpec((block, coefficients.shape[1]), lambda n: (i, 0))]
    specs += [piece] * groups + [row] * groups
    args = [coefficients, shares, *extras, last_share, *last_extras]
    alias = {}
    if final:
        specs.append(small)
        args.append(arrived)
        if whole is not None:
            specs.append(pl.BlockSpec(memory_space=pl.ANY))
            args.append(whole)
            alias = {len(args) - 1: 0}
        out_spec = [
            pl.BlockSpec((each, block, width), lambda n: (0, i, 0)),
            pl.BlockSpec((8, 128), lambda n: (0, 0)),
        ]
        out_shape = [
            jax.ShapeDtypeStruct((each, coefficients.shape[0], width), F32),
            jax.ShapeDtypeStruct((8, 128), F32),
        ]
    else:
        out_spec, out_shape = small, jax.ShapeDtypeStruct((each, block, width), BF)
    return pl.pallas_call(
        kernel,
        grid=(1,),
        in_specs=specs,
        out_specs=out_spec,
        out_shape=out_shape,
        input_output_aliases=alias,
        cost_estimate=cost(4 if final else 3),
        name="mix_final" if final else "mix_inward",
    )(*args)


def hidden_units(x, w_up):
    tokens, width = x.shape
    units = w_up.shape[1]
    block = min(512, units)

    def kernel(x_ref, w, out, slope):
        up = dot(x_ref[...], w[...])
        inside = 0.5 * (1.0 + lax.erf(up * math.sqrt(0.5)))
        out[...] = (up * inside).astype(BF)
        bell = jnp.exp(-0.5 * up * up) * (1.0 / math.sqrt(2.0 * math.pi))
        slope[...] = (inside + up * bell).astype(BF)

    column = pl.BlockSpec((tokens, block), lambda i: (0, i))
    return pl.pallas_call(
        kernel,
        grid=(units // block,),
        in_specs=[
            pl.BlockSpec((tokens, width), lambda i: (0, 0)),
            pl.BlockSpec((width, block), lambda i: (0, i)),
        ],
        out_specs=[column, column],
        out_shape=[jax.ShapeDtypeStruct((tokens, units), BF)] * 2,
        cost_estimate=cost(9),
        name="hidden_units",
    )(x, w_up)


def merge_branches(attended, hidden, w_merge, w_down, stream, flag):
    tokens, inner = attended.shape
    shards, units, cols = w_down.shape
    if cols % 128:
        merged = jnp.einsum("te,ned->tnd", attended, w_merge, preferred_element_type=F32)
        merged = merged + jnp.einsum("tf,nfd->tnd", hidden, w_down, preferred_element_type=F32)
        return merged.reshape(tokens, -1) + flag * stream

    def kernel(a, h, wm, wd, st, flag_ref, out):
        out[...] = dot(a[...], wm[0]) + dot(h[...], wd[0]) + flag_ref[0] * st[...]

    return pl.pallas_call(
        kernel,
        grid=(shards,),
        in_specs=[
            pl.BlockSpec((tokens, inner), lambda n: (0, 0)),
            pl.BlockSpec((tokens, units), lambda n: (0, 0)),
            pl.BlockSpec((1, inner, cols), lambda n: (n, 0, 0)),
            pl.BlockSpec((1, units, cols), lambda n: (n, 0, 0)),
            pl.BlockSpec((tokens, cols), lambda n: (0, n)),
            pl.BlockSpec(memory_space=pltpu.SMEM),
        ],
        out_specs=pl.BlockSpec((tokens, cols), lambda n: (0, n)),
        out_shape=jax.ShapeDtypeStruct((tokens, shards * cols), F32),
        cost_estimate=cost(13),
        name="merge_branches",
    )(attended, hidden, w_merge, w_down, stream, flag)


def back_through(grad, stacked, slope):
    tokens = grad.shape[0]
    shards, units, cols = stacked.shape
    if cols % 128:
        split = grad.reshape(tokens, shards, cols)
        total = jnp.einsum("tnd,nfd->tf", split, stacked, preferred_element_type=F32)
        return (total if slope is None else total * slope.astype(F32)).astype(BF)

    def kernel(*refs):
        g, w = refs[:2]
        out, acc = refs[-2:]
        n = pl.program_id(0)
        part = dot_cols(g[...], w[0])

        @pl.when(n == 0)
        def _():
            acc[...] = part

        @pl.when(n > 0)
        def _():
            acc[...] += part

        @pl.when(n == shards - 1)
        def _():
            total = acc[...]
            if slope is not None:
                total = total * refs[2][...].astype(F32)
            out[...] = total.astype(BF)

    specs = [
        pl.BlockSpec((tokens, cols), lambda n: (0, n)),
        pl.BlockSpec((1, units, cols), lambda n: (n, 0, 0)),
    ]
    args = [grad, stacked]
    if slope is not None:
        specs.append(pl.BlockSpec((tokens, units), lambda n: (0, 0)))
        args.append(slope)
    return pl.pallas_call(
        kernel,
        grid=(shards,),
        in_specs=specs,
        out_specs=pl.BlockSpec((tokens, units), lambda n: (0, 0)),
        out_shape=jax.ShapeDtypeStruct((tokens, units), BF),
        scratch_shapes=[pltpu.VMEM((tokens, units), F32)],
        cost_estimate=cost(13 if slope is not None else 7),
        name="back_through",
    )(*args)


def body(
    history,
    mixing,
    shard_offset,
    norm_gain,
    norm_bias,
    w_heads,
    w_merge,
    w_up,
    w_down,
    mixer_first,
    mixer_second,
    out_cotangent,
    next_cotangent,
):
    member = lax.axis_index("stream")
    members = lax.axis_size("stream")
    shards = lax.axis_size("dp")
    index = lax.axis_index("dp")
    entries, tokens, width = history.shape
    heads_here = w_heads.shape[2] // HD
    half = tokens // 2
    highest = lax.Precision.HIGHEST
    flag = (member == members - 1).astype(F32)
    flags = flag.reshape(1)
    near = shards == 8 and heads_here * 2 == shards and tokens * shards == 2 * SEQ

    got_heads = Gathered(w_heads, direct=near)
    cotangent = lax.all_gather(out_cotangent, "stream", axis=1, tiled=True)
    lanes = jnp.concatenate([norm_gain, norm_bias]).astype(F32).reshape(tokens, -1)
    packed = lax.all_gather(jnp.concatenate([mixing[:, 0, :], lanes], axis=1), "stream", axis=0)
    if near:
        early = (got_heads.by_x, got_heads.by_y, got_heads.across)
        history = after(history, *early)
        w_up, w_merge = after(w_up, *early[:2]), after(w_merge, *early[:2])
    got_up = Gathered(w_up)
    got_merge = Gathered(w_merge)
    mix_all = packed[:, :, :entries]
    norms = packed[:, :, entries:].reshape(members, 2, width)
    gains, biases = norms[:, 0], norms[:, 1]
    mix_rows = jnp.transpose(mix_all, (1, 0, 2)).reshape(tokens, members * entries)

    normed, unit, inv, stream = make_streams(history, mix_rows, gains, biases)
    full_heads = got_heads.whole()
    positions = shard_offset[0] + jnp.arange(tokens, dtype=jnp.int32)
    projected = project(after(normed, got_up.by_x, got_up.by_y), full_heads, rope_tables(positions, 1.0))

    first_rows = mixer_first.astype(F32).reshape(tokens, -1)
    second_flat = mixer_second[:, 0, :].astype(F32).reshape(-1)
    hidden_count = mixer_second.shape[0]
    lines = -(-second_flat.shape[0] // tokens)
    second_rows = jnp.pad(second_flat, (0, lines * tokens - second_flat.shape[0]))
    rest = jnp.concatenate(
        [next_cotangent[:, 0, :], first_rows, second_rows.reshape(tokens, lines)], axis=1
    )
    rest = lax.all_gather(after(rest, projected), "stream", axis=0)
    outputs = next_cotangent.shape[2]
    cut = outputs + first_rows.shape[1]
    next_full = rest[:, :, :outputs]
    first_full = rest[:, :, outputs:cut].astype(BF).reshape(width, -1)
    second_full = rest[:, :, cut:].reshape(members, -1)[:, : second_flat.shape[0]]
    second_full = second_full.reshape(members, hidden_count, outputs)

    if near:
        spread = after(jnp.broadcast_to(shard_offset[:, None], (8, 128)), projected)
        offsets = lax.all_gather(spread, "dp", axis=0)[:, 0, 0]
        side = (index % 2).astype(jnp.int32).reshape(1)
        place = jnp.arange(shards, dtype=jnp.int32)
        first_key = jnp.maximum(place - offsets // tokens, 0).astype(jnp.int32)
        own = lax.all_to_all(projected, "dp", 0, 0, tiled=True)
        own = after(own, next_full, first_full, second_full, cotangent)
        got_down = Gathered(after(w_down, own))
        other = partner(own[:, 1:], 1)
        full_up = got_up.whole(projected)
        full_merge = got_merge.whole(projected)
        result, exact, level = attend(own, other, first_key, side)
        back = lax.all_to_all(result, "dp", 0, 0, tiled=True)
        attended = jnp.transpose(back.reshape(heads_here, tokens, HD), (1, 0, 2)).reshape(tokens, -1)
    else:
        got_down = Gathered(w_down)
        full_up = got_up.whole()
        full_merge = got_merge.whole()
        split = projected.reshape(heads_here, 2, 3, half, HD)
        split = jnp.transpose(split, (2, 1, 3, 0, 4)).reshape(3, tokens, heads_here, HD)
        result, kept = far_attend(split[0], split[1], split[2], shard_offset)
        attended = result.reshape(tokens, -1).astype(BF)
    full_down = got_down.whole()
    flat_up = full_up.reshape(width, -1)
    hidden, slope = hidden_units(normed[members - 1], flat_up)
    attended = after(attended, hidden)
    share = merge_branches(attended, hidden, full_merge, full_down, stream, flags)

    inner = (member == 1) | (member == 2)
    count = 8
    rows = [lax.slice_in_dim(share, i * tokens // count, (i + 1) * tokens // count) for i in range(count)]
    totals = {}

    def middle(i, one):
        return (rows[i] + one.astype(F32)).astype(BF)

    def ends(i, one, two):
        totals[i] = (rows[i] + one.astype(F32) + two.astype(F32)).astype(BF)
        return totals[i]

    _, _, arrived = along_line(count, lambda i, gates: gated(rows[i].astype(BF), gates), middle, ends)
    block_full = jnp.concatenate([jnp.where(inner, totals[i], arrived[i]) for i in range(count)])

    mine = member * (width // members)
    block_out = lax.dynamic_slice_in_dim(block_full, mine, width // members, axis=1)
    out_float = block_full.astype(F32)
    scale = lax.rsqrt(jnp.sum(out_float * out_float, axis=-1) / width + 1e-06)
    proj = dot(block_full, first_full)
    mixer, mixer_back = jax.vjp(exact_gelu, scale[:, None] * proj)
    second_here = mixer_second[:, 0, :].astype(F32)
    next_here = jnp.dot(mixer, second_here, precision=highest, preferred_element_type=F32)
    mixer_grad = jnp.einsum(
        "stn,scn->tc", next_full, second_full, precision=highest, preferred_element_type=F32
    )
    pre_grad = mixer_back(mixer_grad)[0]
    proj_grad = (scale[:, None] * pre_grad).astype(BF)
    scale_grad = jnp.sum(pre_grad * proj, axis=-1)
    second_local = jnp.dot(
        mixer.T, next_cotangent[:, 0, :], precision=highest, preferred_element_type=F32
    )
    first_local = dot_rows(block_out, proj_grad)
    grad_out = (
        cotangent.astype(F32)
        + dot_cols(proj_grad, first_full)
        - (scale * scale * scale * scale_grad)[:, None] * out_float / width
    ).astype(BF)

    attended_grad = back_through(grad_out, full_merge, None)
    up_grad = back_through(grad_out, full_down, slope)
    merge_grad = dot_rows(attended, grad_out).astype(BF)
    last_normed = dot_cols(up_grad, flat_up)
    last_share, last_stats = last_back(
        last_normed, unit[members - 1], inv, gains[members - 1 :], grad_out, flags
    )
    last_one = line_hop(last_share, OUTWARD)
    last_two = line_hop((last_share.astype(F32) + last_one.astype(F32)).astype(BF), MIDDLE)
    if near:
        sent = attended_grad.reshape(tokens, heads_here, HD)
        sent = jnp.transpose(sent, (1, 0, 2)).reshape(shards, half, HD)
        grads = lax.all_to_all(sent, "dp", 0, 0, tiled=True)
        grads = after(grads, last_share)
        kept_grads, given = attend_back(own, other, grads, exact, level, first_key, side)
        taken = partner(given, 1)
        summed = kept_grads[:, 1:].astype(F32) + taken.astype(F32)
        pair = jnp.concatenate([kept_grads[:, :1], summed.astype(BF)], axis=1)
        parts = lax.all_to_all(pair, "dp", 0, 0, tiled=True)
        hidden = after(hidden, pair)
    else:
        grads = far_attend_back(split[0], attended_grad.reshape(tokens, heads_here, HD), kept)
        parts = grads.reshape(3, 2, half, heads_here, HD)
        parts = jnp.transpose(parts, (3, 1, 0, 2, 4)).reshape(2 * heads_here, 3, half, HD)

    down_grad = dot_rows(hidden, grad_out).astype(BF)
    parts = after(parts, last_one, down_grad)
    blocks = 8
    *pieces, heads_share, heads_grad, heads_stats = heads_back(
        parts, full_heads, normed, unit, inv, gains, rope_tables(positions, -1.0), blocks
    )
    up_back = dot_rows(normed[members - 1], after(up_grad, heads_share)).astype(BF)

    grad_merge = lax.psum_scatter(merge_grad, "dp", scatter_dimension=1, tiled=True).astype(F32)
    grad_down = lax.psum_scatter(down_grad, "dp", scatter_dimension=1, tiled=True).astype(F32)
    grad_heads = lax.psum_scatter(heads_grad, "dp", scatter_dimension=1, tiled=True).astype(F32)
    grad_up = lax.psum_scatter(up_back, "dp", scatter_dimension=0, tiled=True).astype(F32)

    each = entries // members

    def weights_for(owner):
        block = lax.dynamic_slice_in_dim(mix_all, owner * each, each, axis=2)
        return jnp.transpose(block, (1, 2, 0)).reshape(tokens, each * members)

    there = weights_for(jnp.where(member == 1, 0, members - 1))
    here = weights_for(member)
    extra = {}

    def first_hop(i, gates):
        if i == 1:
            mix_parts = mixing_back(heads_share, last_share, history)
            stats = jnp.concatenate([heads_stats, last_stats[None]])
            both = jnp.concatenate([mix_parts, stats.reshape(members, tokens, -1)], axis=2)
            extra["both"] = jnp.sum(lax.all_to_all(both, "stream", 0, 0, tiled=True), axis=0)
        if i == 4:
            sums = extra["both"][:, entries:]
            second_sums = jnp.pad(second_local.reshape(-1), (0, lines * tokens - second_flat.shape[0]))
            local = jnp.concatenate(
                [sums, first_local.reshape(tokens, -1), second_sums.reshape(tokens, lines)], axis=1
            )
            extra["all"] = jnp.sum(lax.all_gather(local, "dp", axis=0), axis=0)
            gates = gates + [extra["both"]]
        if i == 2:
            gates = gates + [last_two]
        if i == 7:
            gates = gates + [extra["all"]]
        return gated(pieces[i], gates)

    def second_hop(i, one):
        return (pieces[i].astype(F32) + one.astype(F32)).astype(BF)

    def third_hop(i, one, two):
        return mix_block(i, there, pieces[i], last_share, [two], [last_two], None, None)

    def finish(i, one, two, three):
        extra["history"], token = mix_block(
            i,
            here,
            pieces[i],
            last_share,
            [one, two],
            [last_one, last_two],
            three,
            extra.get("history"),
        )
        return token

    along_line(blocks, first_hop, second_hop, third_hop, finish)
    grad_history = extra["history"]

    grad_mixing = extra["both"][:, :entries][:, None, :]
    sums = extra["all"]
    spans = 2 * width // tokens
    stats = sums[:, :spans].reshape(2, width)
    grad_first = sums[:, spans:-lines].reshape(mixer_first.shape)
    grad_second = sums[:, -lines:].reshape(-1)[: second_flat.shape[0]].reshape(hidden_count, outputs)
    return (
        block_out,
        next_here[:, None, :],
        grad_history,
        grad_mixing,
        stats[:1],
        stats[1:],
        grad_heads,
        grad_merge,
        grad_up,
        grad_down,
        grad_first,
        grad_second[:, None, :],
    )


def solution(mesh):
    in_specs = (
        P(None, "dp", None),
        P("dp", "stream", None),
        P("dp"),
        P("stream", None),
        P("stream", None),
        P(None, "dp", "stream"),
        P("stream", "dp"),
        P("dp", "stream"),
        P("stream", "dp"),
        P("stream", None),
        P(None, "stream", None),
        P("dp", "stream"),
        P("dp", "stream", None),
    )
    out_specs = (
        P("dp", "stream"),
        P("dp", "stream", None),
        P("stream", "dp", None),
        P("dp", "stream", None),
        P("stream", None),
        P("stream", None),
        P(None, "dp", "stream"),
        P("stream", "dp"),
        P("dp", "stream"),
        P("stream", "dp"),
        P("stream", None),
        P(None, "stream", None),
    )
    return jax.shard_map(body, mesh=mesh, in_specs=in_specs, out_specs=out_specs, check_vma=False)
```

```python
import math

import jax
import jax.numpy as jnp
from jax import lax
from jax.experimental import pallas as pl
from jax.experimental.pallas import tpu as pltpu
from jax.sharding import PartitionSpec as P

HD = 128
ROT = 32
SEQ = 2048


def passed_along(shard, axis, by):
    peers = lax.axis_size(axis)
    pairs = [(i, i + by) for i in range(peers) if 0 <= i + by < peers]
    return lax.ppermute(shard, axis, pairs)


def rotate(vectors, positions, sign):
    half = ROT // 2
    counter = jnp.arange(half, dtype=jnp.float32)
    freqs = jnp.exp(counter * (-2.0 * math.log(10000.0) / ROT))
    angles = positions.astype(jnp.float32)[:, None] * freqs[None, :]
    cosine = jnp.cos(angles)[:, None, :]
    sine = sign * jnp.sin(angles)[:, None, :]
    first = vectors[..., :half]
    second = vectors[..., half:ROT]
    return jnp.concatenate(
        [first * cosine - second * sine, second * cosine + first * sine, vectors[..., ROT:]],
        axis=-1,
    )


def exact_gelu(vectors):
    return jax.nn.gelu(vectors, approximate=False)


def block_logits(queries, keys_block, diagonal):
    logits = jnp.einsum("qhd,khd->hqk", queries, keys_block, preferred_element_type=jnp.float32) * (
        1.0 / math.sqrt(queries.shape[-1])
    )
    if diagonal:
        counter = jnp.arange(queries.shape[0], dtype=jnp.int32)
        allowed = counter[None, :] <= counter[:, None]
        logits = jnp.where(allowed[None], logits, -1e30)
    return logits


def keep_same(state):
    return state


BF = jnp.bfloat16
F32 = jnp.float32
OUTWARD = [(0, 1), (3, 2)]
MIDDLE = [(1, 2), (2, 1)]
INWARD = [(1, 0), (2, 3)]


def dot(left, right):
    return jnp.dot(left, right, preferred_element_type=F32)


def dot_rows(left, right):
    return lax.dot_general(left, right, (((0,), (0,)), ((), ())), preferred_element_type=F32)


def dot_cols(left, right):
    return lax.dot_general(left, right, (((1,), (1,)), ((), ())), preferred_element_type=F32)


def partner(shard, bit):
    peers = lax.axis_size("dp")
    return lax.ppermute(shard, "dp", [(i, i ^ bit) for i in range(peers)])


def line_hop(shard, pairs):
    return lax.ppermute(shard, "stream", pairs)


def cost(microseconds):
    return pl.CostEstimate(
        flops=int(microseconds * 0.9e9), bytes_accessed=int(microseconds * 3e6), transcendentals=0
    )


def after(value, *others):
    return lax.optimization_barrier((value, *others))[0]


class Gathered:
    def __init__(self, shard, direct=False):
        self.shard = shard
        self.peers = lax.axis_size("dp")
        if self.peers != 8:
            self.by_x = self.by_y = shard
            return
        self.cut = max(range(shard.ndim - 1), key=lambda dim: shard.shape[dim])
        self.by_x = partner(shard, 2)
        self.by_y = partner(shard, 4)
        self.across = partner(shard, 6) if direct else None

    def whole(self, *earlier):
        shard = self.shard
        if self.peers != 8:
            return lax.all_gather(shard, "dp", axis=0)
        index = lax.axis_index("dp")
        cut = self.cut
        half = shard.shape[cut] // 2
        shard, by_x, by_y = [gated(item, earlier) for item in (shard, self.by_x, self.by_y)]
        pieces = [(shard, 0, 0), (by_x, 2, 0), (by_y, 4, 0)]
        if self.across is None:
            low = lax.slice_in_dim(by_y, 0, half, axis=cut)
            high = lax.slice_in_dim(by_x, half, 2 * half, axis=cut)
            pieces += [(partner(low, 2), 6, 0), (partner(high, 4), 6, half)]
        else:
            pieces.append((gated(self.across, earlier), 6, 0))
        pieces += [(partner(piece, 1), code ^ 1, start) for piece, code, start in pieces]
        return put_together(pieces, shard, self.peers, cut, index)


def put_together(pieces, shard, peers, cut, index):
    codes = [(code, start) for _, code, start in pieces]
    arrays = [piece for piece, _, _ in pieces]

    def kernel(place, *refs):
        out, held, sems, sent = refs[-4:]
        owners = {}
        for n, (code, start) in enumerate(codes):
            size = refs[n].shape[cut]
            span = tuple(
                pl.ds(start, size) if dim == cut else slice(None) for dim in range(shard.ndim)
            )
            copy = pltpu.make_async_copy(refs[n], held.at[(code, *span)], sems.at[n])
            copy.start()
            owners.setdefault(code, []).append(copy)
        leaving = []
        for code, copies in owners.items():
            for copy in copies:
                copy.wait()
            copy = pltpu.make_async_copy(held.at[code], out.at[place[0] ^ code], sent.at[code])
            copy.start()
            leaving.append(copy)
        for copy in leaving:
            copy.wait()

    anywhere = pl.BlockSpec(memory_space=pl.ANY)
    size = peers * shard.size * shard.dtype.itemsize
    return pl.pallas_call(
        kernel,
        in_specs=[pl.BlockSpec(memory_space=pltpu.SMEM)] + [anywhere] * len(arrays),
        out_specs=anywhere,
        out_shape=jax.ShapeDtypeStruct((peers, *shard.shape), shard.dtype),
        scratch_shapes=[
            pltpu.VMEM((peers, *shard.shape), shard.dtype),
            pltpu.SemaphoreType.DMA((len(arrays),)),
            pltpu.SemaphoreType.DMA((peers,)),
        ],
        cost_estimate=cost(2 * size / 3e6),
        name="put_together",
    )(index.astype(jnp.int32).reshape(1), *arrays)


def along_line(count, first, second, third, finish=None):
    ones, twos, threes, ends = [], [], [], []
    for step in range(count + 2):
        if step < count:
            gates = []
            if step >= 2:
                gates.append(ones[step - 2])
            if step >= 3:
                gates.append(twos[step - 3])
            if step >= 4:
                gates.append(threes[step - 4] if finish is None else ends[step - 4])
            ones.append(line_hop(first(step, gates), OUTWARD))
        if 0 <= step - 1 < count:
            twos.append(line_hop(second(step - 1, ones[step - 1]), MIDDLE))
        if 0 <= step - 2 < count:
            back = step - 2
            threes.append(line_hop(third(back, ones[back], twos[back]), INWARD))
            if finish is not None:
                ends.append(finish(back, ones[back], twos[back], threes[back]))
    return ones, twos, threes


def gated(value, gates):
    return after(value, *gates) if gates else value


def rope_tables(positions, sign):
    half = ROT // 2
    lane = jnp.arange(HD, dtype=jnp.int32)
    counter = (lane % half).astype(F32)
    freqs = jnp.exp(counter * (-2.0 * math.log(10000.0) / ROT))
    angles = positions.astype(F32)[:, None] * freqs[None, :]
    cosine = jnp.where(lane < ROT, jnp.cos(angles), 1.0)
    sine = sign * jnp.sin(angles)
    up = jnp.where(lane < half, -sine, 0.0)
    down = jnp.where((lane >= half) & (lane < ROT), sine, 0.0)
    return jnp.stack([cosine, up, down])


def turned(block, tables):
    half = ROT // 2
    return (
        block * tables[0]
        + pltpu.roll(block, HD - half, 1) * tables[1]
        + pltpu.roll(block, half, 1) * tables[2]
    )


def make_streams(history, mix_rows, gains, biases):
    entries, tokens, width = history.shape
    streams = gains.shape[0]
    rows, sub, lanes = min(64, tokens), 16, 512

    def kernel(hist, mix, gain, bias, normed, unit, inv, last, scratch):
        def step(r, carry):
            here = pl.ds(pl.multiple_of(r * sub, sub), sub)
            weights = mix[here, :]
            columns = [
                [weights[:, s * entries + j : s * entries + j + 1] for j in range(entries)]
                for s in range(streams)
            ]
            for lane in range(0, width, lanes):
                span = slice(lane, lane + lanes)
                sums = [None] * streams
                for j in range(entries):
                    part = hist[j, here, span].astype(F32)
                    for s in range(streams):
                        term = columns[s][j] * part
                        sums[s] = term if j == 0 else sums[s] + term
                for s in range(streams):
                    scratch[s, :, span] = sums[s]
            stds = []
            for s in range(streams):
                values = scratch[s]
                center = values - jnp.sum(values, axis=-1, keepdims=True) * (1.0 / width)
                var = jnp.sum(center * center, axis=-1, keepdims=True) * (1.0 / width)
                std = lax.rsqrt(var + 1e-05)
                stds.append(std)
                scaled = center * std
                unit[s, here, :] = scaled.astype(BF)
                normed[s, here, :] = (scaled * gain[s : s + 1] + bias[s : s + 1]).astype(BF)
            last[here, :] = scratch[streams - 1]
            inv[here, :] = jnp.concatenate(stds, axis=-1)
            return carry

        lax.fori_loop(0, rows // sub, step, 0)

    wide = jax.ShapeDtypeStruct((streams, tokens, width), BF)
    return pl.pallas_call(
        kernel,
        grid=(tokens // rows,),
        in_specs=[
            pl.BlockSpec((entries, rows, width), lambda i: (0, i, 0)),
            pl.BlockSpec((rows, streams * entries), lambda i: (i, 0)),
            pl.BlockSpec((streams, width), lambda i: (0, 0)),
            pl.BlockSpec((streams, width), lambda i: (0, 0)),
        ],
        out_specs=[
            pl.BlockSpec((streams, rows, width), lambda i: (0, i, 0)),
            pl.BlockSpec((streams, rows, width), lambda i: (0, i, 0)),
            pl.BlockSpec((rows, streams), lambda i: (i, 0)),
            pl.BlockSpec((rows, width), lambda i: (i, 0)),
        ],
        out_shape=[
            wide,
            wide,
            jax.ShapeDtypeStruct((tokens, streams), F32),
            jax.ShapeDtypeStruct((tokens, width), F32),
        ],
        scratch_shapes=[pltpu.VMEM((streams, sub, width), F32)],
        cost_estimate=cost(22),
        name="make_streams",
    )(history, mix_rows, gains, biases)


def project(normed, w_heads, tables):
    _, tokens, width = normed.shape
    columns = w_heads.shape[3]
    heads, half = columns // HD, tokens // 2

    def kernel(x, w, table, out):
        flat = dot(x[0], w[...].reshape(width, columns))
        turn = pl.program_id(0) < 2

        def put(head, block):
            out[2 * head, 0] = block[:half].astype(BF)
            out[2 * head + 1, 0] = block[half:].astype(BF)

        @pl.when(turn)
        def _():
            for head in range(heads):
                put(head, turned(flat[:, head * HD : (head + 1) * HD], table[...]))

        @pl.when(jnp.logical_not(turn))
        def _():
            for head in range(heads):
                put(head, flat[:, head * HD : (head + 1) * HD])

    return pl.pallas_call(
        kernel,
        grid=(3,),
        in_specs=[
            pl.BlockSpec((1, tokens, width), lambda c: (c, 0, 0)),
            pl.BlockSpec((w_heads.shape[0], 1, w_heads.shape[2], columns), lambda c: (0, c, 0, 0)),
            pl.BlockSpec((3, tokens, HD), lambda c: (0, 0, 0)),
        ],
        out_specs=pl.BlockSpec((2 * heads, 1, half, HD), lambda c: (0, c, 0, 0)),
        out_shape=jax.ShapeDtypeStruct((2 * heads, 3, half, HD), BF),
        cost_estimate=cost(9),
        name="project",
    )(normed, w_heads, tables)


def attend(own, other, first_key, side):
    shards, _, half, _ = own.shape
    factor = 1.0 / math.sqrt(HD)

    def kernel(first, part, mine, theirs, out, exact, norm):
        s = pl.program_id(0)
        query = mine[s, 0]

        def fold(state, keys, values, mask):
            top, total, acc = state
            logits = dot_cols(query, keys) * factor
            if mask is not None:
                logits = jnp.where(mask, logits, -1e30)
            new_top = jnp.maximum(top, jnp.max(logits, axis=-1, keepdims=True))
            probs = jnp.exp(logits - new_top)
            keep = jnp.exp(top - new_top)
            return (
                new_top,
                total * keep + jnp.sum(probs, axis=-1, keepdims=True),
                acc * keep + dot(probs.astype(BF), values),
            )

        row = lax.broadcasted_iota(jnp.int32, (half, half), 0)
        col = lax.broadcasted_iota(jnp.int32, (half, half), 1)
        state = (
            jnp.full((half, 1), -1e30, F32),
            jnp.zeros((half, 1), F32),
            jnp.zeros((half, HD), F32),
        )
        state = fold(state, mine[s, 1], mine[s, 2], col <= row)
        state = lax.fori_loop(
            0, part[0], lambda i, st: fold(st, theirs[s, 0], theirs[s, 1], None), state
        )

        def shard_step(b, st):
            st = fold(st, mine[b, 1], mine[b, 2], None)
            return fold(st, theirs[b, 0], theirs[b, 1], None)

        top, total, acc = lax.fori_loop(first[s], s, shard_step, state)
        result = acc / total
        out[0] = result.astype(BF)
        exact[0] = result
        norm[0] = top + jnp.log(total)

    return pl.pallas_call(
        kernel,
        grid_spec=pltpu.PrefetchScalarGridSpec(
            num_scalar_prefetch=2,
            grid=(shards,),
            in_specs=[
                pl.BlockSpec((shards, 3, half, HD), lambda s, *_: (0, 0, 0, 0)),
                pl.BlockSpec((shards, 2, half, HD), lambda s, *_: (0, 0, 0, 0)),
            ],
            out_specs=[
                pl.BlockSpec((1, half, HD), lambda s, *_: (s, 0, 0)),
                pl.BlockSpec((1, half, HD), lambda s, *_: (s, 0, 0)),
                pl.BlockSpec((1, half, 1), lambda s, *_: (s, 0, 0)),
            ],
        ),
        out_shape=[
            jax.ShapeDtypeStruct((shards, half, HD), BF),
            jax.ShapeDtypeStruct((shards, half, HD), F32),
            jax.ShapeDtypeStruct((shards, half, 1), F32),
        ],
        cost_estimate=cost(16),
        name="attend",
    )(first_key, side, own, other)


def attend_back(own, other, grads, exact, norm, first_key, side):
    shards, _, half, _ = own.shape
    factor = 1.0 / math.sqrt(HD)

    def kernel(first, part, mine, theirs, grad_ref, exact_ref, norm_ref, kept, given, sums):
        s = pl.program_id(0)
        query = mine[s, 0]
        grad = grad_ref[s]
        delta = jnp.sum(grad.astype(F32) * exact_ref[0], axis=-1, keepdims=True)
        level = norm_ref[0]
        lowered = grad

        @pl.when(s == 0)
        def _():
            sums[...] = jnp.zeros_like(sums)

        def fold(query_grad, keys, values, mask, slot, b):
            logits = dot_cols(query, keys) * factor
            probs = jnp.exp(logits - level)
            if mask is not None:
                probs = jnp.where(mask, probs, 0.0)
            score = (probs * (dot_cols(grad, values) - delta)).astype(BF)
            sums[slot, b] += dot_rows(score, query)
            sums[slot + 1, b] += dot_rows(probs.astype(BF), lowered)
            return query_grad + dot(score, keys)

        row = lax.broadcasted_iota(jnp.int32, (half, half), 0)
        col = lax.broadcasted_iota(jnp.int32, (half, half), 1)
        total = fold(jnp.zeros((half, HD), F32), mine[s, 1], mine[s, 2], col <= row, 0, s)
        total = lax.fori_loop(
            0, part[0], lambda i, q: fold(q, theirs[s, 0], theirs[s, 1], None, 2, s), total
        )

        def shard_step(b, q):
            q = fold(q, mine[b, 1], mine[b, 2], None, 0, b)
            return fold(q, theirs[b, 0], theirs[b, 1], None, 2, b)

        total = lax.fori_loop(first[s], s, shard_step, total)
        kept[s, 0] = (total * factor).astype(BF)

        @pl.when(s == shards - 1)
        def _():
            for b in range(shards):
                kept[b, 1] = (sums[0, b] * factor).astype(BF)
                kept[b, 2] = sums[1, b].astype(BF)
                given[b, 0] = (sums[2, b] * factor).astype(BF)
                given[b, 1] = sums[3, b].astype(BF)

    whole = lambda n: pl.BlockSpec((shards, n, half, HD), lambda s, *_: (0, 0, 0, 0))
    return pl.pallas_call(
        kernel,
        grid_spec=pltpu.PrefetchScalarGridSpec(
            num_scalar_prefetch=2,
            grid=(shards,),
            in_specs=[
                whole(3),
                whole(2),
                pl.BlockSpec((shards, half, HD), lambda s, *_: (0, 0, 0)),
                pl.BlockSpec((1, half, HD), lambda s, *_: (s, 0, 0)),
                pl.BlockSpec((1, half, 1), lambda s, *_: (s, 0, 0)),
            ],
            out_specs=[whole(3), whole(2)],
            scratch_shapes=[pltpu.VMEM((4, shards, half, HD), F32)],
        ),
        out_shape=[
            jax.ShapeDtypeStruct((shards, 3, half, HD), BF),
            jax.ShapeDtypeStruct((shards, 2, half, HD), BF),
        ],
        cost_estimate=cost(22),
        name="attend_back",
    )(first_key, side, own, other, grads, exact, norm)


def norm_back(grad, unit, inv, gain, extra):
    width = grad.shape[1]
    scaled = grad * gain
    mean = jnp.sum(scaled, axis=-1, keepdims=True) * (1.0 / width)
    slope = jnp.sum(scaled * unit, axis=-1, keepdims=True) * (1.0 / width)
    result = inv * (scaled - mean - unit * slope)
    return result if extra is None else result + extra


def heads_back(parts, w_heads, normed, unit, inv, gains, tables, count):
    _, tokens, width = normed.shape
    columns = w_heads.shape[3]
    heads, half = columns // HD, tokens // 2
    block = tokens // count

    def kernel(part, w, x, u, istd, gain, table, *refs):
        pieces, (stream, weight, stats, grad, wide) = refs[:count], refs[count:]
        c = pl.program_id(0)
        turn = c < 2

        def take(head):
            return jnp.concatenate([part[2 * head, 0], part[2 * head + 1, 0]], axis=0).astype(F32)

        @pl.when(turn)
        def _():
            for head in range(heads):
                grad[:, head * HD : (head + 1) * HD] = turned(take(head), table[...]).astype(BF)

        @pl.when(jnp.logical_not(turn))
        def _():
            for head in range(heads):
                grad[:, head * HD : (head + 1) * HD] = take(head).astype(BF)

        wide[...] = dot_cols(grad[...], w[...].reshape(width, columns))
        weight[0] = dot_rows(x[0], grad[...]).astype(BF)
        stats[...] = jnp.zeros_like(stats)
        column = lax.broadcasted_iota(jnp.int32, (block, istd.shape[1]), 1)

        for r in range(count):
            here = slice(r * block, (r + 1) * block)
            values = wide[here, :]
            units = u[0, here, :].astype(F32)
            std = jnp.sum(jnp.where(column == c, istd[here, :], 0.0), axis=-1, keepdims=True)
            result = norm_back(values, units, std, gain[0], None).astype(BF)
            stream[0, here, :] = result
            pieces[r][0] = result
            stats[0, 0:1] += jnp.sum(values * units, axis=0, keepdims=True)
            stats[0, 1:2] += jnp.sum(values, axis=0, keepdims=True)

    return pl.pallas_call(
        kernel,
        grid=(3,),
        in_specs=[
            pl.BlockSpec((2 * heads, 1, half, HD), lambda c: (0, c, 0, 0)),
            pl.BlockSpec((w_heads.shape[0], 1, w_heads.shape[2], columns), lambda c: (0, c, 0, 0)),
            pl.BlockSpec((1, tokens, width), lambda c: (c, 0, 0)),
            pl.BlockSpec((1, tokens, width), lambda c: (c, 0, 0)),
            pl.BlockSpec((tokens, inv.shape[1]), lambda c: (0, 0)),
            pl.BlockSpec((1, 1, width), lambda c: (c, 0, 0)),
            pl.BlockSpec((3, tokens, HD), lambda c: (0, 0, 0)),
        ],
        out_specs=[pl.BlockSpec((1, block, width), lambda c: (c, 0, 0))] * count
        + [
            pl.BlockSpec((1, tokens, width), lambda c: (c, 0, 0)),
            pl.BlockSpec((1, width, columns), lambda c: (c, 0, 0)),
            pl.BlockSpec((1, 2, width), lambda c: (c, 0, 0)),
        ],
        out_shape=[jax.ShapeDtypeStruct((3, block, width), BF)] * count
        + [
            jax.ShapeDtypeStruct((3, tokens, width), BF),
            jax.ShapeDtypeStruct((3, width, columns), BF),
            jax.ShapeDtypeStruct((3, 2, width), F32),
        ],
        scratch_shapes=[pltpu.VMEM((tokens, columns), BF), pltpu.VMEM((tokens, width), F32)],
        cost_estimate=cost(18),
        name="heads_back",
    )(parts, w_heads, normed, unit, inv, gains[:, None, :], tables)


def last_back(grad, unit, inv, gain, extra, flag):
    tokens, width = grad.shape
    block = min(128, tokens)

    def kernel(g, u, istd, gain_ref, e, flag_ref, stream, stats):
        @pl.when(pl.program_id(0) == 0)
        def _():
            stats[...] = jnp.zeros_like(stats)

        values = g[...]
        units = u[...].astype(F32)
        std = istd[...][:, -1:]
        added = e[...].astype(F32) * flag_ref[0]
        stream[...] = norm_back(values, units, std, gain_ref[...], added).astype(BF)
        stats[0:1] += jnp.sum(values * units, axis=0, keepdims=True)
        stats[1:2] += jnp.sum(values, axis=0, keepdims=True)

    row = lambda n: pl.BlockSpec((block, n), lambda i: (i, 0))
    return pl.pallas_call(
        kernel,
        grid=(tokens // block,),
        in_specs=[
            row(width),
            row(width),
            row(inv.shape[1]),
            pl.BlockSpec((1, width), lambda i: (0, 0)),
            row(width),
            pl.BlockSpec(memory_space=pltpu.SMEM),
        ],
        out_specs=[row(width), pl.BlockSpec((2, width), lambda i: (0, 0))],
        out_shape=[
            jax.ShapeDtypeStruct((tokens, width), BF),
            jax.ShapeDtypeStruct((2, width), F32),
        ],
        cost_estimate=cost(7),
        name="last_back",
    )(grad, unit, inv, gain, extra, flag)


def mixing_back(heads_part, last_part, history, which, of):
    entries, tokens, width = history.shape
    streams = heads_part.shape[0] + 1
    rows, sub, lanes = min(64, tokens // of), 16, 256
    steps = tokens // of // rows
    base = which * steps

    def kernel(first, last, hist, out):
        def step(r, carry):
            here = pl.ds(pl.multiple_of(r * sub, sub), sub)
            for s in range(streams):
                sums = [None] * entries
                for lane in range(0, width, lanes):
                    span = slice(lane, lane + lanes)
                    part = first[s, here, span] if s < streams - 1 else last[here, span]
                    part = part.astype(F32)
                    for j in range(entries):
                        term = part * hist[j, here, span].astype(F32)
                        sums[j] = term if lane == 0 else sums[j] + term
                columns = [jnp.sum(item, axis=-1, keepdims=True) for item in sums]
                out[s, here, :] = jnp.concatenate(columns, axis=-1)
            return carry

        lax.fori_loop(0, rows // sub, step, 0)

    return pl.pallas_call(
        kernel,
        grid=(steps,),
        in_specs=[
            pl.BlockSpec((streams - 1, rows, width), lambda i: (0, base + i, 0)),
            pl.BlockSpec((rows, width), lambda i: (base + i, 0)),
            pl.BlockSpec((entries, rows, width), lambda i: (0, base + i, 0)),
        ],
        out_specs=pl.BlockSpec((streams, rows, entries), lambda i: (0, i, 0)),
        out_shape=jax.ShapeDtypeStruct((streams, tokens // of, entries), F32),
        cost_estimate=cost(18 / of),
        name="mixing_back",
    )(heads_part, last_part, history)


def far_attend(queries, keys, values, shard_offset):
    tokens, heads_here, head_size = queries.shape
    data_index = lax.axis_index("dp")
    pairs = [jnp.stack([keys, values])]
    reach = 2 * SEQ // tokens
    for back in range(1, reach):
        pairs.append(passed_along(pairs[0], "dp", back))
    usable = [(shard_offset[0] >= back * tokens) & (data_index >= back) for back in range(reach)]
    first_logits = block_logits(queries, keys, True)
    top = jnp.max(first_logits, axis=-1)
    total = jnp.sum(jnp.exp(first_logits - top[..., None]), axis=-1)
    for back in range(1, reach):

        def widen(state, block=pairs[back][0]):
            logits = block_logits(queries, block, False)
            new_top = jnp.maximum(state[0], jnp.max(logits, axis=-1))
            summed = state[1] * jnp.exp(state[0] - new_top) + jnp.sum(
                jnp.exp(logits - new_top[..., None]), axis=-1
            )
            return (new_top, summed)

        top, total = lax.cond(usable[back], widen, keep_same, (top, total))
    log_total = top + jnp.log(total)
    attended = jnp.zeros((tokens, heads_here, head_size), F32)
    for back in range(reach):

        def accumulate(current, block=pairs[back], diagonal=back == 0):
            probs = jnp.exp(block_logits(queries, block[0], diagonal) - log_total[..., None])
            return current + jnp.einsum(
                "hqk,khd->qhd", probs.astype(BF), block[1], preferred_element_type=F32
            )

        attended = lax.cond(usable[back], accumulate, keep_same, attended)
    return attended, (pairs, usable, log_total)


def far_attend_back(queries, attended_grad, kept):
    tokens, heads_here, head_size = queries.shape
    factor = 1.0 / math.sqrt(head_size)
    pairs, usable, log_total = kept
    reach = len(pairs)

    def weights_of(block, diagonal):
        return jnp.exp(block_logits(queries, block, diagonal) - log_total[..., None])

    def prob_grads(block):
        return jnp.einsum("qhd,khd->hqk", attended_grad, block[1], preferred_element_type=F32)

    delta = jnp.zeros((heads_here, tokens), F32)
    for back in range(reach):

        def gather_delta(current, block=pairs[back], diagonal=back == 0):
            return current + jnp.sum(weights_of(block[0], diagonal) * prob_grads(block), axis=-1)

        delta = lax.cond(usable[back], gather_delta, keep_same, delta)

    def skip_block(current):
        return (current, jnp.zeros((2, tokens, heads_here, head_size), F32))

    query_grad = jnp.zeros((tokens, heads_here, head_size), F32)
    key_value_grad = jnp.zeros((2, tokens, heads_here, head_size), F32)
    for back in range(reach):

        def spread(current, block=pairs[back], diagonal=back == 0):
            probs = weights_of(block[0], diagonal)
            score_grad = (probs * (prob_grads(block) - delta[..., None])).astype(BF)
            query_part = (
                current
                + jnp.einsum("hqk,khd->qhd", score_grad, block[0], preferred_element_type=F32)
                * factor
            )
            key_part = (
                jnp.einsum("hqk,qhd->khd", score_grad, queries, preferred_element_type=F32)
                * factor
            )
            value_part = jnp.einsum(
                "hqk,qhd->khd", probs.astype(BF), attended_grad, preferred_element_type=F32
            )
            return (query_part, jnp.stack([key_part, value_part]))

        query_grad, pair_grad = lax.cond(usable[back], spread, skip_block, query_grad)
        if back == 0:
            key_value_grad = pair_grad
        else:
            key_value_grad = key_value_grad + passed_along(pair_grad, "dp", -back)
    return jnp.concatenate([query_grad[None], key_value_grad])


def mix_block(i, coefficients, shares, last_share, extras, last_extras, arrived, whole):
    streams, block, width = shares.shape
    each = coefficients.shape[1] // (streams + 1)
    groups = 1 + len(extras)
    final = arrived is not None
    lanes = 512

    def kernel(*refs):
        weights = refs[0][...]
        heads, lasts = refs[1 : 1 + groups], refs[1 + groups : 1 + 2 * groups]
        out = refs[-2] if final else refs[-1]
        if final:
            refs[-1][...] = jnp.zeros_like(refs[-1])
        columns = [weights[:, n : n + 1] for n in range(weights.shape[1])]
        for lane in range(0, width, lanes):
            span = slice(lane, lane + lanes)
            values = []
            for s in range(streams + 1):
                picks = [r[s, :, span] if s < streams else l[:, span] for r, l in zip(heads, lasts)]
                total = picks[0].astype(F32)
                for pick in picks[1:]:
                    total = total + pick.astype(F32)
                values.append(total)
            for e in range(each):
                total = columns[e * (streams + 1)] * values[0]
                for s in range(1, streams + 1):
                    total = total + columns[e * (streams + 1) + s] * values[s]
                if final:
                    total = total + refs[1 + 2 * groups][e, :, span].astype(F32)
                out[e, :, span] = total.astype(out.dtype)

    piece = pl.BlockSpec((streams, block, width), lambda n: (0, 0, 0))
    row = pl.BlockSpec((block, width), lambda n: (i, 0))
    small = pl.BlockSpec((each, block, width), lambda n: (0, 0, 0))
    specs = [pl.BlockSpec((block, coefficients.shape[1]), lambda n: (i, 0))]
    specs += [piece] * groups + [row] * groups
    args = [coefficients, shares, *extras, last_share, *last_extras]
    alias = {}
    if final:
        specs.append(small)
        args.append(arrived)
        if whole is not None:
            specs.append(pl.BlockSpec(memory_space=pl.ANY))
            args.append(whole)
            alias = {len(args) - 1: 0}
        out_spec = [
            pl.BlockSpec((each, block, width), lambda n: (0, i, 0)),
            pl.BlockSpec((8, 128), lambda n: (0, 0)),
        ]
        out_shape = [
            jax.ShapeDtypeStruct((each, coefficients.shape[0], width), F32),
            jax.ShapeDtypeStruct((8, 128), F32),
        ]
    else:
        out_spec, out_shape = small, jax.ShapeDtypeStruct((each, block, width), BF)
    return pl.pallas_call(
        kernel,
        grid=(1,),
        in_specs=specs,
        out_specs=out_spec,
        out_shape=out_shape,
        input_output_aliases=alias,
        cost_estimate=cost(4 if final else 3),
        name="mix_final" if final else "mix_inward",
    )(*args)


def hidden_units(x, w_up):
    tokens, width = x.shape
    units = w_up.shape[1]
    block = min(512, units)

    def kernel(x_ref, w, out, slope):
        up = dot(x_ref[...], w[...])
        inside = 0.5 * (1.0 + lax.erf(up * math.sqrt(0.5)))
        out[...] = (up * inside).astype(BF)
        bell = jnp.exp(-0.5 * up * up) * (1.0 / math.sqrt(2.0 * math.pi))
        slope[...] = (inside + up * bell).astype(BF)

    column = pl.BlockSpec((tokens, block), lambda i: (0, i))
    return pl.pallas_call(
        kernel,
        grid=(units // block,),
        in_specs=[
            pl.BlockSpec((tokens, width), lambda i: (0, 0)),
            pl.BlockSpec((width, block), lambda i: (0, i)),
        ],
        out_specs=[column, column],
        out_shape=[jax.ShapeDtypeStruct((tokens, units), BF)] * 2,
        cost_estimate=cost(9),
        name="hidden_units",
    )(x, w_up)


def merge_branches(attended, hidden, w_merge, w_down, stream, flag):
    tokens, inner = attended.shape
    shards, units, cols = w_down.shape
    if cols % 128:
        merged = jnp.einsum("te,ned->tnd", attended, w_merge, preferred_element_type=F32)
        merged = merged + jnp.einsum("tf,nfd->tnd", hidden, w_down, preferred_element_type=F32)
        return merged.reshape(tokens, -1) + flag * stream

    def kernel(a, h, wm, wd, st, flag_ref, out):
        out[...] = dot(a[...], wm[0]) + dot(h[...], wd[0]) + flag_ref[0] * st[...]

    return pl.pallas_call(
        kernel,
        grid=(shards,),
        in_specs=[
            pl.BlockSpec((tokens, inner), lambda n: (0, 0)),
            pl.BlockSpec((tokens, units), lambda n: (0, 0)),
            pl.BlockSpec((1, inner, cols), lambda n: (n, 0, 0)),
            pl.BlockSpec((1, units, cols), lambda n: (n, 0, 0)),
            pl.BlockSpec((tokens, cols), lambda n: (0, n)),
            pl.BlockSpec(memory_space=pltpu.SMEM),
        ],
        out_specs=pl.BlockSpec((tokens, cols), lambda n: (0, n)),
        out_shape=jax.ShapeDtypeStruct((tokens, shards * cols), F32),
        cost_estimate=cost(13),
        name="merge_branches",
    )(attended, hidden, w_merge, w_down, stream, flag)


def back_through(grad, stacked, slope):
    tokens = grad.shape[0]
    shards, units, cols = stacked.shape
    if cols % 128:
        split = grad.reshape(tokens, shards, cols)
        total = jnp.einsum("tnd,nfd->tf", split, stacked, preferred_element_type=F32)
        return (total if slope is None else total * slope.astype(F32)).astype(BF)

    def kernel(*refs):
        g, w = refs[:2]
        out, acc = refs[-2:]
        n = pl.program_id(0)
        part = dot_cols(g[...], w[0])

        @pl.when(n == 0)
        def _():
            acc[...] = part

        @pl.when(n > 0)
        def _():
            acc[...] += part

        @pl.when(n == shards - 1)
        def _():
            total = acc[...]
            if slope is not None:
                total = total * refs[2][...].astype(F32)
            out[...] = total.astype(BF)

    specs = [
        pl.BlockSpec((tokens, cols), lambda n: (0, n)),
        pl.BlockSpec((1, units, cols), lambda n: (n, 0, 0)),
    ]
    args = [grad, stacked]
    if slope is not None:
        specs.append(pl.BlockSpec((tokens, units), lambda n: (0, 0)))
        args.append(slope)
    return pl.pallas_call(
        kernel,
        grid=(shards,),
        in_specs=specs,
        out_specs=pl.BlockSpec((tokens, units), lambda n: (0, 0)),
        out_shape=jax.ShapeDtypeStruct((tokens, units), BF),
        scratch_shapes=[pltpu.VMEM((tokens, units), F32)],
        cost_estimate=cost(13 if slope is not None else 7),
        name="back_through",
    )(*args)


def body(
    history,
    mixing,
    shard_offset,
    norm_gain,
    norm_bias,
    w_heads,
    w_merge,
    w_up,
    w_down,
    mixer_first,
    mixer_second,
    out_cotangent,
    next_cotangent,
):
    member = lax.axis_index("stream")
    members = lax.axis_size("stream")
    shards = lax.axis_size("dp")
    index = lax.axis_index("dp")
    entries, tokens, width = history.shape
    heads_here = w_heads.shape[2] // HD
    half = tokens // 2
    highest = lax.Precision.HIGHEST
    flag = (member == members - 1).astype(F32)
    flags = flag.reshape(1)
    near = shards == 8 and heads_here * 2 == shards and tokens * shards == 2 * SEQ

    got_heads = Gathered(w_heads, direct=near)
    cotangent = lax.all_gather(out_cotangent, "stream", axis=1, tiled=True)
    lanes = jnp.concatenate([norm_gain, norm_bias]).astype(F32).reshape(tokens, -1)
    first_rows = mixer_first.astype(F32).reshape(tokens, -1)
    second_flat = mixer_second[:, 0, :].astype(F32).reshape(-1)
    hidden_count = mixer_second.shape[0]
    lines = -(-second_flat.shape[0] // tokens)
    second_rows = jnp.pad(second_flat, (0, lines * tokens - second_flat.shape[0]))
    outputs = next_cotangent.shape[2]
    arrays = [mixing[:, 0, :], lanes, next_cotangent[:, 0, :], first_rows]
    arrays.append(second_rows.reshape(tokens, lines))
    packed = lax.all_gather(jnp.concatenate(arrays, axis=1), "stream", axis=0)
    parts, place = [], 0
    for array in arrays:
        parts.append(packed[:, :, place : place + array.shape[1]])
        place += array.shape[1]
    mix_all, norms, next_full, first_full, second_full = parts
    norms = norms.reshape(members, 2, width)
    first_full = first_full.astype(BF).reshape(width, -1)
    second_full = second_full.reshape(members, -1)[:, : second_flat.shape[0]]
    second_full = second_full.reshape(members, hidden_count, outputs)
    if near:
        spread = jnp.broadcast_to(shard_offset[:, None], (8, 128))
        offsets = lax.all_gather(spread, "dp", axis=0)[:, 0, 0]
        early = (got_heads.by_x, got_heads.by_y, got_heads.across)
        history = after(history, *early, offsets)
        w_up, w_merge = after(w_up, *early[:2]), after(w_merge, *early[:2])
    got_up = Gathered(w_up)
    got_merge = Gathered(w_merge, direct=near)
    gains, biases = norms[:, 0], norms[:, 1]
    mix_rows = jnp.transpose(mix_all, (1, 0, 2)).reshape(tokens, members * entries)

    normed, unit, inv, stream = make_streams(history, mix_rows, gains, biases)
    full_heads = got_heads.whole()
    positions = shard_offset[0] + jnp.arange(tokens, dtype=jnp.int32)
    projected = project(after(normed, got_up.by_x, got_up.by_y), full_heads, rope_tables(positions, 1.0))

    if near:
        side = (index % 2).astype(jnp.int32).reshape(1)
        place = jnp.arange(shards, dtype=jnp.int32)
        first_key = jnp.maximum(place - offsets // tokens, 0).astype(jnp.int32)
        own = lax.all_to_all(projected, "dp", 0, 0, tiled=True)
        got_down = Gathered(after(w_down, own))
        other = partner(own[:, 1:], 1)
        full_up = got_up.whole(projected)
        full_merge = got_merge.whole(own)
        own = after(own, cotangent)
        result, exact, level = attend(own, other, first_key, side)
        back = lax.all_to_all(result, "dp", 0, 0, tiled=True)
        attended = jnp.transpose(back.reshape(heads_here, tokens, HD), (1, 0, 2)).reshape(tokens, -1)
    else:
        got_down = Gathered(w_down)
        full_up = got_up.whole()
        full_merge = got_merge.whole()
        split = projected.reshape(heads_here, 2, 3, half, HD)
        split = jnp.transpose(split, (2, 1, 3, 0, 4)).reshape(3, tokens, heads_here, HD)
        result, kept = far_attend(split[0], split[1], split[2], shard_offset)
        attended = result.reshape(tokens, -1).astype(BF)
    full_down = got_down.whole()
    flat_up = full_up.reshape(width, -1)
    hidden, slope = hidden_units(normed[members - 1], flat_up)
    attended = after(attended, hidden)
    share = merge_branches(attended, hidden, full_merge, full_down, stream, flags)

    inner = (member == 1) | (member == 2)
    count = 8
    rows = [lax.slice_in_dim(share, i * tokens // count, (i + 1) * tokens // count) for i in range(count)]
    totals = {}

    def middle(i, one):
        return (rows[i] + one.astype(F32)).astype(BF)

    def ends(i, one, two):
        totals[i] = (rows[i] + one.astype(F32) + two.astype(F32)).astype(BF)
        return totals[i]

    _, _, arrived = along_line(count, lambda i, gates: gated(rows[i].astype(BF), gates), middle, ends)
    block_full = jnp.concatenate([jnp.where(inner, totals[i], arrived[i]) for i in range(count)])

    mine = member * (width // members)
    block_out = lax.dynamic_slice_in_dim(block_full, mine, width // members, axis=1)
    out_float = block_full.astype(F32)
    scale = lax.rsqrt(jnp.sum(out_float * out_float, axis=-1) / width + 1e-06)
    proj = dot(block_full, first_full)
    mixer, mixer_back = jax.vjp(exact_gelu, scale[:, None] * proj)
    second_here = mixer_second[:, 0, :].astype(F32)
    next_here = jnp.dot(mixer, second_here, precision=highest, preferred_element_type=F32)
    mixer_grad = jnp.einsum(
        "stn,scn->tc", next_full, second_full, precision=highest, preferred_element_type=F32
    )
    pre_grad = mixer_back(mixer_grad)[0]
    proj_grad = (scale[:, None] * pre_grad).astype(BF)
    scale_grad = jnp.sum(pre_grad * proj, axis=-1)
    second_local = jnp.dot(
        mixer.T, next_cotangent[:, 0, :], precision=highest, preferred_element_type=F32
    )
    first_local = dot_rows(block_out, proj_grad)
    grad_out = (
        cotangent.astype(F32)
        + dot_cols(proj_grad, first_full)
        - (scale * scale * scale * scale_grad)[:, None] * out_float / width
    ).astype(BF)

    attended_grad = back_through(grad_out, full_merge, None)
    up_grad = back_through(grad_out, full_down, slope)
    down_grad = dot_rows(hidden, grad_out).astype(BF)
    last_normed = dot_cols(after(up_grad, down_grad), flat_up)
    last_share, last_stats = last_back(
        last_normed, unit[members - 1], inv, gains[members - 1 :], grad_out, flags
    )
    last_one = line_hop(last_share, OUTWARD)
    last_sum = (last_share.astype(F32) + last_one.astype(F32)).astype(BF)
    last_two = line_hop(last_sum, MIDDLE)
    if near:
        sent = attended_grad.reshape(tokens, heads_here, HD)
        sent = jnp.transpose(sent, (1, 0, 2)).reshape(shards, half, HD)
        grads = lax.all_to_all(sent, "dp", 0, 0, tiled=True)
        grads = after(grads, last_share)
        kept_grads, given = attend_back(own, other, grads, exact, level, first_key, side)
        taken = partner(given, 1)
        summed = kept_grads[:, 1:].astype(F32) + taken.astype(F32)
        pair = jnp.concatenate([kept_grads[:, :1], summed.astype(BF)], axis=1)
        pair = after(pair, last_one)
        parts = lax.all_to_all(pair, "dp", 0, 0, tiled=True)
        late_grad, late_up = after(grad_out, pair), after(up_grad, pair)
    else:
        late_grad, late_up = grad_out, up_grad
        grads = far_attend_back(split[0], attended_grad.reshape(tokens, heads_here, HD), kept)
        parts = grads.reshape(3, 2, half, heads_here, HD)
        parts = jnp.transpose(parts, (3, 1, 0, 2, 4)).reshape(2 * heads_here, 3, half, HD)

    up_back = dot_rows(normed[members - 1], late_up).astype(BF)
    merge_grad = dot_rows(attended, late_grad).astype(BF)
    parts = after(parts, up_back, merge_grad, last_sum)
    blocks = 8
    *pieces, heads_share, heads_grad, heads_stats = heads_back(
        parts, full_heads, normed, unit, inv, gains, rope_tables(positions, -1.0), blocks
    )

    grad_merge = lax.psum_scatter(merge_grad, "dp", scatter_dimension=1, tiled=True).astype(F32)
    grad_down = lax.psum_scatter(down_grad, "dp", scatter_dimension=1, tiled=True).astype(F32)
    grad_heads = lax.psum_scatter(heads_grad, "dp", scatter_dimension=1, tiled=True).astype(F32)
    grad_up = lax.psum_scatter(up_back, "dp", scatter_dimension=0, tiled=True).astype(F32)

    each = entries // members

    def weights_for(owner):
        block = lax.dynamic_slice_in_dim(mix_all, owner * each, each, axis=2)
        return jnp.transpose(block, (1, 2, 0)).reshape(tokens, each * members)

    there = weights_for(jnp.where(member == 1, 0, members - 1))
    here = weights_for(member)
    extra = {}

    def first_hop(i, gates):
        gates = list(gates)
        if i == 1:
            gates.append(grad_down)
        if i == 2:
            gates.append(last_two)
        if i == 5:
            gates.append(grad_up)
        if i == 7:
            gates.append(grad_merge)
        return gated(pieces[i], gates)

    def small_sums():
        stats = jnp.concatenate([heads_stats, last_stats[None]]).reshape(members, tokens, -1)
        both = jnp.concatenate([jnp.concatenate(mixes, axis=1), stats], axis=2)
        both = jnp.sum(lax.all_to_all(both, "stream", 0, 0, tiled=True), axis=0)
        second_sums = jnp.pad(second_local.reshape(-1), (0, lines * tokens - second_flat.shape[0]))
        local = [both[:, entries:], first_local.reshape(tokens, -1), second_sums.reshape(tokens, lines)]
        everyone = lax.all_gather(jnp.concatenate(local, axis=1), "dp", axis=0)
        return both[:, :entries], jnp.sum(everyone, axis=0)

    mixes = []
    quarters = 4
    quarter = tokens // quarters

    def second_hop(i, one):
        return (pieces[i].astype(F32) + one.astype(F32)).astype(BF)

    def third_hop(i, one, two):
        return mix_block(i, there, pieces[i], last_share, [two], [last_two], None, None)

    def finish(i, one, two, three):
        if i in (0, 1, 2, 3):
            mixes.append(mixing_back(heads_share, last_share, after(history, two), i, quarters))
        if i == 3:
            extra["both"], extra["all"] = small_sums()
        if i == 5:
            three = after(three, extra["both"], extra["all"])
        extra["history"], token = mix_block(
            i,
            here,
            pieces[i],
            last_share,
            [one, two],
            [last_one, last_two],
            three,
            extra.get("history"),
        )
        return token

    along_line(blocks, first_hop, second_hop, third_hop, finish)
    grad_history = extra["history"]

    grad_mixing = extra["both"][:, None, :]
    sums = extra["all"]
    spans = 2 * width // tokens
    stats = sums[:, :spans].reshape(2, width)
    grad_first = sums[:, spans:-lines].reshape(mixer_first.shape)
    grad_second = sums[:, -lines:].reshape(-1)[: second_flat.shape[0]].reshape(hidden_count, outputs)
    return (
        block_out,
        next_here[:, None, :],
        grad_history,
        grad_mixing,
        stats[:1],
        stats[1:],
        grad_heads,
        grad_merge,
        grad_up,
        grad_down,
        grad_first,
        grad_second[:, None, :],
    )


def solution(mesh):
    in_specs = (
        P(None, "dp", None),
        P("dp", "stream", None),
        P("dp"),
        P("stream", None),
        P("stream", None),
        P(None, "dp", "stream"),
        P("stream", "dp"),
        P("dp", "stream"),
        P("stream", "dp"),
        P("stream", None),
        P(None, "stream", None),
        P("dp", "stream"),
        P("dp", "stream", None),
    )
    out_specs = (
        P("dp", "stream"),
        P("dp", "stream", None),
        P("stream", "dp", None),
        P("dp", "stream", None),
        P("stream", None),
        P("stream", None),
        P(None, "dp", "stream"),
        P("stream", "dp"),
        P("dp", "stream"),
        P("stream", "dp"),
        P("stream", None),
        P(None, "stream", None),
    )
    return jax.shard_map(body, mesh=mesh, in_specs=in_specs, out_specs=out_specs, check_vma=False)
```

```python
import math

import jax
import jax.numpy as jnp
from jax import lax
from jax.experimental import pallas as pl
from jax.experimental.pallas import tpu as pltpu
from jax.sharding import PartitionSpec as P

HD = 128
ROT = 32
SEQ = 2048


def passed_along(shard, axis, by):
    peers = lax.axis_size(axis)
    pairs = [(i, i + by) for i in range(peers) if 0 <= i + by < peers]
    return lax.ppermute(shard, axis, pairs)


def rotate(vectors, positions, sign):
    half = ROT // 2
    counter = jnp.arange(half, dtype=jnp.float32)
    freqs = jnp.exp(counter * (-2.0 * math.log(10000.0) / ROT))
    angles = positions.astype(jnp.float32)[:, None] * freqs[None, :]
    cosine = jnp.cos(angles)[:, None, :]
    sine = sign * jnp.sin(angles)[:, None, :]
    first = vectors[..., :half]
    second = vectors[..., half:ROT]
    return jnp.concatenate(
        [first * cosine - second * sine, second * cosine + first * sine, vectors[..., ROT:]],
        axis=-1,
    )


def exact_gelu(vectors):
    return jax.nn.gelu(vectors, approximate=False)


def block_logits(queries, keys_block, diagonal):
    logits = jnp.einsum("qhd,khd->hqk", queries, keys_block, preferred_element_type=jnp.float32) * (
        1.0 / math.sqrt(queries.shape[-1])
    )
    if diagonal:
        counter = jnp.arange(queries.shape[0], dtype=jnp.int32)
        allowed = counter[None, :] <= counter[:, None]
        logits = jnp.where(allowed[None], logits, -1e30)
    return logits


def keep_same(state):
    return state


BF = jnp.bfloat16
F32 = jnp.float32
OUTWARD = [(0, 1), (3, 2)]
MIDDLE = [(1, 2), (2, 1)]
INWARD = [(1, 0), (2, 3)]


def dot(left, right):
    return jnp.dot(left, right, preferred_element_type=F32)


def dot_rows(left, right):
    return lax.dot_general(left, right, (((0,), (0,)), ((), ())), preferred_element_type=F32)


def dot_cols(left, right):
    return lax.dot_general(left, right, (((1,), (1,)), ((), ())), preferred_element_type=F32)


def partner(shard, bit):
    peers = lax.axis_size("dp")
    return lax.ppermute(shard, "dp", [(i, i ^ bit) for i in range(peers)])


def line_hop(shard, pairs):
    return lax.ppermute(shard, "stream", pairs)


def cost(microseconds):
    return pl.CostEstimate(
        flops=int(microseconds * 0.9e9), bytes_accessed=int(microseconds * 3e6), transcendentals=0
    )


def after(value, *others):
    return lax.optimization_barrier((value, *others))[0]


class Gathered:
    def __init__(self, shard, direct=False):
        self.shard = shard
        self.peers = lax.axis_size("dp")
        if self.peers != 8:
            self.by_x = self.by_y = shard
            return
        self.cut = max(range(shard.ndim - 1), key=lambda dim: shard.shape[dim])
        self.by_x = partner(shard, 2)
        self.by_y = partner(shard, 4)
        self.across = partner(shard, 6) if direct else None

    def whole(self, *earlier):
        shard = self.shard
        if self.peers != 8:
            return lax.all_gather(shard, "dp", axis=0)
        index = lax.axis_index("dp")
        cut = self.cut
        half = shard.shape[cut] // 2
        shard, by_x, by_y = [gated(item, earlier) for item in (shard, self.by_x, self.by_y)]
        pieces = [(shard, 0, 0), (by_x, 2, 0), (by_y, 4, 0)]
        if self.across is None:
            low = lax.slice_in_dim(by_y, 0, half, axis=cut)
            high = lax.slice_in_dim(by_x, half, 2 * half, axis=cut)
            pieces += [(partner(low, 2), 6, 0), (partner(high, 4), 6, half)]
        else:
            pieces.append((gated(self.across, earlier), 6, 0))
        pieces += [(partner(piece, 1), code ^ 1, start) for piece, code, start in pieces]
        return put_together(pieces, shard, self.peers, cut, index)


def put_together(pieces, shard, peers, cut, index):
    codes = [(code, start) for _, code, start in pieces]
    arrays = [piece for piece, _, _ in pieces]

    def kernel(place, *refs):
        out, held, sems, sent = refs[-4:]
        owners = {}
        for n, (code, start) in enumerate(codes):
            size = refs[n].shape[cut]
            span = tuple(
                pl.ds(start, size) if dim == cut else slice(None) for dim in range(shard.ndim)
            )
            copy = pltpu.make_async_copy(refs[n], held.at[(code, *span)], sems.at[n])
            copy.start()
            owners.setdefault(code, []).append(copy)
        leaving = []
        for code, copies in owners.items():
            for copy in copies:
                copy.wait()
            copy = pltpu.make_async_copy(held.at[code], out.at[place[0] ^ code], sent.at[code])
            copy.start()
            leaving.append(copy)
        for copy in leaving:
            copy.wait()

    anywhere = pl.BlockSpec(memory_space=pl.ANY)
    size = peers * shard.size * shard.dtype.itemsize
    return pl.pallas_call(
        kernel,
        in_specs=[pl.BlockSpec(memory_space=pltpu.SMEM)] + [anywhere] * len(arrays),
        out_specs=anywhere,
        out_shape=jax.ShapeDtypeStruct((peers, *shard.shape), shard.dtype),
        scratch_shapes=[
            pltpu.VMEM((peers, *shard.shape), shard.dtype),
            pltpu.SemaphoreType.DMA((len(arrays),)),
            pltpu.SemaphoreType.DMA((peers,)),
        ],
        cost_estimate=cost(2 * size / 3e6),
        name="put_together",
    )(index.astype(jnp.int32).reshape(1), *arrays)


def block_spans(tokens):
    sizes = [tokens // 4] * 3 + [tokens // 8] * 2
    return [(sum(sizes[:i]), size) for i, size in enumerate(sizes)]


def along_line(count, first, second, third, finish=None):
    ones, twos, threes, ends = [], [], [], []
    for step in range(count + 2):
        old = []
        if step >= 4:
            old.append(threes[step - 4] if finish is None else ends[step - 4])
        if step < count:
            gates = list(old)
            if step >= 2:
                gates.append(ones[step - 2])
            if step >= 3:
                gates.append(twos[step - 3])
            ones.append(line_hop(first(step, gates), OUTWARD))
        if 0 <= step - 1 < count:
            load = second(step - 1, ones[step - 1])
            twos.append(line_hop(gated(load, old), MIDDLE))
        if 0 <= step - 2 < count:
            back = step - 2
            load = third(back, ones[back], twos[back])
            threes.append(line_hop(gated(load, old), INWARD))
            if finish is not None:
                ends.append(finish(back, ones[back], twos[back], threes[back]))
    return ones, twos, threes


def sum_along_line(share, count, lag=2):
    tokens, width = share.shape
    block = tokens // count
    member, members = lax.axis_index("stream"), lax.axis_size("stream")
    last = members - 1
    rightward = [(i, i + 1) for i in range(last)]
    leftward = [(i + 1, i) for i in range(last)]

    def kernel(place, *refs):
        del place
        own_right, own_left, from_left, from_right = refs[:4]
        to_right, to_left, kept_right, kept_left = refs[-4:]
        right, left = from_left[...], from_right[...]
        kept_right[0] = right
        kept_left[0] = left
        to_right[...] = (own_right[...] + right.astype(F32)).astype(BF)
        to_left[...] = (own_left[...] + left.astype(F32)).astype(BF)

    def step(t, from_left, from_right, kept):
        numbers = jnp.stack([t - lag * member, t - lag * (last - member)]).astype(jnp.int32)
        valid = (numbers >= 0) & (numbers < count)
        slots = jnp.where(valid, numbers, count)
        places = jnp.concatenate([slots, jnp.minimum(slots, count - 1)])
        plain = pl.BlockSpec((block, width), lambda n, p: (0, 0))
        anywhere = pl.BlockSpec(memory_space=pl.ANY)
        held = jax.ShapeDtypeStruct((count + 1, block, width), BF)
        sent = jax.ShapeDtypeStruct((block, width), BF)
        return pl.pallas_call(
            kernel,
            grid_spec=pltpu.PrefetchScalarGridSpec(
                num_scalar_prefetch=1,
                grid=(1,),
                in_specs=[
                    pl.BlockSpec((block, width), lambda n, p: (p[2], 0)),
                    pl.BlockSpec((block, width), lambda n, p: (p[3], 0)),
                    plain,
                    plain,
                ]
                + [anywhere] * len(kept),
                out_specs=[
                    plain,
                    plain,
                    pl.BlockSpec((1, block, width), lambda n, p: (p[0], 0, 0)),
                    pl.BlockSpec((1, block, width), lambda n, p: (p[1], 0, 0)),
                ],
            ),
            out_shape=[sent, sent, held, held],
            input_output_aliases={5: 2, 6: 3} if kept else {},
            cost_estimate=cost(2),
            name="pass_on",
        )(places, share, share, from_left, from_right, *kept)

    none = jnp.zeros((block, width), BF)
    arrived = [(none, none)] * lag
    kept = []
    for t in range(count + lag * last):
        to_right, to_left, *kept = step(t, *arrived[t], kept)
        if t < count + lag * (last - 1):
            arrived.append((line_hop(to_right, rightward), line_hop(to_left, leftward)))

    def total(own, right, left, out):
        out[...] = (own[...] + right[0].astype(F32) + left[0].astype(F32)).astype(BF)

    row = pl.BlockSpec((block, width), lambda n: (n, 0))
    slot = pl.BlockSpec((1, block, width), lambda n: (n, 0, 0))
    return pl.pallas_call(
        total,
        grid=(count,),
        in_specs=[row, slot, slot],
        out_specs=row,
        out_shape=jax.ShapeDtypeStruct((tokens, width), BF),
        cost_estimate=cost(4),
        name="line_total",
    )(share, *kept)


def gated(value, gates):
    return after(value, *gates) if gates else value


def rope_tables(positions, sign):
    half = ROT // 2
    lane = jnp.arange(HD, dtype=jnp.int32)
    counter = (lane % half).astype(F32)
    freqs = jnp.exp(counter * (-2.0 * math.log(10000.0) / ROT))
    angles = positions.astype(F32)[:, None] * freqs[None, :]
    cosine = jnp.where(lane < ROT, jnp.cos(angles), 1.0)
    sine = sign * jnp.sin(angles)
    up = jnp.where(lane < half, -sine, 0.0)
    down = jnp.where((lane >= half) & (lane < ROT), sine, 0.0)
    return jnp.stack([cosine, up, down])


def turned(block, tables):
    half = ROT // 2
    return (
        block * tables[0]
        + pltpu.roll(block, HD - half, 1) * tables[1]
        + pltpu.roll(block, half, 1) * tables[2]
    )


def make_streams(history, mix_rows, gains, biases):
    entries, tokens, width = history.shape
    streams = gains.shape[0]
    rows, sub, lanes = min(64, tokens), 16, 512

    def kernel(hist, mix, gain, bias, normed, unit, inv, last, scratch):
        def step(r, carry):
            here = pl.ds(pl.multiple_of(r * sub, sub), sub)
            weights = mix[here, :]
            columns = [
                [weights[:, s * entries + j : s * entries + j + 1] for j in range(entries)]
                for s in range(streams)
            ]
            for lane in range(0, width, lanes):
                span = slice(lane, lane + lanes)
                sums = [None] * streams
                for j in range(entries):
                    part = hist[j, here, span].astype(F32)
                    for s in range(streams):
                        term = columns[s][j] * part
                        sums[s] = term if j == 0 else sums[s] + term
                for s in range(streams):
                    scratch[s, :, span] = sums[s]
            stds = []
            for s in range(streams):
                values = scratch[s]
                center = values - jnp.sum(values, axis=-1, keepdims=True) * (1.0 / width)
                var = jnp.sum(center * center, axis=-1, keepdims=True) * (1.0 / width)
                std = lax.rsqrt(var + 1e-05)
                stds.append(std)
                scaled = center * std
                unit[s, here, :] = scaled.astype(BF)
                normed[s, here, :] = (scaled * gain[s : s + 1] + bias[s : s + 1]).astype(BF)
            last[here, :] = scratch[streams - 1]
            inv[here, :] = jnp.concatenate(stds, axis=-1)
            return carry

        lax.fori_loop(0, rows // sub, step, 0)

    wide = jax.ShapeDtypeStruct((streams, tokens, width), BF)
    return pl.pallas_call(
        kernel,
        grid=(tokens // rows,),
        in_specs=[
            pl.BlockSpec((entries, rows, width), lambda i: (0, i, 0)),
            pl.BlockSpec((rows, streams * entries), lambda i: (i, 0)),
            pl.BlockSpec((streams, width), lambda i: (0, 0)),
            pl.BlockSpec((streams, width), lambda i: (0, 0)),
        ],
        out_specs=[
            pl.BlockSpec((streams, rows, width), lambda i: (0, i, 0)),
            pl.BlockSpec((streams, rows, width), lambda i: (0, i, 0)),
            pl.BlockSpec((rows, streams), lambda i: (i, 0)),
            pl.BlockSpec((rows, width), lambda i: (i, 0)),
        ],
        out_shape=[
            wide,
            wide,
            jax.ShapeDtypeStruct((tokens, streams), F32),
            jax.ShapeDtypeStruct((tokens, width), F32),
        ],
        scratch_shapes=[pltpu.VMEM((streams, sub, width), F32)],
        cost_estimate=cost(22),
        name="make_streams",
    )(history, mix_rows, gains, biases)


def project(normed, w_heads, tables):
    _, tokens, width = normed.shape
    columns = w_heads.shape[3]
    heads, half = columns // HD, tokens // 2

    def kernel(x, w, table, out):
        flat = dot(x[0], w[...].reshape(width, columns))
        turn = pl.program_id(0) < 2

        def put(head, block):
            out[2 * head, 0] = block[:half].astype(BF)
            out[2 * head + 1, 0] = block[half:].astype(BF)

        @pl.when(turn)
        def _():
            for head in range(heads):
                put(head, turned(flat[:, head * HD : (head + 1) * HD], table[...]))

        @pl.when(jnp.logical_not(turn))
        def _():
            for head in range(heads):
                put(head, flat[:, head * HD : (head + 1) * HD])

    return pl.pallas_call(
        kernel,
        grid=(3,),
        in_specs=[
            pl.BlockSpec((1, tokens, width), lambda c: (c, 0, 0)),
            pl.BlockSpec((w_heads.shape[0], 1, w_heads.shape[2], columns), lambda c: (0, c, 0, 0)),
            pl.BlockSpec((3, tokens, HD), lambda c: (0, 0, 0)),
        ],
        out_specs=pl.BlockSpec((2 * heads, 1, half, HD), lambda c: (0, c, 0, 0)),
        out_shape=jax.ShapeDtypeStruct((2 * heads, 3, half, HD), BF),
        cost_estimate=cost(9),
        name="project",
    )(normed, w_heads, tables)


def attend(own, other, first_key, side):
    shards, _, half, _ = own.shape
    factor = 1.0 / math.sqrt(HD)

    def kernel(first, part, mine, theirs, out, exact, norm):
        s = pl.program_id(0)
        query = mine[s, 0]

        def fold(state, keys, values, mask):
            top, total, acc = state
            logits = dot_cols(query, keys) * factor
            if mask is not None:
                logits = jnp.where(mask, logits, -1e30)
            new_top = jnp.maximum(top, jnp.max(logits, axis=-1, keepdims=True))
            probs = jnp.exp(logits - new_top)
            keep = jnp.exp(top - new_top)
            return (
                new_top,
                total * keep + jnp.sum(probs, axis=-1, keepdims=True),
                acc * keep + dot(probs.astype(BF), values),
            )

        row = lax.broadcasted_iota(jnp.int32, (half, half), 0)
        col = lax.broadcasted_iota(jnp.int32, (half, half), 1)
        state = (
            jnp.full((half, 1), -1e30, F32),
            jnp.zeros((half, 1), F32),
            jnp.zeros((half, HD), F32),
        )
        state = fold(state, mine[s, 1], mine[s, 2], col <= row)
        state = lax.fori_loop(
            0, part[0], lambda i, st: fold(st, theirs[s, 0], theirs[s, 1], None), state
        )

        def shard_step(b, st):
            st = fold(st, mine[b, 1], mine[b, 2], None)
            return fold(st, theirs[b, 0], theirs[b, 1], None)

        top, total, acc = lax.fori_loop(first[s], s, shard_step, state)
        result = acc / total
        out[0] = result.astype(BF)
        exact[0] = result
        norm[0] = top + jnp.log(total)

    return pl.pallas_call(
        kernel,
        grid_spec=pltpu.PrefetchScalarGridSpec(
            num_scalar_prefetch=2,
            grid=(shards,),
            in_specs=[
                pl.BlockSpec((shards, 3, half, HD), lambda s, *_: (0, 0, 0, 0)),
                pl.BlockSpec((shards, 2, half, HD), lambda s, *_: (0, 0, 0, 0)),
            ],
            out_specs=[
                pl.BlockSpec((1, half, HD), lambda s, *_: (s, 0, 0)),
                pl.BlockSpec((1, half, HD), lambda s, *_: (s, 0, 0)),
                pl.BlockSpec((1, half, 1), lambda s, *_: (s, 0, 0)),
            ],
        ),
        out_shape=[
            jax.ShapeDtypeStruct((shards, half, HD), BF),
            jax.ShapeDtypeStruct((shards, half, HD), F32),
            jax.ShapeDtypeStruct((shards, half, 1), F32),
        ],
        cost_estimate=cost(16),
        name="attend",
    )(first_key, side, own, other)


def attend_back(own, other, grads, exact, norm, first_key, side):
    shards, _, half, _ = own.shape
    factor = 1.0 / math.sqrt(HD)

    def kernel(first, part, mine, theirs, grad_ref, exact_ref, norm_ref, kept, given, sums):
        s = pl.program_id(0)
        query = mine[s, 0]
        grad = grad_ref[s]
        delta = jnp.sum(grad.astype(F32) * exact_ref[0], axis=-1, keepdims=True)
        level = norm_ref[0]
        lowered = grad

        @pl.when(s == 0)
        def _():
            sums[...] = jnp.zeros_like(sums)

        def fold(query_grad, keys, values, mask, slot, b):
            logits = dot_cols(query, keys) * factor
            probs = jnp.exp(logits - level)
            if mask is not None:
                probs = jnp.where(mask, probs, 0.0)
            score = (probs * (dot_cols(grad, values) - delta)).astype(BF)
            sums[slot, b] += dot_rows(score, query)
            sums[slot + 1, b] += dot_rows(probs.astype(BF), lowered)
            return query_grad + dot(score, keys)

        row = lax.broadcasted_iota(jnp.int32, (half, half), 0)
        col = lax.broadcasted_iota(jnp.int32, (half, half), 1)
        total = fold(jnp.zeros((half, HD), F32), mine[s, 1], mine[s, 2], col <= row, 0, s)
        total = lax.fori_loop(
            0, part[0], lambda i, q: fold(q, theirs[s, 0], theirs[s, 1], None, 2, s), total
        )

        def shard_step(b, q):
            q = fold(q, mine[b, 1], mine[b, 2], None, 0, b)
            return fold(q, theirs[b, 0], theirs[b, 1], None, 2, b)

        total = lax.fori_loop(first[s], s, shard_step, total)
        kept[s, 0] = (total * factor).astype(BF)

        @pl.when(s == shards - 1)
        def _():
            for b in range(shards):
                kept[b, 1] = (sums[0, b] * factor).astype(BF)
                kept[b, 2] = sums[1, b].astype(BF)
                given[b, 0] = (sums[2, b] * factor).astype(BF)
                given[b, 1] = sums[3, b].astype(BF)

    whole = lambda n: pl.BlockSpec((shards, n, half, HD), lambda s, *_: (0, 0, 0, 0))
    return pl.pallas_call(
        kernel,
        grid_spec=pltpu.PrefetchScalarGridSpec(
            num_scalar_prefetch=2,
            grid=(shards,),
            in_specs=[
                whole(3),
                whole(2),
                pl.BlockSpec((shards, half, HD), lambda s, *_: (0, 0, 0)),
                pl.BlockSpec((1, half, HD), lambda s, *_: (s, 0, 0)),
                pl.BlockSpec((1, half, 1), lambda s, *_: (s, 0, 0)),
            ],
            out_specs=[whole(3), whole(2)],
            scratch_shapes=[pltpu.VMEM((4, shards, half, HD), F32)],
        ),
        out_shape=[
            jax.ShapeDtypeStruct((shards, 3, half, HD), BF),
            jax.ShapeDtypeStruct((shards, 2, half, HD), BF),
        ],
        cost_estimate=cost(22),
        name="attend_back",
    )(first_key, side, own, other, grads, exact, norm)


def norm_back(grad, unit, inv, gain, extra):
    width = grad.shape[1]
    scaled = grad * gain
    mean = jnp.sum(scaled, axis=-1, keepdims=True) * (1.0 / width)
    slope = jnp.sum(scaled * unit, axis=-1, keepdims=True) * (1.0 / width)
    result = inv * (scaled - mean - unit * slope)
    return result if extra is None else result + extra


def heads_back(parts, w_heads, normed, unit, inv, gains, tables, spans):
    _, tokens, width = normed.shape
    columns = w_heads.shape[3]
    heads, half = columns // HD, tokens // 2
    count = len(spans)

    def kernel(part, w, x, u, istd, gain, table, *refs):
        pieces, (stream, weight, stats, grad, wide) = refs[:count], refs[count:]
        c = pl.program_id(0)
        turn = c < 2

        def take(head):
            return jnp.concatenate([part[2 * head, 0], part[2 * head + 1, 0]], axis=0).astype(F32)

        @pl.when(turn)
        def _():
            for head in range(heads):
                grad[:, head * HD : (head + 1) * HD] = turned(take(head), table[...]).astype(BF)

        @pl.when(jnp.logical_not(turn))
        def _():
            for head in range(heads):
                grad[:, head * HD : (head + 1) * HD] = take(head).astype(BF)

        wide[...] = dot_cols(grad[...], w[...].reshape(width, columns))
        weight[0] = dot_rows(x[0], grad[...]).astype(BF)
        stats[...] = jnp.zeros_like(stats)
        for r, (start, block) in enumerate(spans):
            column = lax.broadcasted_iota(jnp.int32, (block, istd.shape[1]), 1)
            here = slice(start, start + block)
            values = wide[here, :]
            units = u[0, here, :].astype(F32)
            std = jnp.sum(jnp.where(column == c, istd[here, :], 0.0), axis=-1, keepdims=True)
            result = norm_back(values, units, std, gain[0], None).astype(BF)
            stream[0, here, :] = result
            pieces[r][0] = result
            stats[0, 0:1] += jnp.sum(values * units, axis=0, keepdims=True)
            stats[0, 1:2] += jnp.sum(values, axis=0, keepdims=True)

    return pl.pallas_call(
        kernel,
        grid=(3,),
        in_specs=[
            pl.BlockSpec((2 * heads, 1, half, HD), lambda c: (0, c, 0, 0)),
            pl.BlockSpec((w_heads.shape[0], 1, w_heads.shape[2], columns), lambda c: (0, c, 0, 0)),
            pl.BlockSpec((1, tokens, width), lambda c: (c, 0, 0)),
            pl.BlockSpec((1, tokens, width), lambda c: (c, 0, 0)),
            pl.BlockSpec((tokens, inv.shape[1]), lambda c: (0, 0)),
            pl.BlockSpec((1, 1, width), lambda c: (c, 0, 0)),
            pl.BlockSpec((3, tokens, HD), lambda c: (0, 0, 0)),
        ],
        out_specs=[pl.BlockSpec((1, block, width), lambda c: (c, 0, 0)) for _, block in spans]
        + [
            pl.BlockSpec((1, tokens, width), lambda c: (c, 0, 0)),
            pl.BlockSpec((1, width, columns), lambda c: (c, 0, 0)),
            pl.BlockSpec((1, 2, width), lambda c: (c, 0, 0)),
        ],
        out_shape=[jax.ShapeDtypeStruct((3, block, width), BF) for _, block in spans]
        + [
            jax.ShapeDtypeStruct((3, tokens, width), BF),
            jax.ShapeDtypeStruct((3, width, columns), BF),
            jax.ShapeDtypeStruct((3, 2, width), F32),
        ],
        scratch_shapes=[pltpu.VMEM((tokens, columns), BF), pltpu.VMEM((tokens, width), F32)],
        cost_estimate=cost(18),
        name="heads_back",
    )(parts, w_heads, normed, unit, inv, gains[:, None, :], tables)


def last_back(grad, unit, inv, gain, extra, flag):
    tokens, width = grad.shape
    block = min(128, tokens)

    def kernel(g, u, istd, gain_ref, e, flag_ref, stream, stats):
        @pl.when(pl.program_id(0) == 0)
        def _():
            stats[...] = jnp.zeros_like(stats)

        values = g[...]
        units = u[...].astype(F32)
        std = istd[...][:, -1:]
        added = e[...].astype(F32) * flag_ref[0]
        stream[...] = norm_back(values, units, std, gain_ref[...], added).astype(BF)
        stats[0:1] += jnp.sum(values * units, axis=0, keepdims=True)
        stats[1:2] += jnp.sum(values, axis=0, keepdims=True)

    row = lambda n: pl.BlockSpec((block, n), lambda i: (i, 0))
    return pl.pallas_call(
        kernel,
        grid=(tokens // block,),
        in_specs=[
            row(width),
            row(width),
            row(inv.shape[1]),
            pl.BlockSpec((1, width), lambda i: (0, 0)),
            row(width),
            pl.BlockSpec(memory_space=pltpu.SMEM),
        ],
        out_specs=[row(width), pl.BlockSpec((2, width), lambda i: (0, 0))],
        out_shape=[
            jax.ShapeDtypeStruct((tokens, width), BF),
            jax.ShapeDtypeStruct((2, width), F32),
        ],
        cost_estimate=cost(7),
        name="last_back",
    )(grad, unit, inv, gain, extra, flag)


def mixing_back(heads_part, last_part, history, which, of):
    entries, tokens, width = history.shape
    streams = heads_part.shape[0] + 1
    rows, sub, lanes = min(64, tokens // of), 16, 256
    steps = tokens // of // rows
    base = which * steps

    def kernel(first, last, hist, out):
        def step(r, carry):
            here = pl.ds(pl.multiple_of(r * sub, sub), sub)
            for s in range(streams):
                sums = [None] * entries
                for lane in range(0, width, lanes):
                    span = slice(lane, lane + lanes)
                    part = first[s, here, span] if s < streams - 1 else last[here, span]
                    part = part.astype(F32)
                    for j in range(entries):
                        term = part * hist[j, here, span].astype(F32)
                        sums[j] = term if lane == 0 else sums[j] + term
                columns = [jnp.sum(item, axis=-1, keepdims=True) for item in sums]
                out[s, here, :] = jnp.concatenate(columns, axis=-1)
            return carry

        lax.fori_loop(0, rows // sub, step, 0)

    return pl.pallas_call(
        kernel,
        grid=(steps,),
        in_specs=[
            pl.BlockSpec((streams - 1, rows, width), lambda i: (0, base + i, 0)),
            pl.BlockSpec((rows, width), lambda i: (base + i, 0)),
            pl.BlockSpec((entries, rows, width), lambda i: (0, base + i, 0)),
        ],
        out_specs=pl.BlockSpec((streams, rows, entries), lambda i: (0, i, 0)),
        out_shape=jax.ShapeDtypeStruct((streams, tokens // of, entries), F32),
        cost_estimate=cost(18 / of),
        name="mixing_back",
    )(heads_part, last_part, history)


def far_attend(queries, keys, values, shard_offset):
    tokens, heads_here, head_size = queries.shape
    data_index = lax.axis_index("dp")
    pairs = [jnp.stack([keys, values])]
    reach = 2 * SEQ // tokens
    for back in range(1, reach):
        pairs.append(passed_along(pairs[0], "dp", back))
    usable = [(shard_offset[0] >= back * tokens) & (data_index >= back) for back in range(reach)]
    first_logits = block_logits(queries, keys, True)
    top = jnp.max(first_logits, axis=-1)
    total = jnp.sum(jnp.exp(first_logits - top[..., None]), axis=-1)
    for back in range(1, reach):

        def widen(state, block=pairs[back][0]):
            logits = block_logits(queries, block, False)
            new_top = jnp.maximum(state[0], jnp.max(logits, axis=-1))
            summed = state[1] * jnp.exp(state[0] - new_top) + jnp.sum(
                jnp.exp(logits - new_top[..., None]), axis=-1
            )
            return (new_top, summed)

        top, total = lax.cond(usable[back], widen, keep_same, (top, total))
    log_total = top + jnp.log(total)
    attended = jnp.zeros((tokens, heads_here, head_size), F32)
    for back in range(reach):

        def accumulate(current, block=pairs[back], diagonal=back == 0):
            probs = jnp.exp(block_logits(queries, block[0], diagonal) - log_total[..., None])
            return current + jnp.einsum(
                "hqk,khd->qhd", probs.astype(BF), block[1], preferred_element_type=F32
            )

        attended = lax.cond(usable[back], accumulate, keep_same, attended)
    return attended, (pairs, usable, log_total)


def far_attend_back(queries, attended_grad, kept):
    tokens, heads_here, head_size = queries.shape
    factor = 1.0 / math.sqrt(head_size)
    pairs, usable, log_total = kept
    reach = len(pairs)

    def weights_of(block, diagonal):
        return jnp.exp(block_logits(queries, block, diagonal) - log_total[..., None])

    def prob_grads(block):
        return jnp.einsum("qhd,khd->hqk", attended_grad, block[1], preferred_element_type=F32)

    delta = jnp.zeros((heads_here, tokens), F32)
    for back in range(reach):

        def gather_delta(current, block=pairs[back], diagonal=back == 0):
            return current + jnp.sum(weights_of(block[0], diagonal) * prob_grads(block), axis=-1)

        delta = lax.cond(usable[back], gather_delta, keep_same, delta)

    def skip_block(current):
        return (current, jnp.zeros((2, tokens, heads_here, head_size), F32))

    query_grad = jnp.zeros((tokens, heads_here, head_size), F32)
    key_value_grad = jnp.zeros((2, tokens, heads_here, head_size), F32)
    for back in range(reach):

        def spread(current, block=pairs[back], diagonal=back == 0):
            probs = weights_of(block[0], diagonal)
            score_grad = (probs * (prob_grads(block) - delta[..., None])).astype(BF)
            query_part = (
                current
                + jnp.einsum("hqk,khd->qhd", score_grad, block[0], preferred_element_type=F32)
                * factor
            )
            key_part = (
                jnp.einsum("hqk,qhd->khd", score_grad, queries, preferred_element_type=F32)
                * factor
            )
            value_part = jnp.einsum(
                "hqk,qhd->khd", probs.astype(BF), attended_grad, preferred_element_type=F32
            )
            return (query_part, jnp.stack([key_part, value_part]))

        query_grad, pair_grad = lax.cond(usable[back], spread, skip_block, query_grad)
        if back == 0:
            key_value_grad = pair_grad
        else:
            key_value_grad = key_value_grad + passed_along(pair_grad, "dp", -back)
    return jnp.concatenate([query_grad[None], key_value_grad])


def mix_block(start, coefficients, shares, last_share, extras, last_extras, arrived, whole):
    streams, block, width = shares.shape
    each = coefficients.shape[1] // (streams + 1)
    groups = 1 + len(extras)
    final = arrived is not None
    lanes = 512

    def kernel(*refs):
        weights = refs[0][...]
        heads, lasts = refs[1 : 1 + groups], refs[1 + groups : 1 + 2 * groups]
        out = refs[-2] if final else refs[-1]
        if final:
            refs[-1][...] = jnp.zeros_like(refs[-1])
        columns = [weights[:, n : n + 1] for n in range(weights.shape[1])]
        for lane in range(0, width, lanes):
            span = slice(lane, lane + lanes)
            values = []
            for s in range(streams + 1):
                picks = [r[s, :, span] if s < streams else l[:, span] for r, l in zip(heads, lasts)]
                total = picks[0].astype(F32)
                for pick in picks[1:]:
                    total = total + pick.astype(F32)
                values.append(total)
            for e in range(each):
                total = columns[e * (streams + 1)] * values[0]
                for s in range(1, streams + 1):
                    total = total + columns[e * (streams + 1) + s] * values[s]
                if final:
                    total = total + refs[1 + 2 * groups][e, :, span].astype(F32)
                out[e, :, span] = total.astype(out.dtype)

    i = start // block
    piece = pl.BlockSpec((streams, block, width), lambda n: (0, 0, 0))
    rows = [
        pl.BlockSpec((block, width), lambda n, at=start % item.shape[0] // block: (at, 0))
        for item in (last_share, *last_extras)
    ]
    small = pl.BlockSpec((each, block, width), lambda n: (0, 0, 0))
    specs = [pl.BlockSpec((block, coefficients.shape[1]), lambda n: (i, 0))]
    specs += [piece] * groups + rows
    args = [coefficients, shares, *extras, last_share, *last_extras]
    alias = {}
    if final:
        specs.append(small)
        args.append(arrived)
        if whole is not None:
            specs.append(pl.BlockSpec(memory_space=pl.ANY))
            args.append(whole)
            alias = {len(args) - 1: 0}
        out_spec = [
            pl.BlockSpec((each, block, width), lambda n: (0, i, 0)),
            pl.BlockSpec((8, 128), lambda n: (0, 0)),
        ]
        out_shape = [
            jax.ShapeDtypeStruct((each, coefficients.shape[0], width), F32),
            jax.ShapeDtypeStruct((8, 128), F32),
        ]
    else:
        out_spec, out_shape = small, jax.ShapeDtypeStruct((each, block, width), BF)
    return pl.pallas_call(
        kernel,
        grid=(1,),
        in_specs=specs,
        out_specs=out_spec,
        out_shape=out_shape,
        input_output_aliases=alias,
        cost_estimate=cost(4 if final else 3),
        name="mix_final" if final else "mix_inward",
    )(*args)


def hidden_units(x, w_up):
    tokens, width = x.shape
    units = w_up.shape[1]
    block = min(512, units)

    def kernel(x_ref, w, out, slope):
        up = dot(x_ref[...], w[...])
        inside = 0.5 * (1.0 + lax.erf(up * math.sqrt(0.5)))
        out[...] = (up * inside).astype(BF)
        bell = jnp.exp(-0.5 * up * up) * (1.0 / math.sqrt(2.0 * math.pi))
        slope[...] = (inside + up * bell).astype(BF)

    column = pl.BlockSpec((tokens, block), lambda i: (0, i))
    return pl.pallas_call(
        kernel,
        grid=(units // block,),
        in_specs=[
            pl.BlockSpec((tokens, width), lambda i: (0, 0)),
            pl.BlockSpec((width, block), lambda i: (0, i)),
        ],
        out_specs=[column, column],
        out_shape=[jax.ShapeDtypeStruct((tokens, units), BF)] * 2,
        cost_estimate=cost(9),
        name="hidden_units",
    )(x, w_up)


def merge_branches(attended, hidden, w_merge, w_down, stream, flag):
    tokens, inner = attended.shape
    shards, units, cols = w_down.shape
    if cols % 128:
        merged = jnp.einsum("te,ned->tnd", attended, w_merge, preferred_element_type=F32)
        merged = merged + jnp.einsum("tf,nfd->tnd", hidden, w_down, preferred_element_type=F32)
        return merged.reshape(tokens, -1) + flag * stream

    def kernel(a, h, wm, wd, st, flag_ref, out):
        out[...] = dot(a[...], wm[0]) + dot(h[...], wd[0]) + flag_ref[0] * st[...]

    return pl.pallas_call(
        kernel,
        grid=(shards,),
        in_specs=[
            pl.BlockSpec((tokens, inner), lambda n: (0, 0)),
            pl.BlockSpec((tokens, units), lambda n: (0, 0)),
            pl.BlockSpec((1, inner, cols), lambda n: (n, 0, 0)),
            pl.BlockSpec((1, units, cols), lambda n: (n, 0, 0)),
            pl.BlockSpec((tokens, cols), lambda n: (0, n)),
            pl.BlockSpec(memory_space=pltpu.SMEM),
        ],
        out_specs=pl.BlockSpec((tokens, cols), lambda n: (0, n)),
        out_shape=jax.ShapeDtypeStruct((tokens, shards * cols), F32),
        cost_estimate=cost(13),
        name="merge_branches",
    )(attended, hidden, w_merge, w_down, stream, flag)


def back_through(grad, stacked, slope):
    tokens = grad.shape[0]
    shards, units, cols = stacked.shape
    if cols % 128:
        split = grad.reshape(tokens, shards, cols)
        total = jnp.einsum("tnd,nfd->tf", split, stacked, preferred_element_type=F32)
        return (total if slope is None else total * slope.astype(F32)).astype(BF)

    def kernel(*refs):
        g, w = refs[:2]
        out, acc = refs[-2:]
        n = pl.program_id(0)
        part = dot_cols(g[...], w[0])

        @pl.when(n == 0)
        def _():
            acc[...] = part

        @pl.when(n > 0)
        def _():
            acc[...] += part

        @pl.when(n == shards - 1)
        def _():
            total = acc[...]
            if slope is not None:
                total = total * refs[2][...].astype(F32)
            out[...] = total.astype(BF)

    specs = [
        pl.BlockSpec((tokens, cols), lambda n: (0, n)),
        pl.BlockSpec((1, units, cols), lambda n: (n, 0, 0)),
    ]
    args = [grad, stacked]
    if slope is not None:
        specs.append(pl.BlockSpec((tokens, units), lambda n: (0, 0)))
        args.append(slope)
    return pl.pallas_call(
        kernel,
        grid=(shards,),
        in_specs=specs,
        out_specs=pl.BlockSpec((tokens, units), lambda n: (0, 0)),
        out_shape=jax.ShapeDtypeStruct((tokens, units), BF),
        scratch_shapes=[pltpu.VMEM((tokens, units), F32)],
        cost_estimate=cost(13 if slope is not None else 7),
        name="back_through",
    )(*args)


def body(
    history,
    mixing,
    shard_offset,
    norm_gain,
    norm_bias,
    w_heads,
    w_merge,
    w_up,
    w_down,
    mixer_first,
    mixer_second,
    out_cotangent,
    next_cotangent,
):
    member = lax.axis_index("stream")
    members = lax.axis_size("stream")
    shards = lax.axis_size("dp")
    index = lax.axis_index("dp")
    entries, tokens, width = history.shape
    heads_here = w_heads.shape[2] // HD
    half = tokens // 2
    highest = lax.Precision.HIGHEST
    flag = (member == members - 1).astype(F32)
    flags = flag.reshape(1)
    near = shards == 8 and heads_here * 2 == shards and tokens * shards == 2 * SEQ

    if near:
        spread = jnp.broadcast_to(shard_offset[:, None], (8, 128))
        offsets = lax.all_gather(spread, "dp", axis=0)[:, 0, 0]
        w_heads = after(w_heads, offsets)
    got_heads = Gathered(w_heads, direct=near)
    cotangent = lax.all_gather(out_cotangent, "stream", axis=1, tiled=True)
    lanes = jnp.concatenate([norm_gain, norm_bias]).astype(F32).reshape(tokens, -1)
    first_rows = mixer_first.astype(F32).reshape(tokens, -1)
    second_flat = mixer_second[:, 0, :].astype(F32).reshape(-1)
    hidden_count = mixer_second.shape[0]
    lines = -(-second_flat.shape[0] // tokens)
    second_rows = jnp.pad(second_flat, (0, lines * tokens - second_flat.shape[0]))
    outputs = next_cotangent.shape[2]
    arrays = [mixing[:, 0, :], lanes, next_cotangent[:, 0, :], first_rows]
    arrays.append(second_rows.reshape(tokens, lines))
    packed = lax.all_gather(jnp.concatenate(arrays, axis=1), "stream", axis=0)
    parts, place = [], 0
    for array in arrays:
        parts.append(packed[:, :, place : place + array.shape[1]])
        place += array.shape[1]
    mix_all, norms, next_full, first_full, second_full = parts
    norms = norms.reshape(members, 2, width)
    first_full = first_full.astype(BF).reshape(width, -1)
    second_full = second_full.reshape(members, -1)[:, : second_flat.shape[0]]
    second_full = second_full.reshape(members, hidden_count, outputs)
    if near:
        early = (got_heads.by_x, got_heads.by_y, got_heads.across)
        history = after(history, *early)
        w_up, w_merge = after(w_up, *early[:2]), after(w_merge, *early[:2])
    got_up = Gathered(w_up)
    got_merge = Gathered(w_merge, direct=near)
    gains, biases = norms[:, 0], norms[:, 1]
    mix_rows = jnp.transpose(mix_all, (1, 0, 2)).reshape(tokens, members * entries)

    normed, unit, inv, stream = make_streams(history, mix_rows, gains, biases)
    full_heads = got_heads.whole()
    positions = shard_offset[0] + jnp.arange(tokens, dtype=jnp.int32)
    projected = project(after(normed, got_up.by_x, got_up.by_y), full_heads, rope_tables(positions, 1.0))

    if near:
        side = (index % 2).astype(jnp.int32).reshape(1)
        place = jnp.arange(shards, dtype=jnp.int32)
        first_key = jnp.maximum(place - offsets // tokens, 0).astype(jnp.int32)
        own = lax.all_to_all(projected, "dp", 0, 0, tiled=True)
        got_down = Gathered(after(w_down, own))
        other = partner(own[:, 1:], 1)
        full_up = got_up.whole(normed)
        full_merge = got_merge.whole(own)
        own = after(own, cotangent)
        result, exact, level = attend(own, other, first_key, side)
        back = lax.all_to_all(result, "dp", 0, 0, tiled=True)
        attended = jnp.transpose(back.reshape(heads_here, tokens, HD), (1, 0, 2)).reshape(tokens, -1)
    else:
        got_down = Gathered(w_down)
        full_up = got_up.whole()
        full_merge = got_merge.whole()
        split = projected.reshape(heads_here, 2, 3, half, HD)
        split = jnp.transpose(split, (2, 1, 3, 0, 4)).reshape(3, tokens, heads_here, HD)
        result, kept = far_attend(split[0], split[1], split[2], shard_offset)
        attended = result.reshape(tokens, -1).astype(BF)
    full_down = got_down.whole(result)
    flat_up = full_up.reshape(width, -1)
    hidden, slope = hidden_units(normed[members - 1], flat_up)
    attended = after(attended, hidden)
    share = merge_branches(attended, hidden, full_merge, full_down, stream, flags)

    block_full = sum_along_line(share, 8)

    mine = member * (width // members)
    block_out = lax.dynamic_slice_in_dim(block_full, mine, width // members, axis=1)
    out_float = block_full.astype(F32)
    scale = lax.rsqrt(jnp.sum(out_float * out_float, axis=-1) / width + 1e-06)
    proj = dot(block_full, first_full)
    mixer, mixer_back = jax.vjp(exact_gelu, scale[:, None] * proj)
    second_here = mixer_second[:, 0, :].astype(F32)
    next_here = jnp.dot(mixer, second_here, precision=highest, preferred_element_type=F32)
    mixer_grad = jnp.einsum(
        "stn,scn->tc", next_full, second_full, precision=highest, preferred_element_type=F32
    )
    pre_grad = mixer_back(mixer_grad)[0]
    proj_grad = (scale[:, None] * pre_grad).astype(BF)
    scale_grad = jnp.sum(pre_grad * proj, axis=-1)
    second_local = jnp.dot(
        mixer.T, next_cotangent[:, 0, :], precision=highest, preferred_element_type=F32
    )
    first_local = dot_rows(block_out, proj_grad)
    grad_out = (
        cotangent.astype(F32)
        + dot_cols(proj_grad, first_full)
        - (scale * scale * scale * scale_grad)[:, None] * out_float / width
    ).astype(BF)

    attended_grad = back_through(grad_out, full_merge, None)
    up_grad = back_through(grad_out, full_down, slope)
    down_grad = dot_rows(hidden, grad_out).astype(BF)
    last_normed = dot_cols(after(up_grad, down_grad), flat_up)
    last_share, last_stats = last_back(
        last_normed, unit[members - 1], inv, gains[members - 1 :], grad_out, flags
    )
    halves = [last_share[:half], last_share[half:]]
    first_halves = [line_hop(item, OUTWARD) for item in halves]
    sums = [(a.astype(F32) + b.astype(F32)).astype(BF) for a, b in zip(halves, first_halves)]
    second_halves = [line_hop(item, MIDDLE) for item in sums]
    if near:
        sent = attended_grad.reshape(tokens, heads_here, HD)
        sent = jnp.transpose(sent, (1, 0, 2)).reshape(shards, half, HD)
        grads = lax.all_to_all(sent, "dp", 0, 0, tiled=True)
        grads = after(grads, last_share)
        kept_grads, given = attend_back(own, other, grads, exact, level, first_key, side)
        taken = partner(given, 1)
        summed = kept_grads[:, 1:].astype(F32) + taken.astype(F32)
        pair = jnp.concatenate([kept_grads[:, :1], summed.astype(BF)], axis=1)
        pair = after(pair, first_halves[0])
        parts = lax.all_to_all(pair, "dp", 0, 0, tiled=True)
        late_grad, late_up = after(grad_out, pair), after(up_grad, pair)
    else:
        late_grad, late_up = grad_out, up_grad
        grads = far_attend_back(split[0], attended_grad.reshape(tokens, heads_here, HD), kept)
        parts = grads.reshape(3, 2, half, heads_here, HD)
        parts = jnp.transpose(parts, (3, 1, 0, 2, 4)).reshape(2 * heads_here, 3, half, HD)

    up_back = dot_rows(normed[members - 1], late_up).astype(BF)
    merge_grad = dot_rows(attended, late_grad).astype(BF)
    parts = after(parts, up_back, merge_grad, *second_halves)
    spans = block_spans(tokens)
    *pieces, heads_share, heads_grad, heads_stats = heads_back(
        parts, full_heads, normed, unit, inv, gains, rope_tables(positions, -1.0), spans
    )

    grad_merge = lax.psum_scatter(merge_grad, "dp", scatter_dimension=1, tiled=True).astype(F32)
    grad_down = lax.psum_scatter(down_grad, "dp", scatter_dimension=1, tiled=True).astype(F32)
    grad_heads = lax.psum_scatter(heads_grad, "dp", scatter_dimension=1, tiled=True).astype(F32)
    grad_up = lax.psum_scatter(up_back, "dp", scatter_dimension=0, tiled=True).astype(F32)

    each = entries // members

    def weights_for(owner):
        block = lax.dynamic_slice_in_dim(mix_all, owner * each, each, axis=2)
        return jnp.transpose(block, (1, 2, 0)).reshape(tokens, each * members)

    there = weights_for(jnp.where(member == 1, 0, members - 1))
    here = weights_for(member)
    extra = {}

    last_one = lambda i: first_halves[spans[i][0] // half]
    last_two = lambda i: second_halves[spans[i][0] // half]

    def first_hop(i, gates):
        gates = list(gates)
        if i == 1:
            gates.append(grad_down)
        if i == 3:
            gates.append(grad_merge)
        return gated(pieces[i], gates)

    def small_sums():
        stats = jnp.concatenate([heads_stats, last_stats[None]]).reshape(members, tokens, -1)
        both = jnp.concatenate([jnp.concatenate(mixes, axis=1), stats], axis=2)
        both = jnp.sum(lax.all_to_all(both, "stream", 0, 0, tiled=True), axis=0)
        second_sums = jnp.pad(second_local.reshape(-1), (0, lines * tokens - second_flat.shape[0]))
        local = [both[:, entries:], first_local.reshape(tokens, -1), second_sums.reshape(tokens, lines)]
        everyone = lax.all_gather(jnp.concatenate(local, axis=1), "dp", axis=0)
        return both[:, :entries], jnp.sum(everyone, axis=0)

    mixes = []

    def second_hop(i, one):
        return (pieces[i].astype(F32) + one.astype(F32)).astype(BF)

    def third_hop(i, one, two):
        return mix_block(spans[i][0], there, pieces[i], last_share, [two], [last_two(i)], None, None)

    def finish(i, one, two, three):
        if i in (0, 1):
            mixes.append(mixing_back(heads_share, last_share, after(history, two), i, 2))
        if i == 1:
            extra["both"], extra["all"] = small_sums()
        if i == 3:
            three = after(three, extra["both"], grad_heads)
        if i == 4:
            three = after(three, extra["all"])
        extra["history"], token = mix_block(
            spans[i][0],
            here,
            pieces[i],
            last_share,
            [one, two],
            [last_one(i), last_two(i)],
            three,
            extra.get("history"),
        )
        return token

    along_line(len(spans), first_hop, second_hop, third_hop, finish)
    grad_history = extra["history"]

    grad_mixing = extra["both"][:, None, :]
    sums = extra["all"]
    columns = 2 * width // tokens
    stats = sums[:, :columns].reshape(2, width)
    grad_first = sums[:, columns:-lines].reshape(mixer_first.shape)
    grad_second = sums[:, -lines:].reshape(-1)[: second_flat.shape[0]].reshape(hidden_count, outputs)
    return (
        block_out,
        next_here[:, None, :],
        grad_history,
        grad_mixing,
        stats[:1],
        stats[1:],
        grad_heads,
        grad_merge,
        grad_up,
        grad_down,
        grad_first,
        grad_second[:, None, :],
    )


def solution(mesh):
    in_specs = (
        P(None, "dp", None),
        P("dp", "stream", None),
        P("dp"),
        P("stream", None),
        P("stream", None),
        P(None, "dp", "stream"),
        P("stream", "dp"),
        P("dp", "stream"),
        P("stream", "dp"),
        P("stream", None),
        P(None, "stream", None),
        P("dp", "stream"),
        P("dp", "stream", None),
    )
    out_specs = (
        P("dp", "stream"),
        P("dp", "stream", None),
        P("stream", "dp", None),
        P("dp", "stream", None),
        P("stream", None),
        P("stream", None),
        P(None, "dp", "stream"),
        P("stream", "dp"),
        P("dp", "stream"),
        P("stream", "dp"),
        P("stream", None),
        P(None, "stream", None),
    )
    return jax.shard_map(body, mesh=mesh, in_specs=in_specs, out_specs=out_specs, check_vma=False)
```

```python
import math

import jax
import jax.numpy as jnp
from jax import lax
from jax.experimental import pallas as pl
from jax.experimental.pallas import tpu as pltpu
from jax.sharding import PartitionSpec as P

HD = 128
ROT = 32
SEQ = 2048


def passed_along(shard, axis, by):
    peers = lax.axis_size(axis)
    pairs = [(i, i + by) for i in range(peers) if 0 <= i + by < peers]
    return lax.ppermute(shard, axis, pairs)


def rotate(vectors, positions, sign):
    half = ROT // 2
    counter = jnp.arange(half, dtype=jnp.float32)
    freqs = jnp.exp(counter * (-2.0 * math.log(10000.0) / ROT))
    angles = positions.astype(jnp.float32)[:, None] * freqs[None, :]
    cosine = jnp.cos(angles)[:, None, :]
    sine = sign * jnp.sin(angles)[:, None, :]
    first = vectors[..., :half]
    second = vectors[..., half:ROT]
    return jnp.concatenate(
        [first * cosine - second * sine, second * cosine + first * sine, vectors[..., ROT:]],
        axis=-1,
    )


def exact_gelu(vectors):
    return jax.nn.gelu(vectors, approximate=False)


def block_logits(queries, keys_block, diagonal):
    logits = jnp.einsum("qhd,khd->hqk", queries, keys_block, preferred_element_type=jnp.float32) * (
        1.0 / math.sqrt(queries.shape[-1])
    )
    if diagonal:
        counter = jnp.arange(queries.shape[0], dtype=jnp.int32)
        allowed = counter[None, :] <= counter[:, None]
        logits = jnp.where(allowed[None], logits, -1e30)
    return logits


def keep_same(state):
    return state


BF = jnp.bfloat16
SHARE = 1.0
F32 = jnp.float32
OUTWARD = [(0, 1), (3, 2)]
MIDDLE = [(1, 2), (2, 1)]
INWARD = [(1, 0), (2, 3)]


def dot(left, right):
    return jnp.dot(left, right, preferred_element_type=F32)


def dot_rows(left, right):
    return lax.dot_general(left, right, (((0,), (0,)), ((), ())), preferred_element_type=F32)


def dot_cols(left, right):
    return lax.dot_general(left, right, (((1,), (1,)), ((), ())), preferred_element_type=F32)


def partner(shard, bit):
    peers = lax.axis_size("dp")
    return lax.ppermute(shard, "dp", [(i, i ^ bit) for i in range(peers)])


def line_hop(shard, pairs):
    return lax.ppermute(shard, "stream", pairs)


def cost(microseconds):
    return pl.CostEstimate(
        flops=int(microseconds * SHARE * 0.9e9),
        bytes_accessed=int(microseconds * SHARE * 3e6),
        transcendentals=0,
    )


def after(value, *others):
    return lax.optimization_barrier((value, *others))[0]


class Gathered:
    def __init__(self, shard, direct=False):
        self.shard = shard
        self.peers = lax.axis_size("dp")
        if self.peers != 8:
            self.by_x = self.by_y = shard
            return
        self.cut = max(range(shard.ndim - 1), key=lambda dim: shard.shape[dim])
        self.by_x = partner(shard, 2)
        self.by_y = partner(shard, 4)
        self.across = partner(shard, 6) if direct else None

    def whole(self, *earlier):
        shard = self.shard
        if self.peers != 8:
            return lax.all_gather(shard, "dp", axis=0)
        index = lax.axis_index("dp")
        cut = self.cut
        half = shard.shape[cut] // 2
        shard, by_x, by_y = [gated(item, earlier) for item in (shard, self.by_x, self.by_y)]
        pieces = [(shard, 0, 0), (by_x, 2, 0), (by_y, 4, 0)]
        if self.across is None:
            low = lax.slice_in_dim(by_y, 0, half, axis=cut)
            high = lax.slice_in_dim(by_x, half, 2 * half, axis=cut)
            pieces += [(partner(low, 2), 6, 0), (partner(high, 4), 6, half)]
        else:
            pieces.append((gated(self.across, earlier), 6, 0))
        pieces += [(partner(piece, 1), code ^ 1, start) for piece, code, start in pieces]
        return put_together(pieces, shard, self.peers, cut, index)


def put_together(pieces, shard, peers, cut, index):
    codes = [(code, start) for _, code, start in pieces]
    arrays = [piece for piece, _, _ in pieces]

    def kernel(place, *refs):
        out, held, sems, sent = refs[-4:]
        owners = {}
        for n, (code, start) in enumerate(codes):
            size = refs[n].shape[cut]
            span = tuple(
                pl.ds(start, size) if dim == cut else slice(None) for dim in range(shard.ndim)
            )
            copy = pltpu.make_async_copy(refs[n], held.at[(code, *span)], sems.at[n])
            copy.start()
            owners.setdefault(code, []).append(copy)
        leaving = []
        for code, copies in owners.items():
            for copy in copies:
                copy.wait()
            copy = pltpu.make_async_copy(held.at[code], out.at[place[0] ^ code], sent.at[code])
            copy.start()
            leaving.append(copy)
        for copy in leaving:
            copy.wait()

    anywhere = pl.BlockSpec(memory_space=pl.ANY)
    size = peers * shard.size * shard.dtype.itemsize
    return pl.pallas_call(
        kernel,
        in_specs=[pl.BlockSpec(memory_space=pltpu.SMEM)] + [anywhere] * len(arrays),
        out_specs=anywhere,
        out_shape=jax.ShapeDtypeStruct((peers, *shard.shape), shard.dtype),
        scratch_shapes=[
            pltpu.VMEM((peers, *shard.shape), shard.dtype),
            pltpu.SemaphoreType.DMA((len(arrays),)),
            pltpu.SemaphoreType.DMA((peers,)),
        ],
        cost_estimate=cost(2 * size / 3e6),
        name="put_together",
    )(index.astype(jnp.int32).reshape(1), *arrays)


def block_spans(tokens):
    sizes = [tokens // 4] * 3 + [tokens // 8] * 2
    return [(sum(sizes[:i]), size) for i, size in enumerate(sizes)]


def along_line(count, first, second, third, finish=None):
    ones, twos, threes, ends = [], [], [], []
    for step in range(count + 2):
        old = []
        if step >= 4:
            old.append(threes[step - 4] if finish is None else ends[step - 4])
        if step < count:
            gates = list(old)
            if step >= 2:
                gates.append(ones[step - 2])
            if step >= 3:
                gates.append(twos[step - 3])
            ones.append(line_hop(first(step, gates), OUTWARD))
        if 0 <= step - 1 < count:
            load = second(step - 1, ones[step - 1])
            twos.append(line_hop(gated(load, old), MIDDLE))
        if 0 <= step - 2 < count:
            back = step - 2
            load = third(back, ones[back], twos[back])
            threes.append(line_hop(gated(load, old), INWARD))
            if finish is not None:
                ends.append(finish(back, ones[back], twos[back], threes[back]))
    return ones, twos, threes


def gated(value, gates):
    return after(value, *gates) if gates else value


def rope_tables(positions, sign):
    half = ROT // 2
    lane = jnp.arange(HD, dtype=jnp.int32)
    counter = (lane % half).astype(F32)
    freqs = jnp.exp(counter * (-2.0 * math.log(10000.0) / ROT))
    angles = positions.astype(F32)[:, None] * freqs[None, :]
    cosine = jnp.where(lane < ROT, jnp.cos(angles), 1.0)
    sine = sign * jnp.sin(angles)
    up = jnp.where(lane < half, -sine, 0.0)
    down = jnp.where((lane >= half) & (lane < ROT), sine, 0.0)
    return jnp.stack([cosine, up, down])


def turned(block, tables):
    half = ROT // 2
    return (
        block * tables[0]
        + pltpu.roll(block, HD - half, 1) * tables[1]
        + pltpu.roll(block, half, 1) * tables[2]
    )


def make_streams(history, mix_rows, gains, biases):
    entries, tokens, width = history.shape
    streams = gains.shape[0]
    rows, sub, lanes = min(64, tokens), 16, 512

    def kernel(hist, mix, gain, bias, normed, unit, inv, last, scratch):
        def step(r, carry):
            here = pl.ds(pl.multiple_of(r * sub, sub), sub)
            weights = mix[here, :]
            columns = [
                [weights[:, s * entries + j : s * entries + j + 1] for j in range(entries)]
                for s in range(streams)
            ]
            for lane in range(0, width, lanes):
                span = slice(lane, lane + lanes)
                sums = [None] * streams
                for j in range(entries):
                    part = hist[j, here, span].astype(F32)
                    for s in range(streams):
                        term = columns[s][j] * part
                        sums[s] = term if j == 0 else sums[s] + term
                for s in range(streams):
                    scratch[s, :, span] = sums[s]
            stds = []
            for s in range(streams):
                values = scratch[s]
                center = values - jnp.sum(values, axis=-1, keepdims=True) * (1.0 / width)
                var = jnp.sum(center * center, axis=-1, keepdims=True) * (1.0 / width)
                std = lax.rsqrt(var + 1e-05)
                stds.append(std)
                scaled = center * std
                unit[s, here, :] = scaled.astype(BF)
                normed[s, here, :] = (scaled * gain[s : s + 1] + bias[s : s + 1]).astype(BF)
            last[here, :] = scratch[streams - 1]
            inv[here, :] = jnp.concatenate(stds, axis=-1)
            return carry

        lax.fori_loop(0, rows // sub, step, 0)

    wide = jax.ShapeDtypeStruct((streams, tokens, width), BF)
    return pl.pallas_call(
        kernel,
        grid=(tokens // rows,),
        in_specs=[
            pl.BlockSpec((entries, rows, width), lambda i: (0, i, 0)),
            pl.BlockSpec((rows, streams * entries), lambda i: (i, 0)),
            pl.BlockSpec((streams, width), lambda i: (0, 0)),
            pl.BlockSpec((streams, width), lambda i: (0, 0)),
        ],
        out_specs=[
            pl.BlockSpec((streams, rows, width), lambda i: (0, i, 0)),
            pl.BlockSpec((streams, rows, width), lambda i: (0, i, 0)),
            pl.BlockSpec((rows, streams), lambda i: (i, 0)),
            pl.BlockSpec((rows, width), lambda i: (i, 0)),
        ],
        out_shape=[
            wide,
            wide,
            jax.ShapeDtypeStruct((tokens, streams), F32),
            jax.ShapeDtypeStruct((tokens, width), F32),
        ],
        scratch_shapes=[pltpu.VMEM((streams, sub, width), F32)],
        cost_estimate=cost(22),
        name="make_streams",
    )(history, mix_rows, gains, biases)


def project(normed, w_heads, tables):
    _, tokens, width = normed.shape
    columns = w_heads.shape[3]
    heads, half = columns // HD, tokens // 2

    def kernel(x, w, table, out):
        flat = dot(x[0], w[...].reshape(width, columns))
        turn = pl.program_id(0) < 2

        def put(head, block):
            out[2 * head, 0] = block[:half].astype(BF)
            out[2 * head + 1, 0] = block[half:].astype(BF)

        @pl.when(turn)
        def _():
            for head in range(heads):
                put(head, turned(flat[:, head * HD : (head + 1) * HD], table[...]))

        @pl.when(jnp.logical_not(turn))
        def _():
            for head in range(heads):
                put(head, flat[:, head * HD : (head + 1) * HD])

    return pl.pallas_call(
        kernel,
        grid=(3,),
        in_specs=[
            pl.BlockSpec((1, tokens, width), lambda c: (c, 0, 0)),
            pl.BlockSpec((w_heads.shape[0], 1, w_heads.shape[2], columns), lambda c: (0, c, 0, 0)),
            pl.BlockSpec((3, tokens, HD), lambda c: (0, 0, 0)),
        ],
        out_specs=pl.BlockSpec((2 * heads, 1, half, HD), lambda c: (0, c, 0, 0)),
        out_shape=jax.ShapeDtypeStruct((2 * heads, 3, half, HD), BF),
        cost_estimate=cost(9),
        name="project",
    )(normed, w_heads, tables)


def attend(own, other, first_key, side):
    shards, _, half, _ = own.shape
    factor = 1.0 / math.sqrt(HD)

    def kernel(first, part, mine, theirs, out, exact, norm):
        s = pl.program_id(0)
        query = mine[s, 0]

        def fold(state, keys, values, mask):
            top, total, acc = state
            logits = dot_cols(query, keys) * factor
            if mask is not None:
                logits = jnp.where(mask, logits, -1e30)
            new_top = jnp.maximum(top, jnp.max(logits, axis=-1, keepdims=True))
            probs = jnp.exp(logits - new_top)
            keep = jnp.exp(top - new_top)
            return (
                new_top,
                total * keep + jnp.sum(probs, axis=-1, keepdims=True),
                acc * keep + dot(probs.astype(BF), values),
            )

        row = lax.broadcasted_iota(jnp.int32, (half, half), 0)
        col = lax.broadcasted_iota(jnp.int32, (half, half), 1)
        state = (
            jnp.full((half, 1), -1e30, F32),
            jnp.zeros((half, 1), F32),
            jnp.zeros((half, HD), F32),
        )
        state = fold(state, mine[s, 1], mine[s, 2], col <= row)
        state = lax.fori_loop(
            0, part[0], lambda i, st: fold(st, theirs[s, 0], theirs[s, 1], None), state
        )

        def shard_step(b, st):
            st = fold(st, mine[b, 1], mine[b, 2], None)
            return fold(st, theirs[b, 0], theirs[b, 1], None)

        top, total, acc = lax.fori_loop(first[s], s, shard_step, state)
        result = acc / total
        out[0] = result.astype(BF)
        exact[0] = result
        norm[0] = top + jnp.log(total)

    return pl.pallas_call(
        kernel,
        grid_spec=pltpu.PrefetchScalarGridSpec(
            num_scalar_prefetch=2,
            grid=(shards,),
            in_specs=[
                pl.BlockSpec((shards, 3, half, HD), lambda s, *_: (0, 0, 0, 0)),
                pl.BlockSpec((shards, 2, half, HD), lambda s, *_: (0, 0, 0, 0)),
            ],
            out_specs=[
                pl.BlockSpec((1, half, HD), lambda s, *_: (s, 0, 0)),
                pl.BlockSpec((1, half, HD), lambda s, *_: (s, 0, 0)),
                pl.BlockSpec((1, half, 1), lambda s, *_: (s, 0, 0)),
            ],
        ),
        out_shape=[
            jax.ShapeDtypeStruct((shards, half, HD), BF),
            jax.ShapeDtypeStruct((shards, half, HD), F32),
            jax.ShapeDtypeStruct((shards, half, 1), F32),
        ],
        cost_estimate=cost(16),
        name="attend",
    )(first_key, side, own, other)


def attend_back(own, other, grads, exact, norm, first_key, side):
    shards, _, half, _ = own.shape
    factor = 1.0 / math.sqrt(HD)

    def kernel(first, part, mine, theirs, grad_ref, exact_ref, norm_ref, kept, given, sums):
        s = pl.program_id(0)
        query = mine[s, 0]
        grad = grad_ref[s]
        delta = jnp.sum(grad.astype(F32) * exact_ref[0], axis=-1, keepdims=True)
        level = norm_ref[0]
        lowered = grad

        @pl.when(s == 0)
        def _():
            sums[...] = jnp.zeros_like(sums)

        def fold(query_grad, keys, values, mask, slot, b):
            logits = dot_cols(query, keys) * factor
            probs = jnp.exp(logits - level)
            if mask is not None:
                probs = jnp.where(mask, probs, 0.0)
            score = (probs * (dot_cols(grad, values) - delta)).astype(BF)
            sums[slot, b] += dot_rows(score, query)
            sums[slot + 1, b] += dot_rows(probs.astype(BF), lowered)
            return query_grad + dot(score, keys)

        row = lax.broadcasted_iota(jnp.int32, (half, half), 0)
        col = lax.broadcasted_iota(jnp.int32, (half, half), 1)
        total = fold(jnp.zeros((half, HD), F32), mine[s, 1], mine[s, 2], col <= row, 0, s)
        total = lax.fori_loop(
            0, part[0], lambda i, q: fold(q, theirs[s, 0], theirs[s, 1], None, 2, s), total
        )

        def shard_step(b, q):
            q = fold(q, mine[b, 1], mine[b, 2], None, 0, b)
            return fold(q, theirs[b, 0], theirs[b, 1], None, 2, b)

        total = lax.fori_loop(first[s], s, shard_step, total)
        kept[s, 0] = (total * factor).astype(BF)

        @pl.when(s == shards - 1)
        def _():
            for b in range(shards):
                kept[b, 1] = (sums[0, b] * factor).astype(BF)
                kept[b, 2] = sums[1, b].astype(BF)
                given[b, 0] = (sums[2, b] * factor).astype(BF)
                given[b, 1] = sums[3, b].astype(BF)

    whole = lambda n: pl.BlockSpec((shards, n, half, HD), lambda s, *_: (0, 0, 0, 0))
    return pl.pallas_call(
        kernel,
        grid_spec=pltpu.PrefetchScalarGridSpec(
            num_scalar_prefetch=2,
            grid=(shards,),
            in_specs=[
                whole(3),
                whole(2),
                pl.BlockSpec((shards, half, HD), lambda s, *_: (0, 0, 0)),
                pl.BlockSpec((1, half, HD), lambda s, *_: (s, 0, 0)),
                pl.BlockSpec((1, half, 1), lambda s, *_: (s, 0, 0)),
            ],
            out_specs=[whole(3), whole(2)],
            scratch_shapes=[pltpu.VMEM((4, shards, half, HD), F32)],
        ),
        out_shape=[
            jax.ShapeDtypeStruct((shards, 3, half, HD), BF),
            jax.ShapeDtypeStruct((shards, 2, half, HD), BF),
        ],
        cost_estimate=cost(22),
        name="attend_back",
    )(first_key, side, own, other, grads, exact, norm)


def norm_back(grad, unit, inv, gain, extra):
    width = grad.shape[1]
    scaled = grad * gain
    mean = jnp.sum(scaled, axis=-1, keepdims=True) * (1.0 / width)
    slope = jnp.sum(scaled * unit, axis=-1, keepdims=True) * (1.0 / width)
    result = inv * (scaled - mean - unit * slope)
    return result if extra is None else result + extra


def heads_back(parts, w_heads, normed, unit, inv, gains, tables, spans):
    _, tokens, width = normed.shape
    columns = w_heads.shape[3]
    heads, half = columns // HD, tokens // 2
    count = len(spans)

    def kernel(part, w, x, u, istd, gain, table, *refs):
        pieces, (stream, weight, stats, grad, wide) = refs[:count], refs[count:]
        c = pl.program_id(0)
        turn = c < 2

        def take(head):
            return jnp.concatenate([part[2 * head, 0], part[2 * head + 1, 0]], axis=0).astype(F32)

        @pl.when(turn)
        def _():
            for head in range(heads):
                grad[:, head * HD : (head + 1) * HD] = turned(take(head), table[...]).astype(BF)

        @pl.when(jnp.logical_not(turn))
        def _():
            for head in range(heads):
                grad[:, head * HD : (head + 1) * HD] = take(head).astype(BF)

        wide[...] = dot_cols(grad[...], w[...].reshape(width, columns))
        weight[0] = dot_rows(x[0], grad[...]).astype(BF)
        stats[...] = jnp.zeros_like(stats)
        for r, (start, block) in enumerate(spans):
            column = lax.broadcasted_iota(jnp.int32, (block, istd.shape[1]), 1)
            here = slice(start, start + block)
            values = wide[here, :]
            units = u[0, here, :].astype(F32)
            std = jnp.sum(jnp.where(column == c, istd[here, :], 0.0), axis=-1, keepdims=True)
            result = norm_back(values, units, std, gain[0], None).astype(BF)
            stream[0, here, :] = result
            pieces[r][0] = result
            stats[0, 0:1] += jnp.sum(values * units, axis=0, keepdims=True)
            stats[0, 1:2] += jnp.sum(values, axis=0, keepdims=True)

    return pl.pallas_call(
        kernel,
        grid=(3,),
        in_specs=[
            pl.BlockSpec((2 * heads, 1, half, HD), lambda c: (0, c, 0, 0)),
            pl.BlockSpec((w_heads.shape[0], 1, w_heads.shape[2], columns), lambda c: (0, c, 0, 0)),
            pl.BlockSpec((1, tokens, width), lambda c: (c, 0, 0)),
            pl.BlockSpec((1, tokens, width), lambda c: (c, 0, 0)),
            pl.BlockSpec((tokens, inv.shape[1]), lambda c: (0, 0)),
            pl.BlockSpec((1, 1, width), lambda c: (c, 0, 0)),
            pl.BlockSpec((3, tokens, HD), lambda c: (0, 0, 0)),
        ],
        out_specs=[pl.BlockSpec((1, block, width), lambda c: (c, 0, 0)) for _, block in spans]
        + [
            pl.BlockSpec((1, tokens, width), lambda c: (c, 0, 0)),
            pl.BlockSpec((1, width, columns), lambda c: (c, 0, 0)),
            pl.BlockSpec((1, 2, width), lambda c: (c, 0, 0)),
        ],
        out_shape=[jax.ShapeDtypeStruct((3, block, width), BF) for _, block in spans]
        + [
            jax.ShapeDtypeStruct((3, tokens, width), BF),
            jax.ShapeDtypeStruct((3, width, columns), BF),
            jax.ShapeDtypeStruct((3, 2, width), F32),
        ],
        scratch_shapes=[pltpu.VMEM((tokens, columns), BF), pltpu.VMEM((tokens, width), F32)],
        cost_estimate=cost(3),
        name="heads_back",
    )(parts, w_heads, normed, unit, inv, gains[:, None, :], tables)


def last_back(grad, unit, inv, gain, extra, flag):
    tokens, width = grad.shape
    block = min(128, tokens)

    def kernel(g, u, istd, gain_ref, e, flag_ref, stream, stats):
        @pl.when(pl.program_id(0) == 0)
        def _():
            stats[...] = jnp.zeros_like(stats)

        values = g[...]
        units = u[...].astype(F32)
        std = istd[...][:, -1:]
        added = e[...].astype(F32) * flag_ref[0]
        stream[...] = norm_back(values, units, std, gain_ref[...], added).astype(BF)
        stats[0:1] += jnp.sum(values * units, axis=0, keepdims=True)
        stats[1:2] += jnp.sum(values, axis=0, keepdims=True)

    row = lambda n: pl.BlockSpec((block, n), lambda i: (i, 0))
    return pl.pallas_call(
        kernel,
        grid=(tokens // block,),
        in_specs=[
            row(width),
            row(width),
            row(inv.shape[1]),
            pl.BlockSpec((1, width), lambda i: (0, 0)),
            row(width),
            pl.BlockSpec(memory_space=pltpu.SMEM),
        ],
        out_specs=[row(width), pl.BlockSpec((2, width), lambda i: (0, 0))],
        out_shape=[
            jax.ShapeDtypeStruct((tokens, width), BF),
            jax.ShapeDtypeStruct((2, width), F32),
        ],
        cost_estimate=cost(7),
        name="last_back",
    )(grad, unit, inv, gain, extra, flag)


def mixing_back(heads_part, last_part, history, which, of):
    entries, tokens, width = history.shape
    streams = heads_part.shape[0] + 1
    rows, sub, lanes = min(64, tokens // of), 16, 256
    steps = tokens // of // rows
    base = which * steps

    def kernel(first, last, hist, out):
        def step(r, carry):
            here = pl.ds(pl.multiple_of(r * sub, sub), sub)
            for s in range(streams):
                sums = [None] * entries
                for lane in range(0, width, lanes):
                    span = slice(lane, lane + lanes)
                    part = first[s, here, span] if s < streams - 1 else last[here, span]
                    part = part.astype(F32)
                    for j in range(entries):
                        term = part * hist[j, here, span].astype(F32)
                        sums[j] = term if lane == 0 else sums[j] + term
                columns = [jnp.sum(item, axis=-1, keepdims=True) for item in sums]
                out[s, here, :] = jnp.concatenate(columns, axis=-1)
            return carry

        lax.fori_loop(0, rows // sub, step, 0)

    return pl.pallas_call(
        kernel,
        grid=(steps,),
        in_specs=[
            pl.BlockSpec((streams - 1, rows, width), lambda i: (0, base + i, 0)),
            pl.BlockSpec((rows, width), lambda i: (base + i, 0)),
            pl.BlockSpec((entries, rows, width), lambda i: (0, base + i, 0)),
        ],
        out_specs=pl.BlockSpec((streams, rows, entries), lambda i: (0, i, 0)),
        out_shape=jax.ShapeDtypeStruct((streams, tokens // of, entries), F32),
        cost_estimate=cost(0.4),
        name="mixing_back",
    )(heads_part, last_part, history)


def far_attend(queries, keys, values, shard_offset):
    tokens, heads_here, head_size = queries.shape
    data_index = lax.axis_index("dp")
    pairs = [jnp.stack([keys, values])]
    reach = 2 * SEQ // tokens
    for back in range(1, reach):
        pairs.append(passed_along(pairs[0], "dp", back))
    usable = [(shard_offset[0] >= back * tokens) & (data_index >= back) for back in range(reach)]
    first_logits = block_logits(queries, keys, True)
    top = jnp.max(first_logits, axis=-1)
    total = jnp.sum(jnp.exp(first_logits - top[..., None]), axis=-1)
    for back in range(1, reach):

        def widen(state, block=pairs[back][0]):
            logits = block_logits(queries, block, False)
            new_top = jnp.maximum(state[0], jnp.max(logits, axis=-1))
            summed = state[1] * jnp.exp(state[0] - new_top) + jnp.sum(
                jnp.exp(logits - new_top[..., None]), axis=-1
            )
            return (new_top, summed)

        top, total = lax.cond(usable[back], widen, keep_same, (top, total))
    log_total = top + jnp.log(total)
    attended = jnp.zeros((tokens, heads_here, head_size), F32)
    for back in range(reach):

        def accumulate(current, block=pairs[back], diagonal=back == 0):
            probs = jnp.exp(block_logits(queries, block[0], diagonal) - log_total[..., None])
            return current + jnp.einsum(
                "hqk,khd->qhd", probs.astype(BF), block[1], preferred_element_type=F32
            )

        attended = lax.cond(usable[back], accumulate, keep_same, attended)
    return attended, (pairs, usable, log_total)


def far_attend_back(queries, attended_grad, kept):
    tokens, heads_here, head_size = queries.shape
    factor = 1.0 / math.sqrt(head_size)
    pairs, usable, log_total = kept
    reach = len(pairs)

    def weights_of(block, diagonal):
        return jnp.exp(block_logits(queries, block, diagonal) - log_total[..., None])

    def prob_grads(block):
        return jnp.einsum("qhd,khd->hqk", attended_grad, block[1], preferred_element_type=F32)

    delta = jnp.zeros((heads_here, tokens), F32)
    for back in range(reach):

        def gather_delta(current, block=pairs[back], diagonal=back == 0):
            return current + jnp.sum(weights_of(block[0], diagonal) * prob_grads(block), axis=-1)

        delta = lax.cond(usable[back], gather_delta, keep_same, delta)

    def skip_block(current):
        return (current, jnp.zeros((2, tokens, heads_here, head_size), F32))

    query_grad = jnp.zeros((tokens, heads_here, head_size), F32)
    key_value_grad = jnp.zeros((2, tokens, heads_here, head_size), F32)
    for back in range(reach):

        def spread(current, block=pairs[back], diagonal=back == 0):
            probs = weights_of(block[0], diagonal)
            score_grad = (probs * (prob_grads(block) - delta[..., None])).astype(BF)
            query_part = (
                current
                + jnp.einsum("hqk,khd->qhd", score_grad, block[0], preferred_element_type=F32)
                * factor
            )
            key_part = (
                jnp.einsum("hqk,qhd->khd", score_grad, queries, preferred_element_type=F32)
                * factor
            )
            value_part = jnp.einsum(
                "hqk,qhd->khd", probs.astype(BF), attended_grad, preferred_element_type=F32
            )
            return (query_part, jnp.stack([key_part, value_part]))

        query_grad, pair_grad = lax.cond(usable[back], spread, skip_block, query_grad)
        if back == 0:
            key_value_grad = pair_grad
        else:
            key_value_grad = key_value_grad + passed_along(pair_grad, "dp", -back)
    return jnp.concatenate([query_grad[None], key_value_grad])


def mix_block(start, coefficients, shares, last_share, extras, last_extras, arrived, whole):
    streams, block, width = shares.shape
    each = coefficients.shape[1] // (streams + 1)
    groups = 1 + len(extras)
    final = arrived is not None
    lanes = 512

    def kernel(*refs):
        weights = refs[0][...]
        heads, lasts = refs[1 : 1 + groups], refs[1 + groups : 1 + 2 * groups]
        out = refs[-2] if final else refs[-1]
        if final:
            refs[-1][...] = jnp.zeros_like(refs[-1])
        columns = [weights[:, n : n + 1] for n in range(weights.shape[1])]
        for lane in range(0, width, lanes):
            span = slice(lane, lane + lanes)
            values = []
            for s in range(streams + 1):
                picks = [r[s, :, span] if s < streams else l[:, span] for r, l in zip(heads, lasts)]
                total = picks[0].astype(F32)
                for pick in picks[1:]:
                    total = total + pick.astype(F32)
                values.append(total)
            for e in range(each):
                total = columns[e * (streams + 1)] * values[0]
                for s in range(1, streams + 1):
                    total = total + columns[e * (streams + 1) + s] * values[s]
                if final:
                    total = total + refs[1 + 2 * groups][e, :, span].astype(F32)
                out[e, :, span] = total.astype(out.dtype)

    i = start // block
    piece = pl.BlockSpec((streams, block, width), lambda n: (0, 0, 0))
    rows = [
        pl.BlockSpec((block, width), lambda n, at=start % item.shape[0] // block: (at, 0))
        for item in (last_share, *last_extras)
    ]
    small = pl.BlockSpec((each, block, width), lambda n: (0, 0, 0))
    specs = [pl.BlockSpec((block, coefficients.shape[1]), lambda n: (i, 0))]
    specs += [piece] * groups + rows
    args = [coefficients, shares, *extras, last_share, *last_extras]
    alias = {}
    if final:
        specs.append(small)
        args.append(arrived)
        if whole is not None:
            specs.append(pl.BlockSpec(memory_space=pl.ANY))
            args.append(whole)
            alias = {len(args) - 1: 0}
        out_spec = [
            pl.BlockSpec((each, block, width), lambda n: (0, i, 0)),
            pl.BlockSpec((8, 128), lambda n: (0, 0)),
        ]
        out_shape = [
            jax.ShapeDtypeStruct((each, coefficients.shape[0], width), F32),
            jax.ShapeDtypeStruct((8, 128), F32),
        ]
    else:
        out_spec, out_shape = small, jax.ShapeDtypeStruct((each, block, width), BF)
    return pl.pallas_call(
        kernel,
        grid=(1,),
        in_specs=specs,
        out_specs=out_spec,
        out_shape=out_shape,
        input_output_aliases=alias,
        cost_estimate=cost(0.4),
        name="mix_final" if final else "mix_inward",
    )(*args)


def hidden_units(x, w_up):
    tokens, width = x.shape
    units = w_up.shape[1]
    block = min(512, units)

    def kernel(x_ref, w, out, slope):
        up = dot(x_ref[...], w[...])
        inside = 0.5 * (1.0 + lax.erf(up * math.sqrt(0.5)))
        out[...] = (up * inside).astype(BF)
        bell = jnp.exp(-0.5 * up * up) * (1.0 / math.sqrt(2.0 * math.pi))
        slope[...] = (inside + up * bell).astype(BF)

    column = pl.BlockSpec((tokens, block), lambda i: (0, i))
    return pl.pallas_call(
        kernel,
        grid=(units // block,),
        in_specs=[
            pl.BlockSpec((tokens, width), lambda i: (0, 0)),
            pl.BlockSpec((width, block), lambda i: (0, i)),
        ],
        out_specs=[column, column],
        out_shape=[jax.ShapeDtypeStruct((tokens, units), BF)] * 2,
        cost_estimate=cost(9),
        name="hidden_units",
    )(x, w_up)


def merge_branches(attended, hidden, w_merge, w_down, stream, flag):
    tokens, inner = attended.shape
    shards, units, cols = w_down.shape
    members = lax.axis_size("stream")
    each = shards // members
    if cols % 128:
        merged = jnp.einsum("te,ned->tnd", attended, w_merge, preferred_element_type=F32)
        merged = merged + jnp.einsum("tf,nfd->tnd", hidden, w_down, preferred_element_type=F32)
        merged = merged.reshape(tokens, -1) + flag * stream
        return jnp.transpose(merged.reshape(tokens, members, -1), (1, 0, 2)).astype(BF)

    def kernel(a, h, wm, wd, st, flag_ref, out):
        out[0] = (dot(a[...], wm[0]) + dot(h[...], wd[0]) + flag_ref[0] * st[...]).astype(BF)

    return pl.pallas_call(
        kernel,
        grid=(shards,),
        in_specs=[
            pl.BlockSpec((tokens, inner), lambda n: (0, 0)),
            pl.BlockSpec((tokens, units), lambda n: (0, 0)),
            pl.BlockSpec((1, inner, cols), lambda n: (n, 0, 0)),
            pl.BlockSpec((1, units, cols), lambda n: (n, 0, 0)),
            pl.BlockSpec((tokens, cols), lambda n: (0, n)),
            pl.BlockSpec(memory_space=pltpu.SMEM),
        ],
        out_specs=pl.BlockSpec((1, tokens, cols), lambda n: (n // each, 0, n % each)),
        out_shape=jax.ShapeDtypeStruct((members, tokens, each * cols), BF),
        cost_estimate=cost(13),
        name="merge_branches",
    )(attended, hidden, w_merge, w_down, stream, flag)


def back_through(grad, stacked, slope):
    tokens = grad.shape[0]
    shards, units, cols = stacked.shape
    if cols % 128:
        split = grad.reshape(tokens, shards, cols)
        total = jnp.einsum("tnd,nfd->tf", split, stacked, preferred_element_type=F32)
        return (total if slope is None else total * slope.astype(F32)).astype(BF)

    def kernel(*refs):
        g, w = refs[:2]
        out, acc = refs[-2:]
        n = pl.program_id(0)
        part = dot_cols(g[...], w[0])

        @pl.when(n == 0)
        def _():
            acc[...] = part

        @pl.when(n > 0)
        def _():
            acc[...] += part

        @pl.when(n == shards - 1)
        def _():
            total = acc[...]
            if slope is not None:
                total = total * refs[2][...].astype(F32)
            out[...] = total.astype(BF)

    specs = [
        pl.BlockSpec((tokens, cols), lambda n: (0, n)),
        pl.BlockSpec((1, units, cols), lambda n: (n, 0, 0)),
    ]
    args = [grad, stacked]
    if slope is not None:
        specs.append(pl.BlockSpec((tokens, units), lambda n: (0, 0)))
        args.append(slope)
    return pl.pallas_call(
        kernel,
        grid=(shards,),
        in_specs=specs,
        out_specs=pl.BlockSpec((tokens, units), lambda n: (0, 0)),
        out_shape=jax.ShapeDtypeStruct((tokens, units), BF),
        scratch_shapes=[pltpu.VMEM((tokens, units), F32)],
        cost_estimate=cost(13 if slope is not None else 7),
        name="back_through",
    )(*args)


def body(
    history,
    mixing,
    shard_offset,
    norm_gain,
    norm_bias,
    w_heads,
    w_merge,
    w_up,
    w_down,
    mixer_first,
    mixer_second,
    out_cotangent,
    next_cotangent,
):
    member = lax.axis_index("stream")
    members = lax.axis_size("stream")
    shards = lax.axis_size("dp")
    index = lax.axis_index("dp")
    entries, tokens, width = history.shape
    heads_here = w_heads.shape[2] // HD
    half = tokens // 2
    highest = lax.Precision.HIGHEST
    flag = (member == members - 1).astype(F32)
    flags = flag.reshape(1)
    near = shards == 8 and heads_here * 2 == shards and tokens * shards == 2 * SEQ

    if near:
        spread = jnp.broadcast_to(shard_offset[:, None], (8, 128))
        offsets = lax.all_gather(spread, "dp", axis=0)[:, 0, 0]
        w_heads = after(w_heads, offsets)
    got_heads = Gathered(w_heads, direct=near)
    lanes = jnp.concatenate([norm_gain, norm_bias]).astype(F32).reshape(tokens, -1)
    first_rows = mixer_first.astype(F32).reshape(tokens, -1)
    second_flat = mixer_second[:, 0, :].astype(F32).reshape(-1)
    hidden_count = mixer_second.shape[0]
    lines = -(-second_flat.shape[0] // tokens)
    second_rows = jnp.pad(second_flat, (0, lines * tokens - second_flat.shape[0]))
    outputs = next_cotangent.shape[2]
    arrays = [mixing[:, 0, :], lanes, next_cotangent[:, 0, :], first_rows]
    arrays.append(second_rows.reshape(tokens, lines))
    packed = lax.all_gather(jnp.concatenate(arrays, axis=1), "stream", axis=0)
    parts, place = [], 0
    for array in arrays:
        parts.append(packed[:, :, place : place + array.shape[1]])
        place += array.shape[1]
    mix_all, norms, next_full, first_full, second_full = parts
    norms = norms.reshape(members, 2, width)
    first_full = first_full.astype(BF).reshape(width, -1)
    second_full = second_full.reshape(members, -1)[:, : second_flat.shape[0]]
    second_full = second_full.reshape(members, hidden_count, outputs)
    if near:
        early = (got_heads.by_x, got_heads.by_y, got_heads.across)
        history = after(history, *early)
        w_up, w_merge = after(w_up, *early[:2]), after(w_merge, *early[:2])
    got_up = Gathered(w_up)
    got_merge = Gathered(w_merge, direct=near)
    gains, biases = norms[:, 0], norms[:, 1]
    mix_rows = jnp.transpose(mix_all, (1, 0, 2)).reshape(tokens, members * entries)

    normed, unit, inv, stream = make_streams(history, mix_rows, gains, biases)
    full_heads = got_heads.whole()
    cotangent = lax.all_gather(after(out_cotangent, inv), "stream", axis=1, tiled=True)
    positions = shard_offset[0] + jnp.arange(tokens, dtype=jnp.int32)
    projected = project(after(normed, got_up.by_x, got_up.by_y), full_heads, rope_tables(positions, 1.0))

    if near:
        side = (index % 2).astype(jnp.int32).reshape(1)
        place = jnp.arange(shards, dtype=jnp.int32)
        first_key = jnp.maximum(place - offsets // tokens, 0).astype(jnp.int32)
        own = lax.all_to_all(projected, "dp", 0, 0, tiled=True)
        got_down = Gathered(after(w_down, own))
        other = partner(own[:, 1:], 1)
        result, exact, level = attend(own, other, first_key, side)
        full_up = got_up.whole(result)
        full_merge = got_merge.whole(result)
        back = lax.all_to_all(result, "dp", 0, 0, tiled=True)
        attended = jnp.transpose(back.reshape(heads_here, tokens, HD), (1, 0, 2)).reshape(tokens, -1)
    else:
        got_down = Gathered(w_down)
        full_up = got_up.whole()
        full_merge = got_merge.whole()
        split = projected.reshape(heads_here, 2, 3, half, HD)
        split = jnp.transpose(split, (2, 1, 3, 0, 4)).reshape(3, tokens, heads_here, HD)
        result, kept = far_attend(split[0], split[1], split[2], shard_offset)
        attended = result.reshape(tokens, -1).astype(BF)
    full_down = got_down.whole(result)
    flat_up = full_up.reshape(width, -1)
    hidden, slope = hidden_units(normed[members - 1], flat_up)
    attended = after(attended, hidden)
    hidden = after(hidden, cotangent)
    share = merge_branches(attended, hidden, full_merge, full_down, stream, flags)

    columns = lax.all_to_all(share, "stream", 0, 0, tiled=True)
    block_out = jnp.sum(columns.astype(F32), axis=0).astype(BF)
    block_full = lax.all_gather(block_out, "stream", axis=1, tiled=True)
    out_float = block_full.astype(F32)
    scale = lax.rsqrt(jnp.sum(out_float * out_float, axis=-1) / width + 1e-06)
    proj = dot(block_full, first_full)
    mixer, mixer_back = jax.vjp(exact_gelu, scale[:, None] * proj)
    second_here = mixer_second[:, 0, :].astype(F32)
    next_here = jnp.dot(mixer, second_here, precision=highest, preferred_element_type=F32)
    mixer_grad = jnp.einsum(
        "stn,scn->tc", next_full, second_full, precision=highest, preferred_element_type=F32
    )
    pre_grad = mixer_back(mixer_grad)[0]
    proj_grad = (scale[:, None] * pre_grad).astype(BF)
    scale_grad = jnp.sum(pre_grad * proj, axis=-1)
    second_local = jnp.dot(
        mixer.T, next_cotangent[:, 0, :], precision=highest, preferred_element_type=F32
    )
    first_local = dot_rows(block_out, proj_grad)
    grad_out = (
        cotangent.astype(F32)
        + dot_cols(proj_grad, first_full)
        - (scale * scale * scale * scale_grad)[:, None] * out_float / width
    ).astype(BF)

    attended_grad = back_through(grad_out, full_merge, None)
    up_grad = back_through(grad_out, full_down, slope)
    down_grad = dot_rows(hidden, grad_out).astype(BF)
    grad_down = lax.psum_scatter(down_grad, "dp", scatter_dimension=1, tiled=True).astype(F32)
    last_normed = dot_cols(after(up_grad, down_grad), flat_up)
    last_share, last_stats = last_back(
        last_normed, unit[members - 1], inv, gains[members - 1 :], grad_out, flags
    )
    last_hop = line_hop(last_share, OUTWARD)
    last_sum = (last_share.astype(F32) + last_hop.astype(F32)).astype(BF)
    last_next = line_hop(last_sum, MIDDLE)
    if near:
        sent = attended_grad.reshape(tokens, heads_here, HD)
        sent = jnp.transpose(sent, (1, 0, 2)).reshape(shards, half, HD)
        grads = lax.all_to_all(sent, "dp", 0, 0, tiled=True)
        grads = after(grads, last_share)
        kept_grads, given = attend_back(own, other, grads, exact, level, first_key, side)
        taken = partner(given, 1)
        summed = kept_grads[:, 1:].astype(F32) + taken.astype(F32)
        pair = jnp.concatenate([kept_grads[:, :1], summed.astype(BF)], axis=1)
        pair = after(pair, last_hop)
        late_grad, late_up = after(grad_out, pair), after(up_grad, pair)
        up_back = dot_rows(normed[members - 1], late_up).astype(BF)
        merge_grad = dot_rows(attended, late_grad).astype(BF)
        parts = lax.all_to_all(pair, "dp", 0, 0, tiled=True)
    else:
        up_back = dot_rows(normed[members - 1], up_grad).astype(BF)
        merge_grad = dot_rows(attended, grad_out).astype(BF)
        grads = far_attend_back(split[0], attended_grad.reshape(tokens, heads_here, HD), kept)
        parts = grads.reshape(3, 2, half, heads_here, HD)
        parts = jnp.transpose(parts, (3, 1, 0, 2, 4)).reshape(2 * heads_here, 3, half, HD)

    parts = after(parts, last_sum, grad_down, up_back, merge_grad)
    spans = block_spans(tokens)
    *pieces, heads_share, heads_grad, heads_stats = heads_back(
        parts, full_heads, normed, unit, inv, gains, rope_tables(positions, -1.0), spans
    )

    grad_merge = lax.psum_scatter(merge_grad, "dp", scatter_dimension=1, tiled=True).astype(F32)
    grad_heads = lax.psum_scatter(heads_grad, "dp", scatter_dimension=1, tiled=True).astype(F32)
    grad_up = lax.psum_scatter(up_back, "dp", scatter_dimension=0, tiled=True).astype(F32)

    each = entries // members

    def weights_for(owner):
        block = lax.dynamic_slice_in_dim(mix_all, owner * each, each, axis=2)
        return jnp.transpose(block, (1, 2, 0)).reshape(tokens, each * members)

    there = weights_for(jnp.where(member == 1, 0, members - 1))
    here = weights_for(member)
    extra = {}

    last_one = lambda i: last_hop
    last_two = lambda i: last_next

    def first_hop(i, gates):
        gates = list(gates)
        if i == 3:
            gates.append(grad_merge)
        return gated(pieces[i], gates)

    def small_sums():
        stats = jnp.concatenate([heads_stats, last_stats[None]]).reshape(members, tokens, -1)
        both = jnp.concatenate([jnp.concatenate(mixes, axis=1), stats], axis=2)
        both = jnp.sum(lax.all_to_all(both, "stream", 0, 0, tiled=True), axis=0)
        second_sums = jnp.pad(second_local.reshape(-1), (0, lines * tokens - second_flat.shape[0]))
        local = [both[:, entries:], first_local.reshape(tokens, -1), second_sums.reshape(tokens, lines)]
        everyone = lax.all_gather(jnp.concatenate(local, axis=1), "dp", axis=0)
        return both[:, :entries], jnp.sum(everyone, axis=0)

    mixes = []

    def second_hop(i, one):
        return (pieces[i].astype(F32) + one.astype(F32)).astype(BF)

    def third_hop(i, one, two):
        return mix_block(spans[i][0], there, pieces[i], last_share, [two], [last_two(i)], None, None)

    def finish(i, one, two, three):
        if i in (0, 1):
            mixes.append(mixing_back(heads_share, last_share, after(history, two), i, 2))
        if i == 1:
            extra["both"], extra["all"] = small_sums()
        if i == 3:
            three = after(three, extra["both"], grad_heads)
        if i == 4:
            three = after(three, extra["all"])
        extra["history"], token = mix_block(
            spans[i][0],
            here,
            pieces[i],
            last_share,
            [one, two],
            [last_one(i), last_two(i)],
            three,
            extra.get("history"),
        )
        return token

    along_line(len(spans), first_hop, second_hop, third_hop, finish)
    grad_history = extra["history"]

    grad_mixing = extra["both"][:, None, :]
    sums = extra["all"]
    columns = 2 * width // tokens
    stats = sums[:, :columns].reshape(2, width)
    grad_first = sums[:, columns:-lines].reshape(mixer_first.shape)
    grad_second = sums[:, -lines:].reshape(-1)[: second_flat.shape[0]].reshape(hidden_count, outputs)
    return (
        block_out,
        next_here[:, None, :],
        grad_history,
        grad_mixing,
        stats[:1],
        stats[1:],
        grad_heads,
        grad_merge,
        grad_up,
        grad_down,
        grad_first,
        grad_second[:, None, :],
    )


def solution(mesh):
    in_specs = (
        P(None, "dp", None),
        P("dp", "stream", None),
        P("dp"),
        P("stream", None),
        P("stream", None),
        P(None, "dp", "stream"),
        P("stream", "dp"),
        P("dp", "stream"),
        P("stream", "dp"),
        P("stream", None),
        P(None, "stream", None),
        P("dp", "stream"),
        P("dp", "stream", None),
    )
    out_specs = (
        P("dp", "stream"),
        P("dp", "stream", None),
        P("stream", "dp", None),
        P("dp", "stream", None),
        P("stream", None),
        P("stream", None),
        P(None, "dp", "stream"),
        P("stream", "dp"),
        P("dp", "stream"),
        P("stream", "dp"),
        P("stream", None),
        P(None, "stream", None),
    )
    return jax.shard_map(body, mesh=mesh, in_specs=in_specs, out_specs=out_specs, check_vma=False)
```

```python
import math

import jax
import jax.numpy as jnp
from jax import lax
from jax.experimental import pallas as pl
from jax.experimental.pallas import tpu as pltpu
from jax.sharding import PartitionSpec as P

HD = 128
ROT = 32
SEQ = 2048


def passed_along(shard, axis, by):
    peers = lax.axis_size(axis)
    pairs = [(i, i + by) for i in range(peers) if 0 <= i + by < peers]
    return lax.ppermute(shard, axis, pairs)


def rotate(vectors, positions, sign):
    half = ROT // 2
    counter = jnp.arange(half, dtype=jnp.float32)
    freqs = jnp.exp(counter * (-2.0 * math.log(10000.0) / ROT))
    angles = positions.astype(jnp.float32)[:, None] * freqs[None, :]
    cosine = jnp.cos(angles)[:, None, :]
    sine = sign * jnp.sin(angles)[:, None, :]
    first = vectors[..., :half]
    second = vectors[..., half:ROT]
    return jnp.concatenate(
        [first * cosine - second * sine, second * cosine + first * sine, vectors[..., ROT:]],
        axis=-1,
    )


def exact_gelu(vectors):
    return jax.nn.gelu(vectors, approximate=False)


def block_logits(queries, keys_block, diagonal):
    logits = jnp.einsum("qhd,khd->hqk", queries, keys_block, preferred_element_type=jnp.float32) * (
        1.0 / math.sqrt(queries.shape[-1])
    )
    if diagonal:
        counter = jnp.arange(queries.shape[0], dtype=jnp.int32)
        allowed = counter[None, :] <= counter[:, None]
        logits = jnp.where(allowed[None], logits, -1e30)
    return logits


def keep_same(state):
    return state


BF = jnp.bfloat16
SHARE = 1.0
F32 = jnp.float32
OUTWARD = [(0, 1), (3, 2)]
MIDDLE = [(1, 2), (2, 1)]
INWARD = [(1, 0), (2, 3)]


def dot(left, right):
    return jnp.dot(left, right, preferred_element_type=F32)


def dot_rows(left, right):
    return lax.dot_general(left, right, (((0,), (0,)), ((), ())), preferred_element_type=F32)


def dot_cols(left, right):
    return lax.dot_general(left, right, (((1,), (1,)), ((), ())), preferred_element_type=F32)


def partner(shard, bit):
    peers = lax.axis_size("dp")
    return lax.ppermute(shard, "dp", [(i, i ^ bit) for i in range(peers)])


def line_hop(shard, pairs):
    return lax.ppermute(shard, "stream", pairs)


def cost(microseconds):
    return pl.CostEstimate(
        flops=int(microseconds * SHARE * 0.9e9),
        bytes_accessed=int(microseconds * SHARE * 3e6),
        transcendentals=0,
    )


def after(value, *others):
    return lax.optimization_barrier((value, *others))[0]


class Gathered:
    def __init__(self, shard, direct=False):
        self.shard = shard
        self.peers = lax.axis_size("dp")
        if self.peers != 8:
            self.by_x = self.by_y = shard
            return
        self.cut = max(range(shard.ndim - 1), key=lambda dim: shard.shape[dim])
        self.by_x = partner(shard, 2)
        self.by_y = partner(shard, 4)
        self.across = partner(shard, 6) if direct else None

    def whole(self, *earlier):
        shard = self.shard
        if self.peers != 8:
            return lax.all_gather(shard, "dp", axis=0)
        index = lax.axis_index("dp")
        cut = self.cut
        half = shard.shape[cut] // 2
        shard, by_x, by_y = [gated(item, earlier) for item in (shard, self.by_x, self.by_y)]
        pieces = [(shard, 0, 0), (by_x, 2, 0), (by_y, 4, 0)]
        if self.across is None:
            low = lax.slice_in_dim(by_y, 0, half, axis=cut)
            high = lax.slice_in_dim(by_x, half, 2 * half, axis=cut)
            pieces += [(partner(low, 2), 6, 0), (partner(high, 4), 6, half)]
        else:
            pieces.append((gated(self.across, earlier), 6, 0))
        pieces += [(partner(piece, 1), code ^ 1, start) for piece, code, start in pieces]
        return put_together(pieces, shard, self.peers, cut, index)


def put_together(pieces, shard, peers, cut, index):
    codes = [(code, start) for _, code, start in pieces]
    arrays = [piece for piece, _, _ in pieces]

    def kernel(place, *refs):
        out, held, sems, sent = refs[-4:]
        owners = {}
        for n, (code, start) in enumerate(codes):
            size = refs[n].shape[cut]
            span = tuple(
                pl.ds(start, size) if dim == cut else slice(None) for dim in range(shard.ndim)
            )
            copy = pltpu.make_async_copy(refs[n], held.at[(code, *span)], sems.at[n])
            copy.start()
            owners.setdefault(code, []).append(copy)
        leaving = []
        for code, copies in owners.items():
            for copy in copies:
                copy.wait()
            copy = pltpu.make_async_copy(held.at[code], out.at[place[0] ^ code], sent.at[code])
            copy.start()
            leaving.append(copy)
        for copy in leaving:
            copy.wait()

    anywhere = pl.BlockSpec(memory_space=pl.ANY)
    size = peers * shard.size * shard.dtype.itemsize
    return pl.pallas_call(
        kernel,
        in_specs=[pl.BlockSpec(memory_space=pltpu.SMEM)] + [anywhere] * len(arrays),
        out_specs=anywhere,
        out_shape=jax.ShapeDtypeStruct((peers, *shard.shape), shard.dtype),
        scratch_shapes=[
            pltpu.VMEM((peers, *shard.shape), shard.dtype),
            pltpu.SemaphoreType.DMA((len(arrays),)),
            pltpu.SemaphoreType.DMA((peers,)),
        ],
        cost_estimate=cost(2 * size / 3e6),
        name="put_together",
    )(index.astype(jnp.int32).reshape(1), *arrays)


def block_spans(tokens):
    sizes = [tokens // 4] * 3 + [tokens // 8] * 2
    return [(sum(sizes[:i]), size) for i, size in enumerate(sizes)]


def along_line(count, first, second, third, finish=None):
    ones, twos, threes, ends = [], [], [], []
    for step in range(count + 2):
        old = []
        if step >= 4:
            old.append(threes[step - 4] if finish is None else ends[step - 4])
        if step < count:
            gates = list(old)
            if step >= 2:
                gates.append(ones[step - 2])
            if step >= 3:
                gates.append(twos[step - 3])
            ones.append(line_hop(first(step, gates), OUTWARD))
        if 0 <= step - 1 < count:
            load = second(step - 1, ones[step - 1])
            twos.append(line_hop(gated(load, old), MIDDLE))
        if 0 <= step - 2 < count:
            back = step - 2
            load = third(back, ones[back], twos[back])
            ahead = ones[back + 2 : back + 3]
            threes.append(line_hop(gated(load, old + ahead), INWARD))
            if finish is not None:
                ends.append(finish(back, ones[back], twos[back], threes[back]))
    return ones, twos, threes


def gated(value, gates):
    return after(value, *gates) if gates else value


def rope_tables(positions, sign):
    half = ROT // 2
    lane = jnp.arange(HD, dtype=jnp.int32)
    counter = (lane % half).astype(F32)
    freqs = jnp.exp(counter * (-2.0 * math.log(10000.0) / ROT))
    angles = positions.astype(F32)[:, None] * freqs[None, :]
    cosine = jnp.where(lane < ROT, jnp.cos(angles), 1.0)
    sine = sign * jnp.sin(angles)
    up = jnp.where(lane < half, -sine, 0.0)
    down = jnp.where((lane >= half) & (lane < ROT), sine, 0.0)
    return jnp.stack([cosine, up, down])


def turned(block, tables):
    half = ROT // 2
    return (
        block * tables[0]
        + pltpu.roll(block, HD - half, 1) * tables[1]
        + pltpu.roll(block, half, 1) * tables[2]
    )


def make_streams(history, mix_rows, gains, biases):
    entries, tokens, width = history.shape
    streams = gains.shape[0]
    rows, sub, lanes = min(64, tokens), 16, 512

    def kernel(hist, mix, gain, bias, normed, unit, inv, last, scratch):
        def step(r, carry):
            here = pl.ds(pl.multiple_of(r * sub, sub), sub)
            weights = mix[here, :]
            columns = [
                [weights[:, s * entries + j : s * entries + j + 1] for j in range(entries)]
                for s in range(streams)
            ]
            for lane in range(0, width, lanes):
                span = slice(lane, lane + lanes)
                sums = [None] * streams
                for j in range(entries):
                    part = hist[j, here, span].astype(F32)
                    for s in range(streams):
                        term = columns[s][j] * part
                        sums[s] = term if j == 0 else sums[s] + term
                for s in range(streams):
                    scratch[s, :, span] = sums[s]
            stds = []
            for s in range(streams):
                values = scratch[s]
                center = values - jnp.sum(values, axis=-1, keepdims=True) * (1.0 / width)
                var = jnp.sum(center * center, axis=-1, keepdims=True) * (1.0 / width)
                std = lax.rsqrt(var + 1e-05)
                stds.append(std)
                scaled = center * std
                unit[s, here, :] = scaled.astype(BF)
                normed[s, here, :] = (scaled * gain[s : s + 1] + bias[s : s + 1]).astype(BF)
            last[here, :] = scratch[streams - 1]
            inv[here, :] = jnp.concatenate(stds, axis=-1)
            return carry

        lax.fori_loop(0, rows // sub, step, 0)

    wide = jax.ShapeDtypeStruct((streams, tokens, width), BF)
    return pl.pallas_call(
        kernel,
        grid=(tokens // rows,),
        in_specs=[
            pl.BlockSpec((entries, rows, width), lambda i: (0, i, 0)),
            pl.BlockSpec((rows, streams * entries), lambda i: (i, 0)),
            pl.BlockSpec((streams, width), lambda i: (0, 0)),
            pl.BlockSpec((streams, width), lambda i: (0, 0)),
        ],
        out_specs=[
            pl.BlockSpec((streams, rows, width), lambda i: (0, i, 0)),
            pl.BlockSpec((streams, rows, width), lambda i: (0, i, 0)),
            pl.BlockSpec((rows, streams), lambda i: (i, 0)),
            pl.BlockSpec((rows, width), lambda i: (i, 0)),
        ],
        out_shape=[
            wide,
            wide,
            jax.ShapeDtypeStruct((tokens, streams), F32),
            jax.ShapeDtypeStruct((tokens, width), F32),
        ],
        scratch_shapes=[pltpu.VMEM((streams, sub, width), F32)],
        cost_estimate=cost(22),
        name="make_streams",
    )(history, mix_rows, gains, biases)


def project(normed, w_heads, tables):
    _, tokens, width = normed.shape
    columns = w_heads.shape[3]
    heads, half = columns // HD, tokens // 2

    def kernel(x, w, table, out):
        flat = dot(x[0], w[...].reshape(width, columns))
        turn = pl.program_id(0) < 2

        def put(head, block):
            out[2 * head, 0] = block[:half].astype(BF)
            out[2 * head + 1, 0] = block[half:].astype(BF)

        @pl.when(turn)
        def _():
            for head in range(heads):
                put(head, turned(flat[:, head * HD : (head + 1) * HD], table[...]))

        @pl.when(jnp.logical_not(turn))
        def _():
            for head in range(heads):
                put(head, flat[:, head * HD : (head + 1) * HD])

    return pl.pallas_call(
        kernel,
        grid=(3,),
        in_specs=[
            pl.BlockSpec((1, tokens, width), lambda c: (c, 0, 0)),
            pl.BlockSpec((w_heads.shape[0], 1, w_heads.shape[2], columns), lambda c: (0, c, 0, 0)),
            pl.BlockSpec((3, tokens, HD), lambda c: (0, 0, 0)),
        ],
        out_specs=pl.BlockSpec((2 * heads, 1, half, HD), lambda c: (0, c, 0, 0)),
        out_shape=jax.ShapeDtypeStruct((2 * heads, 3, half, HD), BF),
        cost_estimate=cost(9),
        name="project",
    )(normed, w_heads, tables)


def attend(own, other, first_key, side):
    shards, _, half, _ = own.shape
    factor = 1.0 / math.sqrt(HD)

    def kernel(first, part, mine, theirs, out, exact, norm):
        s = pl.program_id(0)
        query = mine[s, 0]

        def fold(state, keys, values, mask):
            top, total, acc = state
            logits = dot_cols(query, keys) * factor
            if mask is not None:
                logits = jnp.where(mask, logits, -1e30)
            new_top = jnp.maximum(top, jnp.max(logits, axis=-1, keepdims=True))
            probs = jnp.exp(logits - new_top)
            keep = jnp.exp(top - new_top)
            return (
                new_top,
                total * keep + jnp.sum(probs, axis=-1, keepdims=True),
                acc * keep + dot(probs.astype(BF), values),
            )

        row = lax.broadcasted_iota(jnp.int32, (half, half), 0)
        col = lax.broadcasted_iota(jnp.int32, (half, half), 1)
        state = (
            jnp.full((half, 1), -1e30, F32),
            jnp.zeros((half, 1), F32),
            jnp.zeros((half, HD), F32),
        )
        state = fold(state, mine[s, 1], mine[s, 2], col <= row)
        state = lax.fori_loop(
            0, part[0], lambda i, st: fold(st, theirs[s, 0], theirs[s, 1], None), state
        )

        def shard_step(b, st):
            st = fold(st, mine[b, 1], mine[b, 2], None)
            return fold(st, theirs[b, 0], theirs[b, 1], None)

        top, total, acc = lax.fori_loop(first[s], s, shard_step, state)
        result = acc / total
        out[0] = result.astype(BF)
        exact[0] = result
        norm[0] = top + jnp.log(total)

    return pl.pallas_call(
        kernel,
        grid_spec=pltpu.PrefetchScalarGridSpec(
            num_scalar_prefetch=2,
            grid=(shards,),
            in_specs=[
                pl.BlockSpec((shards, 3, half, HD), lambda s, *_: (0, 0, 0, 0)),
                pl.BlockSpec((shards, 2, half, HD), lambda s, *_: (0, 0, 0, 0)),
            ],
            out_specs=[
                pl.BlockSpec((1, half, HD), lambda s, *_: (s, 0, 0)),
                pl.BlockSpec((1, half, HD), lambda s, *_: (s, 0, 0)),
                pl.BlockSpec((1, half, 1), lambda s, *_: (s, 0, 0)),
            ],
        ),
        out_shape=[
            jax.ShapeDtypeStruct((shards, half, HD), BF),
            jax.ShapeDtypeStruct((shards, half, HD), F32),
            jax.ShapeDtypeStruct((shards, half, 1), F32),
        ],
        cost_estimate=cost(16),
        name="attend",
    )(first_key, side, own, other)


def attend_back(own, other, grads, exact, norm, first_key, side):
    shards, _, half, _ = own.shape
    factor = 1.0 / math.sqrt(HD)

    def kernel(first, part, mine, theirs, grad_ref, exact_ref, norm_ref, kept, given, sums):
        s = pl.program_id(0)
        query = mine[s, 0]
        grad = grad_ref[s]
        delta = jnp.sum(grad.astype(F32) * exact_ref[0], axis=-1, keepdims=True)
        level = norm_ref[0]
        lowered = grad

        @pl.when(s == 0)
        def _():
            sums[...] = jnp.zeros_like(sums)

        def fold(query_grad, keys, values, mask, slot, b):
            logits = dot_cols(query, keys) * factor
            probs = jnp.exp(logits - level)
            if mask is not None:
                probs = jnp.where(mask, probs, 0.0)
            score = (probs * (dot_cols(grad, values) - delta)).astype(BF)
            sums[slot, b] += dot_rows(score, query)
            sums[slot + 1, b] += dot_rows(probs.astype(BF), lowered)
            return query_grad + dot(score, keys)

        row = lax.broadcasted_iota(jnp.int32, (half, half), 0)
        col = lax.broadcasted_iota(jnp.int32, (half, half), 1)
        total = fold(jnp.zeros((half, HD), F32), mine[s, 1], mine[s, 2], col <= row, 0, s)
        total = lax.fori_loop(
            0, part[0], lambda i, q: fold(q, theirs[s, 0], theirs[s, 1], None, 2, s), total
        )

        def shard_step(b, q):
            q = fold(q, mine[b, 1], mine[b, 2], None, 0, b)
            return fold(q, theirs[b, 0], theirs[b, 1], None, 2, b)

        total = lax.fori_loop(first[s], s, shard_step, total)
        kept[s, 0] = (total * factor).astype(BF)

        @pl.when(s == shards - 1)
        def _():
            for b in range(shards):
                kept[b, 1] = (sums[0, b] * factor).astype(BF)
                kept[b, 2] = sums[1, b].astype(BF)
                given[b, 0] = (sums[2, b] * factor).astype(BF)
                given[b, 1] = sums[3, b].astype(BF)

    whole = lambda n: pl.BlockSpec((shards, n, half, HD), lambda s, *_: (0, 0, 0, 0))
    return pl.pallas_call(
        kernel,
        grid_spec=pltpu.PrefetchScalarGridSpec(
            num_scalar_prefetch=2,
            grid=(shards,),
            in_specs=[
                whole(3),
                whole(2),
                pl.BlockSpec((shards, half, HD), lambda s, *_: (0, 0, 0)),
                pl.BlockSpec((1, half, HD), lambda s, *_: (s, 0, 0)),
                pl.BlockSpec((1, half, 1), lambda s, *_: (s, 0, 0)),
            ],
            out_specs=[whole(3), whole(2)],
            scratch_shapes=[pltpu.VMEM((4, shards, half, HD), F32)],
        ),
        out_shape=[
            jax.ShapeDtypeStruct((shards, 3, half, HD), BF),
            jax.ShapeDtypeStruct((shards, 2, half, HD), BF),
        ],
        cost_estimate=cost(22),
        name="attend_back",
    )(first_key, side, own, other, grads, exact, norm)


def norm_back(grad, unit, inv, gain, extra):
    width = grad.shape[1]
    scaled = grad * gain
    mean = jnp.sum(scaled, axis=-1, keepdims=True) * (1.0 / width)
    slope = jnp.sum(scaled * unit, axis=-1, keepdims=True) * (1.0 / width)
    result = inv * (scaled - mean - unit * slope)
    return result if extra is None else result + extra


def heads_back(parts, w_heads, normed, unit, inv, gains, tables, spans):
    _, tokens, width = normed.shape
    columns = w_heads.shape[3]
    heads, half = columns // HD, tokens // 2
    count = len(spans)

    def kernel(part, w, x, u, istd, gain, table, *refs):
        pieces, (stream, weight, stats, grad, wide) = refs[:count], refs[count:]
        c = pl.program_id(0)
        turn = c < 2

        def take(head):
            return jnp.concatenate([part[2 * head, 0], part[2 * head + 1, 0]], axis=0).astype(F32)

        @pl.when(turn)
        def _():
            for head in range(heads):
                grad[:, head * HD : (head + 1) * HD] = turned(take(head), table[...]).astype(BF)

        @pl.when(jnp.logical_not(turn))
        def _():
            for head in range(heads):
                grad[:, head * HD : (head + 1) * HD] = take(head).astype(BF)

        wide[...] = dot_cols(grad[...], w[...].reshape(width, columns))
        weight[0] = dot_rows(x[0], grad[...]).astype(BF)
        stats[...] = jnp.zeros_like(stats)
        for r, (start, block) in enumerate(spans):
            column = lax.broadcasted_iota(jnp.int32, (block, istd.shape[1]), 1)
            here = slice(start, start + block)
            values = wide[here, :]
            units = u[0, here, :].astype(F32)
            std = jnp.sum(jnp.where(column == c, istd[here, :], 0.0), axis=-1, keepdims=True)
            result = norm_back(values, units, std, gain[0], None).astype(BF)
            stream[0, here, :] = result
            pieces[r][0] = result
            stats[0, 0:1] += jnp.sum(values * units, axis=0, keepdims=True)
            stats[0, 1:2] += jnp.sum(values, axis=0, keepdims=True)

    return pl.pallas_call(
        kernel,
        grid=(3,),
        in_specs=[
            pl.BlockSpec((2 * heads, 1, half, HD), lambda c: (0, c, 0, 0)),
            pl.BlockSpec((w_heads.shape[0], 1, w_heads.shape[2], columns), lambda c: (0, c, 0, 0)),
            pl.BlockSpec((1, tokens, width), lambda c: (c, 0, 0)),
            pl.BlockSpec((1, tokens, width), lambda c: (c, 0, 0)),
            pl.BlockSpec((tokens, inv.shape[1]), lambda c: (0, 0)),
            pl.BlockSpec((1, 1, width), lambda c: (c, 0, 0)),
            pl.BlockSpec((3, tokens, HD), lambda c: (0, 0, 0)),
        ],
        out_specs=[pl.BlockSpec((1, block, width), lambda c: (c, 0, 0)) for _, block in spans]
        + [
            pl.BlockSpec((1, tokens, width), lambda c: (c, 0, 0)),
            pl.BlockSpec((1, width, columns), lambda c: (c, 0, 0)),
            pl.BlockSpec((1, 2, width), lambda c: (c, 0, 0)),
        ],
        out_shape=[jax.ShapeDtypeStruct((3, block, width), BF) for _, block in spans]
        + [
            jax.ShapeDtypeStruct((3, tokens, width), BF),
            jax.ShapeDtypeStruct((3, width, columns), BF),
            jax.ShapeDtypeStruct((3, 2, width), F32),
        ],
        scratch_shapes=[pltpu.VMEM((tokens, columns), BF), pltpu.VMEM((tokens, width), F32)],
        cost_estimate=cost(3),
        name="heads_back",
    )(parts, w_heads, normed, unit, inv, gains[:, None, :], tables)


def last_back(grad, unit, inv, gain, extra, flag):
    tokens, width = grad.shape
    block = min(128, tokens)

    def kernel(g, u, istd, gain_ref, e, flag_ref, stream, stats):
        @pl.when(pl.program_id(0) == 0)
        def _():
            stats[...] = jnp.zeros_like(stats)

        values = g[...]
        units = u[...].astype(F32)
        std = istd[...][:, -1:]
        added = e[...].astype(F32) * flag_ref[0]
        stream[...] = norm_back(values, units, std, gain_ref[...], added).astype(BF)
        stats[0:1] += jnp.sum(values * units, axis=0, keepdims=True)
        stats[1:2] += jnp.sum(values, axis=0, keepdims=True)

    row = lambda n: pl.BlockSpec((block, n), lambda i: (i, 0))
    return pl.pallas_call(
        kernel,
        grid=(tokens // block,),
        in_specs=[
            row(width),
            row(width),
            row(inv.shape[1]),
            pl.BlockSpec((1, width), lambda i: (0, 0)),
            row(width),
            pl.BlockSpec(memory_space=pltpu.SMEM),
        ],
        out_specs=[row(width), pl.BlockSpec((2, width), lambda i: (0, 0))],
        out_shape=[
            jax.ShapeDtypeStruct((tokens, width), BF),
            jax.ShapeDtypeStruct((2, width), F32),
        ],
        cost_estimate=cost(7),
        name="last_back",
    )(grad, unit, inv, gain, extra, flag)


def mixing_back(heads_part, last_part, history, which, of):
    entries, tokens, width = history.shape
    streams = heads_part.shape[0] + 1
    rows, sub, lanes = min(64, tokens // of), 16, 256
    steps = tokens // of // rows
    base = which * steps

    def kernel(first, last, hist, out):
        def step(r, carry):
            here = pl.ds(pl.multiple_of(r * sub, sub), sub)
            for s in range(streams):
                sums = [None] * entries
                for lane in range(0, width, lanes):
                    span = slice(lane, lane + lanes)
                    part = first[s, here, span] if s < streams - 1 else last[here, span]
                    part = part.astype(F32)
                    for j in range(entries):
                        term = part * hist[j, here, span].astype(F32)
                        sums[j] = term if lane == 0 else sums[j] + term
                columns = [jnp.sum(item, axis=-1, keepdims=True) for item in sums]
                out[s, here, :] = jnp.concatenate(columns, axis=-1)
            return carry

        lax.fori_loop(0, rows // sub, step, 0)

    return pl.pallas_call(
        kernel,
        grid=(steps,),
        in_specs=[
            pl.BlockSpec((streams - 1, rows, width), lambda i: (0, base + i, 0)),
            pl.BlockSpec((rows, width), lambda i: (base + i, 0)),
            pl.BlockSpec((entries, rows, width), lambda i: (0, base + i, 0)),
        ],
        out_specs=pl.BlockSpec((streams, rows, entries), lambda i: (0, i, 0)),
        out_shape=jax.ShapeDtypeStruct((streams, tokens // of, entries), F32),
        cost_estimate=cost(0.4),
        name="mixing_back",
    )(heads_part, last_part, history)


def far_attend(queries, keys, values, shard_offset):
    tokens, heads_here, head_size = queries.shape
    data_index = lax.axis_index("dp")
    pairs = [jnp.stack([keys, values])]
    reach = 2 * SEQ // tokens
    for back in range(1, reach):
        pairs.append(passed_along(pairs[0], "dp", back))
    usable = [(shard_offset[0] >= back * tokens) & (data_index >= back) for back in range(reach)]
    first_logits = block_logits(queries, keys, True)
    top = jnp.max(first_logits, axis=-1)
    total = jnp.sum(jnp.exp(first_logits - top[..., None]), axis=-1)
    for back in range(1, reach):

        def widen(state, block=pairs[back][0]):
            logits = block_logits(queries, block, False)
            new_top = jnp.maximum(state[0], jnp.max(logits, axis=-1))
            summed = state[1] * jnp.exp(state[0] - new_top) + jnp.sum(
                jnp.exp(logits - new_top[..., None]), axis=-1
            )
            return (new_top, summed)

        top, total = lax.cond(usable[back], widen, keep_same, (top, total))
    log_total = top + jnp.log(total)
    attended = jnp.zeros((tokens, heads_here, head_size), F32)
    for back in range(reach):

        def accumulate(current, block=pairs[back], diagonal=back == 0):
            probs = jnp.exp(block_logits(queries, block[0], diagonal) - log_total[..., None])
            return current + jnp.einsum(
                "hqk,khd->qhd", probs.astype(BF), block[1], preferred_element_type=F32
            )

        attended = lax.cond(usable[back], accumulate, keep_same, attended)
    return attended, (pairs, usable, log_total)


def far_attend_back(queries, attended_grad, kept):
    tokens, heads_here, head_size = queries.shape
    factor = 1.0 / math.sqrt(head_size)
    pairs, usable, log_total = kept
    reach = len(pairs)

    def weights_of(block, diagonal):
        return jnp.exp(block_logits(queries, block, diagonal) - log_total[..., None])

    def prob_grads(block):
        return jnp.einsum("qhd,khd->hqk", attended_grad, block[1], preferred_element_type=F32)

    delta = jnp.zeros((heads_here, tokens), F32)
    for back in range(reach):

        def gather_delta(current, block=pairs[back], diagonal=back == 0):
            return current + jnp.sum(weights_of(block[0], diagonal) * prob_grads(block), axis=-1)

        delta = lax.cond(usable[back], gather_delta, keep_same, delta)

    def skip_block(current):
        return (current, jnp.zeros((2, tokens, heads_here, head_size), F32))

    query_grad = jnp.zeros((tokens, heads_here, head_size), F32)
    key_value_grad = jnp.zeros((2, tokens, heads_here, head_size), F32)
    for back in range(reach):

        def spread(current, block=pairs[back], diagonal=back == 0):
            probs = weights_of(block[0], diagonal)
            score_grad = (probs * (prob_grads(block) - delta[..., None])).astype(BF)
            query_part = (
                current
                + jnp.einsum("hqk,khd->qhd", score_grad, block[0], preferred_element_type=F32)
                * factor
            )
            key_part = (
                jnp.einsum("hqk,qhd->khd", score_grad, queries, preferred_element_type=F32)
                * factor
            )
            value_part = jnp.einsum(
                "hqk,qhd->khd", probs.astype(BF), attended_grad, preferred_element_type=F32
            )
            return (query_part, jnp.stack([key_part, value_part]))

        query_grad, pair_grad = lax.cond(usable[back], spread, skip_block, query_grad)
        if back == 0:
            key_value_grad = pair_grad
        else:
            key_value_grad = key_value_grad + passed_along(pair_grad, "dp", -back)
    return jnp.concatenate([query_grad[None], key_value_grad])


def mix_block(start, coefficients, shares, last_share, extras, last_extras, arrived, whole):
    streams, block, width = shares.shape
    each = coefficients.shape[1] // (streams + 1)
    groups = 1 + len(extras)
    final = arrived is not None
    lanes = 512

    def kernel(*refs):
        weights = refs[0][...]
        heads, lasts = refs[1 : 1 + groups], refs[1 + groups : 1 + 2 * groups]
        out = refs[-2] if final else refs[-1]
        if final:
            refs[-1][...] = jnp.zeros_like(refs[-1])
        columns = [weights[:, n : n + 1] for n in range(weights.shape[1])]
        for lane in range(0, width, lanes):
            span = slice(lane, lane + lanes)
            values = []
            for s in range(streams + 1):
                picks = [r[s, :, span] if s < streams else l[:, span] for r, l in zip(heads, lasts)]
                total = picks[0].astype(F32)
                for pick in picks[1:]:
                    total = total + pick.astype(F32)
                values.append(total)
            for e in range(each):
                total = columns[e * (streams + 1)] * values[0]
                for s in range(1, streams + 1):
                    total = total + columns[e * (streams + 1) + s] * values[s]
                if final:
                    total = total + refs[1 + 2 * groups][e, :, span].astype(F32)
                out[e, :, span] = total.astype(out.dtype)

    i = start // block
    piece = pl.BlockSpec((streams, block, width), lambda n: (0, 0, 0))
    rows = [
        pl.BlockSpec((block, width), lambda n, at=start % item.shape[0] // block: (at, 0))
        for item in (last_share, *last_extras)
    ]
    small = pl.BlockSpec((each, block, width), lambda n: (0, 0, 0))
    specs = [pl.BlockSpec((block, coefficients.shape[1]), lambda n: (i, 0))]
    specs += [piece] * groups + rows
    args = [coefficients, shares, *extras, last_share, *last_extras]
    alias = {}
    if final:
        specs.append(small)
        args.append(arrived)
        if whole is not None:
            specs.append(pl.BlockSpec(memory_space=pl.ANY))
            args.append(whole)
            alias = {len(args) - 1: 0}
        out_spec = [
            pl.BlockSpec((each, block, width), lambda n: (0, i, 0)),
            pl.BlockSpec((8, 128), lambda n: (0, 0)),
        ]
        out_shape = [
            jax.ShapeDtypeStruct((each, coefficients.shape[0], width), F32),
            jax.ShapeDtypeStruct((8, 128), F32),
        ]
    else:
        out_spec, out_shape = small, jax.ShapeDtypeStruct((each, block, width), BF)
    return pl.pallas_call(
        kernel,
        grid=(1,),
        in_specs=specs,
        out_specs=out_spec,
        out_shape=out_shape,
        input_output_aliases=alias,
        cost_estimate=cost(0.4),
        name="mix_final" if final else "mix_inward",
    )(*args)


def hidden_units(x, w_up):
    tokens, width = x.shape
    units = w_up.shape[1]
    block = min(512, units)

    def kernel(x_ref, w, out, slope):
        up = dot(x_ref[...], w[...])
        inside = 0.5 * (1.0 + lax.erf(up * math.sqrt(0.5)))
        out[...] = (up * inside).astype(BF)
        bell = jnp.exp(-0.5 * up * up) * (1.0 / math.sqrt(2.0 * math.pi))
        slope[...] = (inside + up * bell).astype(BF)

    column = pl.BlockSpec((tokens, block), lambda i: (0, i))
    return pl.pallas_call(
        kernel,
        grid=(units // block,),
        in_specs=[
            pl.BlockSpec((tokens, width), lambda i: (0, 0)),
            pl.BlockSpec((width, block), lambda i: (0, i)),
        ],
        out_specs=[column, column],
        out_shape=[jax.ShapeDtypeStruct((tokens, units), BF)] * 2,
        cost_estimate=cost(9),
        name="hidden_units",
    )(x, w_up)


def merge_branches(attended, hidden, w_merge, w_down, stream, flag):
    tokens, inner = attended.shape
    shards, units, cols = w_down.shape
    members = lax.axis_size("stream")
    each = shards // members
    if cols % 128:
        merged = jnp.einsum("te,ned->tnd", attended, w_merge, preferred_element_type=F32)
        merged = merged + jnp.einsum("tf,nfd->tnd", hidden, w_down, preferred_element_type=F32)
        merged = merged.reshape(tokens, -1) + flag * stream
        return jnp.transpose(merged.reshape(tokens, members, -1), (1, 0, 2)).astype(BF)

    def kernel(a, h, wm, wd, st, flag_ref, out):
        out[0] = (dot(a[...], wm[0]) + dot(h[...], wd[0]) + flag_ref[0] * st[...]).astype(BF)

    return pl.pallas_call(
        kernel,
        grid=(shards,),
        in_specs=[
            pl.BlockSpec((tokens, inner), lambda n: (0, 0)),
            pl.BlockSpec((tokens, units), lambda n: (0, 0)),
            pl.BlockSpec((1, inner, cols), lambda n: (n, 0, 0)),
            pl.BlockSpec((1, units, cols), lambda n: (n, 0, 0)),
            pl.BlockSpec((tokens, cols), lambda n: (0, n)),
            pl.BlockSpec(memory_space=pltpu.SMEM),
        ],
        out_specs=pl.BlockSpec((1, tokens, cols), lambda n: (n // each, 0, n % each)),
        out_shape=jax.ShapeDtypeStruct((members, tokens, each * cols), BF),
        cost_estimate=cost(13),
        name="merge_branches",
    )(attended, hidden, w_merge, w_down, stream, flag)


def back_through(grad, stacked, slope):
    tokens = grad.shape[0]
    shards, units, cols = stacked.shape
    if cols % 128:
        split = grad.reshape(tokens, shards, cols)
        total = jnp.einsum("tnd,nfd->tf", split, stacked, preferred_element_type=F32)
        return (total if slope is None else total * slope.astype(F32)).astype(BF)

    def kernel(*refs):
        g, w = refs[:2]
        out, acc = refs[-2:]
        n = pl.program_id(0)
        part = dot_cols(g[...], w[0])

        @pl.when(n == 0)
        def _():
            acc[...] = part

        @pl.when(n > 0)
        def _():
            acc[...] += part

        @pl.when(n == shards - 1)
        def _():
            total = acc[...]
            if slope is not None:
                total = total * refs[2][...].astype(F32)
            out[...] = total.astype(BF)

    specs = [
        pl.BlockSpec((tokens, cols), lambda n: (0, n)),
        pl.BlockSpec((1, units, cols), lambda n: (n, 0, 0)),
    ]
    args = [grad, stacked]
    if slope is not None:
        specs.append(pl.BlockSpec((tokens, units), lambda n: (0, 0)))
        args.append(slope)
    return pl.pallas_call(
        kernel,
        grid=(shards,),
        in_specs=specs,
        out_specs=pl.BlockSpec((tokens, units), lambda n: (0, 0)),
        out_shape=jax.ShapeDtypeStruct((tokens, units), BF),
        scratch_shapes=[pltpu.VMEM((tokens, units), F32)],
        cost_estimate=cost(13 if slope is not None else 7),
        name="back_through",
    )(*args)


def body(
    history,
    mixing,
    shard_offset,
    norm_gain,
    norm_bias,
    w_heads,
    w_merge,
    w_up,
    w_down,
    mixer_first,
    mixer_second,
    out_cotangent,
    next_cotangent,
):
    member = lax.axis_index("stream")
    members = lax.axis_size("stream")
    shards = lax.axis_size("dp")
    index = lax.axis_index("dp")
    entries, tokens, width = history.shape
    heads_here = w_heads.shape[2] // HD
    half = tokens // 2
    highest = lax.Precision.HIGHEST
    flag = (member == members - 1).astype(F32)
    flags = flag.reshape(1)
    near = shards == 8 and heads_here * 2 == shards and tokens * shards == 2 * SEQ

    if near:
        spread = jnp.broadcast_to(shard_offset[:, None], (8, 128))
        offsets = lax.all_gather(spread, "dp", axis=0)[:, 0, 0]
        w_heads = after(w_heads, offsets)
    got_heads = Gathered(w_heads, direct=near)
    lanes = jnp.concatenate([norm_gain, norm_bias]).astype(F32).reshape(tokens, -1)
    first_rows = mixer_first.astype(F32).reshape(tokens, -1)
    second_flat = mixer_second[:, 0, :].astype(F32).reshape(-1)
    hidden_count = mixer_second.shape[0]
    lines = -(-second_flat.shape[0] // tokens)
    second_rows = jnp.pad(second_flat, (0, lines * tokens - second_flat.shape[0]))
    outputs = next_cotangent.shape[2]
    arrays = [mixing[:, 0, :], lanes, next_cotangent[:, 0, :], first_rows]
    arrays.append(second_rows.reshape(tokens, lines))
    packed = lax.all_gather(jnp.concatenate(arrays, axis=1), "stream", axis=0)
    parts, place = [], 0
    for array in arrays:
        parts.append(packed[:, :, place : place + array.shape[1]])
        place += array.shape[1]
    mix_all, norms, next_full, first_full, second_full = parts
    norms = norms.reshape(members, 2, width)
    first_full = first_full.astype(BF).reshape(width, -1)
    second_full = second_full.reshape(members, -1)[:, : second_flat.shape[0]]
    second_full = second_full.reshape(members, hidden_count, outputs)
    if near:
        early = (got_heads.by_x, got_heads.by_y, got_heads.across)
        history = after(history, *early)
        w_up, w_merge = after(w_up, *early[:2]), after(w_merge, *early[:2])
    got_up = Gathered(w_up)
    got_merge = Gathered(w_merge, direct=near)
    gains, biases = norms[:, 0], norms[:, 1]
    mix_rows = jnp.transpose(mix_all, (1, 0, 2)).reshape(tokens, members * entries)

    normed, unit, inv, stream = make_streams(history, mix_rows, gains, biases)
    full_heads = got_heads.whole()
    cotangent = lax.all_gather(after(out_cotangent, inv), "stream", axis=1, tiled=True)
    positions = shard_offset[0] + jnp.arange(tokens, dtype=jnp.int32)
    projected = project(after(normed, got_up.by_x, got_up.by_y), full_heads, rope_tables(positions, 1.0))

    if near:
        side = (index % 2).astype(jnp.int32).reshape(1)
        place = jnp.arange(shards, dtype=jnp.int32)
        first_key = jnp.maximum(place - offsets // tokens, 0).astype(jnp.int32)
        own = lax.all_to_all(projected, "dp", 0, 0, tiled=True)
        got_down = Gathered(after(w_down, own))
        other = partner(own[:, 1:], 1)
        result, exact, level = attend(own, other, first_key, side)
        full_up = got_up.whole(result)
        full_merge = got_merge.whole(result)
        back = lax.all_to_all(result, "dp", 0, 0, tiled=True)
        attended = jnp.transpose(back.reshape(heads_here, tokens, HD), (1, 0, 2)).reshape(tokens, -1)
    else:
        got_down = Gathered(w_down)
        full_up = got_up.whole()
        full_merge = got_merge.whole()
        split = projected.reshape(heads_here, 2, 3, half, HD)
        split = jnp.transpose(split, (2, 1, 3, 0, 4)).reshape(3, tokens, heads_here, HD)
        result, kept = far_attend(split[0], split[1], split[2], shard_offset)
        attended = result.reshape(tokens, -1).astype(BF)
    full_down = got_down.whole(result)
    flat_up = full_up.reshape(width, -1)
    hidden, slope = hidden_units(normed[members - 1], flat_up)
    attended = after(attended, hidden)
    hidden = after(hidden, cotangent)
    share = merge_branches(attended, hidden, full_merge, full_down, stream, flags)

    columns = lax.all_to_all(share, "stream", 0, 0, tiled=True)
    block_out = jnp.sum(columns.astype(F32), axis=0).astype(BF)
    block_full = lax.all_gather(block_out, "stream", axis=1, tiled=True)
    out_float = block_full.astype(F32)
    scale = lax.rsqrt(jnp.sum(out_float * out_float, axis=-1) / width + 1e-06)
    proj = dot(block_full, first_full)
    mixer, mixer_back = jax.vjp(exact_gelu, scale[:, None] * proj)
    second_here = mixer_second[:, 0, :].astype(F32)
    next_here = jnp.dot(mixer, second_here, precision=highest, preferred_element_type=F32)
    mixer_grad = jnp.einsum(
        "stn,scn->tc", next_full, second_full, precision=highest, preferred_element_type=F32
    )
    pre_grad = mixer_back(mixer_grad)[0]
    proj_grad = (scale[:, None] * pre_grad).astype(BF)
    scale_grad = jnp.sum(pre_grad * proj, axis=-1)
    second_local = jnp.dot(
        mixer.T, next_cotangent[:, 0, :], precision=highest, preferred_element_type=F32
    )
    first_local = dot_rows(block_out, proj_grad)
    grad_out = (
        cotangent.astype(F32)
        + dot_cols(proj_grad, first_full)
        - (scale * scale * scale * scale_grad)[:, None] * out_float / width
    ).astype(BF)

    attended_grad = back_through(grad_out, full_merge, None)
    up_grad = back_through(grad_out, full_down, slope)
    down_grad = dot_rows(hidden, grad_out).astype(BF)
    grad_down = lax.psum_scatter(down_grad, "dp", scatter_dimension=1, tiled=True).astype(F32)
    last_normed = dot_cols(after(up_grad, down_grad), flat_up)
    last_share, last_stats = last_back(
        last_normed, unit[members - 1], inv, gains[members - 1 :], grad_out, flags
    )
    last_hop = line_hop(last_share, OUTWARD)
    last_sum = (last_share.astype(F32) + last_hop.astype(F32)).astype(BF)
    last_next = line_hop(last_sum, MIDDLE)
    if near:
        sent = attended_grad.reshape(tokens, heads_here, HD)
        sent = jnp.transpose(sent, (1, 0, 2)).reshape(shards, half, HD)
        grads = lax.all_to_all(sent, "dp", 0, 0, tiled=True)
        grads = after(grads, last_share)
        kept_grads, given = attend_back(own, other, grads, exact, level, first_key, side)
        taken = partner(given, 1)
        summed = kept_grads[:, 1:].astype(F32) + taken.astype(F32)
        pair = jnp.concatenate([kept_grads[:, :1], summed.astype(BF)], axis=1)
        pair = after(pair, last_hop)
        late_grad, late_up = after(grad_out, pair), after(up_grad, pair)
        up_back = dot_rows(normed[members - 1], late_up).astype(BF)
        merge_grad = dot_rows(attended, late_grad).astype(BF)
        parts = lax.all_to_all(pair, "dp", 0, 0, tiled=True)
    else:
        up_back = dot_rows(normed[members - 1], up_grad).astype(BF)
        merge_grad = dot_rows(attended, grad_out).astype(BF)
        grads = far_attend_back(split[0], attended_grad.reshape(tokens, heads_here, HD), kept)
        parts = grads.reshape(3, 2, half, heads_here, HD)
        parts = jnp.transpose(parts, (3, 1, 0, 2, 4)).reshape(2 * heads_here, 3, half, HD)

    parts = after(parts, last_sum, grad_down, up_back, merge_grad)
    spans = block_spans(tokens)
    *pieces, heads_share, heads_grad, heads_stats = heads_back(
        parts, full_heads, normed, unit, inv, gains, rope_tables(positions, -1.0), spans
    )

    grad_merge = lax.psum_scatter(merge_grad, "dp", scatter_dimension=1, tiled=True).astype(F32)
    grad_heads = lax.psum_scatter(heads_grad, "dp", scatter_dimension=1, tiled=True).astype(F32)
    grad_up = lax.psum_scatter(up_back, "dp", scatter_dimension=0, tiled=True).astype(F32)

    each = entries // members

    def weights_for(owner):
        block = lax.dynamic_slice_in_dim(mix_all, owner * each, each, axis=2)
        return jnp.transpose(block, (1, 2, 0)).reshape(tokens, each * members)

    there = weights_for(jnp.where(member == 1, 0, members - 1))
    here = weights_for(member)
    extra = {}

    last_one = lambda i: last_hop
    last_two = lambda i: last_next

    def first_hop(i, gates):
        gates = list(gates)
        if i == 3:
            gates.append(grad_merge)
        return gated(pieces[i], gates)

    def small_sums():
        stats = jnp.concatenate([heads_stats, last_stats[None]]).reshape(members, tokens, -1)
        both = jnp.concatenate([jnp.concatenate(mixes, axis=1), stats], axis=2)
        both = jnp.sum(lax.all_to_all(both, "stream", 0, 0, tiled=True), axis=0)
        second_sums = jnp.pad(second_local.reshape(-1), (0, lines * tokens - second_flat.shape[0]))
        local = [both[:, entries:], first_local.reshape(tokens, -1), second_sums.reshape(tokens, lines)]
        everyone = lax.all_gather(jnp.concatenate(local, axis=1), "dp", axis=0)
        return both[:, :entries], jnp.sum(everyone, axis=0)

    mixes = [mixing_back(heads_share, last_share, history, i, 2) for i in range(2)]

    extra["both"], extra["all"] = small_sums()

    def second_hop(i, one):
        load = (pieces[i].astype(F32) + one.astype(F32)).astype(BF)
        return after(load, *mixes) if i == 0 else load

    def third_hop(i, one, two):
        load = mix_block(spans[i][0], there, pieces[i], last_share, [two], [last_two(i)], None, None)
        return after(load, extra["both" if i == 0 else "all"]) if i < 2 else load

    def finish(i, one, two, three):
        if i == 3:
            three = after(three, grad_heads)
        extra["history"], token = mix_block(
            spans[i][0],
            here,
            pieces[i],
            last_share,
            [one, two],
            [last_one(i), last_two(i)],
            three,
            extra.get("history"),
        )
        return token

    along_line(len(spans), first_hop, second_hop, third_hop, finish)
    grad_history = extra["history"]

    grad_mixing = extra["both"][:, None, :]
    sums = extra["all"]
    columns = 2 * width // tokens
    stats = sums[:, :columns].reshape(2, width)
    grad_first = sums[:, columns:-lines].reshape(mixer_first.shape)
    grad_second = sums[:, -lines:].reshape(-1)[: second_flat.shape[0]].reshape(hidden_count, outputs)
    return (
        block_out,
        next_here[:, None, :],
        grad_history,
        grad_mixing,
        stats[:1],
        stats[1:],
        grad_heads,
        grad_merge,
        grad_up,
        grad_down,
        grad_first,
        grad_second[:, None, :],
    )


def solution(mesh):
    in_specs = (
        P(None, "dp", None),
        P("dp", "stream", None),
        P("dp"),
        P("stream", None),
        P("stream", None),
        P(None, "dp", "stream"),
        P("stream", "dp"),
        P("dp", "stream"),
        P("stream", "dp"),
        P("stream", None),
        P(None, "stream", None),
        P("dp", "stream"),
        P("dp", "stream", None),
    )
    out_specs = (
        P("dp", "stream"),
        P("dp", "stream", None),
        P("stream", "dp", None),
        P("dp", "stream", None),
        P("stream", None),
        P("stream", None),
        P(None, "dp", "stream"),
        P("stream", "dp"),
        P("dp", "stream"),
        P("stream", "dp"),
        P("stream", None),
        P(None, "stream", None),
    )
    return jax.shard_map(body, mesh=mesh, in_specs=in_specs, out_specs=out_specs, check_vma=False)
```

```python
import math

import jax
import jax.numpy as jnp
from jax import lax
from jax.experimental import pallas as pl
from jax.experimental.pallas import tpu as pltpu
from jax.sharding import PartitionSpec as P

HD = 128
ROT = 32
SEQ = 2048


def passed_along(shard, axis, by):
    peers = lax.axis_size(axis)
    pairs = [(i, i + by) for i in range(peers) if 0 <= i + by < peers]
    return lax.ppermute(shard, axis, pairs)


def rotate(vectors, positions, sign):
    half = ROT // 2
    counter = jnp.arange(half, dtype=jnp.float32)
    freqs = jnp.exp(counter * (-2.0 * math.log(10000.0) / ROT))
    angles = positions.astype(jnp.float32)[:, None] * freqs[None, :]
    cosine = jnp.cos(angles)[:, None, :]
    sine = sign * jnp.sin(angles)[:, None, :]
    first = vectors[..., :half]
    second = vectors[..., half:ROT]
    return jnp.concatenate(
        [first * cosine - second * sine, second * cosine + first * sine, vectors[..., ROT:]],
        axis=-1,
    )


def exact_gelu(vectors):
    return jax.nn.gelu(vectors, approximate=False)


def block_logits(queries, keys_block, diagonal):
    logits = jnp.einsum("qhd,khd->hqk", queries, keys_block, preferred_element_type=jnp.float32) * (
        1.0 / math.sqrt(queries.shape[-1])
    )
    if diagonal:
        counter = jnp.arange(queries.shape[0], dtype=jnp.int32)
        allowed = counter[None, :] <= counter[:, None]
        logits = jnp.where(allowed[None], logits, -1e30)
    return logits


def keep_same(state):
    return state


BF = jnp.bfloat16
SHARE = 1.0
F32 = jnp.float32
OUTWARD = [(0, 1), (3, 2)]
MIDDLE = [(1, 2), (2, 1)]
INWARD = [(1, 0), (2, 3)]


def dot(left, right):
    return jnp.dot(left, right, preferred_element_type=F32)


def dot_rows(left, right):
    return lax.dot_general(left, right, (((0,), (0,)), ((), ())), preferred_element_type=F32)


def dot_cols(left, right):
    return lax.dot_general(left, right, (((1,), (1,)), ((), ())), preferred_element_type=F32)


def partner(shard, bit):
    peers = lax.axis_size("dp")
    return lax.ppermute(shard, "dp", [(i, i ^ bit) for i in range(peers)])


def line_hop(shard, pairs):
    return lax.ppermute(shard, "stream", pairs)


def cost(microseconds):
    return pl.CostEstimate(
        flops=int(microseconds * SHARE * 0.9e9),
        bytes_accessed=int(microseconds * SHARE * 3e6),
        transcendentals=0,
    )


def after(value, *others):
    return lax.optimization_barrier((value, *others))[0]


class Gathered:
    def __init__(self, shard, direct=False):
        self.shard = shard
        self.peers = lax.axis_size("dp")
        if self.peers != 8:
            self.by_x = self.by_y = shard
            return
        self.cut = max(range(shard.ndim - 1), key=lambda dim: shard.shape[dim])
        self.by_x = partner(shard, 2)
        self.by_y = partner(shard, 4)
        self.across = partner(shard, 6) if direct else None

    def whole(self, *earlier):
        shard = self.shard
        if self.peers != 8:
            return lax.all_gather(shard, "dp", axis=0)
        index = lax.axis_index("dp")
        cut = self.cut
        half = shard.shape[cut] // 2
        shard, by_x, by_y = [gated(item, earlier) for item in (shard, self.by_x, self.by_y)]
        pieces = [(shard, 0, 0), (by_x, 2, 0), (by_y, 4, 0)]
        if self.across is None:
            low = lax.slice_in_dim(by_y, 0, half, axis=cut)
            high = lax.slice_in_dim(by_x, half, 2 * half, axis=cut)
            pieces += [(partner(low, 2), 6, 0), (partner(high, 4), 6, half)]
        else:
            pieces.append((gated(self.across, earlier), 6, 0))
        pieces += [(partner(piece, 1), code ^ 1, start) for piece, code, start in pieces]
        return put_together(pieces, shard, self.peers, cut, index)


def put_together(pieces, shard, peers, cut, index):
    codes = [(code, start) for _, code, start in pieces]
    arrays = [piece for piece, _, _ in pieces]

    def kernel(place, *refs):
        out, held, sems, sent = refs[-4:]
        owners = {}
        for n, (code, start) in enumerate(codes):
            size = refs[n].shape[cut]
            span = tuple(
                pl.ds(start, size) if dim == cut else slice(None) for dim in range(shard.ndim)
            )
            copy = pltpu.make_async_copy(refs[n], held.at[(code, *span)], sems.at[n])
            copy.start()
            owners.setdefault(code, []).append(copy)
        leaving = []
        for code, copies in owners.items():
            for copy in copies:
                copy.wait()
            copy = pltpu.make_async_copy(held.at[code], out.at[place[0] ^ code], sent.at[code])
            copy.start()
            leaving.append(copy)
        for copy in leaving:
            copy.wait()

    anywhere = pl.BlockSpec(memory_space=pl.ANY)
    size = peers * shard.size * shard.dtype.itemsize
    return pl.pallas_call(
        kernel,
        in_specs=[pl.BlockSpec(memory_space=pltpu.SMEM)] + [anywhere] * len(arrays),
        out_specs=anywhere,
        out_shape=jax.ShapeDtypeStruct((peers, *shard.shape), shard.dtype),
        scratch_shapes=[
            pltpu.VMEM((peers, *shard.shape), shard.dtype),
            pltpu.SemaphoreType.DMA((len(arrays),)),
            pltpu.SemaphoreType.DMA((peers,)),
        ],
        cost_estimate=cost(2 * size / 3e6),
        name="put_together",
    )(index.astype(jnp.int32).reshape(1), *arrays)


def block_spans(tokens):
    sizes = [tokens // 4] * 3 + [tokens // 8] * 2
    return [(sum(sizes[:i]), size) for i, size in enumerate(sizes)]


def along_line(count, first, second, third, finish=None):
    ones, twos, threes, ends = [], [], [], []
    for step in range(count + 2):
        old = []
        if step >= 4:
            old.append(threes[step - 4] if finish is None else ends[step - 4])
        if step < count:
            gates = list(old)
            if step >= 2:
                gates.append(ones[step - 2])
            if step >= 3:
                gates.append(twos[step - 3])
            ones.append(line_hop(first(step, gates), OUTWARD))
        if 0 <= step - 1 < count:
            load = second(step - 1, ones[step - 1])
            twos.append(line_hop(gated(load, old), MIDDLE))
        if 0 <= step - 2 < count:
            back = step - 2
            load = third(back, ones[back], twos[back])
            ahead = ones[back + 2 : back + 3]
            threes.append(line_hop(gated(load, old + ahead), INWARD))
            if finish is not None:
                ends.append(finish(back, ones[back], twos[back], threes[back]))
    return ones, twos, threes


def gated(value, gates):
    return after(value, *gates) if gates else value


def rope_tables(positions, sign):
    half = ROT // 2
    lane = jnp.arange(HD, dtype=jnp.int32)
    counter = (lane % half).astype(F32)
    freqs = jnp.exp(counter * (-2.0 * math.log(10000.0) / ROT))
    angles = positions.astype(F32)[:, None] * freqs[None, :]
    cosine = jnp.where(lane < ROT, jnp.cos(angles), 1.0)
    sine = sign * jnp.sin(angles)
    up = jnp.where(lane < half, -sine, 0.0)
    down = jnp.where((lane >= half) & (lane < ROT), sine, 0.0)
    return jnp.stack([cosine, up, down])


def turned(block, tables):
    half = ROT // 2
    return (
        block * tables[0]
        + pltpu.roll(block, HD - half, 1) * tables[1]
        + pltpu.roll(block, half, 1) * tables[2]
    )


def make_streams(history, mix_rows, gains, biases):
    entries, tokens, width = history.shape
    streams = gains.shape[0]
    rows, sub, lanes = min(64, tokens), 16, 512

    def kernel(hist, mix, gain, bias, normed, unit, inv, last, scratch):
        def step(r, carry):
            here = pl.ds(pl.multiple_of(r * sub, sub), sub)
            weights = mix[here, :]
            columns = [
                [weights[:, s * entries + j : s * entries + j + 1] for j in range(entries)]
                for s in range(streams)
            ]
            for lane in range(0, width, lanes):
                span = slice(lane, lane + lanes)
                sums = [None] * streams
                for j in range(entries):
                    part = hist[j, here, span].astype(F32)
                    for s in range(streams):
                        term = columns[s][j] * part
                        sums[s] = term if j == 0 else sums[s] + term
                for s in range(streams):
                    scratch[s, :, span] = sums[s]
            stds = []
            for s in range(streams):
                values = scratch[s]
                center = values - jnp.sum(values, axis=-1, keepdims=True) * (1.0 / width)
                var = jnp.sum(center * center, axis=-1, keepdims=True) * (1.0 / width)
                std = lax.rsqrt(var + 1e-05)
                stds.append(std)
                scaled = center * std
                unit[s, here, :] = scaled.astype(BF)
                normed[s, here, :] = (scaled * gain[s : s + 1] + bias[s : s + 1]).astype(BF)
            last[here, :] = scratch[streams - 1]
            inv[here, :] = jnp.concatenate(stds, axis=-1)
            return carry

        lax.fori_loop(0, rows // sub, step, 0)

    wide = jax.ShapeDtypeStruct((streams, tokens, width), BF)
    return pl.pallas_call(
        kernel,
        grid=(tokens // rows,),
        in_specs=[
            pl.BlockSpec((entries, rows, width), lambda i: (0, i, 0)),
            pl.BlockSpec((rows, streams * entries), lambda i: (i, 0)),
            pl.BlockSpec((streams, width), lambda i: (0, 0)),
            pl.BlockSpec((streams, width), lambda i: (0, 0)),
        ],
        out_specs=[
            pl.BlockSpec((streams, rows, width), lambda i: (0, i, 0)),
            pl.BlockSpec((streams, rows, width), lambda i: (0, i, 0)),
            pl.BlockSpec((rows, streams), lambda i: (i, 0)),
            pl.BlockSpec((rows, width), lambda i: (i, 0)),
        ],
        out_shape=[
            wide,
            wide,
            jax.ShapeDtypeStruct((tokens, streams), F32),
            jax.ShapeDtypeStruct((tokens, width), F32),
        ],
        scratch_shapes=[pltpu.VMEM((streams, sub, width), F32)],
        cost_estimate=cost(22),
        name="make_streams",
    )(history, mix_rows, gains, biases)


def project(normed, w_heads, tables):
    _, tokens, width = normed.shape
    columns = w_heads.shape[3]
    heads, half = columns // HD, tokens // 2

    def kernel(x, w, table, out):
        flat = dot(x[0], w[...].reshape(width, columns))
        turn = pl.program_id(0) < 2

        def put(head, block):
            out[2 * head, 0] = block[:half].astype(BF)
            out[2 * head + 1, 0] = block[half:].astype(BF)

        @pl.when(turn)
        def _():
            for head in range(heads):
                put(head, turned(flat[:, head * HD : (head + 1) * HD], table[...]))

        @pl.when(jnp.logical_not(turn))
        def _():
            for head in range(heads):
                put(head, flat[:, head * HD : (head + 1) * HD])

    return pl.pallas_call(
        kernel,
        grid=(3,),
        in_specs=[
            pl.BlockSpec((1, tokens, width), lambda c: (c, 0, 0)),
            pl.BlockSpec((w_heads.shape[0], 1, w_heads.shape[2], columns), lambda c: (0, c, 0, 0)),
            pl.BlockSpec((3, tokens, HD), lambda c: (0, 0, 0)),
        ],
        out_specs=pl.BlockSpec((2 * heads, 1, half, HD), lambda c: (0, c, 0, 0)),
        out_shape=jax.ShapeDtypeStruct((2 * heads, 3, half, HD), BF),
        cost_estimate=cost(9),
        name="project",
    )(normed, w_heads, tables)


def attend(own, other, first_key, side):
    shards, _, half, _ = own.shape
    factor = 1.0 / math.sqrt(HD)

    def kernel(first, part, mine, theirs, out, exact, norm):
        s = pl.program_id(0)
        query = mine[s, 0]

        def fold(state, keys, values, mask):
            top, total, acc = state
            logits = dot_cols(query, keys) * factor
            if mask is not None:
                logits = jnp.where(mask, logits, -1e30)
            new_top = jnp.maximum(top, jnp.max(logits, axis=-1, keepdims=True))
            probs = jnp.exp(logits - new_top)
            keep = jnp.exp(top - new_top)
            return (
                new_top,
                total * keep + jnp.sum(probs, axis=-1, keepdims=True),
                acc * keep + dot(probs.astype(BF), values),
            )

        row = lax.broadcasted_iota(jnp.int32, (half, half), 0)
        col = lax.broadcasted_iota(jnp.int32, (half, half), 1)
        state = (
            jnp.full((half, 1), -1e30, F32),
            jnp.zeros((half, 1), F32),
            jnp.zeros((half, HD), F32),
        )
        state = fold(state, mine[s, 1], mine[s, 2], col <= row)
        state = lax.fori_loop(
            0, part[0], lambda i, st: fold(st, theirs[s, 0], theirs[s, 1], None), state
        )

        def shard_step(b, st):
            st = fold(st, mine[b, 1], mine[b, 2], None)
            return fold(st, theirs[b, 0], theirs[b, 1], None)

        top, total, acc = lax.fori_loop(first[s], s, shard_step, state)
        result = acc / total
        out[0] = result.astype(BF)
        exact[0] = result
        norm[0] = top + jnp.log(total)

    return pl.pallas_call(
        kernel,
        grid_spec=pltpu.PrefetchScalarGridSpec(
            num_scalar_prefetch=2,
            grid=(shards,),
            in_specs=[
                pl.BlockSpec((shards, 3, half, HD), lambda s, *_: (0, 0, 0, 0)),
                pl.BlockSpec((shards, 2, half, HD), lambda s, *_: (0, 0, 0, 0)),
            ],
            out_specs=[
                pl.BlockSpec((1, half, HD), lambda s, *_: (s, 0, 0)),
                pl.BlockSpec((1, half, HD), lambda s, *_: (s, 0, 0)),
                pl.BlockSpec((1, half, 1), lambda s, *_: (s, 0, 0)),
            ],
        ),
        out_shape=[
            jax.ShapeDtypeStruct((shards, half, HD), BF),
            jax.ShapeDtypeStruct((shards, half, HD), F32),
            jax.ShapeDtypeStruct((shards, half, 1), F32),
        ],
        cost_estimate=cost(16),
        name="attend",
    )(first_key, side, own, other)


def attend_back(own, other, grads, exact, norm, first_key, side):
    shards, _, half, _ = own.shape
    factor = 1.0 / math.sqrt(HD)

    def kernel(first, part, mine, theirs, grad_ref, exact_ref, norm_ref, kept, given, sums):
        s = pl.program_id(0)
        query = mine[s, 0]
        grad = grad_ref[s]
        delta = jnp.sum(grad.astype(F32) * exact_ref[0], axis=-1, keepdims=True)
        level = norm_ref[0]
        lowered = grad

        @pl.when(s == 0)
        def _():
            sums[...] = jnp.zeros_like(sums)

        def fold(query_grad, keys, values, mask, slot, b):
            logits = dot_cols(query, keys) * factor
            probs = jnp.exp(logits - level)
            if mask is not None:
                probs = jnp.where(mask, probs, 0.0)
            score = (probs * (dot_cols(grad, values) - delta)).astype(BF)
            sums[slot, b] += dot_rows(score, query)
            sums[slot + 1, b] += dot_rows(probs.astype(BF), lowered)
            return query_grad + dot(score, keys)

        row = lax.broadcasted_iota(jnp.int32, (half, half), 0)
        col = lax.broadcasted_iota(jnp.int32, (half, half), 1)
        total = fold(jnp.zeros((half, HD), F32), mine[s, 1], mine[s, 2], col <= row, 0, s)
        total = lax.fori_loop(
            0, part[0], lambda i, q: fold(q, theirs[s, 0], theirs[s, 1], None, 2, s), total
        )

        def shard_step(b, q):
            q = fold(q, mine[b, 1], mine[b, 2], None, 0, b)
            return fold(q, theirs[b, 0], theirs[b, 1], None, 2, b)

        total = lax.fori_loop(first[s], s, shard_step, total)
        kept[s, 0] = (total * factor).astype(BF)

        @pl.when(s == shards - 1)
        def _():
            for b in range(shards):
                kept[b, 1] = (sums[0, b] * factor).astype(BF)
                kept[b, 2] = sums[1, b].astype(BF)
                given[b, 0] = (sums[2, b] * factor).astype(BF)
                given[b, 1] = sums[3, b].astype(BF)

    whole = lambda n: pl.BlockSpec((shards, n, half, HD), lambda s, *_: (0, 0, 0, 0))
    return pl.pallas_call(
        kernel,
        grid_spec=pltpu.PrefetchScalarGridSpec(
            num_scalar_prefetch=2,
            grid=(shards,),
            in_specs=[
                whole(3),
                whole(2),
                pl.BlockSpec((shards, half, HD), lambda s, *_: (0, 0, 0)),
                pl.BlockSpec((1, half, HD), lambda s, *_: (s, 0, 0)),
                pl.BlockSpec((1, half, 1), lambda s, *_: (s, 0, 0)),
            ],
            out_specs=[whole(3), whole(2)],
            scratch_shapes=[pltpu.VMEM((4, shards, half, HD), F32)],
        ),
        out_shape=[
            jax.ShapeDtypeStruct((shards, 3, half, HD), BF),
            jax.ShapeDtypeStruct((shards, 2, half, HD), BF),
        ],
        cost_estimate=cost(22),
        name="attend_back",
    )(first_key, side, own, other, grads, exact, norm)


def norm_back(grad, unit, inv, gain, extra):
    width = grad.shape[1]
    scaled = grad * gain
    mean = jnp.sum(scaled, axis=-1, keepdims=True) * (1.0 / width)
    slope = jnp.sum(scaled * unit, axis=-1, keepdims=True) * (1.0 / width)
    result = inv * (scaled - mean - unit * slope)
    return result if extra is None else result + extra


def heads_back(parts, w_heads, normed, unit, inv, gains, tables, spans):
    _, tokens, width = normed.shape
    columns = w_heads.shape[3]
    heads, half = columns // HD, tokens // 2
    count = len(spans)

    def kernel(part, w, x, u, istd, gain, table, *refs):
        pieces, (stream, weight, stats, grad, wide) = refs[:count], refs[count:]
        c = pl.program_id(0)
        turn = c < 2

        def take(head):
            return jnp.concatenate([part[2 * head, 0], part[2 * head + 1, 0]], axis=0).astype(F32)

        @pl.when(turn)
        def _():
            for head in range(heads):
                grad[:, head * HD : (head + 1) * HD] = turned(take(head), table[...]).astype(BF)

        @pl.when(jnp.logical_not(turn))
        def _():
            for head in range(heads):
                grad[:, head * HD : (head + 1) * HD] = take(head).astype(BF)

        wide[...] = dot_cols(grad[...], w[...].reshape(width, columns))
        weight[0] = dot_rows(x[0], grad[...]).astype(BF)
        stats[...] = jnp.zeros_like(stats)
        for r, (start, block) in enumerate(spans):
            column = lax.broadcasted_iota(jnp.int32, (block, istd.shape[1]), 1)
            here = slice(start, start + block)
            values = wide[here, :]
            units = u[0, here, :].astype(F32)
            std = jnp.sum(jnp.where(column == c, istd[here, :], 0.0), axis=-1, keepdims=True)
            result = norm_back(values, units, std, gain[0], None).astype(BF)
            stream[0, here, :] = result
            pieces[r][0] = result
            stats[0, 0:1] += jnp.sum(values * units, axis=0, keepdims=True)
            stats[0, 1:2] += jnp.sum(values, axis=0, keepdims=True)

    return pl.pallas_call(
        kernel,
        grid=(3,),
        in_specs=[
            pl.BlockSpec((2 * heads, 1, half, HD), lambda c: (0, c, 0, 0)),
            pl.BlockSpec((w_heads.shape[0], 1, w_heads.shape[2], columns), lambda c: (0, c, 0, 0)),
            pl.BlockSpec((1, tokens, width), lambda c: (c, 0, 0)),
            pl.BlockSpec((1, tokens, width), lambda c: (c, 0, 0)),
            pl.BlockSpec((tokens, inv.shape[1]), lambda c: (0, 0)),
            pl.BlockSpec((1, 1, width), lambda c: (c, 0, 0)),
            pl.BlockSpec((3, tokens, HD), lambda c: (0, 0, 0)),
        ],
        out_specs=[pl.BlockSpec((1, block, width), lambda c: (c, 0, 0)) for _, block in spans]
        + [
            pl.BlockSpec((1, tokens, width), lambda c: (c, 0, 0)),
            pl.BlockSpec((1, width, columns), lambda c: (c, 0, 0)),
            pl.BlockSpec((1, 2, width), lambda c: (c, 0, 0)),
        ],
        out_shape=[jax.ShapeDtypeStruct((3, block, width), BF) for _, block in spans]
        + [
            jax.ShapeDtypeStruct((3, tokens, width), BF),
            jax.ShapeDtypeStruct((3, width, columns), BF),
            jax.ShapeDtypeStruct((3, 2, width), F32),
        ],
        scratch_shapes=[pltpu.VMEM((tokens, columns), BF), pltpu.VMEM((tokens, width), F32)],
        cost_estimate=cost(3),
        name="heads_back",
    )(parts, w_heads, normed, unit, inv, gains[:, None, :], tables)


def last_back(grad, unit, inv, gain, extra, flag):
    tokens, width = grad.shape
    block = min(128, tokens)

    def kernel(g, u, istd, gain_ref, e, flag_ref, stream, stats):
        @pl.when(pl.program_id(0) == 0)
        def _():
            stats[...] = jnp.zeros_like(stats)

        values = g[...]
        units = u[...].astype(F32)
        std = istd[...][:, -1:]
        added = e[...].astype(F32) * flag_ref[0]
        stream[...] = norm_back(values, units, std, gain_ref[...], added).astype(BF)
        stats[0:1] += jnp.sum(values * units, axis=0, keepdims=True)
        stats[1:2] += jnp.sum(values, axis=0, keepdims=True)

    row = lambda n: pl.BlockSpec((block, n), lambda i: (i, 0))
    return pl.pallas_call(
        kernel,
        grid=(tokens // block,),
        in_specs=[
            row(width),
            row(width),
            row(inv.shape[1]),
            pl.BlockSpec((1, width), lambda i: (0, 0)),
            row(width),
            pl.BlockSpec(memory_space=pltpu.SMEM),
        ],
        out_specs=[row(width), pl.BlockSpec((2, width), lambda i: (0, 0))],
        out_shape=[
            jax.ShapeDtypeStruct((tokens, width), BF),
            jax.ShapeDtypeStruct((2, width), F32),
        ],
        cost_estimate=cost(7),
        name="last_back",
    )(grad, unit, inv, gain, extra, flag)


def mixing_back(heads_part, last_part, history, which, of):
    entries, tokens, width = history.shape
    streams = heads_part.shape[0] + 1
    rows, sub, lanes = min(64, tokens // of), 16, 256
    steps = tokens // of // rows
    base = which * steps

    def kernel(first, last, hist, out):
        def step(r, carry):
            here = pl.ds(pl.multiple_of(r * sub, sub), sub)
            for s in range(streams):
                sums = [None] * entries
                for lane in range(0, width, lanes):
                    span = slice(lane, lane + lanes)
                    part = first[s, here, span] if s < streams - 1 else last[here, span]
                    part = part.astype(F32)
                    for j in range(entries):
                        term = part * hist[j, here, span].astype(F32)
                        sums[j] = term if lane == 0 else sums[j] + term
                columns = [jnp.sum(item, axis=-1, keepdims=True) for item in sums]
                out[s, here, :] = jnp.concatenate(columns, axis=-1)
            return carry

        lax.fori_loop(0, rows // sub, step, 0)

    return pl.pallas_call(
        kernel,
        grid=(steps,),
        in_specs=[
            pl.BlockSpec((streams - 1, rows, width), lambda i: (0, base + i, 0)),
            pl.BlockSpec((rows, width), lambda i: (base + i, 0)),
            pl.BlockSpec((entries, rows, width), lambda i: (0, base + i, 0)),
        ],
        out_specs=pl.BlockSpec((streams, rows, entries), lambda i: (0, i, 0)),
        out_shape=jax.ShapeDtypeStruct((streams, tokens // of, entries), F32),
        cost_estimate=cost(0.4),
        name="mixing_back",
    )(heads_part, last_part, history)


def far_attend(queries, keys, values, shard_offset):
    tokens, heads_here, head_size = queries.shape
    data_index = lax.axis_index("dp")
    pairs = [jnp.stack([keys, values])]
    reach = 2 * SEQ // tokens
    for back in range(1, reach):
        pairs.append(passed_along(pairs[0], "dp", back))
    usable = [(shard_offset[0] >= back * tokens) & (data_index >= back) for back in range(reach)]
    first_logits = block_logits(queries, keys, True)
    top = jnp.max(first_logits, axis=-1)
    total = jnp.sum(jnp.exp(first_logits - top[..., None]), axis=-1)
    for back in range(1, reach):

        def widen(state, block=pairs[back][0]):
            logits = block_logits(queries, block, False)
            new_top = jnp.maximum(state[0], jnp.max(logits, axis=-1))
            summed = state[1] * jnp.exp(state[0] - new_top) + jnp.sum(
                jnp.exp(logits - new_top[..., None]), axis=-1
            )
            return (new_top, summed)

        top, total = lax.cond(usable[back], widen, keep_same, (top, total))
    log_total = top + jnp.log(total)
    attended = jnp.zeros((tokens, heads_here, head_size), F32)
    for back in range(reach):

        def accumulate(current, block=pairs[back], diagonal=back == 0):
            probs = jnp.exp(block_logits(queries, block[0], diagonal) - log_total[..., None])
            return current + jnp.einsum(
                "hqk,khd->qhd", probs.astype(BF), block[1], preferred_element_type=F32
            )

        attended = lax.cond(usable[back], accumulate, keep_same, attended)
    return attended, (pairs, usable, log_total)


def far_attend_back(queries, attended_grad, kept):
    tokens, heads_here, head_size = queries.shape
    factor = 1.0 / math.sqrt(head_size)
    pairs, usable, log_total = kept
    reach = len(pairs)

    def weights_of(block, diagonal):
        return jnp.exp(block_logits(queries, block, diagonal) - log_total[..., None])

    def prob_grads(block):
        return jnp.einsum("qhd,khd->hqk", attended_grad, block[1], preferred_element_type=F32)

    delta = jnp.zeros((heads_here, tokens), F32)
    for back in range(reach):

        def gather_delta(current, block=pairs[back], diagonal=back == 0):
            return current + jnp.sum(weights_of(block[0], diagonal) * prob_grads(block), axis=-1)

        delta = lax.cond(usable[back], gather_delta, keep_same, delta)

    def skip_block(current):
        return (current, jnp.zeros((2, tokens, heads_here, head_size), F32))

    query_grad = jnp.zeros((tokens, heads_here, head_size), F32)
    key_value_grad = jnp.zeros((2, tokens, heads_here, head_size), F32)
    for back in range(reach):

        def spread(current, block=pairs[back], diagonal=back == 0):
            probs = weights_of(block[0], diagonal)
            score_grad = (probs * (prob_grads(block) - delta[..., None])).astype(BF)
            query_part = (
                current
                + jnp.einsum("hqk,khd->qhd", score_grad, block[0], preferred_element_type=F32)
                * factor
            )
            key_part = (
                jnp.einsum("hqk,qhd->khd", score_grad, queries, preferred_element_type=F32)
                * factor
            )
            value_part = jnp.einsum(
                "hqk,qhd->khd", probs.astype(BF), attended_grad, preferred_element_type=F32
            )
            return (query_part, jnp.stack([key_part, value_part]))

        query_grad, pair_grad = lax.cond(usable[back], spread, skip_block, query_grad)
        if back == 0:
            key_value_grad = pair_grad
        else:
            key_value_grad = key_value_grad + passed_along(pair_grad, "dp", -back)
    return jnp.concatenate([query_grad[None], key_value_grad])


def mix_block(start, coefficients, shares, last_share, extras, last_extras, arrived, whole):
    streams, block, width = shares.shape
    each = coefficients.shape[1] // (streams + 1)
    groups = 1 + len(extras)
    final = arrived is not None
    lanes = 512

    def kernel(*refs):
        weights = refs[0][...]
        heads, lasts = refs[1 : 1 + groups], refs[1 + groups : 1 + 2 * groups]
        out = refs[-2] if final else refs[-1]
        if final:
            refs[-1][...] = jnp.zeros_like(refs[-1])
        columns = [weights[:, n : n + 1] for n in range(weights.shape[1])]
        for lane in range(0, width, lanes):
            span = slice(lane, lane + lanes)
            values = []
            for s in range(streams + 1):
                picks = [r[s, :, span] if s < streams else l[:, span] for r, l in zip(heads, lasts)]
                total = picks[0].astype(F32)
                for pick in picks[1:]:
                    total = total + pick.astype(F32)
                values.append(total)
            for e in range(each):
                total = columns[e * (streams + 1)] * values[0]
                for s in range(1, streams + 1):
                    total = total + columns[e * (streams + 1) + s] * values[s]
                if final:
                    total = total + refs[1 + 2 * groups][e, :, span].astype(F32)
                out[e, :, span] = total.astype(out.dtype)

    i = start // block
    piece = pl.BlockSpec((streams, block, width), lambda n: (0, 0, 0))
    rows = [
        pl.BlockSpec((block, width), lambda n, at=start % item.shape[0] // block: (at, 0))
        for item in (last_share, *last_extras)
    ]
    small = pl.BlockSpec((each, block, width), lambda n: (0, 0, 0))
    specs = [pl.BlockSpec((block, coefficients.shape[1]), lambda n: (i, 0))]
    specs += [piece] * groups + rows
    args = [coefficients, shares, *extras, last_share, *last_extras]
    alias = {}
    if final:
        specs.append(small)
        args.append(arrived)
        if whole is not None:
            specs.append(pl.BlockSpec(memory_space=pl.ANY))
            args.append(whole)
            alias = {len(args) - 1: 0}
        out_spec = [
            pl.BlockSpec((each, block, width), lambda n: (0, i, 0)),
            pl.BlockSpec((8, 128), lambda n: (0, 0)),
        ]
        out_shape = [
            jax.ShapeDtypeStruct((each, coefficients.shape[0], width), F32),
            jax.ShapeDtypeStruct((8, 128), F32),
        ]
    else:
        out_spec, out_shape = small, jax.ShapeDtypeStruct((each, block, width), BF)
    return pl.pallas_call(
        kernel,
        grid=(1,),
        in_specs=specs,
        out_specs=out_spec,
        out_shape=out_shape,
        input_output_aliases=alias,
        cost_estimate=cost(0.4),
        name="mix_final" if final else "mix_inward",
    )(*args)


def hidden_units(x, w_up):
    tokens, width = x.shape
    units = w_up.shape[1]
    block = min(512, units)

    def kernel(x_ref, w, out, slope):
        up = dot(x_ref[...], w[...])
        inside = 0.5 * (1.0 + lax.erf(up * math.sqrt(0.5)))
        out[...] = (up * inside).astype(BF)
        bell = jnp.exp(-0.5 * up * up) * (1.0 / math.sqrt(2.0 * math.pi))
        slope[...] = (inside + up * bell).astype(BF)

    column = pl.BlockSpec((tokens, block), lambda i: (0, i))
    return pl.pallas_call(
        kernel,
        grid=(units // block,),
        in_specs=[
            pl.BlockSpec((tokens, width), lambda i: (0, 0)),
            pl.BlockSpec((width, block), lambda i: (0, i)),
        ],
        out_specs=[column, column],
        out_shape=[jax.ShapeDtypeStruct((tokens, units), BF)] * 2,
        cost_estimate=cost(9),
        name="hidden_units",
    )(x, w_up)


def merge_branches(attended, hidden, w_merge, w_down, stream, flag):
    tokens, inner = attended.shape
    shards, units, cols = w_down.shape
    members = lax.axis_size("stream")
    each = shards // members
    if cols % 128:
        merged = jnp.einsum("te,ned->tnd", attended, w_merge, preferred_element_type=F32)
        merged = merged + jnp.einsum("tf,nfd->tnd", hidden, w_down, preferred_element_type=F32)
        merged = merged.reshape(tokens, -1) + flag * stream
        return jnp.transpose(merged.reshape(tokens, members, -1), (1, 0, 2)).astype(BF)

    def kernel(a, h, wm, wd, st, flag_ref, out):
        out[0] = (dot(a[...], wm[0]) + dot(h[...], wd[0]) + flag_ref[0] * st[...]).astype(BF)

    return pl.pallas_call(
        kernel,
        grid=(shards,),
        in_specs=[
            pl.BlockSpec((tokens, inner), lambda n: (0, 0)),
            pl.BlockSpec((tokens, units), lambda n: (0, 0)),
            pl.BlockSpec((1, inner, cols), lambda n: (n, 0, 0)),
            pl.BlockSpec((1, units, cols), lambda n: (n, 0, 0)),
            pl.BlockSpec((tokens, cols), lambda n: (0, n)),
            pl.BlockSpec(memory_space=pltpu.SMEM),
        ],
        out_specs=pl.BlockSpec((1, tokens, cols), lambda n: (n // each, 0, n % each)),
        out_shape=jax.ShapeDtypeStruct((members, tokens, each * cols), BF),
        cost_estimate=cost(13),
        name="merge_branches",
    )(attended, hidden, w_merge, w_down, stream, flag)


def back_through(grad, stacked, slope):
    tokens = grad.shape[0]
    shards, units, cols = stacked.shape
    if cols % 128:
        split = grad.reshape(tokens, shards, cols)
        total = jnp.einsum("tnd,nfd->tf", split, stacked, preferred_element_type=F32)
        return (total if slope is None else total * slope.astype(F32)).astype(BF)

    def kernel(*refs):
        g, w = refs[:2]
        out, acc = refs[-2:]
        n = pl.program_id(0)
        part = dot_cols(g[...], w[0])

        @pl.when(n == 0)
        def _():
            acc[...] = part

        @pl.when(n > 0)
        def _():
            acc[...] += part

        @pl.when(n == shards - 1)
        def _():
            total = acc[...]
            if slope is not None:
                total = total * refs[2][...].astype(F32)
            out[...] = total.astype(BF)

    specs = [
        pl.BlockSpec((tokens, cols), lambda n: (0, n)),
        pl.BlockSpec((1, units, cols), lambda n: (n, 0, 0)),
    ]
    args = [grad, stacked]
    if slope is not None:
        specs.append(pl.BlockSpec((tokens, units), lambda n: (0, 0)))
        args.append(slope)
    return pl.pallas_call(
        kernel,
        grid=(shards,),
        in_specs=specs,
        out_specs=pl.BlockSpec((tokens, units), lambda n: (0, 0)),
        out_shape=jax.ShapeDtypeStruct((tokens, units), BF),
        scratch_shapes=[pltpu.VMEM((tokens, units), F32)],
        cost_estimate=cost(13 if slope is not None else 7),
        name="back_through",
    )(*args)


def body(
    history,
    mixing,
    shard_offset,
    norm_gain,
    norm_bias,
    w_heads,
    w_merge,
    w_up,
    w_down,
    mixer_first,
    mixer_second,
    out_cotangent,
    next_cotangent,
):
    member = lax.axis_index("stream")
    members = lax.axis_size("stream")
    shards = lax.axis_size("dp")
    index = lax.axis_index("dp")
    entries, tokens, width = history.shape
    heads_here = w_heads.shape[2] // HD
    half = tokens // 2
    highest = lax.Precision.HIGHEST
    flag = (member == members - 1).astype(F32)
    flags = flag.reshape(1)
    near = shards == 8 and heads_here * 2 == shards and tokens * shards == 2 * SEQ

    if near:
        spread = jnp.broadcast_to(shard_offset[:, None], (8, 128))
        offsets = lax.all_gather(spread, "dp", axis=0)[:, 0, 0]
        w_heads = after(w_heads, offsets)
    got_heads = Gathered(w_heads, direct=near)
    lanes = jnp.concatenate([norm_gain, norm_bias]).astype(F32).reshape(tokens, -1)
    first_rows = mixer_first.astype(F32).reshape(tokens, -1)
    second_flat = mixer_second[:, 0, :].astype(F32).reshape(-1)
    hidden_count = mixer_second.shape[0]
    lines = -(-second_flat.shape[0] // tokens)
    second_rows = jnp.pad(second_flat, (0, lines * tokens - second_flat.shape[0]))
    outputs = next_cotangent.shape[2]
    arrays = [mixing[:, 0, :], lanes, next_cotangent[:, 0, :], first_rows]
    arrays.append(second_rows.reshape(tokens, lines))
    packed = lax.all_gather(jnp.concatenate(arrays, axis=1), "stream", axis=0)
    parts, place = [], 0
    for array in arrays:
        parts.append(packed[:, :, place : place + array.shape[1]])
        place += array.shape[1]
    mix_all, norms, next_full, first_full, second_full = parts
    norms = norms.reshape(members, 2, width)
    first_full = first_full.astype(BF).reshape(width, -1)
    second_full = second_full.reshape(members, -1)[:, : second_flat.shape[0]]
    second_full = second_full.reshape(members, hidden_count, outputs)
    if near:
        early = (got_heads.by_x, got_heads.by_y, got_heads.across)
        history = after(history, *early)
        w_up = after(w_up, *early[:2])
    got_up = Gathered(w_up)
    gains, biases = norms[:, 0], norms[:, 1]
    mix_rows = jnp.transpose(mix_all, (1, 0, 2)).reshape(tokens, members * entries)

    normed, unit, inv, stream = make_streams(history, mix_rows, gains, biases)
    full_heads = got_heads.whole()
    cotangent = lax.all_gather(after(out_cotangent, inv), "stream", axis=1, tiled=True)
    positions = shard_offset[0] + jnp.arange(tokens, dtype=jnp.int32)
    projected = project(after(normed, got_up.by_x, got_up.by_y), full_heads, rope_tables(positions, 1.0))

    if near:
        side = (index % 2).astype(jnp.int32).reshape(1)
        place = jnp.arange(shards, dtype=jnp.int32)
        first_key = jnp.maximum(place - offsets // tokens, 0).astype(jnp.int32)
        own = lax.all_to_all(projected, "dp", 0, 0, tiled=True)
        other = partner(own[:, 1:], 1)
        full_up = got_up.whole(own)
        result, exact, level = attend(own, other, first_key, side)
        got_down = Gathered(after(w_down, result))
        got_merge = Gathered(after(w_merge, result), direct=True)
        full_merge = got_merge.whole()
        back = lax.all_to_all(result, "dp", 0, 0, tiled=True)
        attended = jnp.transpose(back.reshape(heads_here, tokens, HD), (1, 0, 2)).reshape(tokens, -1)
    else:
        got_down = Gathered(w_down)
        full_up = got_up.whole()
        full_merge = Gathered(w_merge).whole()
        split = projected.reshape(heads_here, 2, 3, half, HD)
        split = jnp.transpose(split, (2, 1, 3, 0, 4)).reshape(3, tokens, heads_here, HD)
        result, kept = far_attend(split[0], split[1], split[2], shard_offset)
        attended = result.reshape(tokens, -1).astype(BF)
    full_down = got_down.whole()
    flat_up = full_up.reshape(width, -1)
    hidden, slope = hidden_units(normed[members - 1], flat_up)
    attended = after(attended, hidden)
    hidden = after(hidden, cotangent)
    share = merge_branches(attended, hidden, full_merge, full_down, stream, flags)

    columns = lax.all_to_all(share, "stream", 0, 0, tiled=True)
    block_out = jnp.sum(columns.astype(F32), axis=0).astype(BF)
    block_full = lax.all_gather(block_out, "stream", axis=1, tiled=True)
    out_float = block_full.astype(F32)
    scale = lax.rsqrt(jnp.sum(out_float * out_float, axis=-1) / width + 1e-06)
    proj = dot(block_full, first_full)
    mixer, mixer_back = jax.vjp(exact_gelu, scale[:, None] * proj)
    second_here = mixer_second[:, 0, :].astype(F32)
    next_here = jnp.dot(mixer, second_here, precision=highest, preferred_element_type=F32)
    mixer_grad = jnp.einsum(
        "stn,scn->tc", next_full, second_full, precision=highest, preferred_element_type=F32
    )
    pre_grad = mixer_back(mixer_grad)[0]
    proj_grad = (scale[:, None] * pre_grad).astype(BF)
    scale_grad = jnp.sum(pre_grad * proj, axis=-1)
    second_local = jnp.dot(
        mixer.T, next_cotangent[:, 0, :], precision=highest, preferred_element_type=F32
    )
    first_local = dot_rows(block_out, proj_grad)
    grad_out = (
        cotangent.astype(F32)
        + dot_cols(proj_grad, first_full)
        - (scale * scale * scale * scale_grad)[:, None] * out_float / width
    ).astype(BF)

    attended_grad = back_through(grad_out, full_merge, None)
    up_grad = back_through(grad_out, full_down, slope)
    down_grad = dot_rows(hidden, grad_out).astype(BF)
    grad_down = lax.psum_scatter(down_grad, "dp", scatter_dimension=1, tiled=True).astype(F32)
    last_normed = dot_cols(after(up_grad, down_grad), flat_up)
    last_share, last_stats = last_back(
        last_normed, unit[members - 1], inv, gains[members - 1 :], grad_out, flags
    )
    last_hop = line_hop(last_share, OUTWARD)
    last_sum = (last_share.astype(F32) + last_hop.astype(F32)).astype(BF)
    last_next = line_hop(last_sum, MIDDLE)
    if near:
        sent = attended_grad.reshape(tokens, heads_here, HD)
        sent = jnp.transpose(sent, (1, 0, 2)).reshape(shards, half, HD)
        grads = lax.all_to_all(sent, "dp", 0, 0, tiled=True)
        grads = after(grads, last_share)
        kept_grads, given = attend_back(own, other, grads, exact, level, first_key, side)
        taken = partner(given, 1)
        summed = kept_grads[:, 1:].astype(F32) + taken.astype(F32)
        pair = jnp.concatenate([kept_grads[:, :1], summed.astype(BF)], axis=1)
        pair = after(pair, last_hop)
        late_grad, late_up = after(grad_out, pair), after(up_grad, pair)
        up_back = dot_rows(normed[members - 1], late_up).astype(BF)
        merge_grad = dot_rows(attended, late_grad).astype(BF)
        parts = lax.all_to_all(pair, "dp", 0, 0, tiled=True)
    else:
        up_back = dot_rows(normed[members - 1], up_grad).astype(BF)
        merge_grad = dot_rows(attended, grad_out).astype(BF)
        grads = far_attend_back(split[0], attended_grad.reshape(tokens, heads_here, HD), kept)
        parts = grads.reshape(3, 2, half, heads_here, HD)
        parts = jnp.transpose(parts, (3, 1, 0, 2, 4)).reshape(2 * heads_here, 3, half, HD)

    parts = after(parts, last_sum, grad_down, up_back, merge_grad)
    spans = block_spans(tokens)
    *pieces, heads_share, heads_grad, heads_stats = heads_back(
        parts, full_heads, normed, unit, inv, gains, rope_tables(positions, -1.0), spans
    )

    grad_merge = lax.psum_scatter(merge_grad, "dp", scatter_dimension=1, tiled=True).astype(F32)
    grad_heads = lax.psum_scatter(heads_grad, "dp", scatter_dimension=1, tiled=True).astype(F32)
    grad_up = lax.psum_scatter(up_back, "dp", scatter_dimension=0, tiled=True).astype(F32)

    each = entries // members

    def weights_for(owner):
        block = lax.dynamic_slice_in_dim(mix_all, owner * each, each, axis=2)
        return jnp.transpose(block, (1, 2, 0)).reshape(tokens, each * members)

    there = weights_for(jnp.where(member == 1, 0, members - 1))
    here = weights_for(member)
    extra = {}

    last_one = lambda i: last_hop
    last_two = lambda i: last_next

    def first_hop(i, gates):
        gates = list(gates)
        if i == 3:
            gates.append(grad_merge)
        return gated(pieces[i], gates)

    def small_sums():
        stats = jnp.concatenate([heads_stats, last_stats[None]]).reshape(members, tokens, -1)
        both = jnp.concatenate([jnp.concatenate(mixes, axis=1), stats], axis=2)
        both = jnp.sum(lax.all_to_all(both, "stream", 0, 0, tiled=True), axis=0)
        second_sums = jnp.pad(second_local.reshape(-1), (0, lines * tokens - second_flat.shape[0]))
        local = [both[:, entries:], first_local.reshape(tokens, -1), second_sums.reshape(tokens, lines)]
        everyone = lax.all_gather(jnp.concatenate(local, axis=1), "dp", axis=0)
        return both[:, :entries], jnp.sum(everyone, axis=0)

    mixes = [mixing_back(heads_share, last_share, history, i, 2) for i in range(2)]

    extra["both"], extra["all"] = small_sums()

    def second_hop(i, one):
        load = (pieces[i].astype(F32) + one.astype(F32)).astype(BF)
        return after(load, *mixes) if i == 0 else load

    def third_hop(i, one, two):
        load = mix_block(spans[i][0], there, pieces[i], last_share, [two], [last_two(i)], None, None)
        return after(load, extra["both"]) if i == 2 else load

    def finish(i, one, two, three):
        if i == 3:
            three = after(three, grad_heads, extra["all"])
        extra["history"], token = mix_block(
            spans[i][0],
            here,
            pieces[i],
            last_share,
            [one, two],
            [last_one(i), last_two(i)],
            three,
            extra.get("history"),
        )
        return token

    along_line(len(spans), first_hop, second_hop, third_hop, finish)
    grad_history = extra["history"]

    grad_mixing = extra["both"][:, None, :]
    sums = extra["all"]
    columns = 2 * width // tokens
    stats = sums[:, :columns].reshape(2, width)
    grad_first = sums[:, columns:-lines].reshape(mixer_first.shape)
    grad_second = sums[:, -lines:].reshape(-1)[: second_flat.shape[0]].reshape(hidden_count, outputs)
    return (
        block_out,
        next_here[:, None, :],
        grad_history,
        grad_mixing,
        stats[:1],
        stats[1:],
        grad_heads,
        grad_merge,
        grad_up,
        grad_down,
        grad_first,
        grad_second[:, None, :],
    )


def solution(mesh):
    in_specs = (
        P(None, "dp", None),
        P("dp", "stream", None),
        P("dp"),
        P("stream", None),
        P("stream", None),
        P(None, "dp", "stream"),
        P("stream", "dp"),
        P("dp", "stream"),
        P("stream", "dp"),
        P("stream", None),
        P(None, "stream", None),
        P("dp", "stream"),
        P("dp", "stream", None),
    )
    out_specs = (
        P("dp", "stream"),
        P("dp", "stream", None),
        P("stream", "dp", None),
        P("dp", "stream", None),
        P("stream", None),
        P("stream", None),
        P(None, "dp", "stream"),
        P("stream", "dp"),
        P("dp", "stream"),
        P("stream", "dp"),
        P("stream", None),
        P(None, "stream", None),
    )
    return jax.shard_map(body, mesh=mesh, in_specs=in_specs, out_specs=out_specs, check_vma=False)
```

```python
import math

import jax
import jax.numpy as jnp
from jax import lax
from jax.experimental import pallas as pl
from jax.experimental.pallas import tpu as pltpu
from jax.sharding import PartitionSpec as P

HD = 128
ROT = 32
SEQ = 2048


def passed_along(shard, axis, by):
    peers = lax.axis_size(axis)
    pairs = [(i, i + by) for i in range(peers) if 0 <= i + by < peers]
    return lax.ppermute(shard, axis, pairs)


def rotate(vectors, positions, sign):
    half = ROT // 2
    counter = jnp.arange(half, dtype=jnp.float32)
    freqs = jnp.exp(counter * (-2.0 * math.log(10000.0) / ROT))
    angles = positions.astype(jnp.float32)[:, None] * freqs[None, :]
    cosine = jnp.cos(angles)[:, None, :]
    sine = sign * jnp.sin(angles)[:, None, :]
    first = vectors[..., :half]
    second = vectors[..., half:ROT]
    return jnp.concatenate(
        [first * cosine - second * sine, second * cosine + first * sine, vectors[..., ROT:]],
        axis=-1,
    )


def exact_gelu(vectors):
    return jax.nn.gelu(vectors, approximate=False)


def block_logits(queries, keys_block, diagonal):
    logits = jnp.einsum("qhd,khd->hqk", queries, keys_block, preferred_element_type=jnp.float32) * (
        1.0 / math.sqrt(queries.shape[-1])
    )
    if diagonal:
        counter = jnp.arange(queries.shape[0], dtype=jnp.int32)
        allowed = counter[None, :] <= counter[:, None]
        logits = jnp.where(allowed[None], logits, -1e30)
    return logits


def keep_same(state):
    return state


BF = jnp.bfloat16
SHARE = 1.0
F32 = jnp.float32
OUTWARD = [(0, 1), (3, 2)]
MIDDLE = [(1, 2), (2, 1)]
INWARD = [(1, 0), (2, 3)]


def dot(left, right):
    return jnp.dot(left, right, preferred_element_type=F32)


def dot_rows(left, right):
    return lax.dot_general(left, right, (((0,), (0,)), ((), ())), preferred_element_type=F32)


def dot_cols(left, right):
    return lax.dot_general(left, right, (((1,), (1,)), ((), ())), preferred_element_type=F32)


def partner(shard, bit):
    peers = lax.axis_size("dp")
    return lax.ppermute(shard, "dp", [(i, i ^ bit) for i in range(peers)])


def line_hop(shard, pairs):
    return lax.ppermute(shard, "stream", pairs)


def cost(microseconds):
    return pl.CostEstimate(
        flops=int(microseconds * SHARE * 0.9e9),
        bytes_accessed=int(microseconds * SHARE * 3e6),
        transcendentals=0,
    )


def after(value, *others):
    return lax.optimization_barrier((value, *others))[0]


class Gathered:
    def __init__(self, shard, direct=False):
        self.shard = shard
        self.peers = lax.axis_size("dp")
        if self.peers != 8:
            self.by_x = self.by_y = shard
            return
        self.cut = max(range(shard.ndim - 1), key=lambda dim: shard.shape[dim])
        self.by_x = partner(shard, 2)
        self.by_y = partner(shard, 4)
        self.across = partner(shard, 6) if direct else None

    def whole(self, *earlier):
        shard = self.shard
        if self.peers != 8:
            return lax.all_gather(shard, "dp", axis=0)
        index = lax.axis_index("dp")
        cut = self.cut
        half = shard.shape[cut] // 2
        shard, by_x, by_y = [gated(item, earlier) for item in (shard, self.by_x, self.by_y)]
        pieces = [(shard, 0, 0), (by_x, 2, 0), (by_y, 4, 0)]
        if self.across is None:
            low = lax.slice_in_dim(by_y, 0, half, axis=cut)
            high = lax.slice_in_dim(by_x, half, 2 * half, axis=cut)
            pieces += [(partner(low, 2), 6, 0), (partner(high, 4), 6, half)]
        else:
            pieces.append((gated(self.across, earlier), 6, 0))
        pieces += [(partner(piece, 1), code ^ 1, start) for piece, code, start in pieces]
        return put_together(pieces, shard, self.peers, cut, index)


def put_together(pieces, shard, peers, cut, index):
    codes = [(code, start) for _, code, start in pieces]
    arrays = [piece for piece, _, _ in pieces]

    def kernel(place, *refs):
        out, held, sems, sent = refs[-4:]
        owners = {}
        for n, (code, start) in enumerate(codes):
            size = refs[n].shape[cut]
            span = tuple(
                pl.ds(start, size) if dim == cut else slice(None) for dim in range(shard.ndim)
            )
            copy = pltpu.make_async_copy(refs[n], held.at[(code, *span)], sems.at[n])
            copy.start()
            owners.setdefault(code, []).append(copy)
        leaving = []
        for code, copies in owners.items():
            for copy in copies:
                copy.wait()
            copy = pltpu.make_async_copy(held.at[code], out.at[place[0] ^ code], sent.at[code])
            copy.start()
            leaving.append(copy)
        for copy in leaving:
            copy.wait()

    anywhere = pl.BlockSpec(memory_space=pl.ANY)
    size = peers * shard.size * shard.dtype.itemsize
    return pl.pallas_call(
        kernel,
        in_specs=[pl.BlockSpec(memory_space=pltpu.SMEM)] + [anywhere] * len(arrays),
        out_specs=anywhere,
        out_shape=jax.ShapeDtypeStruct((peers, *shard.shape), shard.dtype),
        scratch_shapes=[
            pltpu.VMEM((peers, *shard.shape), shard.dtype),
            pltpu.SemaphoreType.DMA((len(arrays),)),
            pltpu.SemaphoreType.DMA((peers,)),
        ],
        cost_estimate=cost(2 * size / 3e6),
        name="put_together",
    )(index.astype(jnp.int32).reshape(1), *arrays)


def block_spans(tokens):
    sizes = [tokens // 4] * 3 + [tokens // 8] * 2
    return [(sum(sizes[:i]), size) for i, size in enumerate(sizes)]


def along_line(count, first, second, third, finish=None):
    ones, twos, threes, ends = [], [], [], []
    for step in range(count + 2):
        old = []
        if step >= 4:
            old.append(threes[step - 4] if finish is None else ends[step - 4])
        if step < count:
            gates = list(old)
            if step >= 2:
                gates.append(ones[step - 2])
            if step >= 3:
                gates.append(twos[step - 3])
            ones.append(line_hop(first(step, gates), OUTWARD))
        if 0 <= step - 1 < count:
            load = second(step - 1, ones[step - 1])
            twos.append(line_hop(gated(load, old), MIDDLE))
        if 0 <= step - 2 < count:
            back = step - 2
            load = third(back, ones[back], twos[back])
            ahead = ones[back + 2 : back + 3]
            threes.append(line_hop(gated(load, old + ahead), INWARD))
            if finish is not None:
                ends.append(finish(back, ones[back], twos[back], threes[back]))
    return ones, twos, threes


def gated(value, gates):
    return after(value, *gates) if gates else value


def rope_tables(positions, sign):
    half = ROT // 2
    lane = jnp.arange(HD, dtype=jnp.int32)
    counter = (lane % half).astype(F32)
    freqs = jnp.exp(counter * (-2.0 * math.log(10000.0) / ROT))
    angles = positions.astype(F32)[:, None] * freqs[None, :]
    cosine = jnp.where(lane < ROT, jnp.cos(angles), 1.0)
    sine = sign * jnp.sin(angles)
    up = jnp.where(lane < half, -sine, 0.0)
    down = jnp.where((lane >= half) & (lane < ROT), sine, 0.0)
    return jnp.stack([cosine, up, down])


def turned(block, tables):
    half = ROT // 2
    return (
        block * tables[0]
        + pltpu.roll(block, HD - half, 1) * tables[1]
        + pltpu.roll(block, half, 1) * tables[2]
    )


def make_streams(history, mix_rows, gains, biases):
    entries, tokens, width = history.shape
    streams = gains.shape[0]
    rows, sub, lanes = min(64, tokens), 16, 512

    def kernel(hist, mix, gain, bias, normed, unit, inv, last, scratch):
        def step(r, carry):
            here = pl.ds(pl.multiple_of(r * sub, sub), sub)
            weights = mix[here, :]
            columns = [
                [weights[:, s * entries + j : s * entries + j + 1] for j in range(entries)]
                for s in range(streams)
            ]
            for lane in range(0, width, lanes):
                span = slice(lane, lane + lanes)
                sums = [None] * streams
                for j in range(entries):
                    part = hist[j, here, span].astype(F32)
                    for s in range(streams):
                        term = columns[s][j] * part
                        sums[s] = term if j == 0 else sums[s] + term
                for s in range(streams):
                    scratch[s, :, span] = sums[s]
            stds = []
            for s in range(streams):
                values = scratch[s]
                center = values - jnp.sum(values, axis=-1, keepdims=True) * (1.0 / width)
                var = jnp.sum(center * center, axis=-1, keepdims=True) * (1.0 / width)
                std = lax.rsqrt(var + 1e-05)
                stds.append(std)
                scaled = center * std
                unit[s, here, :] = scaled.astype(BF)
                normed[s, here, :] = (scaled * gain[s : s + 1] + bias[s : s + 1]).astype(BF)
            last[here, :] = scratch[streams - 1]
            inv[here, :] = jnp.concatenate(stds, axis=-1)
            return carry

        lax.fori_loop(0, rows // sub, step, 0)

    wide = jax.ShapeDtypeStruct((streams, tokens, width), BF)
    return pl.pallas_call(
        kernel,
        grid=(tokens // rows,),
        in_specs=[
            pl.BlockSpec((entries, rows, width), lambda i: (0, i, 0)),
            pl.BlockSpec((rows, streams * entries), lambda i: (i, 0)),
            pl.BlockSpec((streams, width), lambda i: (0, 0)),
            pl.BlockSpec((streams, width), lambda i: (0, 0)),
        ],
        out_specs=[
            pl.BlockSpec((streams, rows, width), lambda i: (0, i, 0)),
            pl.BlockSpec((streams, rows, width), lambda i: (0, i, 0)),
            pl.BlockSpec((rows, streams), lambda i: (i, 0)),
            pl.BlockSpec((rows, width), lambda i: (i, 0)),
        ],
        out_shape=[
            wide,
            wide,
            jax.ShapeDtypeStruct((tokens, streams), F32),
            jax.ShapeDtypeStruct((tokens, width), F32),
        ],
        scratch_shapes=[pltpu.VMEM((streams, sub, width), F32)],
        cost_estimate=cost(22),
        name="make_streams",
    )(history, mix_rows, gains, biases)


def project(normed, w_heads, tables):
    _, tokens, width = normed.shape
    columns = w_heads.shape[3]
    heads, half = columns // HD, tokens // 2

    def kernel(x, w, table, out):
        flat = dot(x[0], w[...].reshape(width, columns))
        turn = pl.program_id(0) < 2

        def put(head, block):
            out[2 * head, 0] = block[:half].astype(BF)
            out[2 * head + 1, 0] = block[half:].astype(BF)

        @pl.when(turn)
        def _():
            for head in range(heads):
                put(head, turned(flat[:, head * HD : (head + 1) * HD], table[...]))

        @pl.when(jnp.logical_not(turn))
        def _():
            for head in range(heads):
                put(head, flat[:, head * HD : (head + 1) * HD])

    return pl.pallas_call(
        kernel,
        grid=(3,),
        in_specs=[
            pl.BlockSpec((1, tokens, width), lambda c: (c, 0, 0)),
            pl.BlockSpec((w_heads.shape[0], 1, w_heads.shape[2], columns), lambda c: (0, c, 0, 0)),
            pl.BlockSpec((3, tokens, HD), lambda c: (0, 0, 0)),
        ],
        out_specs=pl.BlockSpec((2 * heads, 1, half, HD), lambda c: (0, c, 0, 0)),
        out_shape=jax.ShapeDtypeStruct((2 * heads, 3, half, HD), BF),
        cost_estimate=cost(9),
        name="project",
    )(normed, w_heads, tables)


def attend(own, other, first_key, side):
    shards, _, half, _ = own.shape
    factor = 1.0 / math.sqrt(HD)

    def kernel(first, part, mine, theirs, out, exact, norm):
        s = pl.program_id(0)
        query = mine[s, 0]

        def fold(state, keys, values, mask):
            top, total, acc = state
            logits = dot_cols(query, keys) * factor
            if mask is not None:
                logits = jnp.where(mask, logits, -1e30)
            new_top = jnp.maximum(top, jnp.max(logits, axis=-1, keepdims=True))
            probs = jnp.exp(logits - new_top)
            keep = jnp.exp(top - new_top)
            return (
                new_top,
                total * keep + jnp.sum(probs, axis=-1, keepdims=True),
                acc * keep + dot(probs.astype(BF), values),
            )

        row = lax.broadcasted_iota(jnp.int32, (half, half), 0)
        col = lax.broadcasted_iota(jnp.int32, (half, half), 1)
        state = (
            jnp.full((half, 1), -1e30, F32),
            jnp.zeros((half, 1), F32),
            jnp.zeros((half, HD), F32),
        )
        state = fold(state, mine[s, 1], mine[s, 2], col <= row)
        state = lax.fori_loop(
            0, part[0], lambda i, st: fold(st, theirs[s, 0], theirs[s, 1], None), state
        )

        def shard_step(b, st):
            st = fold(st, mine[b, 1], mine[b, 2], None)
            return fold(st, theirs[b, 0], theirs[b, 1], None)

        top, total, acc = lax.fori_loop(first[s], s, shard_step, state)
        result = acc / total
        out[0] = result.astype(BF)
        exact[0] = result
        norm[0] = top + jnp.log(total)

    return pl.pallas_call(
        kernel,
        grid_spec=pltpu.PrefetchScalarGridSpec(
            num_scalar_prefetch=2,
            grid=(shards,),
            in_specs=[
                pl.BlockSpec((shards, 3, half, HD), lambda s, *_: (0, 0, 0, 0)),
                pl.BlockSpec((shards, 2, half, HD), lambda s, *_: (0, 0, 0, 0)),
            ],
            out_specs=[
                pl.BlockSpec((1, half, HD), lambda s, *_: (s, 0, 0)),
                pl.BlockSpec((1, half, HD), lambda s, *_: (s, 0, 0)),
                pl.BlockSpec((1, half, 1), lambda s, *_: (s, 0, 0)),
            ],
        ),
        out_shape=[
            jax.ShapeDtypeStruct((shards, half, HD), BF),
            jax.ShapeDtypeStruct((shards, half, HD), F32),
            jax.ShapeDtypeStruct((shards, half, 1), F32),
        ],
        cost_estimate=cost(16),
        name="attend",
    )(first_key, side, own, other)


def attend_back(own, other, grads, exact, norm, first_key, side):
    shards, _, half, _ = own.shape
    factor = 1.0 / math.sqrt(HD)

    def kernel(first, part, mine, theirs, grad_ref, exact_ref, norm_ref, kept, given, sums):
        s = pl.program_id(0)
        query = mine[s, 0]
        grad = grad_ref[s]
        delta = jnp.sum(grad.astype(F32) * exact_ref[0], axis=-1, keepdims=True)
        level = norm_ref[0]
        lowered = grad

        @pl.when(s == 0)
        def _():
            sums[...] = jnp.zeros_like(sums)

        def fold(query_grad, keys, values, mask, slot, b):
            logits = dot_cols(query, keys) * factor
            probs = jnp.exp(logits - level)
            if mask is not None:
                probs = jnp.where(mask, probs, 0.0)
            score = (probs * (dot_cols(grad, values) - delta)).astype(BF)
            sums[slot, b] += dot_rows(score, query)
            sums[slot + 1, b] += dot_rows(probs.astype(BF), lowered)
            return query_grad + dot(score, keys)

        row = lax.broadcasted_iota(jnp.int32, (half, half), 0)
        col = lax.broadcasted_iota(jnp.int32, (half, half), 1)
        total = fold(jnp.zeros((half, HD), F32), mine[s, 1], mine[s, 2], col <= row, 0, s)
        total = lax.fori_loop(
            0, part[0], lambda i, q: fold(q, theirs[s, 0], theirs[s, 1], None, 2, s), total
        )

        def shard_step(b, q):
            q = fold(q, mine[b, 1], mine[b, 2], None, 0, b)
            return fold(q, theirs[b, 0], theirs[b, 1], None, 2, b)

        total = lax.fori_loop(first[s], s, shard_step, total)
        kept[s, 0] = (total * factor).astype(BF)

        @pl.when(s == shards - 1)
        def _():
            for b in range(shards):
                kept[b, 1] = (sums[0, b] * factor).astype(BF)
                kept[b, 2] = sums[1, b].astype(BF)
                given[b, 0] = (sums[2, b] * factor).astype(BF)
                given[b, 1] = sums[3, b].astype(BF)

    whole = lambda n: pl.BlockSpec((shards, n, half, HD), lambda s, *_: (0, 0, 0, 0))
    return pl.pallas_call(
        kernel,
        grid_spec=pltpu.PrefetchScalarGridSpec(
            num_scalar_prefetch=2,
            grid=(shards,),
            in_specs=[
                whole(3),
                whole(2),
                pl.BlockSpec((shards, half, HD), lambda s, *_: (0, 0, 0)),
                pl.BlockSpec((1, half, HD), lambda s, *_: (s, 0, 0)),
                pl.BlockSpec((1, half, 1), lambda s, *_: (s, 0, 0)),
            ],
            out_specs=[whole(3), whole(2)],
            scratch_shapes=[pltpu.VMEM((4, shards, half, HD), F32)],
        ),
        out_shape=[
            jax.ShapeDtypeStruct((shards, 3, half, HD), BF),
            jax.ShapeDtypeStruct((shards, 2, half, HD), BF),
        ],
        cost_estimate=cost(22),
        name="attend_back",
    )(first_key, side, own, other, grads, exact, norm)


def norm_back(grad, unit, inv, gain, extra):
    width = grad.shape[1]
    scaled = grad * gain
    mean = jnp.sum(scaled, axis=-1, keepdims=True) * (1.0 / width)
    slope = jnp.sum(scaled * unit, axis=-1, keepdims=True) * (1.0 / width)
    result = inv * (scaled - mean - unit * slope)
    return result if extra is None else result + extra


def heads_back(parts, w_heads, normed, unit, inv, gains, tables, spans):
    _, tokens, width = normed.shape
    columns = w_heads.shape[3]
    heads, half = columns // HD, tokens // 2
    count = len(spans)

    def kernel(part, w, x, u, istd, gain, table, *refs):
        pieces, (stream, weight, stats, grad, wide) = refs[:count], refs[count:]
        c = pl.program_id(0)
        turn = c < 2

        def take(head):
            return jnp.concatenate([part[2 * head, 0], part[2 * head + 1, 0]], axis=0).astype(F32)

        @pl.when(turn)
        def _():
            for head in range(heads):
                grad[:, head * HD : (head + 1) * HD] = turned(take(head), table[...]).astype(BF)

        @pl.when(jnp.logical_not(turn))
        def _():
            for head in range(heads):
                grad[:, head * HD : (head + 1) * HD] = take(head).astype(BF)

        wide[...] = dot_cols(grad[...], w[...].reshape(width, columns))
        weight[0] = dot_rows(x[0], grad[...]).astype(BF)
        stats[...] = jnp.zeros_like(stats)
        for r, (start, block) in enumerate(spans):
            column = lax.broadcasted_iota(jnp.int32, (block, istd.shape[1]), 1)
            here = slice(start, start + block)
            values = wide[here, :]
            units = u[0, here, :].astype(F32)
            std = jnp.sum(jnp.where(column == c, istd[here, :], 0.0), axis=-1, keepdims=True)
            result = norm_back(values, units, std, gain[0], None).astype(BF)
            stream[0, here, :] = result
            pieces[r][0] = result
            stats[0, 0:1] += jnp.sum(values * units, axis=0, keepdims=True)
            stats[0, 1:2] += jnp.sum(values, axis=0, keepdims=True)

    return pl.pallas_call(
        kernel,
        grid=(3,),
        in_specs=[
            pl.BlockSpec((2 * heads, 1, half, HD), lambda c: (0, c, 0, 0)),
            pl.BlockSpec((w_heads.shape[0], 1, w_heads.shape[2], columns), lambda c: (0, c, 0, 0)),
            pl.BlockSpec((1, tokens, width), lambda c: (c, 0, 0)),
            pl.BlockSpec((1, tokens, width), lambda c: (c, 0, 0)),
            pl.BlockSpec((tokens, inv.shape[1]), lambda c: (0, 0)),
            pl.BlockSpec((1, 1, width), lambda c: (c, 0, 0)),
            pl.BlockSpec((3, tokens, HD), lambda c: (0, 0, 0)),
        ],
        out_specs=[pl.BlockSpec((1, block, width), lambda c: (c, 0, 0)) for _, block in spans]
        + [
            pl.BlockSpec((1, tokens, width), lambda c: (c, 0, 0)),
            pl.BlockSpec((1, width, columns), lambda c: (c, 0, 0)),
            pl.BlockSpec((1, 2, width), lambda c: (c, 0, 0)),
        ],
        out_shape=[jax.ShapeDtypeStruct((3, block, width), BF) for _, block in spans]
        + [
            jax.ShapeDtypeStruct((3, tokens, width), BF),
            jax.ShapeDtypeStruct((3, width, columns), BF),
            jax.ShapeDtypeStruct((3, 2, width), F32),
        ],
        scratch_shapes=[pltpu.VMEM((tokens, columns), BF), pltpu.VMEM((tokens, width), F32)],
        cost_estimate=cost(3),
        name="heads_back",
    )(parts, w_heads, normed, unit, inv, gains[:, None, :], tables)


def last_back(grad, unit, inv, gain, extra, flag):
    tokens, width = grad.shape
    block = min(128, tokens)

    def kernel(g, u, istd, gain_ref, e, flag_ref, stream, stats):
        @pl.when(pl.program_id(0) == 0)
        def _():
            stats[...] = jnp.zeros_like(stats)

        values = g[...]
        units = u[...].astype(F32)
        std = istd[...][:, -1:]
        added = e[...].astype(F32) * flag_ref[0]
        stream[...] = norm_back(values, units, std, gain_ref[...], added).astype(BF)
        stats[0:1] += jnp.sum(values * units, axis=0, keepdims=True)
        stats[1:2] += jnp.sum(values, axis=0, keepdims=True)

    row = lambda n: pl.BlockSpec((block, n), lambda i: (i, 0))
    return pl.pallas_call(
        kernel,
        grid=(tokens // block,),
        in_specs=[
            row(width),
            row(width),
            row(inv.shape[1]),
            pl.BlockSpec((1, width), lambda i: (0, 0)),
            row(width),
            pl.BlockSpec(memory_space=pltpu.SMEM),
        ],
        out_specs=[row(width), pl.BlockSpec((2, width), lambda i: (0, 0))],
        out_shape=[
            jax.ShapeDtypeStruct((tokens, width), BF),
            jax.ShapeDtypeStruct((2, width), F32),
        ],
        cost_estimate=cost(7),
        name="last_back",
    )(grad, unit, inv, gain, extra, flag)


def mixing_back(heads_part, last_part, history, which, of):
    entries, tokens, width = history.shape
    streams = heads_part.shape[0] + 1
    rows, sub, lanes = min(64, tokens // of), 16, 256
    steps = tokens // of // rows
    base = which * steps

    def kernel(first, last, hist, out):
        def step(r, carry):
            here = pl.ds(pl.multiple_of(r * sub, sub), sub)
            for s in range(streams):
                sums = [None] * entries
                for lane in range(0, width, lanes):
                    span = slice(lane, lane + lanes)
                    part = first[s, here, span] if s < streams - 1 else last[here, span]
                    part = part.astype(F32)
                    for j in range(entries):
                        term = part * hist[j, here, span].astype(F32)
                        sums[j] = term if lane == 0 else sums[j] + term
                columns = [jnp.sum(item, axis=-1, keepdims=True) for item in sums]
                out[s, here, :] = jnp.concatenate(columns, axis=-1)
            return carry

        lax.fori_loop(0, rows // sub, step, 0)

    return pl.pallas_call(
        kernel,
        grid=(steps,),
        in_specs=[
            pl.BlockSpec((streams - 1, rows, width), lambda i: (0, base + i, 0)),
            pl.BlockSpec((rows, width), lambda i: (base + i, 0)),
            pl.BlockSpec((entries, rows, width), lambda i: (0, base + i, 0)),
        ],
        out_specs=pl.BlockSpec((streams, rows, entries), lambda i: (0, i, 0)),
        out_shape=jax.ShapeDtypeStruct((streams, tokens // of, entries), F32),
        cost_estimate=cost(0.4),
        name="mixing_back",
    )(heads_part, last_part, history)


def far_attend(queries, keys, values, shard_offset):
    tokens, heads_here, head_size = queries.shape
    data_index = lax.axis_index("dp")
    pairs = [jnp.stack([keys, values])]
    reach = 2 * SEQ // tokens
    for back in range(1, reach):
        pairs.append(passed_along(pairs[0], "dp", back))
    usable = [(shard_offset[0] >= back * tokens) & (data_index >= back) for back in range(reach)]
    first_logits = block_logits(queries, keys, True)
    top = jnp.max(first_logits, axis=-1)
    total = jnp.sum(jnp.exp(first_logits - top[..., None]), axis=-1)
    for back in range(1, reach):

        def widen(state, block=pairs[back][0]):
            logits = block_logits(queries, block, False)
            new_top = jnp.maximum(state[0], jnp.max(logits, axis=-1))
            summed = state[1] * jnp.exp(state[0] - new_top) + jnp.sum(
                jnp.exp(logits - new_top[..., None]), axis=-1
            )
            return (new_top, summed)

        top, total = lax.cond(usable[back], widen, keep_same, (top, total))
    log_total = top + jnp.log(total)
    attended = jnp.zeros((tokens, heads_here, head_size), F32)
    for back in range(reach):

        def accumulate(current, block=pairs[back], diagonal=back == 0):
            probs = jnp.exp(block_logits(queries, block[0], diagonal) - log_total[..., None])
            return current + jnp.einsum(
                "hqk,khd->qhd", probs.astype(BF), block[1], preferred_element_type=F32
            )

        attended = lax.cond(usable[back], accumulate, keep_same, attended)
    return attended, (pairs, usable, log_total)


def far_attend_back(queries, attended_grad, kept):
    tokens, heads_here, head_size = queries.shape
    factor = 1.0 / math.sqrt(head_size)
    pairs, usable, log_total = kept
    reach = len(pairs)

    def weights_of(block, diagonal):
        return jnp.exp(block_logits(queries, block, diagonal) - log_total[..., None])

    def prob_grads(block):
        return jnp.einsum("qhd,khd->hqk", attended_grad, block[1], preferred_element_type=F32)

    delta = jnp.zeros((heads_here, tokens), F32)
    for back in range(reach):

        def gather_delta(current, block=pairs[back], diagonal=back == 0):
            return current + jnp.sum(weights_of(block[0], diagonal) * prob_grads(block), axis=-1)

        delta = lax.cond(usable[back], gather_delta, keep_same, delta)

    def skip_block(current):
        return (current, jnp.zeros((2, tokens, heads_here, head_size), F32))

    query_grad = jnp.zeros((tokens, heads_here, head_size), F32)
    key_value_grad = jnp.zeros((2, tokens, heads_here, head_size), F32)
    for back in range(reach):

        def spread(current, block=pairs[back], diagonal=back == 0):
            probs = weights_of(block[0], diagonal)
            score_grad = (probs * (prob_grads(block) - delta[..., None])).astype(BF)
            query_part = (
                current
                + jnp.einsum("hqk,khd->qhd", score_grad, block[0], preferred_element_type=F32)
                * factor
            )
            key_part = (
                jnp.einsum("hqk,qhd->khd", score_grad, queries, preferred_element_type=F32)
                * factor
            )
            value_part = jnp.einsum(
                "hqk,qhd->khd", probs.astype(BF), attended_grad, preferred_element_type=F32
            )
            return (query_part, jnp.stack([key_part, value_part]))

        query_grad, pair_grad = lax.cond(usable[back], spread, skip_block, query_grad)
        if back == 0:
            key_value_grad = pair_grad
        else:
            key_value_grad = key_value_grad + passed_along(pair_grad, "dp", -back)
    return jnp.concatenate([query_grad[None], key_value_grad])


def mix_block(start, coefficients, shares, last_share, extras, last_extras, arrived, whole):
    streams, block, width = shares.shape
    each = coefficients.shape[1] // (streams + 1)
    groups = 1 + len(extras)
    final = arrived is not None
    lanes = 512

    def kernel(*refs):
        weights = refs[0][...]
        heads, lasts = refs[1 : 1 + groups], refs[1 + groups : 1 + 2 * groups]
        out = refs[-2] if final else refs[-1]
        if final:
            refs[-1][...] = jnp.zeros_like(refs[-1])
        columns = [weights[:, n : n + 1] for n in range(weights.shape[1])]
        for lane in range(0, width, lanes):
            span = slice(lane, lane + lanes)
            values = []
            for s in range(streams + 1):
                picks = [r[s, :, span] if s < streams else l[:, span] for r, l in zip(heads, lasts)]
                total = picks[0].astype(F32)
                for pick in picks[1:]:
                    total = total + pick.astype(F32)
                values.append(total)
            for e in range(each):
                total = columns[e * (streams + 1)] * values[0]
                for s in range(1, streams + 1):
                    total = total + columns[e * (streams + 1) + s] * values[s]
                if final:
                    total = total + refs[1 + 2 * groups][e, :, span].astype(F32)
                out[e, :, span] = total.astype(out.dtype)

    i = start // block
    piece = pl.BlockSpec((streams, block, width), lambda n: (0, 0, 0))
    rows = [
        pl.BlockSpec((block, width), lambda n, at=start % item.shape[0] // block: (at, 0))
        for item in (last_share, *last_extras)
    ]
    small = pl.BlockSpec((each, block, width), lambda n: (0, 0, 0))
    specs = [pl.BlockSpec((block, coefficients.shape[1]), lambda n: (i, 0))]
    specs += [piece] * groups + rows
    args = [coefficients, shares, *extras, last_share, *last_extras]
    alias = {}
    if final:
        specs.append(small)
        args.append(arrived)
        if whole is not None:
            specs.append(pl.BlockSpec(memory_space=pl.ANY))
            args.append(whole)
            alias = {len(args) - 1: 0}
        out_spec = [
            pl.BlockSpec((each, block, width), lambda n: (0, i, 0)),
            pl.BlockSpec((8, 128), lambda n: (0, 0)),
        ]
        out_shape = [
            jax.ShapeDtypeStruct((each, coefficients.shape[0], width), F32),
            jax.ShapeDtypeStruct((8, 128), F32),
        ]
    else:
        out_spec, out_shape = small, jax.ShapeDtypeStruct((each, block, width), BF)
    return pl.pallas_call(
        kernel,
        grid=(1,),
        in_specs=specs,
        out_specs=out_spec,
        out_shape=out_shape,
        input_output_aliases=alias,
        cost_estimate=cost(0.4),
        name="mix_final" if final else "mix_inward",
    )(*args)


def hidden_units(x, w_up):
    tokens, width = x.shape
    units = w_up.shape[1]
    block = min(512, units)

    def kernel(x_ref, w, out, slope):
        up = dot(x_ref[...], w[...])
        inside = 0.5 * (1.0 + lax.erf(up * math.sqrt(0.5)))
        out[...] = (up * inside).astype(BF)
        bell = jnp.exp(-0.5 * up * up) * (1.0 / math.sqrt(2.0 * math.pi))
        slope[...] = (inside + up * bell).astype(BF)

    column = pl.BlockSpec((tokens, block), lambda i: (0, i))
    return pl.pallas_call(
        kernel,
        grid=(units // block,),
        in_specs=[
            pl.BlockSpec((tokens, width), lambda i: (0, 0)),
            pl.BlockSpec((width, block), lambda i: (0, i)),
        ],
        out_specs=[column, column],
        out_shape=[jax.ShapeDtypeStruct((tokens, units), BF)] * 2,
        cost_estimate=cost(9),
        name="hidden_units",
    )(x, w_up)


def merge_branches(attended, hidden, w_merge, w_down, stream, flag):
    tokens, inner = attended.shape
    shards, units, cols = w_down.shape
    members = lax.axis_size("stream")
    each = shards // members
    if cols % 128:
        merged = jnp.einsum("te,ned->tnd", attended, w_merge, preferred_element_type=F32)
        merged = merged + jnp.einsum("tf,nfd->tnd", hidden, w_down, preferred_element_type=F32)
        merged = merged.reshape(tokens, -1) + flag * stream
        return jnp.transpose(merged.reshape(tokens, members, -1), (1, 0, 2)).astype(BF)

    def kernel(a, h, wm, wd, st, flag_ref, out):
        out[0] = (dot(a[...], wm[0]) + dot(h[...], wd[0]) + flag_ref[0] * st[...]).astype(BF)

    return pl.pallas_call(
        kernel,
        grid=(shards,),
        in_specs=[
            pl.BlockSpec((tokens, inner), lambda n: (0, 0)),
            pl.BlockSpec((tokens, units), lambda n: (0, 0)),
            pl.BlockSpec((1, inner, cols), lambda n: (n, 0, 0)),
            pl.BlockSpec((1, units, cols), lambda n: (n, 0, 0)),
            pl.BlockSpec((tokens, cols), lambda n: (0, n)),
            pl.BlockSpec(memory_space=pltpu.SMEM),
        ],
        out_specs=pl.BlockSpec((1, tokens, cols), lambda n: (n // each, 0, n % each)),
        out_shape=jax.ShapeDtypeStruct((members, tokens, each * cols), BF),
        cost_estimate=cost(13),
        name="merge_branches",
    )(attended, hidden, w_merge, w_down, stream, flag)


def back_through(grad, stacked, slope):
    tokens = grad.shape[0]
    shards, units, cols = stacked.shape
    if cols % 128:
        split = grad.reshape(tokens, shards, cols)
        total = jnp.einsum("tnd,nfd->tf", split, stacked, preferred_element_type=F32)
        return (total if slope is None else total * slope.astype(F32)).astype(BF)

    def kernel(*refs):
        g, w = refs[:2]
        out, acc = refs[-2:]
        n = pl.program_id(0)
        part = dot_cols(g[...], w[0])

        @pl.when(n == 0)
        def _():
            acc[...] = part

        @pl.when(n > 0)
        def _():
            acc[...] += part

        @pl.when(n == shards - 1)
        def _():
            total = acc[...]
            if slope is not None:
                total = total * refs[2][...].astype(F32)
            out[...] = total.astype(BF)

    specs = [
        pl.BlockSpec((tokens, cols), lambda n: (0, n)),
        pl.BlockSpec((1, units, cols), lambda n: (n, 0, 0)),
    ]
    args = [grad, stacked]
    if slope is not None:
        specs.append(pl.BlockSpec((tokens, units), lambda n: (0, 0)))
        args.append(slope)
    return pl.pallas_call(
        kernel,
        grid=(shards,),
        in_specs=specs,
        out_specs=pl.BlockSpec((tokens, units), lambda n: (0, 0)),
        out_shape=jax.ShapeDtypeStruct((tokens, units), BF),
        scratch_shapes=[pltpu.VMEM((tokens, units), F32)],
        cost_estimate=cost(13 if slope is not None else 7),
        name="back_through",
    )(*args)


def body(
    history,
    mixing,
    shard_offset,
    norm_gain,
    norm_bias,
    w_heads,
    w_merge,
    w_up,
    w_down,
    mixer_first,
    mixer_second,
    out_cotangent,
    next_cotangent,
):
    member = lax.axis_index("stream")
    members = lax.axis_size("stream")
    shards = lax.axis_size("dp")
    index = lax.axis_index("dp")
    entries, tokens, width = history.shape
    heads_here = w_heads.shape[2] // HD
    half = tokens // 2
    highest = lax.Precision.HIGHEST
    flag = (member == members - 1).astype(F32)
    flags = flag.reshape(1)
    near = shards == 8 and heads_here * 2 == shards and tokens * shards == 2 * SEQ

    if near:
        spread = jnp.broadcast_to(shard_offset[:, None], (8, 128))
        offsets = lax.all_gather(spread, "dp", axis=0)[:, 0, 0]
        w_heads = after(w_heads, offsets)
    got_heads = Gathered(w_heads, direct=near)
    lanes = jnp.concatenate([norm_gain, norm_bias]).astype(F32).reshape(tokens, -1)
    first_rows = mixer_first.astype(F32).reshape(tokens, -1)
    second_flat = mixer_second[:, 0, :].astype(F32).reshape(-1)
    hidden_count = mixer_second.shape[0]
    lines = -(-second_flat.shape[0] // tokens)
    second_rows = jnp.pad(second_flat, (0, lines * tokens - second_flat.shape[0]))
    outputs = next_cotangent.shape[2]
    arrays = [mixing[:, 0, :], lanes, next_cotangent[:, 0, :], first_rows]
    arrays.append(second_rows.reshape(tokens, lines))
    packed = lax.all_gather(jnp.concatenate(arrays, axis=1), "stream", axis=0)
    parts, place = [], 0
    for array in arrays:
        parts.append(packed[:, :, place : place + array.shape[1]])
        place += array.shape[1]
    mix_all, norms, next_full, first_full, second_full = parts
    norms = norms.reshape(members, 2, width)
    first_full = first_full.astype(BF).reshape(width, -1)
    second_full = second_full.reshape(members, -1)[:, : second_flat.shape[0]]
    second_full = second_full.reshape(members, hidden_count, outputs)
    if near:
        early = (got_heads.by_x, got_heads.by_y, got_heads.across)
        history = after(history, *early)
        w_up, w_merge = after(w_up, *early[:2]), after(w_merge, *early[:2])
    got_up = Gathered(w_up)
    got_merge = Gathered(w_merge, direct=near)
    gains, biases = norms[:, 0], norms[:, 1]
    mix_rows = jnp.transpose(mix_all, (1, 0, 2)).reshape(tokens, members * entries)

    normed, unit, inv, stream = make_streams(history, mix_rows, gains, biases)
    full_heads = got_heads.whole()
    cotangent = lax.all_gather(after(out_cotangent, inv), "stream", axis=1, tiled=True)
    positions = shard_offset[0] + jnp.arange(tokens, dtype=jnp.int32)
    projected = project(after(normed, got_up.by_x, got_up.by_y), full_heads, rope_tables(positions, 1.0))

    if near:
        side = (index % 2).astype(jnp.int32).reshape(1)
        place = jnp.arange(shards, dtype=jnp.int32)
        first_key = jnp.maximum(place - offsets // tokens, 0).astype(jnp.int32)
        own = lax.all_to_all(projected, "dp", 0, 0, tiled=True)
        got_down = Gathered(after(w_down, own))
        other = partner(own[:, 1:], 1)
        result, exact, level = attend(own, other, first_key, side)
        full_up = got_up.whole(result)
        full_merge = got_merge.whole(result)
        back = lax.all_to_all(result, "dp", 0, 0, tiled=True)
        attended = jnp.transpose(back.reshape(heads_here, tokens, HD), (1, 0, 2)).reshape(tokens, -1)
    else:
        got_down = Gathered(w_down)
        full_up = got_up.whole()
        full_merge = got_merge.whole()
        split = projected.reshape(heads_here, 2, 3, half, HD)
        split = jnp.transpose(split, (2, 1, 3, 0, 4)).reshape(3, tokens, heads_here, HD)
        result, kept = far_attend(split[0], split[1], split[2], shard_offset)
        attended = result.reshape(tokens, -1).astype(BF)
    full_down = got_down.whole(result)
    flat_up = full_up.reshape(width, -1)
    hidden, slope = hidden_units(normed[members - 1], flat_up)
    attended = after(attended, hidden)
    hidden = after(hidden, cotangent)
    share = merge_branches(attended, hidden, full_merge, full_down, stream, flags)

    columns = lax.all_to_all(share, "stream", 0, 0, tiled=True)
    block_out = jnp.sum(columns.astype(F32), axis=0).astype(BF)
    block_full = lax.all_gather(block_out, "stream", axis=1, tiled=True)
    out_float = block_full.astype(F32)
    scale = lax.rsqrt(jnp.sum(out_float * out_float, axis=-1) / width + 1e-06)
    proj = dot(block_full, first_full)
    mixer, mixer_back = jax.vjp(exact_gelu, scale[:, None] * proj)
    second_here = mixer_second[:, 0, :].astype(F32)
    next_here = jnp.dot(mixer, second_here, precision=highest, preferred_element_type=F32)
    mixer_grad = jnp.einsum(
        "stn,scn->tc", next_full, second_full, precision=highest, preferred_element_type=F32
    )
    pre_grad = mixer_back(mixer_grad)[0]
    proj_grad = (scale[:, None] * pre_grad).astype(BF)
    scale_grad = jnp.sum(pre_grad * proj, axis=-1)
    second_local = jnp.dot(
        mixer.T, next_cotangent[:, 0, :], precision=highest, preferred_element_type=F32
    )
    first_local = dot_rows(block_out, proj_grad)
    grad_out = (
        cotangent.astype(F32)
        + dot_cols(proj_grad, first_full)
        - (scale * scale * scale * scale_grad)[:, None] * out_float / width
    ).astype(BF)

    attended_grad = back_through(grad_out, full_merge, None)
    up_grad = back_through(grad_out, full_down, slope)
    down_grad = dot_rows(hidden, grad_out).astype(BF)
    grad_down = lax.psum_scatter(down_grad, "dp", scatter_dimension=1, tiled=True).astype(F32)
    last_normed = dot_cols(after(up_grad, down_grad), flat_up)
    last_share, last_stats = last_back(
        last_normed, unit[members - 1], inv, gains[members - 1 :], grad_out, flags
    )
    last_hop = line_hop(last_share, OUTWARD)
    last_sum = (last_share.astype(F32) + last_hop.astype(F32)).astype(BF)
    last_next = line_hop(last_sum, MIDDLE)
    if near:
        sent = attended_grad.reshape(tokens, heads_here, HD)
        sent = jnp.transpose(sent, (1, 0, 2)).reshape(shards, half, HD)
        grads = lax.all_to_all(sent, "dp", 0, 0, tiled=True)
        grads = after(grads, last_share)
        kept_grads, given = attend_back(own, other, grads, exact, level, first_key, side)
        taken = partner(given, 1)
        summed = kept_grads[:, 1:].astype(F32) + taken.astype(F32)
        pair = jnp.concatenate([kept_grads[:, :1], summed.astype(BF)], axis=1)
        pair = after(pair, last_hop)
        late_grad, late_up = after(grad_out, pair), after(up_grad, pair)
        up_back = dot_rows(normed[members - 1], late_up).astype(BF)
        merge_grad = dot_rows(attended, late_grad).astype(BF)
        parts = lax.all_to_all(pair, "dp", 0, 0, tiled=True)
    else:
        up_back = dot_rows(normed[members - 1], up_grad).astype(BF)
        merge_grad = dot_rows(attended, grad_out).astype(BF)
        grads = far_attend_back(split[0], attended_grad.reshape(tokens, heads_here, HD), kept)
        parts = grads.reshape(3, 2, half, heads_here, HD)
        parts = jnp.transpose(parts, (3, 1, 0, 2, 4)).reshape(2 * heads_here, 3, half, HD)

    parts = after(parts, last_sum, grad_down, up_back, merge_grad)
    spans = block_spans(tokens)
    *pieces, heads_share, heads_grad, heads_stats = heads_back(
        parts, full_heads, normed, unit, inv, gains, rope_tables(positions, -1.0), spans
    )

    grad_merge = lax.psum_scatter(merge_grad, "dp", scatter_dimension=1, tiled=True).astype(F32)
    grad_heads = lax.psum_scatter(heads_grad, "dp", scatter_dimension=1, tiled=True).astype(F32)
    grad_up = lax.psum_scatter(up_back, "dp", scatter_dimension=0, tiled=True).astype(F32)

    each = entries // members

    def weights_for(owner):
        block = lax.dynamic_slice_in_dim(mix_all, owner * each, each, axis=2)
        return jnp.transpose(block, (1, 2, 0)).reshape(tokens, each * members)

    there = weights_for(jnp.where(member == 1, 0, members - 1))
    here = weights_for(member)
    extra = {}

    last_one = lambda i: last_hop
    last_two = lambda i: last_next

    def first_hop(i, gates):
        gates = list(gates)
        if i == 3:
            gates.append(grad_merge)
        return gated(pieces[i], gates)

    def small_sums():
        stats = jnp.concatenate([heads_stats, last_stats[None]]).reshape(members, tokens, -1)
        both = jnp.concatenate([jnp.concatenate(mixes, axis=1), stats], axis=2)
        both = jnp.sum(lax.all_to_all(both, "stream", 0, 0, tiled=True), axis=0)
        second_sums = jnp.pad(second_local.reshape(-1), (0, lines * tokens - second_flat.shape[0]))
        local = [both[:, entries:], first_local.reshape(tokens, -1), second_sums.reshape(tokens, lines)]
        everyone = lax.all_gather(jnp.concatenate(local, axis=1), "dp", axis=0)
        return both[:, :entries], jnp.sum(everyone, axis=0)

    mixes = [mixing_back(heads_share, last_share, history, i, 2) for i in range(2)]

    extra["both"], extra["all"] = small_sums()

    def second_hop(i, one):
        load = (pieces[i].astype(F32) + one.astype(F32)).astype(BF)
        return after(load, *mixes) if i == 0 else load

    def third_hop(i, one, two):
        load = mix_block(spans[i][0], there, pieces[i], last_share, [two], [last_two(i)], None, None)
        return after(load, extra["both"]) if i == 2 else load

    def finish(i, one, two, three):
        if i == 3:
            three = after(three, grad_heads, extra["all"])
        extra["history"], token = mix_block(
            spans[i][0],
            here,
            pieces[i],
            last_share,
            [one, two],
            [last_one(i), last_two(i)],
            three,
            extra.get("history"),
        )
        return token

    along_line(len(spans), first_hop, second_hop, third_hop, finish)
    grad_history = extra["history"]

    grad_mixing = extra["both"][:, None, :]
    sums = extra["all"]
    columns = 2 * width // tokens
    stats = sums[:, :columns].reshape(2, width)
    grad_first = sums[:, columns:-lines].reshape(mixer_first.shape)
    grad_second = sums[:, -lines:].reshape(-1)[: second_flat.shape[0]].reshape(hidden_count, outputs)
    return (
        block_out,
        next_here[:, None, :],
        grad_history,
        grad_mixing,
        stats[:1],
        stats[1:],
        grad_heads,
        grad_merge,
        grad_up,
        grad_down,
        grad_first,
        grad_second[:, None, :],
    )


def solution(mesh):
    in_specs = (
        P(None, "dp", None),
        P("dp", "stream", None),
        P("dp"),
        P("stream", None),
        P("stream", None),
        P(None, "dp", "stream"),
        P("stream", "dp"),
        P("dp", "stream"),
        P("stream", "dp"),
        P("stream", None),
        P(None, "stream", None),
        P("dp", "stream"),
        P("dp", "stream", None),
    )
    out_specs = (
        P("dp", "stream"),
        P("dp", "stream", None),
        P("stream", "dp", None),
        P("dp", "stream", None),
        P("stream", None),
        P("stream", None),
        P(None, "dp", "stream"),
        P("stream", "dp"),
        P("dp", "stream"),
        P("stream", "dp"),
        P("stream", None),
        P(None, "stream", None),
    )
    return jax.shard_map(body, mesh=mesh, in_specs=in_specs, out_specs=out_specs, check_vma=False)
```

```python
import math

import jax
import jax.numpy as jnp
from jax import lax
from jax.experimental import pallas as pl
from jax.experimental.pallas import tpu as pltpu
from jax.sharding import PartitionSpec as P

HD = 128
ROT = 32
SEQ = 2048


def passed_along(shard, axis, by):
    peers = lax.axis_size(axis)
    pairs = [(i, i + by) for i in range(peers) if 0 <= i + by < peers]
    return lax.ppermute(shard, axis, pairs)


def rotate(vectors, positions, sign):
    half = ROT // 2
    counter = jnp.arange(half, dtype=jnp.float32)
    freqs = jnp.exp(counter * (-2.0 * math.log(10000.0) / ROT))
    angles = positions.astype(jnp.float32)[:, None] * freqs[None, :]
    cosine = jnp.cos(angles)[:, None, :]
    sine = sign * jnp.sin(angles)[:, None, :]
    first = vectors[..., :half]
    second = vectors[..., half:ROT]
    return jnp.concatenate(
        [first * cosine - second * sine, second * cosine + first * sine, vectors[..., ROT:]],
        axis=-1,
    )


def exact_gelu(vectors):
    return jax.nn.gelu(vectors, approximate=False)


def block_logits(queries, keys_block, diagonal):
    logits = jnp.einsum("qhd,khd->hqk", queries, keys_block, preferred_element_type=jnp.float32) * (
        1.0 / math.sqrt(queries.shape[-1])
    )
    if diagonal:
        counter = jnp.arange(queries.shape[0], dtype=jnp.int32)
        allowed = counter[None, :] <= counter[:, None]
        logits = jnp.where(allowed[None], logits, -1e30)
    return logits


def keep_same(state):
    return state


BF = jnp.bfloat16
SHARE = 1.0
F32 = jnp.float32
OUTWARD = [(0, 1), (3, 2)]
MIDDLE = [(1, 2), (2, 1)]
INWARD = [(1, 0), (2, 3)]


def dot(left, right):
    return jnp.dot(left, right, preferred_element_type=F32)


def dot_rows(left, right):
    return lax.dot_general(left, right, (((0,), (0,)), ((), ())), preferred_element_type=F32)


def dot_cols(left, right):
    return lax.dot_general(left, right, (((1,), (1,)), ((), ())), preferred_element_type=F32)


def partner(shard, bit):
    peers = lax.axis_size("dp")
    return lax.ppermute(shard, "dp", [(i, i ^ bit) for i in range(peers)])


def line_hop(shard, pairs):
    return lax.ppermute(shard, "stream", pairs)


def cost(microseconds):
    return pl.CostEstimate(
        flops=int(microseconds * SHARE * 0.9e9),
        bytes_accessed=int(microseconds * SHARE * 3e6),
        transcendentals=0,
    )


def after(value, *others):
    return lax.optimization_barrier((value, *others))[0]


class Gathered:
    def __init__(self, shard, direct=False):
        self.shard = shard
        self.peers = lax.axis_size("dp")
        if self.peers != 8:
            self.by_x = self.by_y = shard
            return
        self.cut = max(range(shard.ndim - 1), key=lambda dim: shard.shape[dim])
        self.by_x = partner(shard, 2)
        self.by_y = partner(shard, 4)
        self.across = partner(shard, 6) if direct else None

    def whole(self, *earlier):
        shard = self.shard
        if self.peers != 8:
            return lax.all_gather(shard, "dp", axis=0)
        index = lax.axis_index("dp")
        cut = self.cut
        half = shard.shape[cut] // 2
        shard, by_x, by_y = [gated(item, earlier) for item in (shard, self.by_x, self.by_y)]
        pieces = [(shard, 0, 0), (by_x, 2, 0), (by_y, 4, 0)]
        if self.across is None:
            low = lax.slice_in_dim(by_y, 0, half, axis=cut)
            high = lax.slice_in_dim(by_x, half, 2 * half, axis=cut)
            pieces += [(partner(low, 2), 6, 0), (partner(high, 4), 6, half)]
        else:
            pieces.append((gated(self.across, earlier), 6, 0))
        pieces += [(partner(piece, 1), code ^ 1, start) for piece, code, start in pieces]
        return put_together(pieces, shard, self.peers, cut, index)


def put_together(pieces, shard, peers, cut, index):
    codes = [(code, start) for _, code, start in pieces]
    arrays = [piece for piece, _, _ in pieces]

    def kernel(place, *refs):
        out, held, sems, sent = refs[-4:]
        owners = {}
        for n, (code, start) in enumerate(codes):
            size = refs[n].shape[cut]
            span = tuple(
                pl.ds(start, size) if dim == cut else slice(None) for dim in range(shard.ndim)
            )
            copy = pltpu.make_async_copy(refs[n], held.at[(code, *span)], sems.at[n])
            copy.start()
            owners.setdefault(code, []).append(copy)
        leaving = []
        for code, copies in owners.items():
            for copy in copies:
                copy.wait()
            copy = pltpu.make_async_copy(held.at[code], out.at[place[0] ^ code], sent.at[code])
            copy.start()
            leaving.append(copy)
        for copy in leaving:
            copy.wait()

    anywhere = pl.BlockSpec(memory_space=pl.ANY)
    size = peers * shard.size * shard.dtype.itemsize
    return pl.pallas_call(
        kernel,
        in_specs=[pl.BlockSpec(memory_space=pltpu.SMEM)] + [anywhere] * len(arrays),
        out_specs=anywhere,
        out_shape=jax.ShapeDtypeStruct((peers, *shard.shape), shard.dtype),
        scratch_shapes=[
            pltpu.VMEM((peers, *shard.shape), shard.dtype),
            pltpu.SemaphoreType.DMA((len(arrays),)),
            pltpu.SemaphoreType.DMA((peers,)),
        ],
        cost_estimate=cost(2 * size / 3e6),
        name="put_together",
    )(index.astype(jnp.int32).reshape(1), *arrays)


def block_spans(tokens):
    sizes = [tokens // 4] * 4
    return [(sum(sizes[:i]), size) for i, size in enumerate(sizes)]


def along_line(count, first, second, third, finish=None):
    ones, twos, threes, ends = [], [], [], []
    for step in range(count + 2):
        old = []
        if step >= 4:
            old.append(threes[step - 4] if finish is None else ends[step - 4])
        if step < count:
            gates = list(old)
            if step >= 2:
                gates.append(ones[step - 2])
            if step >= 3:
                gates.append(twos[step - 3])
            ones.append(line_hop(first(step, gates), OUTWARD))
        if 0 <= step - 1 < count:
            load = second(step - 1, ones[step - 1])
            twos.append(line_hop(gated(load, old), MIDDLE))
        if 0 <= step - 2 < count:
            back = step - 2
            load = third(back, ones[back], twos[back])
            ahead = ones[back + 2 : back + 3]
            threes.append(line_hop(gated(load, old + ahead), INWARD))
            if finish is not None:
                ends.append(finish(back, ones[back], twos[back], threes[back]))
    return ones, twos, threes


def gated(value, gates):
    return after(value, *gates) if gates else value


def rope_tables(positions, sign):
    half = ROT // 2
    lane = jnp.arange(HD, dtype=jnp.int32)
    counter = (lane % half).astype(F32)
    freqs = jnp.exp(counter * (-2.0 * math.log(10000.0) / ROT))
    angles = positions.astype(F32)[:, None] * freqs[None, :]
    cosine = jnp.where(lane < ROT, jnp.cos(angles), 1.0)
    sine = sign * jnp.sin(angles)
    up = jnp.where(lane < half, -sine, 0.0)
    down = jnp.where((lane >= half) & (lane < ROT), sine, 0.0)
    return jnp.stack([cosine, up, down])


def turned(block, tables):
    half = ROT // 2
    return (
        block * tables[0]
        + pltpu.roll(block, HD - half, 1) * tables[1]
        + pltpu.roll(block, half, 1) * tables[2]
    )


def make_streams(history, mix_rows, gains, biases):
    entries, tokens, width = history.shape
    streams = gains.shape[0]
    rows, sub, lanes = min(64, tokens), 16, 512

    def kernel(hist, mix, gain, bias, normed, unit, inv, last, scratch):
        def step(r, carry):
            here = pl.ds(pl.multiple_of(r * sub, sub), sub)
            weights = mix[here, :]
            columns = [
                [weights[:, s * entries + j : s * entries + j + 1] for j in range(entries)]
                for s in range(streams)
            ]
            for lane in range(0, width, lanes):
                span = slice(lane, lane + lanes)
                sums = [None] * streams
                for j in range(entries):
                    part = hist[j, here, span].astype(F32)
                    for s in range(streams):
                        term = columns[s][j] * part
                        sums[s] = term if j == 0 else sums[s] + term
                for s in range(streams):
                    scratch[s, :, span] = sums[s]
            stds = []
            for s in range(streams):
                values = scratch[s]
                center = values - jnp.sum(values, axis=-1, keepdims=True) * (1.0 / width)
                var = jnp.sum(center * center, axis=-1, keepdims=True) * (1.0 / width)
                std = lax.rsqrt(var + 1e-05)
                stds.append(std)
                scaled = center * std
                unit[s, here, :] = scaled.astype(BF)
                normed[s, here, :] = (scaled * gain[s : s + 1] + bias[s : s + 1]).astype(BF)
            last[here, :] = scratch[streams - 1]
            inv[here, :] = jnp.concatenate(stds, axis=-1)
            return carry

        lax.fori_loop(0, rows // sub, step, 0)

    wide = jax.ShapeDtypeStruct((streams, tokens, width), BF)
    return pl.pallas_call(
        kernel,
        grid=(tokens // rows,),
        in_specs=[
            pl.BlockSpec((entries, rows, width), lambda i: (0, i, 0)),
            pl.BlockSpec((rows, streams * entries), lambda i: (i, 0)),
            pl.BlockSpec((streams, width), lambda i: (0, 0)),
            pl.BlockSpec((streams, width), lambda i: (0, 0)),
        ],
        out_specs=[
            pl.BlockSpec((streams, rows, width), lambda i: (0, i, 0)),
            pl.BlockSpec((streams, rows, width), lambda i: (0, i, 0)),
            pl.BlockSpec((rows, streams), lambda i: (i, 0)),
            pl.BlockSpec((rows, width), lambda i: (i, 0)),
        ],
        out_shape=[
            wide,
            wide,
            jax.ShapeDtypeStruct((tokens, streams), F32),
            jax.ShapeDtypeStruct((tokens, width), F32),
        ],
        scratch_shapes=[pltpu.VMEM((streams, sub, width), F32)],
        cost_estimate=cost(22),
        name="make_streams",
    )(history, mix_rows, gains, biases)


def project(normed, w_heads, tables):
    _, tokens, width = normed.shape
    columns = w_heads.shape[3]
    heads, half = columns // HD, tokens // 2

    def kernel(x, w, table, out):
        flat = dot(x[0], w[...].reshape(width, columns))
        turn = pl.program_id(0) < 2

        def put(head, block):
            out[2 * head, 0] = block[:half].astype(BF)
            out[2 * head + 1, 0] = block[half:].astype(BF)

        @pl.when(turn)
        def _():
            for head in range(heads):
                put(head, turned(flat[:, head * HD : (head + 1) * HD], table[...]))

        @pl.when(jnp.logical_not(turn))
        def _():
            for head in range(heads):
                put(head, flat[:, head * HD : (head + 1) * HD])

    return pl.pallas_call(
        kernel,
        grid=(3,),
        in_specs=[
            pl.BlockSpec((1, tokens, width), lambda c: (c, 0, 0)),
            pl.BlockSpec((w_heads.shape[0], 1, w_heads.shape[2], columns), lambda c: (0, c, 0, 0)),
            pl.BlockSpec((3, tokens, HD), lambda c: (0, 0, 0)),
        ],
        out_specs=pl.BlockSpec((2 * heads, 1, half, HD), lambda c: (0, c, 0, 0)),
        out_shape=jax.ShapeDtypeStruct((2 * heads, 3, half, HD), BF),
        cost_estimate=cost(9),
        name="project",
    )(normed, w_heads, tables)


def attend(own, other, first_key, side):
    shards, _, half, _ = own.shape
    factor = 1.0 / math.sqrt(HD)

    def kernel(first, part, mine, theirs, out, exact, norm):
        s = pl.program_id(0)
        query = mine[s, 0]

        def fold(state, keys, values, mask):
            top, total, acc = state
            logits = dot_cols(query, keys) * factor
            if mask is not None:
                logits = jnp.where(mask, logits, -1e30)
            new_top = jnp.maximum(top, jnp.max(logits, axis=-1, keepdims=True))
            probs = jnp.exp(logits - new_top)
            keep = jnp.exp(top - new_top)
            return (
                new_top,
                total * keep + jnp.sum(probs, axis=-1, keepdims=True),
                acc * keep + dot(probs.astype(BF), values),
            )

        row = lax.broadcasted_iota(jnp.int32, (half, half), 0)
        col = lax.broadcasted_iota(jnp.int32, (half, half), 1)
        state = (
            jnp.full((half, 1), -1e30, F32),
            jnp.zeros((half, 1), F32),
            jnp.zeros((half, HD), F32),
        )
        state = fold(state, mine[s, 1], mine[s, 2], col <= row)
        state = lax.fori_loop(
            0, part[0], lambda i, st: fold(st, theirs[s, 0], theirs[s, 1], None), state
        )

        def shard_step(b, st):
            st = fold(st, mine[b, 1], mine[b, 2], None)
            return fold(st, theirs[b, 0], theirs[b, 1], None)

        top, total, acc = lax.fori_loop(first[s], s, shard_step, state)
        result = acc / total
        out[0] = result.astype(BF)
        exact[0] = result
        norm[0] = top + jnp.log(total)

    return pl.pallas_call(
        kernel,
        grid_spec=pltpu.PrefetchScalarGridSpec(
            num_scalar_prefetch=2,
            grid=(shards,),
            in_specs=[
                pl.BlockSpec((shards, 3, half, HD), lambda s, *_: (0, 0, 0, 0)),
                pl.BlockSpec((shards, 2, half, HD), lambda s, *_: (0, 0, 0, 0)),
            ],
            out_specs=[
                pl.BlockSpec((1, half, HD), lambda s, *_: (s, 0, 0)),
                pl.BlockSpec((1, half, HD), lambda s, *_: (s, 0, 0)),
                pl.BlockSpec((1, half, 1), lambda s, *_: (s, 0, 0)),
            ],
        ),
        out_shape=[
            jax.ShapeDtypeStruct((shards, half, HD), BF),
            jax.ShapeDtypeStruct((shards, half, HD), F32),
            jax.ShapeDtypeStruct((shards, half, 1), F32),
        ],
        cost_estimate=cost(16),
        name="attend",
    )(first_key, side, own, other)


def attend_back(own, other, grads, exact, norm, first_key, side):
    shards, _, half, _ = own.shape
    factor = 1.0 / math.sqrt(HD)

    def kernel(first, part, mine, theirs, grad_ref, exact_ref, norm_ref, kept, given, sums):
        s = pl.program_id(0)
        query = mine[s, 0]
        grad = grad_ref[s]
        delta = jnp.sum(grad.astype(F32) * exact_ref[0], axis=-1, keepdims=True)
        level = norm_ref[0]
        lowered = grad

        @pl.when(s == 0)
        def _():
            sums[...] = jnp.zeros_like(sums)

        def fold(query_grad, keys, values, mask, slot, b):
            logits = dot_cols(query, keys) * factor
            probs = jnp.exp(logits - level)
            if mask is not None:
                probs = jnp.where(mask, probs, 0.0)
            score = (probs * (dot_cols(grad, values) - delta)).astype(BF)
            sums[slot, b] += dot_rows(score, query)
            sums[slot + 1, b] += dot_rows(probs.astype(BF), lowered)
            return query_grad + dot(score, keys)

        row = lax.broadcasted_iota(jnp.int32, (half, half), 0)
        col = lax.broadcasted_iota(jnp.int32, (half, half), 1)
        total = fold(jnp.zeros((half, HD), F32), mine[s, 1], mine[s, 2], col <= row, 0, s)
        total = lax.fori_loop(
            0, part[0], lambda i, q: fold(q, theirs[s, 0], theirs[s, 1], None, 2, s), total
        )

        def shard_step(b, q):
            q = fold(q, mine[b, 1], mine[b, 2], None, 0, b)
            return fold(q, theirs[b, 0], theirs[b, 1], None, 2, b)

        total = lax.fori_loop(first[s], s, shard_step, total)
        kept[s, 0] = (total * factor).astype(BF)

        @pl.when(s == shards - 1)
        def _():
            for b in range(shards):
                kept[b, 1] = (sums[0, b] * factor).astype(BF)
                kept[b, 2] = sums[1, b].astype(BF)
                given[b, 0] = (sums[2, b] * factor).astype(BF)
                given[b, 1] = sums[3, b].astype(BF)

    whole = lambda n: pl.BlockSpec((shards, n, half, HD), lambda s, *_: (0, 0, 0, 0))
    return pl.pallas_call(
        kernel,
        grid_spec=pltpu.PrefetchScalarGridSpec(
            num_scalar_prefetch=2,
            grid=(shards,),
            in_specs=[
                whole(3),
                whole(2),
                pl.BlockSpec((shards, half, HD), lambda s, *_: (0, 0, 0)),
                pl.BlockSpec((1, half, HD), lambda s, *_: (s, 0, 0)),
                pl.BlockSpec((1, half, 1), lambda s, *_: (s, 0, 0)),
            ],
            out_specs=[whole(3), whole(2)],
            scratch_shapes=[pltpu.VMEM((4, shards, half, HD), F32)],
        ),
        out_shape=[
            jax.ShapeDtypeStruct((shards, 3, half, HD), BF),
            jax.ShapeDtypeStruct((shards, 2, half, HD), BF),
        ],
        cost_estimate=cost(22),
        name="attend_back",
    )(first_key, side, own, other, grads, exact, norm)


def norm_back(grad, unit, inv, gain, extra):
    width = grad.shape[1]
    scaled = grad * gain
    mean = jnp.sum(scaled, axis=-1, keepdims=True) * (1.0 / width)
    slope = jnp.sum(scaled * unit, axis=-1, keepdims=True) * (1.0 / width)
    result = inv * (scaled - mean - unit * slope)
    return result if extra is None else result + extra


def heads_back(parts, w_heads, normed, unit, inv, gains, tables, spans):
    _, tokens, width = normed.shape
    columns = w_heads.shape[3]
    heads, half = columns // HD, tokens // 2
    count = len(spans)

    def kernel(part, w, x, u, istd, gain, table, *refs):
        pieces, (stream, weight, stats, grad, wide) = refs[:count], refs[count:]
        c = pl.program_id(0)
        turn = c < 2

        def take(head):
            return jnp.concatenate([part[2 * head, 0], part[2 * head + 1, 0]], axis=0).astype(F32)

        @pl.when(turn)
        def _():
            for head in range(heads):
                grad[:, head * HD : (head + 1) * HD] = turned(take(head), table[...]).astype(BF)

        @pl.when(jnp.logical_not(turn))
        def _():
            for head in range(heads):
                grad[:, head * HD : (head + 1) * HD] = take(head).astype(BF)

        wide[...] = dot_cols(grad[...], w[...].reshape(width, columns))
        weight[0] = dot_rows(x[0], grad[...]).astype(BF)
        stats[...] = jnp.zeros_like(stats)
        for r, (start, block) in enumerate(spans):
            column = lax.broadcasted_iota(jnp.int32, (block, istd.shape[1]), 1)
            here = slice(start, start + block)
            values = wide[here, :]
            units = u[0, here, :].astype(F32)
            std = jnp.sum(jnp.where(column == c, istd[here, :], 0.0), axis=-1, keepdims=True)
            result = norm_back(values, units, std, gain[0], None).astype(BF)
            stream[0, here, :] = result
            pieces[r][0] = result
            stats[0, 0:1] += jnp.sum(values * units, axis=0, keepdims=True)
            stats[0, 1:2] += jnp.sum(values, axis=0, keepdims=True)

    return pl.pallas_call(
        kernel,
        grid=(3,),
        in_specs=[
            pl.BlockSpec((2 * heads, 1, half, HD), lambda c: (0, c, 0, 0)),
            pl.BlockSpec((w_heads.shape[0], 1, w_heads.shape[2], columns), lambda c: (0, c, 0, 0)),
            pl.BlockSpec((1, tokens, width), lambda c: (c, 0, 0)),
            pl.BlockSpec((1, tokens, width), lambda c: (c, 0, 0)),
            pl.BlockSpec((tokens, inv.shape[1]), lambda c: (0, 0)),
            pl.BlockSpec((1, 1, width), lambda c: (c, 0, 0)),
            pl.BlockSpec((3, tokens, HD), lambda c: (0, 0, 0)),
        ],
        out_specs=[pl.BlockSpec((1, block, width), lambda c: (c, 0, 0)) for _, block in spans]
        + [
            pl.BlockSpec((1, tokens, width), lambda c: (c, 0, 0)),
            pl.BlockSpec((1, width, columns), lambda c: (c, 0, 0)),
            pl.BlockSpec((1, 2, width), lambda c: (c, 0, 0)),
        ],
        out_shape=[jax.ShapeDtypeStruct((3, block, width), BF) for _, block in spans]
        + [
            jax.ShapeDtypeStruct((3, tokens, width), BF),
            jax.ShapeDtypeStruct((3, width, columns), BF),
            jax.ShapeDtypeStruct((3, 2, width), F32),
        ],
        scratch_shapes=[pltpu.VMEM((tokens, columns), BF), pltpu.VMEM((tokens, width), F32)],
        cost_estimate=cost(3),
        name="heads_back",
    )(parts, w_heads, normed, unit, inv, gains[:, None, :], tables)


def last_back(grad, unit, inv, gain, extra, flag):
    tokens, width = grad.shape
    block = min(128, tokens)

    def kernel(g, u, istd, gain_ref, e, flag_ref, stream, stats):
        @pl.when(pl.program_id(0) == 0)
        def _():
            stats[...] = jnp.zeros_like(stats)

        values = g[...]
        units = u[...].astype(F32)
        std = istd[...][:, -1:]
        added = e[...].astype(F32) * flag_ref[0]
        stream[...] = norm_back(values, units, std, gain_ref[...], added).astype(BF)
        stats[0:1] += jnp.sum(values * units, axis=0, keepdims=True)
        stats[1:2] += jnp.sum(values, axis=0, keepdims=True)

    row = lambda n: pl.BlockSpec((block, n), lambda i: (i, 0))
    return pl.pallas_call(
        kernel,
        grid=(tokens // block,),
        in_specs=[
            row(width),
            row(width),
            row(inv.shape[1]),
            pl.BlockSpec((1, width), lambda i: (0, 0)),
            row(width),
            pl.BlockSpec(memory_space=pltpu.SMEM),
        ],
        out_specs=[row(width), pl.BlockSpec((2, width), lambda i: (0, 0))],
        out_shape=[
            jax.ShapeDtypeStruct((tokens, width), BF),
            jax.ShapeDtypeStruct((2, width), F32),
        ],
        cost_estimate=cost(7),
        name="last_back",
    )(grad, unit, inv, gain, extra, flag)


def mixing_back(heads_part, last_part, history, which, of):
    entries, tokens, width = history.shape
    streams = heads_part.shape[0] + 1
    rows, sub, lanes = min(64, tokens // of), 16, 256
    steps = tokens // of // rows
    base = which * steps

    def kernel(first, last, hist, out):
        def step(r, carry):
            here = pl.ds(pl.multiple_of(r * sub, sub), sub)
            for s in range(streams):
                sums = [None] * entries
                for lane in range(0, width, lanes):
                    span = slice(lane, lane + lanes)
                    part = first[s, here, span] if s < streams - 1 else last[here, span]
                    part = part.astype(F32)
                    for j in range(entries):
                        term = part * hist[j, here, span].astype(F32)
                        sums[j] = term if lane == 0 else sums[j] + term
                columns = [jnp.sum(item, axis=-1, keepdims=True) for item in sums]
                out[s, here, :] = jnp.concatenate(columns, axis=-1)
            return carry

        lax.fori_loop(0, rows // sub, step, 0)

    return pl.pallas_call(
        kernel,
        grid=(steps,),
        in_specs=[
            pl.BlockSpec((streams - 1, rows, width), lambda i: (0, base + i, 0)),
            pl.BlockSpec((rows, width), lambda i: (base + i, 0)),
            pl.BlockSpec((entries, rows, width), lambda i: (0, base + i, 0)),
        ],
        out_specs=pl.BlockSpec((streams, rows, entries), lambda i: (0, i, 0)),
        out_shape=jax.ShapeDtypeStruct((streams, tokens // of, entries), F32),
        cost_estimate=cost(0.4),
        name="mixing_back",
    )(heads_part, last_part, history)


def far_attend(queries, keys, values, shard_offset):
    tokens, heads_here, head_size = queries.shape
    data_index = lax.axis_index("dp")
    pairs = [jnp.stack([keys, values])]
    reach = 2 * SEQ // tokens
    for back in range(1, reach):
        pairs.append(passed_along(pairs[0], "dp", back))
    usable = [(shard_offset[0] >= back * tokens) & (data_index >= back) for back in range(reach)]
    first_logits = block_logits(queries, keys, True)
    top = jnp.max(first_logits, axis=-1)
    total = jnp.sum(jnp.exp(first_logits - top[..., None]), axis=-1)
    for back in range(1, reach):

        def widen(state, block=pairs[back][0]):
            logits = block_logits(queries, block, False)
            new_top = jnp.maximum(state[0], jnp.max(logits, axis=-1))
            summed = state[1] * jnp.exp(state[0] - new_top) + jnp.sum(
                jnp.exp(logits - new_top[..., None]), axis=-1
            )
            return (new_top, summed)

        top, total = lax.cond(usable[back], widen, keep_same, (top, total))
    log_total = top + jnp.log(total)
    attended = jnp.zeros((tokens, heads_here, head_size), F32)
    for back in range(reach):

        def accumulate(current, block=pairs[back], diagonal=back == 0):
            probs = jnp.exp(block_logits(queries, block[0], diagonal) - log_total[..., None])
            return current + jnp.einsum(
                "hqk,khd->qhd", probs.astype(BF), block[1], preferred_element_type=F32
            )

        attended = lax.cond(usable[back], accumulate, keep_same, attended)
    return attended, (pairs, usable, log_total)


def far_attend_back(queries, attended_grad, kept):
    tokens, heads_here, head_size = queries.shape
    factor = 1.0 / math.sqrt(head_size)
    pairs, usable, log_total = kept
    reach = len(pairs)

    def weights_of(block, diagonal):
        return jnp.exp(block_logits(queries, block, diagonal) - log_total[..., None])

    def prob_grads(block):
        return jnp.einsum("qhd,khd->hqk", attended_grad, block[1], preferred_element_type=F32)

    delta = jnp.zeros((heads_here, tokens), F32)
    for back in range(reach):

        def gather_delta(current, block=pairs[back], diagonal=back == 0):
            return current + jnp.sum(weights_of(block[0], diagonal) * prob_grads(block), axis=-1)

        delta = lax.cond(usable[back], gather_delta, keep_same, delta)

    def skip_block(current):
        return (current, jnp.zeros((2, tokens, heads_here, head_size), F32))

    query_grad = jnp.zeros((tokens, heads_here, head_size), F32)
    key_value_grad = jnp.zeros((2, tokens, heads_here, head_size), F32)
    for back in range(reach):

        def spread(current, block=pairs[back], diagonal=back == 0):
            probs = weights_of(block[0], diagonal)
            score_grad = (probs * (prob_grads(block) - delta[..., None])).astype(BF)
            query_part = (
                current
                + jnp.einsum("hqk,khd->qhd", score_grad, block[0], preferred_element_type=F32)
                * factor
            )
            key_part = (
                jnp.einsum("hqk,qhd->khd", score_grad, queries, preferred_element_type=F32)
                * factor
            )
            value_part = jnp.einsum(
                "hqk,qhd->khd", probs.astype(BF), attended_grad, preferred_element_type=F32
            )
            return (query_part, jnp.stack([key_part, value_part]))

        query_grad, pair_grad = lax.cond(usable[back], spread, skip_block, query_grad)
        if back == 0:
            key_value_grad = pair_grad
        else:
            key_value_grad = key_value_grad + passed_along(pair_grad, "dp", -back)
    return jnp.concatenate([query_grad[None], key_value_grad])


def mix_block(start, coefficients, shares, last_share, extras, last_extras, arrived, whole):
    streams, block, width = shares.shape
    each = coefficients.shape[1] // (streams + 1)
    groups = 1 + len(extras)
    final = arrived is not None
    lanes = 512

    def kernel(*refs):
        weights = refs[0][...]
        heads, lasts = refs[1 : 1 + groups], refs[1 + groups : 1 + 2 * groups]
        out = refs[-2] if final else refs[-1]
        if final:
            refs[-1][...] = jnp.zeros_like(refs[-1])
        columns = [weights[:, n : n + 1] for n in range(weights.shape[1])]
        for lane in range(0, width, lanes):
            span = slice(lane, lane + lanes)
            values = []
            for s in range(streams + 1):
                picks = [r[s, :, span] if s < streams else l[:, span] for r, l in zip(heads, lasts)]
                total = picks[0].astype(F32)
                for pick in picks[1:]:
                    total = total + pick.astype(F32)
                values.append(total)
            for e in range(each):
                total = columns[e * (streams + 1)] * values[0]
                for s in range(1, streams + 1):
                    total = total + columns[e * (streams + 1) + s] * values[s]
                if final:
                    total = total + refs[1 + 2 * groups][e, :, span].astype(F32)
                out[e, :, span] = total.astype(out.dtype)

    i = start // block
    piece = pl.BlockSpec((streams, block, width), lambda n: (0, 0, 0))
    rows = [
        pl.BlockSpec((block, width), lambda n, at=start % item.shape[0] // block: (at, 0))
        for item in (last_share, *last_extras)
    ]
    small = pl.BlockSpec((each, block, width), lambda n: (0, 0, 0))
    specs = [pl.BlockSpec((block, coefficients.shape[1]), lambda n: (i, 0))]
    specs += [piece] * groups + rows
    args = [coefficients, shares, *extras, last_share, *last_extras]
    alias = {}
    if final:
        specs.append(small)
        args.append(arrived)
        if whole is not None:
            specs.append(pl.BlockSpec(memory_space=pl.ANY))
            args.append(whole)
            alias = {len(args) - 1: 0}
        out_spec = [
            pl.BlockSpec((each, block, width), lambda n: (0, i, 0)),
            pl.BlockSpec((8, 128), lambda n: (0, 0)),
        ]
        out_shape = [
            jax.ShapeDtypeStruct((each, coefficients.shape[0], width), F32),
            jax.ShapeDtypeStruct((8, 128), F32),
        ]
    else:
        out_spec, out_shape = small, jax.ShapeDtypeStruct((each, block, width), BF)
    return pl.pallas_call(
        kernel,
        grid=(1,),
        in_specs=specs,
        out_specs=out_spec,
        out_shape=out_shape,
        input_output_aliases=alias,
        cost_estimate=cost(0.4),
        name="mix_final" if final else "mix_inward",
    )(*args)


def hidden_units(x, w_up):
    tokens, width = x.shape
    units = w_up.shape[1]
    block = min(512, units)

    def kernel(x_ref, w, out, slope):
        up = dot(x_ref[...], w[...])
        inside = 0.5 * (1.0 + lax.erf(up * math.sqrt(0.5)))
        out[...] = (up * inside).astype(BF)
        bell = jnp.exp(-0.5 * up * up) * (1.0 / math.sqrt(2.0 * math.pi))
        slope[...] = (inside + up * bell).astype(BF)

    column = pl.BlockSpec((tokens, block), lambda i: (0, i))
    return pl.pallas_call(
        kernel,
        grid=(units // block,),
        in_specs=[
            pl.BlockSpec((tokens, width), lambda i: (0, 0)),
            pl.BlockSpec((width, block), lambda i: (0, i)),
        ],
        out_specs=[column, column],
        out_shape=[jax.ShapeDtypeStruct((tokens, units), BF)] * 2,
        cost_estimate=cost(9),
        name="hidden_units",
    )(x, w_up)


def merge_branches(attended, hidden, w_merge, w_down, stream, flag):
    tokens, inner = attended.shape
    shards, units, cols = w_down.shape
    members = lax.axis_size("stream")
    each = shards // members
    if cols % 128:
        merged = jnp.einsum("te,ned->tnd", attended, w_merge, preferred_element_type=F32)
        merged = merged + jnp.einsum("tf,nfd->tnd", hidden, w_down, preferred_element_type=F32)
        merged = merged.reshape(tokens, -1) + flag * stream
        return jnp.transpose(merged.reshape(tokens, members, -1), (1, 0, 2)).astype(BF)

    def kernel(a, h, wm, wd, st, flag_ref, out):
        out[0] = (dot(a[...], wm[0]) + dot(h[...], wd[0]) + flag_ref[0] * st[...]).astype(BF)

    return pl.pallas_call(
        kernel,
        grid=(shards,),
        in_specs=[
            pl.BlockSpec((tokens, inner), lambda n: (0, 0)),
            pl.BlockSpec((tokens, units), lambda n: (0, 0)),
            pl.BlockSpec((1, inner, cols), lambda n: (n, 0, 0)),
            pl.BlockSpec((1, units, cols), lambda n: (n, 0, 0)),
            pl.BlockSpec((tokens, cols), lambda n: (0, n)),
            pl.BlockSpec(memory_space=pltpu.SMEM),
        ],
        out_specs=pl.BlockSpec((1, tokens, cols), lambda n: (n // each, 0, n % each)),
        out_shape=jax.ShapeDtypeStruct((members, tokens, each * cols), BF),
        cost_estimate=cost(13),
        name="merge_branches",
    )(attended, hidden, w_merge, w_down, stream, flag)


def back_through(grad, stacked, slope):
    tokens = grad.shape[0]
    shards, units, cols = stacked.shape
    if cols % 128:
        split = grad.reshape(tokens, shards, cols)
        total = jnp.einsum("tnd,nfd->tf", split, stacked, preferred_element_type=F32)
        return (total if slope is None else total * slope.astype(F32)).astype(BF)

    def kernel(*refs):
        g, w = refs[:2]
        out, acc = refs[-2:]
        n = pl.program_id(0)
        part = dot_cols(g[...], w[0])

        @pl.when(n == 0)
        def _():
            acc[...] = part

        @pl.when(n > 0)
        def _():
            acc[...] += part

        @pl.when(n == shards - 1)
        def _():
            total = acc[...]
            if slope is not None:
                total = total * refs[2][...].astype(F32)
            out[...] = total.astype(BF)

    specs = [
        pl.BlockSpec((tokens, cols), lambda n: (0, n)),
        pl.BlockSpec((1, units, cols), lambda n: (n, 0, 0)),
    ]
    args = [grad, stacked]
    if slope is not None:
        specs.append(pl.BlockSpec((tokens, units), lambda n: (0, 0)))
        args.append(slope)
    return pl.pallas_call(
        kernel,
        grid=(shards,),
        in_specs=specs,
        out_specs=pl.BlockSpec((tokens, units), lambda n: (0, 0)),
        out_shape=jax.ShapeDtypeStruct((tokens, units), BF),
        scratch_shapes=[pltpu.VMEM((tokens, units), F32)],
        cost_estimate=cost(13 if slope is not None else 7),
        name="back_through",
    )(*args)


def body(
    history,
    mixing,
    shard_offset,
    norm_gain,
    norm_bias,
    w_heads,
    w_merge,
    w_up,
    w_down,
    mixer_first,
    mixer_second,
    out_cotangent,
    next_cotangent,
):
    member = lax.axis_index("stream")
    members = lax.axis_size("stream")
    shards = lax.axis_size("dp")
    index = lax.axis_index("dp")
    entries, tokens, width = history.shape
    heads_here = w_heads.shape[2] // HD
    half = tokens // 2
    highest = lax.Precision.HIGHEST
    flag = (member == members - 1).astype(F32)
    flags = flag.reshape(1)
    near = shards == 8 and heads_here * 2 == shards and tokens * shards == 2 * SEQ

    if near:
        spread = jnp.broadcast_to(shard_offset[:, None], (8, 128))
        offsets = lax.all_gather(spread, "dp", axis=0)[:, 0, 0]
        w_heads = after(w_heads, offsets)
    got_heads = Gathered(w_heads, direct=near)
    lanes = jnp.concatenate([norm_gain, norm_bias]).astype(F32).reshape(tokens, -1)
    first_rows = mixer_first.astype(F32).reshape(tokens, -1)
    second_flat = mixer_second[:, 0, :].astype(F32).reshape(-1)
    hidden_count = mixer_second.shape[0]
    lines = -(-second_flat.shape[0] // tokens)
    second_rows = jnp.pad(second_flat, (0, lines * tokens - second_flat.shape[0]))
    outputs = next_cotangent.shape[2]
    arrays = [mixing[:, 0, :], lanes, next_cotangent[:, 0, :], first_rows]
    arrays.append(second_rows.reshape(tokens, lines))
    packed = lax.all_gather(jnp.concatenate(arrays, axis=1), "stream", axis=0)
    parts, place = [], 0
    for array in arrays:
        parts.append(packed[:, :, place : place + array.shape[1]])
        place += array.shape[1]
    mix_all, norms, next_full, first_full, second_full = parts
    norms = norms.reshape(members, 2, width)
    first_full = first_full.astype(BF).reshape(width, -1)
    second_full = second_full.reshape(members, -1)[:, : second_flat.shape[0]]
    second_full = second_full.reshape(members, hidden_count, outputs)
    if near:
        early = (got_heads.by_x, got_heads.by_y, got_heads.across)
        history = after(history, *early)
        w_up, w_merge = after(w_up, *early[:2]), after(w_merge, *early[:2])
    got_up = Gathered(w_up)
    got_merge = Gathered(w_merge, direct=near)
    gains, biases = norms[:, 0], norms[:, 1]
    mix_rows = jnp.transpose(mix_all, (1, 0, 2)).reshape(tokens, members * entries)

    normed, unit, inv, stream = make_streams(history, mix_rows, gains, biases)
    full_heads = got_heads.whole()
    cotangent = lax.all_gather(after(out_cotangent, inv), "stream", axis=1, tiled=True)
    positions = shard_offset[0] + jnp.arange(tokens, dtype=jnp.int32)
    projected = project(after(normed, got_up.by_x, got_up.by_y), full_heads, rope_tables(positions, 1.0))

    if near:
        side = (index % 2).astype(jnp.int32).reshape(1)
        place = jnp.arange(shards, dtype=jnp.int32)
        first_key = jnp.maximum(place - offsets // tokens, 0).astype(jnp.int32)
        own = lax.all_to_all(projected, "dp", 0, 0, tiled=True)
        got_down = Gathered(after(w_down, own))
        other = partner(own[:, 1:], 1)
        result, exact, level = attend(own, other, first_key, side)
        full_up = got_up.whole(result)
        full_merge = got_merge.whole(result)
        back = lax.all_to_all(result, "dp", 0, 0, tiled=True)
        attended = jnp.transpose(back.reshape(heads_here, tokens, HD), (1, 0, 2)).reshape(tokens, -1)
    else:
        got_down = Gathered(w_down)
        full_up = got_up.whole()
        full_merge = got_merge.whole()
        split = projected.reshape(heads_here, 2, 3, half, HD)
        split = jnp.transpose(split, (2, 1, 3, 0, 4)).reshape(3, tokens, heads_here, HD)
        result, kept = far_attend(split[0], split[1], split[2], shard_offset)
        attended = result.reshape(tokens, -1).astype(BF)
    full_down = got_down.whole(result)
    flat_up = full_up.reshape(width, -1)
    hidden, slope = hidden_units(normed[members - 1], flat_up)
    attended = after(attended, hidden)
    hidden = after(hidden, cotangent)
    share = merge_branches(attended, hidden, full_merge, full_down, stream, flags)

    columns = lax.all_to_all(share, "stream", 0, 0, tiled=True)
    block_out = jnp.sum(columns.astype(F32), axis=0).astype(BF)
    block_full = lax.all_gather(block_out, "stream", axis=1, tiled=True)
    out_float = block_full.astype(F32)
    scale = lax.rsqrt(jnp.sum(out_float * out_float, axis=-1) / width + 1e-06)
    proj = dot(block_full, first_full)
    mixer, mixer_back = jax.vjp(exact_gelu, scale[:, None] * proj)
    second_here = mixer_second[:, 0, :].astype(F32)
    next_here = jnp.dot(mixer, second_here, precision=highest, preferred_element_type=F32)
    mixer_grad = jnp.einsum(
        "stn,scn->tc", next_full, second_full, precision=highest, preferred_element_type=F32
    )
    pre_grad = mixer_back(mixer_grad)[0]
    proj_grad = (scale[:, None] * pre_grad).astype(BF)
    scale_grad = jnp.sum(pre_grad * proj, axis=-1)
    second_local = jnp.dot(
        mixer.T, next_cotangent[:, 0, :], precision=highest, preferred_element_type=F32
    )
    first_local = dot_rows(block_out, proj_grad)
    grad_out = (
        cotangent.astype(F32)
        + dot_cols(proj_grad, first_full)
        - (scale * scale * scale * scale_grad)[:, None] * out_float / width
    ).astype(BF)

    attended_grad = back_through(grad_out, full_merge, None)
    up_grad = back_through(grad_out, full_down, slope)
    down_grad = dot_rows(hidden, grad_out).astype(BF)
    grad_down = lax.psum_scatter(down_grad, "dp", scatter_dimension=1, tiled=True).astype(F32)
    last_normed = dot_cols(after(up_grad, down_grad), flat_up)
    last_share, last_stats = last_back(
        last_normed, unit[members - 1], inv, gains[members - 1 :], grad_out, flags
    )
    last_hop = line_hop(last_share, OUTWARD)
    last_sum = (last_share.astype(F32) + last_hop.astype(F32)).astype(BF)
    last_next = line_hop(last_sum, MIDDLE)
    if near:
        sent = attended_grad.reshape(tokens, heads_here, HD)
        sent = jnp.transpose(sent, (1, 0, 2)).reshape(shards, half, HD)
        grads = lax.all_to_all(sent, "dp", 0, 0, tiled=True)
        grads = after(grads, last_share)
        kept_grads, given = attend_back(own, other, grads, exact, level, first_key, side)
        taken = partner(given, 1)
        summed = kept_grads[:, 1:].astype(F32) + taken.astype(F32)
        pair = jnp.concatenate([kept_grads[:, :1], summed.astype(BF)], axis=1)
        pair = after(pair, last_hop)
        late_grad, late_up = after(grad_out, pair), after(up_grad, pair)
        up_back = dot_rows(normed[members - 1], late_up).astype(BF)
        merge_grad = dot_rows(attended, late_grad).astype(BF)
        parts = lax.all_to_all(pair, "dp", 0, 0, tiled=True)
    else:
        up_back = dot_rows(normed[members - 1], up_grad).astype(BF)
        merge_grad = dot_rows(attended, grad_out).astype(BF)
        grads = far_attend_back(split[0], attended_grad.reshape(tokens, heads_here, HD), kept)
        parts = grads.reshape(3, 2, half, heads_here, HD)
        parts = jnp.transpose(parts, (3, 1, 0, 2, 4)).reshape(2 * heads_here, 3, half, HD)

    parts = after(parts, last_sum, grad_down, up_back, merge_grad)
    spans = block_spans(tokens)
    *pieces, heads_share, heads_grad, heads_stats = heads_back(
        parts, full_heads, normed, unit, inv, gains, rope_tables(positions, -1.0), spans
    )

    grad_merge = lax.psum_scatter(merge_grad, "dp", scatter_dimension=1, tiled=True).astype(F32)
    grad_heads = lax.psum_scatter(heads_grad, "dp", scatter_dimension=1, tiled=True).astype(F32)
    grad_up = lax.psum_scatter(up_back, "dp", scatter_dimension=0, tiled=True).astype(F32)

    each = entries // members

    def weights_for(owner):
        block = lax.dynamic_slice_in_dim(mix_all, owner * each, each, axis=2)
        return jnp.transpose(block, (1, 2, 0)).reshape(tokens, each * members)

    there = weights_for(jnp.where(member == 1, 0, members - 1))
    here = weights_for(member)
    extra = {}

    last_one = lambda i: last_hop
    last_two = lambda i: last_next

    def first_hop(i, gates):
        gates = list(gates)
        if i == 3:
            gates.append(grad_merge)
        return gated(pieces[i], gates)

    def small_sums():
        stats = jnp.concatenate([heads_stats, last_stats[None]]).reshape(members, tokens, -1)
        both = jnp.concatenate([jnp.concatenate(mixes, axis=1), stats], axis=2)
        both = jnp.sum(lax.all_to_all(both, "stream", 0, 0, tiled=True), axis=0)
        second_sums = jnp.pad(second_local.reshape(-1), (0, lines * tokens - second_flat.shape[0]))
        local = [both[:, entries:], first_local.reshape(tokens, -1), second_sums.reshape(tokens, lines)]
        everyone = lax.all_gather(jnp.concatenate(local, axis=1), "dp", axis=0)
        return both[:, :entries], jnp.sum(everyone, axis=0)

    mixes = [mixing_back(heads_share, last_share, history, i, 2) for i in range(2)]

    extra["both"], extra["all"] = small_sums()

    def second_hop(i, one):
        load = (pieces[i].astype(F32) + one.astype(F32)).astype(BF)
        return after(load, *mixes) if i == 0 else load

    def third_hop(i, one, two):
        load = mix_block(spans[i][0], there, pieces[i], last_share, [two], [last_two(i)], None, None)
        return after(load, extra["both"]) if i == 2 else load

    def finish(i, one, two, three):
        if i == 3:
            three = after(three, grad_heads, extra["all"])
        extra["history"], token = mix_block(
            spans[i][0],
            here,
            pieces[i],
            last_share,
            [one, two],
            [last_one(i), last_two(i)],
            three,
            extra.get("history"),
        )
        return token

    along_line(len(spans), first_hop, second_hop, third_hop, finish)
    grad_history = extra["history"]

    grad_mixing = extra["both"][:, None, :]
    sums = extra["all"]
    columns = 2 * width // tokens
    stats = sums[:, :columns].reshape(2, width)
    grad_first = sums[:, columns:-lines].reshape(mixer_first.shape)
    grad_second = sums[:, -lines:].reshape(-1)[: second_flat.shape[0]].reshape(hidden_count, outputs)
    return (
        block_out,
        next_here[:, None, :],
        grad_history,
        grad_mixing,
        stats[:1],
        stats[1:],
        grad_heads,
        grad_merge,
        grad_up,
        grad_down,
        grad_first,
        grad_second[:, None, :],
    )


def solution(mesh):
    in_specs = (
        P(None, "dp", None),
        P("dp", "stream", None),
        P("dp"),
        P("stream", None),
        P("stream", None),
        P(None, "dp", "stream"),
        P("stream", "dp"),
        P("dp", "stream"),
        P("stream", "dp"),
        P("stream", None),
        P(None, "stream", None),
        P("dp", "stream"),
        P("dp", "stream", None),
    )
    out_specs = (
        P("dp", "stream"),
        P("dp", "stream", None),
        P("stream", "dp", None),
        P("dp", "stream", None),
        P("stream", None),
        P("stream", None),
        P(None, "dp", "stream"),
        P("stream", "dp"),
        P("dp", "stream"),
        P("stream", "dp"),
        P("stream", None),
        P(None, "stream", None),
    )
    return jax.shard_map(body, mesh=mesh, in_specs=in_specs, out_specs=out_specs, check_vma=False)
```
